32 devices in a mesh: tok: 16 (over z, x, core), ffn: 2 (over y).
Axes of the slice: x: 2, y: 2, z: 4, core: 2. Of those that a mesh axis runs over, the one named last changes fastest.
Arguments:
- tokens: bfloat16 [16384, 768], P(('tok', 'ffn')), may hold values from -6 to 6
- rel_ids: int32 [32, 512, 512], P(('tok', 'ffn')), may hold values from 1 to 511, as said below
- mask_pos: int32 [32, 80], P(('tok', 'ffn')), may hold values from -1 to 511, as said below
- grad_vals: bfloat16 [32, 80, 768], P(('tok', 'ffn')), may hold values from -6 to 6
- w_query: bfloat16 [768, 768], replicated, may hold values from -0.21875 to 0.21875
- w_key: bfloat16 [768, 768], replicated, may hold values from -0.21875 to 0.21875
- w_value: bfloat16 [768, 768], replicated, may hold values from -0.21875 to 0.21875
- w_out: bfloat16 [768, 768], replicated, may hold values from -3 to 3
- b_query: float32 [768], replicated, may hold values from -3 to 3
- b_key: float32 [768], replicated, may hold values from -3 to 3
- b_value: float32 [768], replicated, may hold values from -3 to 3
- b_out: float32 [768], replicated, may hold values from -3 to 3
- rel_table: bfloat16 [512, 768], replicated, may hold values from -6 to 6
- ln1_gain: float32 [768], replicated, may hold values from 0.5 to 1.5
- ln1_bias: float32 [768], replicated, may hold values from -2 to 2
- w_in: bfloat16 [768, 3072], P(None, 'ffn'), may hold values from -0.21875 to 0.21875
- b_in: float32 [3072], P('ffn'), may hold values from -3 to 3
- w_down: bfloat16 [3072, 768], P('ffn'), may hold values from -0.109375 to 0.109375
- b_down: float32 [768], replicated, may hold values from -2 to 2
- ln2_gain: float32 [768], replicated, may hold values from 0.5 to 1.5
- ln2_bias: float32 [768], replicated, may hold values from -2 to 2
Outputs:
- output: bfloat16 [16384, 768], P(('tok', 'ffn'))
- grad_tokens: float32 [16384, 768], P(('tok', 'ffn'))
- grad_w_query: float32 [768, 768], P(('tok', 'ffn'))
- grad_w_key: float32 [768, 768], P(('tok', 'ffn'))
- grad_w_value: float32 [768, 768], P(('tok', 'ffn'))
- grad_w_out: float32 [768, 768], P(('tok', 'ffn'))
- grad_b_query: float32 [768], P(('tok', 'ffn'))
- grad_b_key: float32 [768], P(('tok', 'ffn'))
- grad_b_value: float32 [768], P(('tok', 'ffn'))
- grad_b_out: float32 [768], P(('tok', 'ffn'))
- grad_rel_table: float32 [512, 768], P(('tok', 'ffn'))
- grad_ln1_gain: float32 [768], P(('tok', 'ffn'))
- grad_ln1_bias: float32 [768], P(('tok', 'ffn'))
- grad_w_in: float32 [768, 3072], P('tok', 'ffn')
- grad_b_in: float32 [2, 1536], P('ffn', 'tok')
- grad_w_down: float32 [3072, 768], P('ffn', 'tok')
- grad_b_down: float32 [768], P(('tok', 'ffn'))
- grad_ln2_gain: float32 [768], P(('tok', 'ffn'))
- grad_ln2_bias: float32 [768], P(('tok', 'ffn'))
The draws below stay inside these ranges and needn't reach their ends.
Inputs may be any that keep to these rules, and one draw needn't show every extreme that they name: `mask_pos`: row s names distinct positions of sequence s in its first slots and -1 in the others; each row names 64 to 80 positions, and some row names 80. rel_ids[s, i, j] = 256 + the DeBERTa log bucket (identity up to 128, logarithmic beyond, maximum position 512) of p_i - p_j, where p_i counts word starts before token i of sequence s, tokens of one word sharing it; so rel_ids[s, j, i] = 512 - rel_ids[s, i, j].
All inputs are finite; a program needn't handle non-finite values.
Results may differ from the reference program's by a relative error of at most 0.034.
Values may be sent and summed in bfloat16 or wider, within the bound.
No kernel may reach another device: no remote copies, remote signals or barrier semaphores. Data moves between devices by JAX's collectives and lax.ppermute only.
A program may use at most 256 MiB of HBM per device.

```python
import math
from functools import partial
import jax
import jax.numpy as jnp
import numpy as np
from jax import lax

D = 768
H = 12
DH = 64
FF = 3072
BUCK = 256
SEQ = 512
MS = 80
FFC = 1536
SEQS = 32
TOKENS = 16384
N_FFN = 2


def bucket_table():
    middle = BUCK // 2
    entries = []
    for offset in range(-(SEQ - 1), SEQ):
        magnitude = abs(offset)
        if magnitude <= middle:
            entries.append(offset)
        else:
            logged = int(math.ceil(math.log(magnitude / middle) / math.log((2 * BUCK - 1) / middle) * (middle - 1))) + middle
            entries.append(logged if offset > 0 else -logged)
    return np.array(entries, dtype=np.int32)


def draw_rel_ids(key, part):
    starts = jax.random.randint(jax.random.fold_in(key, 11), (SEQS, SEQ), 0, 4)
    begins = jnp.where(starts > 0, 1, 0).astype(jnp.int32)
    begins = begins.at[0, :].set(1)
    begins = begins.at[:, 0].set(0)
    places = jnp.cumsum(begins, axis=1)
    differ = places[:, :, None] - places[:, None, :]
    table = jnp.asarray(bucket_table())
    return (jnp.take(table, differ + SEQ - 1) + BUCK).astype(jnp.int32)


def permute_one(single_key):
    return jax.random.permutation(single_key, SEQ)


def draw_mask_pos(key, part):
    key_perm = jax.random.fold_in(key, 21)
    key_count = jax.random.fold_in(key, 22)
    key_full = jax.random.fold_in(key, 23)
    orders = jax.vmap(permute_one)(jax.random.split(key_perm, SEQS))
    counts = jax.random.randint(key_count, (SEQS,), MS - MS // 5, MS + 1)
    fullest = jax.random.randint(key_full, (), 0, SEQS)
    counts = counts.at[fullest].set(MS)
    slot_ids = jnp.arange(MS, dtype=jnp.int32)
    return jnp.where(slot_ids[None, :] < counts[:, None], orders[:, :MS], -1).astype(jnp.int32)


def shard_levels(rng, dims, pieces, least, top_value):
    factor_of, own = 1.0, jax.random.fold_in(rng, 6)
    for dim, shards_of in pieces:
        heights = jnp.exp(jax.random.uniform(jax.random.fold_in(own, dim), (shards_of,), jnp.float32, least / len(pieces), top_value / len(pieces)))
        factor_of = factor_of * jnp.repeat(heights, dims[dim] // shards_of).reshape([-1 if axis == dim else 1 for axis in range(len(dims))])
    return factor_of


def noise(stream_key, extent, width, reach, cuts=(), kind=jnp.bfloat16):
    gain = shard_levels(stream_key, extent, cuts, -0.22, 0.18) if cuts else 1.0
    drawn = jax.random.normal(stream_key, extent, jnp.float32) * width * gain
    return jnp.minimum(jnp.maximum(drawn, -reach), reach).astype(kind)


def setup_inputs(seed: int = 0) -> dict:
    key_of = jax.random.split(jax.random.key(seed), 22)
    return {
        "tokens": noise(key_of[0], (TOKENS, D), 1.0, 6.0, ((0, 32),)),
        "rel_ids": draw_rel_ids(jax.random.fold_in(key_of[21], 71), 0),
        "mask_pos": draw_mask_pos(jax.random.fold_in(key_of[21], 71), 0),
        "grad_vals": noise(key_of[3], (SEQS, MS, D), 1.0, 6.0, ((0, 32),)),
        "w_query": noise(key_of[4], (D, D), D ** -0.5, 0.21875),
        "w_key": noise(key_of[5], (D, D), D ** -0.5, 0.21875),
        "w_value": noise(key_of[6], (D, D), D ** -0.5, 0.21875),
        "w_out": noise(key_of[7], (D, D), (max(1, 3 * D // SEQ)) ** -0.5, 3.0),
        "b_query": noise(key_of[8], (D,), 0.5, 3.0, (), jnp.float32),
        "b_key": noise(key_of[9], (D,), 0.5, 3.0, (), jnp.float32),
        "b_value": noise(key_of[10], (D,), 0.5, 3.0, (), jnp.float32),
        "b_out": noise(key_of[11], (D,), 0.5, 3.0, (), jnp.float32),
        "rel_table": noise(key_of[12], (2 * BUCK, D), 1.0, 6.0),
        "ln1_gain": jnp.clip(1.0 + 0.1 * jax.random.normal(key_of[13], (D,), jnp.float32), 0.5, 1.5),
        "ln1_bias": noise(key_of[14], (D,), 0.3, 2.0, (), jnp.float32),
        "w_in": noise(key_of[15], (D, FF), D ** -0.5, 0.21875, ((1, 2),)),
        "b_in": noise(key_of[16], (FF,), 0.5, 3.0, ((0, 2),), jnp.float32),
        "w_down": noise(key_of[17], (FF, D), FF ** -0.5, 0.109375, ((0, 2),)),
        "b_down": noise(key_of[18], (D,), 0.3, 2.0, (), jnp.float32),
        "ln2_gain": jnp.clip(1.0 + 0.1 * jax.random.normal(key_of[19], (D,), jnp.float32), 0.5, 1.5),
        "ln2_bias": noise(key_of[20], (D,), 0.3, 2.0, (), jnp.float32),
    }


norm_eps = 1e-07
highest = lax.Precision.HIGHEST

@jax.custom_vjp
def low(v):
    return lax.optimization_barrier(v.astype(jnp.bfloat16)).astype(jnp.float32)

@jax.custom_vjp
def low_back(v):
    return v

def low_keep(v):
    return (low(v), None)

def low_pass(kept, grad):
    return (grad,)

def back_keep(v):
    return (v, None)

def back_low(kept, grad):
    return (low(grad),)
low.defvjp(low_keep, low_pass)
low_back.defvjp(back_keep, back_low)

def exact_dot(first_op, second_op):
    return jnp.dot(first_op, second_op, precision=highest, preferred_element_type=jnp.float32)

def layer_norm(values, norm_gain, norm_bias):
    centered = values - lax.optimization_barrier(jnp.mean(values, axis=-1, keepdims=True))
    variance = lax.optimization_barrier(jnp.mean(centered * centered, axis=-1, keepdims=True))
    return centered * lax.rsqrt(variance + norm_eps) * norm_gain + norm_bias

def block_forward(weights, pos_query, pos_key, block_rows, block_ids):
    w_query, w_key, w_value, w_out, b_query, b_key, b_value, b_out, ln1_gain, ln1_bias, w_in, b_in, w_down, b_down, ln2_gain, ln2_bias = weights
    group_size = block_ids.shape[0]
    flat_rows = block_rows.reshape(group_size * SEQ, D)
    queries = low_back(low(exact_dot(flat_rows, w_query) + b_query)).reshape(group_size, SEQ, H, DH)
    key_rows = low_back(low(exact_dot(flat_rows, w_key) + b_key)).reshape(group_size, SEQ, H, DH)
    value_rows = low_back(low(exact_dot(flat_rows, w_value) + b_value)).reshape(group_size, SEQ, H, DH)
    pos_key_h = pos_key.reshape(2 * BUCK, H, DH)
    pos_query_h = pos_query.reshape(2 * BUCK, H, DH)
    direct = low_back(jnp.einsum('gihd,gjhd->ghij', queries, key_rows, precision=highest))
    to_pos = low_back(jnp.einsum('gihd,rhd->ghir', queries, pos_key_h, precision=highest))
    from_pos = low_back(jnp.einsum('gjhd,rhd->ghjr', key_rows, pos_query_h, precision=highest))
    take_index = jnp.broadcast_to(block_ids[:, None], (group_size, H, SEQ, SEQ))
    picked = jnp.take_along_axis(to_pos, take_index, axis=3)
    mirrored = jnp.swapaxes(jnp.take_along_axis(from_pos, take_index, axis=3), 2, 3)
    scores = (direct + picked + mirrored) * (1.0 / math.sqrt(3.0 * DH))
    attn_probs = low(jax.nn.softmax(scores, axis=3))
    mixed_ctx = low_back(low(jnp.einsum('ghij,gjhd->gihd', attn_probs, value_rows, precision=highest)))
    context = mixed_ctx.reshape(group_size * SEQ, D)
    attn_out = low_back(exact_dot(context, w_out) + b_out)
    middle = layer_norm(flat_rows + attn_out, ln1_gain, ln1_bias)
    pre_act = low_back(exact_dot(low(middle), w_in) + b_in)
    hidden = low(jax.nn.gelu(pre_act, approximate=False))
    branch = low_back(exact_dot(hidden, w_down) + b_down)
    return layer_norm(middle + branch, ln2_gain, ln2_bias).reshape(group_size, SEQ, D)

def reference(tokens, rel_ids, mask_pos, grad_vals, w_query, w_key, w_value, w_out, b_query, b_key, b_value, b_out, rel_table, ln1_gain, ln1_bias, w_in, b_in, w_down, b_down, ln2_gain, ln2_bias):
    floats = [item.astype(jnp.float32) for item in (tokens, w_query, w_key, w_value, w_out, b_query, b_key, b_value, b_out, rel_table, ln1_gain, ln1_bias, w_in, b_in, w_down, b_down, ln2_gain, ln2_bias)]

    def forward(x_rows, wq_f, wk_f, wv_f, wo_f, bq_f, bk_f, bv_f, bo_f, table_f, g1_f, c1_f, win_f, bin_f, wdown_f, bdown_f, g2_f, c2_f):
        pos_query = low(exact_dot(table_f, wq_f) + bq_f)
        pos_key = low(exact_dot(table_f, wk_f) + bk_f)
        weights = (wq_f, wk_f, wv_f, wo_f, bq_f, bk_f, bv_f, bo_f, g1_f, c1_f, win_f, bin_f, wdown_f, bdown_f, g2_f, c2_f)
        block_step = jax.checkpoint(partial(block_forward, weights, pos_query, pos_key))
        blocks = x_rows.reshape(SEQS // 8, 8, SEQ, D)
        id_blocks = rel_ids.reshape(SEQS // 8, 8, SEQ, SEQ)

        def scan_step(carried, inputs):
            return (carried, block_step(inputs[0], inputs[1]))
        _, outputs = lax.scan(scan_step, jnp.zeros((), jnp.float32), (blocks, id_blocks))
        return outputs.reshape(TOKENS, D)
    positions = jnp.arange(SEQ, dtype=jnp.int32)
    one_hot = (mask_pos[:, :, None] == positions[None, None, :]).astype(jnp.float32)
    cotangent = jnp.einsum('smt,smd->std', one_hot, grad_vals.astype(jnp.float32), precision=highest).reshape(TOKENS, D)
    result, pullback = jax.vjp(forward, *floats)
    gradients = pullback(cotangent)
    g_tokens, g_wq, g_wk, g_wv, g_wo, g_bq, g_bk, g_bv, g_bo, g_table, g_g1, g_c1, g_win, g_bin, g_wdown, g_bdown, g_g2, g_c2 = gradients
    return (result.astype(jnp.bfloat16), g_tokens, g_wq, g_wk, g_wv, g_wo, g_bq, g_bk, g_bv, g_bo, g_table, g_g1, g_c1, g_win, g_bin.reshape(N_FFN, FFC), g_wdown, g_bdown, g_g2, g_c2)
```

```python
import math

import numpy as np

import jax
import jax.numpy as jnp
from jax import lax
from jax.experimental import pallas as pl
from jax.experimental.pallas import tpu as pltpu
from jax.sharding import PartitionSpec as P

HEAD = 64
LANES = 128
ROWS = 32
norm_eps = 1e-07
bf16 = jnp.bfloat16
f32 = jnp.float32


def dot_nn(first_op, second_op):
    return lax.dot_general(
        first_op, second_op, (((1,), (0,)), ((), ())), preferred_element_type=f32
    )


def dot_nt(first_op, second_op):
    return lax.dot_general(
        first_op, second_op, (((1,), (1,)), ((), ())), preferred_element_type=f32
    )


def dot_tn(first_op, second_op):
    return lax.dot_general(
        first_op, second_op, (((0,), (0,)), ((), ())), preferred_element_type=f32
    )


def distance_rows(seq_len, table_rows):
    side = table_rows // 2
    middle = side // 2
    rows = []
    for m in range(2 * seq_len):
        offset = max(seq_len - 1 - m, 1 - seq_len)
        size = abs(offset)
        if size > middle:
            ratio = math.log(size / middle) / math.log((2 * side - 1) / middle)
            size = int(math.ceil(ratio * (middle - 1))) + middle
        rows.append(side + (size if offset > 0 else -size))
    return np.array(rows, dtype=np.int32)


def lane_iota(rows=1):
    return lax.broadcasted_iota(jnp.int32, (rows, LANES), 1)


def member_chunk(words, c):
    return (words == lane_iota(words.shape[0]) + c * LANES).astype(f32).astype(bf16)


def shift_in_order(source, words_ref, base, emit):
    seq = words_ref.shape[0]
    chunks = seq // LANES
    lane = lane_iota()
    for g in range(chunks):
        first = base[g]
        for sub in range(LANES // ROWS):
            start = g * LANES + sub * ROWS
            rows = slice(start, start + ROWS)
            place = lane + (seq - 1) - words_ref[rows, :] - first * LANES
            index = place & (LANES - 1)
            turned = []
            for c in range(chunks + 2):
                at = pl.multiple_of(jnp.minimum(first + c, 2 * chunks - 1) * LANES, LANES)
                turned.append(
                    jnp.take_along_axis(source[rows, pl.ds(at, LANES)], index, axis=1)
                )
            near = place < LANES
            mid = place < 2 * LANES
            for c in range(chunks):
                value = jnp.where(
                    near, turned[c], jnp.where(mid, turned[c + 1], turned[c + 2])
                )
                emit(rows, c, value)


def unshift_in_order(source, words_ref, base, dest):
    seq = words_ref.shape[0]
    chunks = seq // LANES
    lane = lane_iota()
    zero = jnp.zeros((ROWS, LANES), f32)
    for g in range(chunks):
        first = base[g]
        for sub in range(LANES // ROWS):
            start = g * LANES + sub * ROWS
            rows = slice(start, start + ROWS)
            place = lane - (seq - 1) + words_ref[rows, :] + first * LANES
            index = place & (LANES - 1)
            turned = [
                jnp.take_along_axis(
                    source[rows, c * LANES : (c + 1) * LANES], index, axis=1
                )
                for c in range(chunks)
            ]

            def pick(c):
                return turned[c] if 0 <= c < chunks else zero

            near = place >= 0
            mid = place >= -LANES
            for c in range(chunks + 2):
                value = jnp.where(near, pick(c), jnp.where(mid, pick(c - 1), pick(c - 2)))
                at = pl.multiple_of((first + c) * LANES, LANES)
                dest[rows, pl.ds(at, LANES)] = value.astype(bf16)


def group_bases(words, base):
    seq = words.shape[0]
    for g in range(seq // LANES):
        top = jnp.max(words[g * LANES : (g + 1) * LANES])
        base[g] = (seq - 1 - top) // LANES


def split_store(dest, rows, upper_at, lower_at, value):
    upper = value.astype(bf16)
    dest[rows, upper_at : upper_at + LANES] = upper
    dest[rows, lower_at : lower_at + LANES] = (value - upper.astype(f32)).astype(bf16)


def softmax_rows(scores):
    factor = math.log2(math.e) / math.sqrt(3.0 * HEAD)
    weights = jnp.exp2((scores - jnp.max(scores, axis=1, keepdims=True)) * factor)
    return (weights * (1.0 / jnp.sum(weights, axis=1, keepdims=True))).astype(bf16)


def picked_kernel(
    rel_ref, pick_ref, qc_ref, k_ref, v_ref, pk_ref, pq_ref,
    ctx_ref, prob_ref, keyrow_ref, word_ref, wordc_ref,
    left, right, crel, base,
):
    seq = k_ref.shape[0]
    picks = qc_ref.shape[0]
    chunks = seq // LANES
    at = [LANES + n * seq for n in range(4)]

    @pl.when(pl.program_id(0) == 0)
    def _():
        row = lax.broadcasted_iota(jnp.int32, (seq, seq), 0)
        col = lax.broadcasted_iota(jnp.int32, (seq, seq), 1)
        side = pk_ref.shape[0] // 4
        step = jnp.sum(jnp.where(col == row - 1, rel_ref[...] - side, 0), axis=1, keepdims=True)
        steps = jnp.broadcast_to(step.astype(f32), (seq, LANES)).astype(bf16)
        words = dot_nn((col <= row).astype(f32).astype(bf16), steps).astype(jnp.int32)
        word_ref[...] = words
        group_bases(words, base)
        for c in range(chunks):
            member = member_chunk(words, c)
            right[:, at[0] + c * LANES : at[0] + (c + 1) * LANES] = member
            right[:, at[1] + c * LANES : at[1] + (c + 1) * LANES] = member
        memberc = dot_nn(pick_ref[...], right[:, at[0] : at[1]])
        left[:, at[2] : at[3]] = memberc.astype(bf16)
        left[:, at[3] : at[3] + seq] = memberc.astype(bf16)
        index = lax.broadcasted_iota(jnp.int32, (picks, seq), 1).astype(f32)
        total = jnp.sum(memberc * index, axis=1, keepdims=True)
        wordc_ref[...] = jnp.broadcast_to(total, (picks, LANES)).astype(jnp.int32)

    lane = lane_iota()
    zero = jnp.zeros((), bf16)
    for a in range(2):
        mine = (lane < HEAD) if a == 0 else (lane >= HEAD)
        q_a = jnp.where(mine, qc_ref[...], zero)
        k_a = jnp.where(mine, k_ref[...], zero)
        left[:, :LANES] = q_a
        right[:, :LANES] = k_a
        crel[...] = dot_nt(k_a, pq_ref[...])
        far = dot_nt(q_a, pk_ref[...])

        def emit(rows, c, value):
            split_store(right, rows, at[2] + c * LANES, at[3] + c * LANES, value)

        shift_in_order(crel, word_ref, base, emit)
        keyrow_ref[a] = right[:, at[2] :]
        place = lane + (seq - 1) - wordc_ref[...]
        index = place & (LANES - 1)
        turned = [
            jnp.take_along_axis(far[:, c * LANES : (c + 1) * LANES], index, axis=1)
            for c in range(2 * chunks)
        ]
        for c in range(chunks):
            value = turned[c]
            for n in range(1, chunks + 1):
                if c + n < 2 * chunks:
                    value = jnp.where(place >= n * LANES, turned[c + n], value)
            split_store(left, slice(None), at[0] + c * LANES, at[1] + c * LANES, value)
        probs = softmax_rows(dot_nt(left[...], right[...]))
        prob_ref[a] = probs
        mixed = dot_nn(probs, v_ref[...]).astype(bf16)
        if a == 0:
            ctx_ref[...] = mixed
        else:
            ctx_ref[...] = jnp.where(mine, mixed, ctx_ref[...])


def attend_picked(rel_ids, pick, q_pick, k, v, pos_query, pos_key):
    seq, width = k.shape
    picks = q_pick.shape[0]
    pairs = width // LANES
    wide = LANES + 4 * seq
    whole = lambda rows, cols: pl.BlockSpec((rows, cols), lambda h: (0, 0))
    col = lambda rows: pl.BlockSpec((rows, LANES), lambda h: (0, h))
    return pl.pallas_call(
        picked_kernel,
        grid=(pairs,),
        in_specs=[
            whole(seq, seq), whole(picks, seq),
            col(picks), col(seq), col(seq), col(2 * seq), col(2 * seq),
        ],
        out_specs=[
            col(picks),
            pl.BlockSpec((2, picks, seq), lambda h: (h, 0, 0)),
            pl.BlockSpec((2, seq, 2 * seq), lambda h: (h, 0, 0)),
            whole(seq, LANES), whole(picks, LANES),
        ],
        out_shape=[
            jax.ShapeDtypeStruct((picks, width), bf16),
            jax.ShapeDtypeStruct((2 * pairs, picks, seq), bf16),
            jax.ShapeDtypeStruct((2 * pairs, seq, 2 * seq), bf16),
            jax.ShapeDtypeStruct((seq, LANES), jnp.int32),
            jax.ShapeDtypeStruct((picks, LANES), jnp.int32),
        ],
        scratch_shapes=[
            pltpu.VMEM((picks, wide), bf16),
            pltpu.VMEM((seq, wide), bf16),
            pltpu.VMEM((seq, 2 * seq), f32),
            pltpu.SMEM((seq // LANES,), jnp.int32),
        ],
        compiler_params=pltpu.CompilerParams(vmem_limit_bytes=48 * 2**20),
        name="attend_picked",
    )(rel_ids, pick, q_pick, k, v, pos_key, pos_query)


def full_kernel(
    word_ref, q_ref, k_ref, v_ref, pk_ref, keyrow_ref, ctx_ref, left, right, crel, base
):
    seq = q_ref.shape[0]
    chunks = seq // LANES
    at = [LANES + n * seq for n in range(4)]

    @pl.when(pl.program_id(0) == 0)
    def _():
        words = word_ref[...]
        group_bases(words, base)
        for c in range(chunks):
            member = member_chunk(words, c)
            for ref, n in ((right, 0), (right, 1), (left, 2), (left, 3)):
                ref[:, at[n] + c * LANES : at[n] + (c + 1) * LANES] = member

    lane = lane_iota()
    zero = jnp.zeros((), bf16)
    for a in range(2):
        mine = (lane < HEAD) if a == 0 else (lane >= HEAD)
        q_a = jnp.where(mine, q_ref[...], zero)
        left[:, :LANES] = q_a
        right[:, :LANES] = k_ref[...]
        right[:, at[2] :] = keyrow_ref[a]
        crel[...] = dot_nt(q_a, pk_ref[...])

        def emit(rows, c, value):
            split_store(left, rows, at[0] + c * LANES, at[1] + c * LANES, value)

        shift_in_order(crel, word_ref, base, emit)
        for g in range(chunks):
            rows = slice(g * LANES, (g + 1) * LANES)
            probs = softmax_rows(dot_nt(left[rows, :], right[...]))
            mixed = dot_nn(probs, v_ref[...]).astype(bf16)
            if a == 0:
                ctx_ref[rows, :] = mixed
            else:
                ctx_ref[rows, :] = jnp.where(mine, mixed, ctx_ref[rows, :])


def attend_full(words, q, k, v, pos_key, keyrows):
    seq, width = k.shape
    pairs = width // LANES
    wide = LANES + 4 * seq
    col = lambda rows: pl.BlockSpec((rows, LANES), lambda h: (0, h))
    return pl.pallas_call(
        full_kernel,
        grid=(pairs,),
        in_specs=[
            pl.BlockSpec((seq, LANES), lambda h: (0, 0)),
            col(seq), col(seq), col(seq), col(2 * seq),
            pl.BlockSpec((2, seq, 2 * seq), lambda h: (h, 0, 0)),
        ],
        out_specs=col(seq),
        out_shape=jax.ShapeDtypeStruct((seq, width), bf16),
        scratch_shapes=[
            pltpu.VMEM((seq, wide), bf16),
            pltpu.VMEM((seq, wide), bf16),
            pltpu.VMEM((seq, 2 * seq), f32),
            pltpu.SMEM((seq // LANES,), jnp.int32),
        ],
        compiler_params=pltpu.CompilerParams(vmem_limit_bytes=48 * 2**20),
        name="attend_full",
    )(words, q, k, v, pos_key, keyrows)


def back_kernel(
    word_ref, wordc_ref, qc_ref, k_ref, v_ref, dctx_ref, prob_ref, pk_ref, pq_ref,
    dq_ref, dk_ref, dv_ref, dpk_ref, dpq_ref,
    side, sidec, moved, movedc, grel, base,
):
    seq = k_ref.shape[0]
    picks = qc_ref.shape[0]
    chunks = seq // LANES

    @pl.when(pl.program_id(0) == 0)
    def _():
        words = word_ref[...]
        for c in range(chunks):
            side[:, c * LANES : (c + 1) * LANES] = member_chunk(words, c)
            sidec[:, c * LANES : (c + 1) * LANES] = member_chunk(wordc_ref[...], c)
        group_bases(words, base)
        moved[...] = jnp.zeros_like(moved)

    lane = lane_iota()
    scale = 1.0 / math.sqrt(3.0 * HEAD)
    zero = jnp.zeros((), bf16)
    for a in range(2):
        mine = (lane < HEAD) if a == 0 else (lane >= HEAD)
        keep = lambda value: jnp.where(mine, value, zero)
        dctx_a = keep(dctx_ref[...])
        q_a = keep(qc_ref[...])
        k_a = keep(k_ref[...])
        side[:, seq:] = k_a
        sidec[:, seq:] = q_a
        dprobs = dot_nt(dctx_a, v_ref[...])
        probs = prob_ref[a].astype(f32)
        prod = probs * dprobs
        gs = ((prod - probs * jnp.sum(prod, axis=1, keepdims=True)) * scale).astype(bf16)
        dv = dot_tn(prob_ref[a], dctx_a)

        out = dot_nn(gs, side[...])
        place = lane - (seq - 1) + wordc_ref[...]
        index = place & (LANES - 1)
        turned = [
            jnp.take_along_axis(out[:, c * LANES : (c + 1) * LANES], index, axis=1)
            for c in range(chunks)
        ]
        blank = jnp.zeros((picks, LANES), f32)
        for c in range(2 * chunks):
            value = turned[c] if c < chunks else blank
            for n in range(1, chunks + 1):
                other = turned[c - n] if 0 <= c - n < chunks else blank
                value = jnp.where(place < -LANES * (n - 1), other, value)
            movedc[:, c * LANES : (c + 1) * LANES] = value.astype(bf16)
        dq = out[:, seq:] + dot_nn(movedc[...], keep(pk_ref[...]))
        dpk = dot_tn(movedc[...], q_a)

        out = dot_tn(gs, sidec[...])
        grel[...] = out[:, :seq]
        unshift_in_order(grel, word_ref, base, moved)
        dk = out[:, seq:] + dot_nn(moved[:, : 2 * seq], keep(pq_ref[...]))
        dpq = dot_tn(moved[:, : 2 * seq], k_a)
        for ref, value in (
            (dq_ref, dq), (dk_ref, dk), (dv_ref, dv), (dpk_ref, dpk), (dpq_ref, dpq),
        ):
            low = value.astype(bf16)
            ref[...] = low if a == 0 else jnp.where(mine, low, ref[...])


def attend_back(words, words_pick, q_pick, k, v, dctx, probs, pos_query, pos_key):
    seq, width = k.shape
    picks = q_pick.shape[0]
    pairs = width // LANES
    whole = lambda rows, cols: pl.BlockSpec((rows, cols), lambda h: (0, 0))
    col = lambda rows: pl.BlockSpec((rows, LANES), lambda h: (0, h))
    shape = lambda rows: jax.ShapeDtypeStruct((rows, width), bf16)
    return pl.pallas_call(
        back_kernel,
        grid=(pairs,),
        in_specs=[
            whole(seq, LANES), whole(picks, LANES),
            col(picks), col(seq), col(seq), col(picks),
            pl.BlockSpec((2, picks, seq), lambda h: (h, 0, 0)),
            col(2 * seq), col(2 * seq),
        ],
        out_specs=[col(picks), col(seq), col(seq), col(2 * seq), col(2 * seq)],
        out_shape=[shape(picks), shape(seq), shape(seq), shape(2 * seq), shape(2 * seq)],
        scratch_shapes=[
            pltpu.VMEM((seq, seq + LANES), bf16),
            pltpu.VMEM((picks, seq + LANES), bf16),
            pltpu.VMEM((seq, 2 * seq + LANES), bf16),
            pltpu.VMEM((picks, 2 * seq), bf16),
            pltpu.VMEM((seq, seq), f32),
            pltpu.SMEM((seq // LANES,), jnp.int32),
        ],
        compiler_params=pltpu.CompilerParams(vmem_limit_bytes=48 * 2**20),
        name="attend_back",
    )(words, words_pick, q_pick, k, v, dctx, probs, pos_key, pos_query)


def norm_stats(values):
    centered = values - jnp.mean(values, axis=1, keepdims=True)
    inv_std = lax.rsqrt(jnp.mean(centered * centered, axis=1, keepdims=True) + norm_eps)
    return centered * inv_std, inv_std


def norm_backward(upstream, normed, inv_std, norm_gain):
    scaled = upstream * norm_gain
    adjusted = (
        scaled
        - jnp.mean(scaled, axis=1, keepdims=True)
        - normed * jnp.mean(scaled * normed, axis=1, keepdims=True)
    )
    return (inv_std * adjusted, jnp.sum(upstream * normed, axis=0), jnp.sum(upstream, axis=0))


def normal_cdf(pre_act):
    return 0.5 * (1.0 + lax.erf(pre_act * (1.0 / math.sqrt(2.0))))


def swap(values, axis, bit):
    size = lax.axis_size(axis)
    return lax.ppermute(values, axis, [(n, n ^ bit) for n in range(size)])


def halve_over(values, axis):
    size = lax.axis_size(axis)
    me = lax.axis_index(axis)
    bit = 1
    while bit < size:
        mine = (me // bit) % 2
        view = values.reshape((values.shape[0] // 2, 2) + values.shape[1:])
        send = lax.dynamic_index_in_dim(view, 1 - mine, 1, keepdims=False)
        keep = lax.dynamic_index_in_dim(view, mine, 1, keepdims=False)
        values = (keep.astype(f32) + swap(send, axis, bit).astype(f32)).astype(bf16)
        bit *= 2
    return values[0]


def local(
    tokens, rel_ids, mask_pos, grad_vals, w_query, w_key, w_value, w_out, b_query, b_key,
    b_value, b_out, rel_table, ln1_gain, ln1_bias, w_in, b_in, w_down, b_down, ln2_gain, ln2_bias,
):
    seq_count, seq_len = rel_ids.shape[0], rel_ids.shape[1]
    rows_here, width = tokens.shape
    table_rows = rel_table.shape[0]
    hidden_cols = w_in.shape[1]
    slots = mask_pos.shape[1]
    n_tok = lax.axis_size("tok")
    n_ffn = lax.axis_size("ffn")
    low = lambda value: value.astype(bf16)

    q = low(dot_nn(tokens, w_query) + b_query)
    k = low(dot_nn(tokens, w_key) + b_key)
    v = low(dot_nn(tokens, w_value) + b_value)
    to_rows = (
        distance_rows(seq_len, table_rows)[:, None] == np.arange(table_rows)[None, :]
    ).astype(np.float32)
    expand = jnp.asarray(to_rows, bf16)
    pos_query = low(dot_nn(expand, low(dot_nn(rel_table, w_query) + b_query)))
    pos_key = low(dot_nn(expand, low(dot_nn(rel_table, w_key) + b_key)))

    place = mask_pos + lax.broadcasted_iota(jnp.int32, mask_pos.shape, 0) * seq_len
    place = jnp.where(mask_pos >= 0, place, -1).reshape(-1)
    pick = low(place[:, None] == lax.broadcasted_iota(jnp.int32, (place.shape[0], rows_here), 1))
    x_pick = dot_nn(pick, tokens)
    q_pick = low(dot_nn(pick, q))

    def seq_rows(values, s, count):
        return values if seq_count == 1 else values[s * count : (s + 1) * count]

    firsts = []
    for s in range(seq_count):
        rows = lambda value: seq_rows(value, s, seq_len)
        own_pick = seq_rows(pick, s, slots)
        if seq_count > 1:
            own_pick = own_pick[:, s * seq_len : (s + 1) * seq_len]
        firsts.append(
            attend_picked(
                rel_ids[s], own_pick, seq_rows(q_pick, s, slots), rows(k), rows(v), pos_query, pos_key
            )
        )
    join = lambda parts: parts[0] if seq_count == 1 else jnp.concatenate(parts, axis=0)
    ctx_pick = join([first[0] for first in firsts])

    h1_normed, h1_inv = norm_stats(x_pick + (dot_nn(ctx_pick, w_out) + b_out))
    h1_pick = h1_normed * ln1_gain + ln1_bias
    h1_mine = low(h1_pick)
    pair = lambda value: jnp.concatenate([value, swap(value, "ffn", 1)], axis=0)
    count = h1_mine.shape[0]
    both = lambda value: low(value)[:count].astype(f32) + swap(low(value)[count:], "ffn", 1).astype(f32)
    h1_both = pair(h1_mine)
    pre = dot_nn(h1_both, w_in) + b_in
    cdf = normal_cdf(pre)
    hidden = low(pre * cdf)
    branch = both(dot_nn(hidden, w_down)) + b_down
    z2_normed, z2_inv = norm_stats(h1_pick + branch)
    cot = jnp.where(mask_pos.reshape(-1, 1) >= 0, grad_vals.reshape(-1, width).astype(f32), 0.0)
    dz2, g_ln2_gain, g_ln2_bias = norm_backward(cot, z2_normed, z2_inv, ln2_gain)
    dffn = low(dz2)
    g_b_down = jnp.sum(dffn.astype(f32), axis=0)
    dffn_both = pair(dffn)
    slope = cdf + pre * (jnp.exp(-0.5 * pre * pre) * (1.0 / math.sqrt(2.0 * math.pi)))
    dpre = low(dot_nt(dffn_both, w_down) * slope)
    dh1 = dz2 + both(dot_nt(dpre, w_in))
    gw_down_t = low(dot_tn(dffn_both, hidden))
    gw_in = low(dot_tn(h1_both, dpre))
    gb_in = low(jnp.sum(dpre.astype(f32), axis=0))
    dz1, g_ln1_gain, g_ln1_bias = norm_backward(dh1, h1_normed, h1_inv, ln1_gain)
    dattn = low(dz1)
    g_b_out = jnp.sum(dattn.astype(f32), axis=0)
    g_w_out = dot_tn(ctx_pick, dattn)
    dctx = low(dot_nt(dattn, w_out))

    part = width // n_tok
    ffn_blocks = jnp.concatenate(
        [
            gw_in.reshape(n_tok, part, hidden_cols),
            gw_down_t.reshape(n_tok, part, hidden_cols),
            jnp.pad(
                gb_in.reshape(n_tok, 1, hidden_cols // n_tok),
                ((0, 0), (0, 7), (0, hidden_cols - hidden_cols // n_tok)),
            ),
        ],
        axis=1,
    )
    s_ffn = halve_over(ffn_blocks, "tok")

    backs = []
    for s in range(seq_count):
        rows = lambda value: seq_rows(value, s, seq_len)
        picks = lambda value: seq_rows(value, s, slots)
        _, probs, _, words, words_pick = firsts[s]
        backs.append(
            attend_back(
                words, words_pick, picks(q_pick), rows(k), rows(v), picks(dctx), probs, pos_query, pos_key
            )
        )
    dq = join([back[0] for back in backs])
    dk = join([back[1] for back in backs])
    dv = join([back[2] for back in backs])
    dpos_key = dot_tn(expand, sum(back[3].astype(f32) for back in backs).astype(bf16))
    dpos_query = dot_tn(expand, sum(back[4].astype(f32) for back in backs).astype(bf16))
    sparse = dz1 + dot_nt(dq, w_query)
    sparse_up = low(sparse)
    sparse_lo = low(sparse - sparse_up.astype(f32))
    grad_tokens = (
        dot_tn(pick, sparse_up) + dot_tn(pick, sparse_lo) + dot_nt(dk, w_key) + dot_nt(dv, w_value)
    )
    g_w_query = dot_tn(low(x_pick), dq) + dot_tn(rel_table, low(dpos_query))
    g_w_key = dot_tn(tokens, dk) + dot_tn(rel_table, low(dpos_key))
    g_w_value = dot_tn(tokens, dv)
    g_rel = dot_nt(low(dpos_query), w_query) + dot_nt(low(dpos_key), w_key)
    total = lambda value: jnp.sum(value.astype(f32), axis=0)
    vectors = [
        total(dq) + total(dpos_query),
        total(dk) + total(dpos_key),
        total(dv),
        g_b_out, g_ln1_gain, g_ln1_bias, g_b_down, g_ln2_gain, g_ln2_bias,
    ]
    n_all = n_tok * n_ffn
    own = width // n_all
    vec_blocks = jnp.stack([value.reshape(n_all, own) for value in vectors], axis=1)
    vec_blocks = vec_blocks.reshape(n_all, 1, len(vectors) * own)
    vec_blocks = jnp.pad(vec_blocks, ((0, 0), (0, 7), (0, width - len(vectors) * own)))
    all_blocks = jnp.concatenate(
        [low(value).reshape(n_all, own, width) for value in (g_w_query, g_w_key, g_w_value, g_w_out)]
        + [low(g_rel).reshape(n_all, table_rows // n_all, width), low(vec_blocks)],
        axis=1,
    )
    tok_first = all_blocks.reshape((n_tok, n_ffn) + all_blocks.shape[1:])
    s_tok = halve_over(tok_first, "tok")
    s_all = halve_over(s_tok, "ffn")

    ctx = join(
        [
            attend_full(
                firsts[s][3],
                seq_rows(q, s, seq_len),
                seq_rows(k, s, seq_len),
                seq_rows(v, s, seq_len),
                pos_key,
                firsts[s][2],
            )
            for s in range(seq_count)
        ]
    )
    normed, _ = norm_stats(tokens.astype(f32) + (dot_nn(ctx, w_out) + b_out))
    middle = normed * ln1_gain + ln1_bias
    mine = low(middle)
    theirs = swap(mine, "ffn", 1)

    def ffn_part(value):
        pre_act = dot_nn(value, w_in) + b_in
        return low(dot_nn(low(pre_act * normal_cdf(pre_act)), w_down))

    back = swap(ffn_part(theirs), "ffn", 1)
    branch_all = ffn_part(mine).astype(f32) + back.astype(f32) + b_down
    final, _ = norm_stats(middle + branch_all)
    output = low(final * ln2_gain + ln2_bias)

    wide = lambda value: value.astype(f32)
    s_vec = wide(s_all[4 * own + table_rows // n_all, : len(vectors) * own]).reshape(len(vectors), own)
    s_w = [wide(s_all[n * own : (n + 1) * own]) for n in range(4)]
    s_rel = wide(s_all[4 * own : 4 * own + table_rows // n_all])
    return (
        output,
        grad_tokens,
        s_w[0],
        s_w[1],
        s_w[2],
        s_w[3],
        s_vec[0],
        s_vec[1],
        s_vec[2],
        s_vec[3],
        s_rel,
        s_vec[4],
        s_vec[5],
        wide(s_ffn[:part]),
        wide(s_ffn[2 * part : 2 * part + 1, : hidden_cols // n_tok]),
        jnp.transpose(wide(s_ffn[part : 2 * part])),
        s_vec[6],
        s_vec[7],
        s_vec[8],
    )


def solution(mesh):
    every = ("tok", "ffn")
    placed = (
        P(every, None), P(every, None, None), P(every, None), P(every, None, None),
        P(), P(), P(), P(), P(), P(), P(), P(), P(), P(), P(),
        P(None, "ffn"), P("ffn"), P("ffn", None), P(), P(), P(),
    )
    given = (
        P(every, None), P(every, None),
        P(every, None), P(every, None), P(every, None), P(every, None),
        P(every), P(every), P(every), P(every),
        P(every, None), P(every), P(every),
        P("tok", "ffn"), P("ffn", "tok"), P("ffn", "tok"),
        P(every), P(every), P(every),
    )
    return jax.shard_map(local, mesh=mesh, in_specs=placed, out_specs=given, check_vma=False)
```

```python
import functools
import math

import numpy as np

import jax
import jax.numpy as jnp
from jax import lax
from jax.experimental import pallas as pl
from jax.experimental.pallas import tpu as pltpu
from jax.sharding import PartitionSpec as P

HEAD = 64
LANES = 128
HALF = 64
ROWS = 32
norm_eps = 1e-07
bf16 = jnp.bfloat16
f32 = jnp.float32


def dot_nn(first_op, second_op):
    return lax.dot_general(
        first_op, second_op, (((1,), (0,)), ((), ())), preferred_element_type=f32
    )


def dot_nt(first_op, second_op):
    return lax.dot_general(
        first_op, second_op, (((1,), (1,)), ((), ())), preferred_element_type=f32
    )


def dot_tn(first_op, second_op):
    return lax.dot_general(
        first_op, second_op, (((0,), (0,)), ((), ())), preferred_element_type=f32
    )


def distance_rows(seq_len, table_rows):
    side = table_rows // 2
    middle = side // 2
    rows = []
    for m in range(2 * seq_len):
        offset = max(seq_len - 1 - m, 1 - seq_len)
        size = abs(offset)
        if size > middle:
            ratio = math.log(size / middle) / math.log((2 * side - 1) / middle)
            size = int(math.ceil(ratio * (middle - 1))) + middle
        rows.append(side + (size if offset > 0 else -size))
    return np.array(rows, dtype=np.int32)


def lane_iota(rows=1):
    return lax.broadcasted_iota(jnp.int32, (rows, LANES), 1)


def member_chunk(words, c):
    return (words == lane_iota(words.shape[0]) + c * LANES).astype(f32).astype(bf16)


def id_bases(rel_ref, base):
    seq = rel_ref.shape[0]
    chunks = seq // LANES
    last = chunks * 2 - 2
    for g in range(seq // HALF):
        for c in range(chunks):
            block = rel_ref[g * HALF : (g + 1) * HALF, c * LANES : (c + 1) * LANES]
            base[g * chunks + c] = jnp.minimum(jnp.min(block) // HALF, last)


def both_alignments(table):
    return jnp.concatenate([table, table[HALF:], table[:HALF]], axis=0)


def longest(rows):
    wide = rows.astype(f32)
    return jnp.sqrt(jnp.max(jnp.sum(wide * wide, axis=1, keepdims=True)))


def pack_heads(first, second, dest, top):
    top = jnp.maximum(top, 1e-30)
    scale = 32000.0 / top
    upper = (first * scale).astype(jnp.int32)
    lower = (second * scale).astype(jnp.int32)
    dest[...] = upper * 65536 + lower
    return top * (1.0 / 32000.0)


def unpack_heads(words, step):
    lower = lax.shift_right_arithmetic(lax.shift_left(words, 16), 16)
    return words.astype(f32) * (step * (1.0 / 65536.0)), lower.astype(f32) * step


def picked_words(source, rel_ref, base, rows, c):
    chunks = rel_ref.shape[1] // LANES
    first = base[(rows.start // HALF) * chunks + c]
    place = rel_ref[rows, c * LANES : (c + 1) * LANES] - first * HALF
    index = place & (LANES - 1)
    at = pl.multiple_of((first % 2) * (chunks * LANES) + (first // 2) * LANES, LANES)
    near = jnp.take_along_axis(source[rows, pl.ds(at, LANES)], index, axis=1)
    at = pl.multiple_of(at + LANES, LANES)
    far = jnp.take_along_axis(source[rows, pl.ds(at, LANES)], index, axis=1)
    return jnp.where(place < LANES, near, far)


def unshift_in_order(source, words_ref, base, dest):
    seq = words_ref.shape[0]
    chunks = seq // LANES
    lane = lane_iota()
    zero = jnp.zeros((ROWS, LANES), f32)
    for g in range(chunks):
        first = base[g]
        for sub in range(LANES // ROWS):
            start = g * LANES + sub * ROWS
            rows = slice(start, start + ROWS)
            place = lane - (seq - 1) + words_ref[rows, :] + first * LANES
            index = place & (LANES - 1)
            turned = [
                jnp.take_along_axis(
                    source[rows, c * LANES : (c + 1) * LANES], index, axis=1
                )
                for c in range(chunks)
            ]

            def pick(c):
                return turned[c] if 0 <= c < chunks else zero

            near = place >= 0
            mid = place >= -LANES
            for c in range(chunks + 2):
                value = jnp.where(near, pick(c), jnp.where(mid, pick(c - 1), pick(c - 2)))
                at = pl.multiple_of((first + c) * LANES, LANES)
                dest[rows, pl.ds(at, LANES)] = value.astype(bf16)


def group_bases(words, base):
    seq = words.shape[0]
    for g in range(seq // LANES):
        top = jnp.max(words[g * LANES : (g + 1) * LANES])
        base[g] = (seq - 1 - top) // LANES


def softmax_weights(scores):
    factor = math.log2(math.e) / math.sqrt(3.0 * HEAD)
    top = jnp.max(functools.reduce(jnp.maximum, scores), axis=1, keepdims=True)
    return [jnp.exp2((score - top) * factor) for score in scores]


def head_lanes(a):
    return (lane_iota() < HEAD) if a == 0 else (lane_iota() >= HEAD)


def picked_kernel(
    pos_ref, rel_ref, qc_ref, k_ref, v_ref, pk_ref, pq_ref,
    ctx_ref, prob_ref, key_ref, word_ref, wordc_ref,
    packed, cpick, relc, keyc, base,
):
    seq = k_ref.shape[0]
    picks = qc_ref.shape[0]
    chunks = seq // LANES

    @pl.when(pl.program_id(0) == 0)
    def _():
        row = lax.broadcasted_iota(jnp.int32, (seq, seq), 0)
        col = lax.broadcasted_iota(jnp.int32, (seq, seq), 1)
        side = pk_ref.shape[0] // 2
        step = jnp.sum(jnp.where(col == row - 1, rel_ref[...] - side, 0), axis=1, keepdims=True)
        steps = jnp.broadcast_to(step.astype(f32), (seq, LANES)).astype(bf16)
        word_ref[...] = dot_nn((col <= row).astype(f32).astype(bf16), steps).astype(jnp.int32)
        id_bases(rel_ref, base)
        for n in range(picks):
            place = jnp.maximum(pos_ref[n], 0)
            relc[n : n + 1, :] = rel_ref[pl.ds(place, 1), :]
            wordc_ref[n : n + 1, :] = word_ref[pl.ds(place, 1), :]

    zero = jnp.zeros((), bf16)
    table = both_alignments(pq_ref[...])
    keys = [dot_nt(jnp.where(head_lanes(a), k_ref[...], zero), table) for a in range(2)]
    unit = pack_heads(keys[0], keys[1], packed, longest(k_ref[...]) * longest(pq_ref[...]))
    for a in range(2):
        cpick[a] = dot_nt(jnp.where(head_lanes(a), qc_ref[...], zero), pk_ref[...])
    for g in range(chunks):
        for c in range(chunks):
            parts = []
            for start in range(g * LANES, (g + 1) * LANES, ROWS):
                parts.append(picked_words(packed, rel_ref, base, slice(start, start + ROWS), c))
            block = jnp.concatenate(parts, axis=0).T
            for a, value in enumerate(unpack_heads(block, unit)):
                key_ref[a, c * LANES : (c + 1) * LANES, g * LANES : (g + 1) * LANES] = value

    for n in range(picks):
        place = jnp.maximum(pos_ref[n], 0)
        for a in range(2):
            keyc[a, n : n + 1, :] = key_ref[a, pl.ds(place, 1), :]
    for a in range(2):
        mine = head_lanes(a)
        direct = dot_nt(jnp.where(mine, qc_ref[...], zero), k_ref[...])
        scores = []
        for c in range(chunks):
            ids = relc[:, c * LANES : (c + 1) * LANES]
            index = ids & (LANES - 1)
            value = jnp.take_along_axis(cpick[a, :, :LANES], index, axis=1)
            for n in range(1, pk_ref.shape[0] // LANES):
                other = cpick[a, :, n * LANES : (n + 1) * LANES]
                value = jnp.where(
                    ids >= n * LANES, jnp.take_along_axis(other, index, axis=1), value
                )
            cols = slice(c * LANES, (c + 1) * LANES)
            scores.append(direct[:, cols] + value + keyc[a, :, cols])
        weights = softmax_weights(scores)
        inverse = 1.0 / jnp.sum(sum(weights[1:], weights[0]), axis=1, keepdims=True)
        probs = jnp.concatenate([(weight * inverse).astype(bf16) for weight in weights], axis=1)
        prob_ref[a] = probs
        mixed = dot_nn(probs, v_ref[...]).astype(bf16)
        ctx_ref[...] = mixed if a == 0 else jnp.where(mine, mixed, ctx_ref[...])


def attend_picked(positions, rel_ids, q_pick, k, v, pos_query, pos_key):
    seq, width = k.shape
    picks = q_pick.shape[0]
    table = pos_key.shape[0]
    pairs = width // LANES
    whole = lambda rows, cols: pl.BlockSpec((rows, cols), lambda h: (0, 0))
    col = lambda rows: pl.BlockSpec((rows, LANES), lambda h: (0, h))
    heads = lambda rows: pl.BlockSpec((2, rows, seq), lambda h: (h, 0, 0))
    return pl.pallas_call(
        picked_kernel,
        grid=(pairs,),
        in_specs=[
            pl.BlockSpec(memory_space=pltpu.SMEM), whole(seq, seq),
            col(picks), col(seq), col(seq), col(table), col(table),
        ],
        out_specs=[
            col(picks), heads(picks), heads(seq), whole(seq, LANES), whole(picks, LANES),
        ],
        out_shape=[
            jax.ShapeDtypeStruct((picks, width), bf16),
            jax.ShapeDtypeStruct((2 * pairs, picks, seq), bf16),
            jax.ShapeDtypeStruct((2 * pairs, seq, seq), f32),
            jax.ShapeDtypeStruct((seq, LANES), jnp.int32),
            jax.ShapeDtypeStruct((picks, LANES), jnp.int32),
        ],
        scratch_shapes=[
            pltpu.VMEM((seq, 2 * table), jnp.int32),
            pltpu.VMEM((2, picks, table), f32),
            pltpu.VMEM((picks, seq), jnp.int32),
            pltpu.VMEM((2, picks, seq), f32),
            pltpu.SMEM((seq // HALF * (seq // LANES),), jnp.int32),
        ],
        compiler_params=pltpu.CompilerParams(vmem_limit_bytes=48 * 2**20),
        name="attend_picked",
    )(positions, rel_ids, q_pick, k, v, pos_key, pos_query)


def full_kernel(rel_ref, q_ref, k_ref, v_ref, pk_ref, key_ref, ctx_ref, packed, direct, low, base):
    seq = q_ref.shape[0]
    chunks = seq // LANES

    @pl.when(pl.program_id(0) == 0)
    def _():
        id_bases(rel_ref, base)

    zero = jnp.zeros((), bf16)
    table = both_alignments(pk_ref[...])
    far = []
    for a in range(2):
        q_a = jnp.where(head_lanes(a), q_ref[...], zero)
        far.append(dot_nt(q_a, table))
        direct[a] = dot_nt(q_a, k_ref[...])
    unit = pack_heads(far[0], far[1], packed, longest(q_ref[...]) * longest(pk_ref[...]))
    for start in range(0, seq, HALF):
        rows = slice(start, start + HALF)
        scores = [[], []]
        for c in range(chunks):
            cols = slice(c * LANES, (c + 1) * LANES)
            values = unpack_heads(picked_words(packed, rel_ref, base, rows, c), unit)
            for a in range(2):
                scores[a].append(values[a] + direct[a, rows, cols] + key_ref[a, rows, cols])
        for a in range(2):
            for c, weight in enumerate(softmax_weights(scores[a])):
                low[a, rows, c * LANES : (c + 1) * LANES] = weight.astype(bf16)
    mixed = [
        dot_nn(low[a], jnp.where(head_lanes(a), v_ref[...], jnp.ones((), bf16))) for a in range(2)
    ]
    upper = head_lanes(0)
    totals = pltpu.roll(jnp.where(upper, mixed[1], mixed[0]), HEAD, 1)
    ctx_ref[...] = (jnp.where(upper, mixed[0], mixed[1]) * (1.0 / totals)).astype(bf16)


def attend_full(rel_ids, q, k, v, pos_key, key_scores):
    seq, width = k.shape
    table = pos_key.shape[0]
    pairs = width // LANES
    col = lambda rows: pl.BlockSpec((rows, LANES), lambda h: (0, h))
    return pl.pallas_call(
        full_kernel,
        grid=(pairs,),
        in_specs=[
            pl.BlockSpec((seq, seq), lambda h: (0, 0)),
            col(seq), col(seq), col(seq), col(table),
            pl.BlockSpec((2, seq, seq), lambda h: (h, 0, 0)),
        ],
        out_specs=col(seq),
        out_shape=jax.ShapeDtypeStruct((seq, width), bf16),
        scratch_shapes=[
            pltpu.VMEM((seq, 2 * table), jnp.int32),
            pltpu.VMEM((2, seq, seq), f32),
            pltpu.VMEM((2, seq, seq), bf16),
            pltpu.SMEM((seq // HALF * (seq // LANES),), jnp.int32),
        ],
        compiler_params=pltpu.CompilerParams(vmem_limit_bytes=48 * 2**20),
        name="attend_full",
    )(rel_ids, q, k, v, pos_key, key_scores)


def back_kernel(
    word_ref, wordc_ref, qc_ref, k_ref, v_ref, dctx_ref, prob_ref, pk_ref, pq_ref,
    dq_ref, dk_ref, dv_ref, dpk_ref, dpq_ref,
    side, sidec, moved, movedc, grel, base,
):
    seq = k_ref.shape[0]
    picks = qc_ref.shape[0]
    chunks = seq // LANES

    @pl.when(pl.program_id(0) == 0)
    def _():
        words = word_ref[...]
        for c in range(chunks):
            side[:, c * LANES : (c + 1) * LANES] = member_chunk(words, c)
            sidec[:, c * LANES : (c + 1) * LANES] = member_chunk(wordc_ref[...], c)
        group_bases(words, base)
        moved[...] = jnp.zeros_like(moved)

    lane = lane_iota()
    scale = 1.0 / math.sqrt(3.0 * HEAD)
    zero = jnp.zeros((), bf16)
    for a in range(2):
        mine = (lane < HEAD) if a == 0 else (lane >= HEAD)
        keep = lambda value: jnp.where(mine, value, zero)
        dctx_a = keep(dctx_ref[...])
        q_a = keep(qc_ref[...])
        k_a = keep(k_ref[...])
        side[:, seq:] = k_a
        sidec[:, seq:] = q_a
        dprobs = dot_nt(dctx_a, v_ref[...])
        probs = prob_ref[a].astype(f32)
        prod = probs * dprobs
        gs = ((prod - probs * jnp.sum(prod, axis=1, keepdims=True)) * scale).astype(bf16)
        dv = dot_tn(prob_ref[a], dctx_a)

        out = dot_nn(gs, side[...])
        place = lane - (seq - 1) + wordc_ref[...]
        index = place & (LANES - 1)
        turned = [
            jnp.take_along_axis(out[:, c * LANES : (c + 1) * LANES], index, axis=1)
            for c in range(chunks)
        ]
        blank = jnp.zeros((picks, LANES), f32)
        for c in range(2 * chunks):
            value = turned[c] if c < chunks else blank
            for n in range(1, chunks + 1):
                other = turned[c - n] if 0 <= c - n < chunks else blank
                value = jnp.where(place < -LANES * (n - 1), other, value)
            movedc[:, c * LANES : (c + 1) * LANES] = value.astype(bf16)
        dq = out[:, seq:] + dot_nn(movedc[...], keep(pk_ref[...]))
        dpk = dot_tn(movedc[...], q_a)

        out = dot_tn(gs, sidec[...])
        grel[...] = out[:, :seq]
        unshift_in_order(grel, word_ref, base, moved)
        dk = out[:, seq:] + dot_nn(moved[:, : 2 * seq], keep(pq_ref[...]))
        dpq = dot_tn(moved[:, : 2 * seq], k_a)
        for ref, value in (
            (dq_ref, dq), (dk_ref, dk), (dv_ref, dv), (dpk_ref, dpk), (dpq_ref, dpq),
        ):
            low = value.astype(bf16)
            ref[...] = low if a == 0 else jnp.where(mine, low, ref[...])


def attend_back(words, words_pick, q_pick, k, v, dctx, probs, pos_query, pos_key):
    seq, width = k.shape
    picks = q_pick.shape[0]
    pairs = width // LANES
    whole = lambda rows, cols: pl.BlockSpec((rows, cols), lambda h: (0, 0))
    col = lambda rows: pl.BlockSpec((rows, LANES), lambda h: (0, h))
    shape = lambda rows: jax.ShapeDtypeStruct((rows, width), bf16)
    return pl.pallas_call(
        back_kernel,
        grid=(pairs,),
        in_specs=[
            whole(seq, LANES), whole(picks, LANES),
            col(picks), col(seq), col(seq), col(picks),
            pl.BlockSpec((2, picks, seq), lambda h: (h, 0, 0)),
            col(2 * seq), col(2 * seq),
        ],
        out_specs=[col(picks), col(seq), col(seq), col(2 * seq), col(2 * seq)],
        out_shape=[shape(picks), shape(seq), shape(seq), shape(2 * seq), shape(2 * seq)],
        scratch_shapes=[
            pltpu.VMEM((seq, seq + LANES), bf16),
            pltpu.VMEM((picks, seq + LANES), bf16),
            pltpu.VMEM((seq, 2 * seq + LANES), bf16),
            pltpu.VMEM((picks, 2 * seq), bf16),
            pltpu.VMEM((seq, seq), f32),
            pltpu.SMEM((seq // LANES,), jnp.int32),
        ],
        compiler_params=pltpu.CompilerParams(vmem_limit_bytes=48 * 2**20),
        name="attend_back",
    )(words, words_pick, q_pick, k, v, dctx, probs, pos_key, pos_query)


def norm_stats(values):
    centered = values - jnp.mean(values, axis=1, keepdims=True)
    inv_std = lax.rsqrt(jnp.mean(centered * centered, axis=1, keepdims=True) + norm_eps)
    return centered * inv_std, inv_std


def norm_backward(upstream, normed, inv_std, norm_gain):
    scaled = upstream * norm_gain
    adjusted = (
        scaled
        - jnp.mean(scaled, axis=1, keepdims=True)
        - normed * jnp.mean(scaled * normed, axis=1, keepdims=True)
    )
    return (inv_std * adjusted, jnp.sum(upstream * normed, axis=0), jnp.sum(upstream, axis=0))


def normal_cdf(pre_act):
    return 0.5 * (1.0 + lax.erf(pre_act * (1.0 / math.sqrt(2.0))))


def swap(values, axis, bit):
    size = lax.axis_size(axis)
    return lax.ppermute(values, axis, [(n, n ^ bit) for n in range(size)])


def halve_over(values, axis):
    size = lax.axis_size(axis)
    me = lax.axis_index(axis)
    bit = 1
    while bit < size:
        mine = (me // bit) % 2
        view = values.reshape((values.shape[0] // 2, 2) + values.shape[1:])
        send = lax.dynamic_index_in_dim(view, 1 - mine, 1, keepdims=False)
        keep = lax.dynamic_index_in_dim(view, mine, 1, keepdims=False)
        values = (keep.astype(f32) + swap(send, axis, bit).astype(f32)).astype(bf16)
        bit *= 2
    return values[0]


def local(
    tokens, rel_ids, mask_pos, grad_vals, w_query, w_key, w_value, w_out, b_query, b_key,
    b_value, b_out, rel_table, ln1_gain, ln1_bias, w_in, b_in, w_down, b_down, ln2_gain, ln2_bias,
):
    seq_count, seq_len = rel_ids.shape[0], rel_ids.shape[1]
    rows_here, width = tokens.shape
    table_rows = rel_table.shape[0]
    hidden_cols = w_in.shape[1]
    slots = mask_pos.shape[1]
    n_tok = lax.axis_size("tok")
    n_ffn = lax.axis_size("ffn")
    low = lambda value: value.astype(bf16)

    q = low(dot_nn(tokens, w_query) + b_query)
    k = low(dot_nn(tokens, w_key) + b_key)
    v = low(dot_nn(tokens, w_value) + b_value)
    to_rows = (
        distance_rows(seq_len, table_rows)[:, None] == np.arange(table_rows)[None, :]
    ).astype(np.float32)
    expand = jnp.asarray(to_rows, bf16)
    pos_query = low(dot_nn(rel_table, w_query) + b_query)
    pos_key = low(dot_nn(rel_table, w_key) + b_key)
    far_query = low(dot_nn(expand, pos_query))
    far_key = low(dot_nn(expand, pos_key))

    place = mask_pos + lax.broadcasted_iota(jnp.int32, mask_pos.shape, 0) * seq_len
    place = jnp.where(mask_pos >= 0, place, -1).reshape(-1)
    pick = low(place[:, None] == lax.broadcasted_iota(jnp.int32, (place.shape[0], rows_here), 1))
    x_pick = dot_nn(pick, tokens)
    q_pick = low(dot_nn(pick, q))

    def seq_rows(values, s, count):
        return values if seq_count == 1 else values[s * count : (s + 1) * count]

    firsts = []
    for s in range(seq_count):
        rows = lambda value: seq_rows(value, s, seq_len)
        firsts.append(
            attend_picked(
                mask_pos[s], rel_ids[s], seq_rows(q_pick, s, slots), rows(k), rows(v), pos_query, pos_key
            )
        )
    join = lambda parts: parts[0] if seq_count == 1 else jnp.concatenate(parts, axis=0)
    ctx_pick = join([first[0] for first in firsts])

    h1_normed, h1_inv = norm_stats(x_pick + (dot_nn(ctx_pick, w_out) + b_out))
    h1_pick = h1_normed * ln1_gain + ln1_bias
    h1_mine = low(h1_pick)
    pair = lambda value: jnp.concatenate([value, swap(value, "ffn", 1)], axis=0)
    count = h1_mine.shape[0]
    both = lambda value: low(value)[:count].astype(f32) + swap(low(value)[count:], "ffn", 1).astype(f32)
    h1_both = pair(h1_mine)
    pre = dot_nn(h1_both, w_in) + b_in
    cdf = normal_cdf(pre)
    hidden = low(pre * cdf)
    branch = both(dot_nn(hidden, w_down)) + b_down
    z2_normed, z2_inv = norm_stats(h1_pick + branch)
    cot = jnp.where(mask_pos.reshape(-1, 1) >= 0, grad_vals.reshape(-1, width).astype(f32), 0.0)
    dz2, g_ln2_gain, g_ln2_bias = norm_backward(cot, z2_normed, z2_inv, ln2_gain)
    dffn = low(dz2)
    g_b_down = jnp.sum(dffn.astype(f32), axis=0)
    dffn_both = pair(dffn)
    slope = cdf + pre * (jnp.exp(-0.5 * pre * pre) * (1.0 / math.sqrt(2.0 * math.pi)))
    dpre = low(dot_nt(dffn_both, w_down) * slope)
    dh1 = dz2 + both(dot_nt(dpre, w_in))
    gw_down_t = low(dot_tn(dffn_both, hidden))
    gw_in = low(dot_tn(h1_both, dpre))
    gb_in = low(jnp.sum(dpre.astype(f32), axis=0))
    dz1, g_ln1_gain, g_ln1_bias = norm_backward(dh1, h1_normed, h1_inv, ln1_gain)
    dattn = low(dz1)
    g_b_out = jnp.sum(dattn.astype(f32), axis=0)
    g_w_out = dot_tn(ctx_pick, dattn)
    dctx = low(dot_nt(dattn, w_out))

    part = width // n_tok
    ffn_blocks = jnp.concatenate(
        [
            gw_in.reshape(n_tok, part, hidden_cols),
            gw_down_t.reshape(n_tok, part, hidden_cols),
            jnp.pad(
                gb_in.reshape(n_tok, 1, hidden_cols // n_tok),
                ((0, 0), (0, 7), (0, hidden_cols - hidden_cols // n_tok)),
            ),
        ],
        axis=1,
    )
    s_ffn = halve_over(ffn_blocks, "tok")

    backs = []
    for s in range(seq_count):
        rows = lambda value: seq_rows(value, s, seq_len)
        picks = lambda value: seq_rows(value, s, slots)
        _, probs, _, words, words_pick = firsts[s]
        backs.append(
            attend_back(
                words, words_pick, picks(q_pick), rows(k), rows(v), picks(dctx), probs, far_query, far_key
            )
        )
    dq = join([back[0] for back in backs])
    dk = join([back[1] for back in backs])
    dv = join([back[2] for back in backs])
    dpos_key = dot_tn(expand, sum(back[3].astype(f32) for back in backs).astype(bf16))
    dpos_query = dot_tn(expand, sum(back[4].astype(f32) for back in backs).astype(bf16))
    sparse = dz1 + dot_nt(dq, w_query)
    sparse_up = low(sparse)
    sparse_lo = low(sparse - sparse_up.astype(f32))
    grad_tokens = (
        dot_tn(pick, sparse_up) + dot_tn(pick, sparse_lo) + dot_nt(dk, w_key) + dot_nt(dv, w_value)
    )
    g_w_query = dot_tn(low(x_pick), dq) + dot_tn(rel_table, low(dpos_query))
    g_w_key = dot_tn(tokens, dk) + dot_tn(rel_table, low(dpos_key))
    g_w_value = dot_tn(tokens, dv)
    g_rel = dot_nt(low(dpos_query), w_query) + dot_nt(low(dpos_key), w_key)
    total = lambda value: jnp.sum(value.astype(f32), axis=0)
    vectors = [
        total(dq) + total(dpos_query),
        total(dk) + total(dpos_key),
        total(dv),
        g_b_out, g_ln1_gain, g_ln1_bias, g_b_down, g_ln2_gain, g_ln2_bias,
    ]
    n_all = n_tok * n_ffn
    own = width // n_all
    vec_blocks = jnp.stack([value.reshape(n_all, own) for value in vectors], axis=1)
    vec_blocks = vec_blocks.reshape(n_all, 1, len(vectors) * own)
    vec_blocks = jnp.pad(vec_blocks, ((0, 0), (0, 7), (0, width - len(vectors) * own)))
    all_blocks = jnp.concatenate(
        [low(value).reshape(n_all, own, width) for value in (g_w_query, g_w_key, g_w_value, g_w_out)]
        + [low(g_rel).reshape(n_all, table_rows // n_all, width), low(vec_blocks)],
        axis=1,
    )
    tok_first = all_blocks.reshape((n_tok, n_ffn) + all_blocks.shape[1:])
    s_tok = halve_over(tok_first, "tok")
    s_all = halve_over(s_tok, "ffn")

    ctx = join(
        [
            attend_full(
                rel_ids[s],
                seq_rows(q, s, seq_len),
                seq_rows(k, s, seq_len),
                seq_rows(v, s, seq_len),
                pos_key,
                firsts[s][2],
            )
            for s in range(seq_count)
        ]
    )
    normed, _ = norm_stats(tokens.astype(f32) + (dot_nn(ctx, w_out) + b_out))
    middle = normed * ln1_gain + ln1_bias
    mine = low(middle)
    theirs = swap(mine, "ffn", 1)

    def ffn_part(value):
        pre_act = dot_nn(value, w_in) + b_in
        return low(dot_nn(low(pre_act * normal_cdf(pre_act)), w_down))

    back = swap(ffn_part(theirs), "ffn", 1)
    branch_all = ffn_part(mine).astype(f32) + back.astype(f32) + b_down
    final, _ = norm_stats(middle + branch_all)
    output = low(final * ln2_gain + ln2_bias)

    wide = lambda value: value.astype(f32)
    s_vec = wide(s_all[4 * own + table_rows // n_all, : len(vectors) * own]).reshape(len(vectors), own)
    s_w = [wide(s_all[n * own : (n + 1) * own]) for n in range(4)]
    s_rel = wide(s_all[4 * own : 4 * own + table_rows // n_all])
    return (
        output,
        grad_tokens,
        s_w[0],
        s_w[1],
        s_w[2],
        s_w[3],
        s_vec[0],
        s_vec[1],
        s_vec[2],
        s_vec[3],
        s_rel,
        s_vec[4],
        s_vec[5],
        wide(s_ffn[:part]),
        wide(s_ffn[2 * part : 2 * part + 1, : hidden_cols // n_tok]),
        jnp.transpose(wide(s_ffn[part : 2 * part])),
        s_vec[6],
        s_vec[7],
        s_vec[8],
    )


def solution(mesh):
    every = ("tok", "ffn")
    placed = (
        P(every, None), P(every, None, None), P(every, None), P(every, None, None),
        P(), P(), P(), P(), P(), P(), P(), P(), P(), P(), P(),
        P(None, "ffn"), P("ffn"), P("ffn", None), P(), P(), P(),
    )
    given = (
        P(every, None), P(every, None),
        P(every, None), P(every, None), P(every, None), P(every, None),
        P(every), P(every), P(every), P(every),
        P(every, None), P(every), P(every),
        P("tok", "ffn"), P("ffn", "tok"), P("ffn", "tok"),
        P(every), P(every), P(every),
    )
    return jax.shard_map(local, mesh=mesh, in_specs=placed, out_specs=given, check_vma=False)
```

```python
import functools
import math

import numpy as np

import jax
import jax.numpy as jnp
from jax import lax
from jax.experimental import pallas as pl
from jax.experimental.pallas import tpu as pltpu
from jax.sharding import PartitionSpec as P

HEAD = 64
LANES = 128
HALF = 64
ROWS = 32
norm_eps = 1e-07
bf16 = jnp.bfloat16
f32 = jnp.float32


def dot_nn(first_op, second_op):
    return lax.dot_general(
        first_op, second_op, (((1,), (0,)), ((), ())), preferred_element_type=f32
    )


def dot_nt(first_op, second_op):
    return lax.dot_general(
        first_op, second_op, (((1,), (1,)), ((), ())), preferred_element_type=f32
    )


def dot_tn(first_op, second_op):
    return lax.dot_general(
        first_op, second_op, (((0,), (0,)), ((), ())), preferred_element_type=f32
    )


def distance_rows(seq_len, table_rows):
    side = table_rows // 2
    middle = side // 2
    rows = []
    for m in range(2 * seq_len):
        offset = max(seq_len - 1 - m, 1 - seq_len)
        size = abs(offset)
        if size > middle:
            ratio = math.log(size / middle) / math.log((2 * side - 1) / middle)
            size = int(math.ceil(ratio * (middle - 1))) + middle
        rows.append(side + (size if offset > 0 else -size))
    return np.array(rows, dtype=np.int32)


def lane_iota(rows=1):
    return lax.broadcasted_iota(jnp.int32, (rows, LANES), 1)


def member_chunk(words, c):
    return (words == lane_iota(words.shape[0]) + c * LANES).astype(f32).astype(bf16)


def id_bases(rel_ref, base):
    seq = rel_ref.shape[0]
    chunks = seq // LANES
    last = chunks * 2 - 2
    for g in range(seq // HALF):
        for c in range(chunks):
            block = rel_ref[g * HALF : (g + 1) * HALF, c * LANES : (c + 1) * LANES]
            base[g * chunks + c] = jnp.minimum(jnp.min(block) // HALF, last)


def both_alignments(table):
    return jnp.concatenate([table, table[HALF:], table[:HALF]], axis=0)


def longest(rows):
    wide = rows.astype(f32)
    return jnp.sqrt(jnp.max(jnp.sum(wide * wide, axis=1, keepdims=True)))


def pack_heads(first, second, dest, top):
    top = jnp.maximum(top, 1e-30)
    scale = 32000.0 / top
    upper = (first * scale).astype(jnp.int32)
    lower = (second * scale).astype(jnp.int32)
    dest[...] = upper * 65536 + lower
    return top * (1.0 / 32000.0)


def unpack_heads(words, step):
    lower = lax.shift_right_arithmetic(lax.shift_left(words, 16), 16)
    return words.astype(f32) * (step * (1.0 / 65536.0)), lower.astype(f32) * step


def picked_words(source, rel_ref, base, rows, c):
    chunks = rel_ref.shape[1] // LANES
    first = base[(rows.start // HALF) * chunks + c]
    place = rel_ref[rows, c * LANES : (c + 1) * LANES] - first * HALF
    index = place & (LANES - 1)
    at = pl.multiple_of((first % 2) * (chunks * LANES) + (first // 2) * LANES, LANES)
    near = jnp.take_along_axis(source[rows, pl.ds(at, LANES)], index, axis=1)
    at = pl.multiple_of(at + LANES, LANES)
    far = jnp.take_along_axis(source[rows, pl.ds(at, LANES)], index, axis=1)
    return jnp.where(place < LANES, near, far)


def unshift_in_order(source, words_ref, base, dest):
    seq = words_ref.shape[0]
    chunks = seq // LANES
    lane = lane_iota()
    zero = jnp.zeros((ROWS, LANES), f32)
    for g in range(chunks):
        first = base[g]
        for sub in range(LANES // ROWS):
            start = g * LANES + sub * ROWS
            rows = slice(start, start + ROWS)
            place = lane - (seq - 1) + words_ref[rows, :] + first * LANES
            index = place & (LANES - 1)
            turned = [
                jnp.take_along_axis(
                    source[rows, c * LANES : (c + 1) * LANES], index, axis=1
                )
                for c in range(chunks)
            ]

            def pick(c):
                return turned[c] if 0 <= c < chunks else zero

            near = place >= 0
            mid = place >= -LANES
            for c in range(chunks + 2):
                value = jnp.where(near, pick(c), jnp.where(mid, pick(c - 1), pick(c - 2)))
                at = pl.multiple_of((first + c) * LANES, LANES)
                dest[rows, pl.ds(at, LANES)] = value.astype(bf16)


def group_bases(words, base):
    seq = words.shape[0]
    for g in range(seq // LANES):
        top = jnp.max(words[g * LANES : (g + 1) * LANES])
        base[g] = (seq - 1 - top) // LANES


def softmax_weights(scores):
    factor = math.log2(math.e) / math.sqrt(3.0 * HEAD)
    top = jnp.max(functools.reduce(jnp.maximum, scores), axis=1, keepdims=True)
    return [jnp.exp2((score - top) * factor) for score in scores]


def head_lanes(a):
    return (lane_iota() < HEAD) if a == 0 else (lane_iota() >= HEAD)


def picked_kernel(
    pos_ref, rel_ref, qc_ref, k_ref, v_ref, pk_ref, pq_ref,
    ctx_ref, prob_ref, key_ref, word_ref, wordc_ref,
    packed, cpick, relc, keyc, base,
):
    seq = k_ref.shape[0]
    picks = qc_ref.shape[0]
    chunks = seq // LANES

    @pl.when(pl.program_id(0) == 0)
    def _():
        row = lax.broadcasted_iota(jnp.int32, (seq, seq), 0)
        col = lax.broadcasted_iota(jnp.int32, (seq, seq), 1)
        side = pk_ref.shape[0] // 2
        step = jnp.sum(jnp.where(col == row - 1, rel_ref[...] - side, 0), axis=1, keepdims=True)
        steps = jnp.broadcast_to(step.astype(f32), (seq, LANES)).astype(bf16)
        word_ref[...] = dot_nn((col <= row).astype(f32).astype(bf16), steps).astype(jnp.int32)
        id_bases(rel_ref, base)
        for n in range(picks):
            place = jnp.maximum(pos_ref[n], 0)
            relc[n : n + 1, :] = rel_ref[pl.ds(place, 1), :]
            wordc_ref[n : n + 1, :] = word_ref[pl.ds(place, 1), :]

    zero = jnp.zeros((), bf16)
    table = both_alignments(pq_ref[...])
    keys = [dot_nt(jnp.where(head_lanes(a), k_ref[...], zero), table) for a in range(2)]
    unit = pack_heads(keys[0], keys[1], packed, longest(k_ref[...]) * longest(pq_ref[...]))
    for a in range(2):
        cpick[a] = dot_nt(jnp.where(head_lanes(a), qc_ref[...], zero), pk_ref[...])
    for g in range(chunks):
        for c in range(chunks):
            parts = []
            for start in range(g * LANES, (g + 1) * LANES, ROWS):
                parts.append(picked_words(packed, rel_ref, base, slice(start, start + ROWS), c))
            block = jnp.concatenate(parts, axis=0).T
            for a, value in enumerate(unpack_heads(block, unit)):
                key_ref[a, c * LANES : (c + 1) * LANES, g * LANES : (g + 1) * LANES] = value

    for n in range(picks):
        place = jnp.maximum(pos_ref[n], 0)
        for a in range(2):
            keyc[a, n : n + 1, :] = key_ref[a, pl.ds(place, 1), :]
    for a in range(2):
        mine = head_lanes(a)
        direct = dot_nt(jnp.where(mine, qc_ref[...], zero), k_ref[...])
        scores = []
        for c in range(chunks):
            ids = relc[:, c * LANES : (c + 1) * LANES]
            index = ids & (LANES - 1)
            value = jnp.take_along_axis(cpick[a, :, :LANES], index, axis=1)
            for n in range(1, pk_ref.shape[0] // LANES):
                other = cpick[a, :, n * LANES : (n + 1) * LANES]
                value = jnp.where(
                    ids >= n * LANES, jnp.take_along_axis(other, index, axis=1), value
                )
            cols = slice(c * LANES, (c + 1) * LANES)
            scores.append(direct[:, cols] + value + keyc[a, :, cols])
        weights = softmax_weights(scores)
        inverse = 1.0 / jnp.sum(sum(weights[1:], weights[0]), axis=1, keepdims=True)
        probs = jnp.concatenate([(weight * inverse).astype(bf16) for weight in weights], axis=1)
        prob_ref[a] = probs
        mixed = dot_nn(probs, v_ref[...]).astype(bf16)
        ctx_ref[...] = mixed if a == 0 else jnp.where(mine, mixed, ctx_ref[...])


def attend_picked(positions, rel_ids, q_pick, k, v, pos_query, pos_key):
    seq, width = k.shape
    picks = q_pick.shape[0]
    table = pos_key.shape[0]
    pairs = width // LANES
    whole = lambda rows, cols: pl.BlockSpec((rows, cols), lambda h: (0, 0))
    col = lambda rows: pl.BlockSpec((rows, LANES), lambda h: (0, h))
    heads = lambda rows: pl.BlockSpec((2, rows, seq), lambda h: (h, 0, 0))
    return pl.pallas_call(
        picked_kernel,
        grid=(pairs,),
        in_specs=[
            pl.BlockSpec(memory_space=pltpu.SMEM), whole(seq, seq),
            col(picks), col(seq), col(seq), col(table), col(table),
        ],
        out_specs=[
            col(picks), heads(picks), heads(seq), whole(seq, LANES), whole(picks, LANES),
        ],
        out_shape=[
            jax.ShapeDtypeStruct((picks, width), bf16),
            jax.ShapeDtypeStruct((2 * pairs, picks, seq), bf16),
            jax.ShapeDtypeStruct((2 * pairs, seq, seq), f32),
            jax.ShapeDtypeStruct((seq, LANES), jnp.int32),
            jax.ShapeDtypeStruct((picks, LANES), jnp.int32),
        ],
        scratch_shapes=[
            pltpu.VMEM((seq, 2 * table), jnp.int32),
            pltpu.VMEM((2, picks, table), f32),
            pltpu.VMEM((picks, seq), jnp.int32),
            pltpu.VMEM((2, picks, seq), f32),
            pltpu.SMEM((seq // HALF * (seq // LANES),), jnp.int32),
        ],
        compiler_params=pltpu.CompilerParams(vmem_limit_bytes=48 * 2**20),
        name="attend_picked",
    )(positions, rel_ids, q_pick, k, v, pos_key, pos_query)


def full_kernel(rel_ref, q_ref, k_ref, v_ref, pk_ref, key_ref, ctx_ref, packed, direct, low, base):
    seq = q_ref.shape[0]
    chunks = seq // LANES

    @pl.when(pl.program_id(0) == 0)
    def _():
        id_bases(rel_ref, base)

    zero = jnp.zeros((), bf16)
    table = both_alignments(pk_ref[...])
    far = []
    for a in range(2):
        q_a = jnp.where(head_lanes(a), q_ref[...], zero)
        far.append(dot_nt(q_a, table))
        direct[a] = dot_nt(q_a, k_ref[...])
    unit = pack_heads(far[0], far[1], packed, longest(q_ref[...]) * longest(pk_ref[...]))
    for start in range(0, seq, HALF):
        rows = slice(start, start + HALF)
        scores = [[], []]
        for c in range(chunks):
            cols = slice(c * LANES, (c + 1) * LANES)
            values = unpack_heads(picked_words(packed, rel_ref, base, rows, c), unit)
            for a in range(2):
                scores[a].append(values[a] + direct[a, rows, cols] + key_ref[a, rows, cols])
        for a in range(2):
            for c, weight in enumerate(softmax_weights(scores[a])):
                low[a, rows, c * LANES : (c + 1) * LANES] = weight.astype(bf16)
    mixed = [
        dot_nn(low[a], jnp.where(head_lanes(a), v_ref[...], jnp.ones((), bf16))) for a in range(2)
    ]
    upper = head_lanes(0)
    totals = pltpu.roll(jnp.where(upper, mixed[1], mixed[0]), HEAD, 1)
    ctx_ref[...] = (jnp.where(upper, mixed[0], mixed[1]) * (1.0 / totals)).astype(bf16)


def attend_full(rel_ids, q, k, v, pos_key, key_scores, first, pairs):
    seq = k.shape[0]
    table = pos_key.shape[0]
    col = lambda rows: pl.BlockSpec((rows, LANES), lambda h: (0, h + first))
    return pl.pallas_call(
        full_kernel,
        grid=(pairs,),
        in_specs=[
            pl.BlockSpec((seq, seq), lambda h: (0, 0)),
            col(seq), col(seq), col(seq), col(table),
            pl.BlockSpec((2, seq, seq), lambda h: (h + first, 0, 0)),
        ],
        out_specs=pl.BlockSpec((seq, LANES), lambda h: (0, h)),
        out_shape=jax.ShapeDtypeStruct((seq, pairs * LANES), bf16),
        scratch_shapes=[
            pltpu.VMEM((seq, 2 * table), jnp.int32),
            pltpu.VMEM((2, seq, seq), f32),
            pltpu.VMEM((2, seq, seq), bf16),
            pltpu.SMEM((seq // HALF * (seq // LANES),), jnp.int32),
        ],
        compiler_params=pltpu.CompilerParams(vmem_limit_bytes=48 * 2**20),
        name="attend_full",
    )(rel_ids, q, k, v, pos_key, key_scores)


def back_kernel(
    word_ref, wordc_ref, qc_ref, k_ref, v_ref, dctx_ref, prob_ref, pk_ref, pq_ref,
    dq_ref, dk_ref, dv_ref, dpos_ref,
    side, sidec, moved, movedc, grel, base,
):
    seq = k_ref.shape[0]
    picks = qc_ref.shape[0]
    chunks = seq // LANES

    @pl.when(pl.program_id(0) == 0)
    def _():
        words = word_ref[...]
        for c in range(chunks):
            side[:, c * LANES : (c + 1) * LANES] = member_chunk(words, c)
            sidec[:, c * LANES : (c + 1) * LANES] = member_chunk(wordc_ref[...], c)
        group_bases(words, base)
        moved[...] = jnp.zeros_like(moved)

    lane = lane_iota()
    scale = 1.0 / math.sqrt(3.0 * HEAD)
    zero = jnp.zeros((), bf16)
    for a in range(2):
        mine = (lane < HEAD) if a == 0 else (lane >= HEAD)
        keep = lambda value: jnp.where(mine, value, zero)
        dctx_a = keep(dctx_ref[...])
        q_a = keep(qc_ref[...])
        k_a = keep(k_ref[...])
        side[:, seq:] = k_a
        sidec[:, seq:] = q_a
        dprobs = dot_nt(dctx_a, v_ref[...])
        probs = prob_ref[a].astype(f32)
        prod = probs * dprobs
        gs = ((prod - probs * jnp.sum(prod, axis=1, keepdims=True)) * scale).astype(bf16)
        dv = dot_tn(prob_ref[a], dctx_a)

        out = dot_nn(gs, side[...])
        place = lane - (seq - 1) + wordc_ref[...]
        index = place & (LANES - 1)
        turned = [
            jnp.take_along_axis(out[:, c * LANES : (c + 1) * LANES], index, axis=1)
            for c in range(chunks)
        ]
        blank = jnp.zeros((picks, LANES), f32)
        for c in range(2 * chunks):
            value = turned[c] if c < chunks else blank
            for n in range(1, chunks + 1):
                other = turned[c - n] if 0 <= c - n < chunks else blank
                value = jnp.where(place < -LANES * (n - 1), other, value)
            movedc[:, c * LANES : (c + 1) * LANES] = value.astype(bf16)
        dq = out[:, seq:] + dot_nn(movedc[...], keep(pk_ref[...]))
        dpk = dot_tn(movedc[...], q_a)

        out = dot_tn(gs, sidec[...])
        grel[...] = out[:, :seq]
        unshift_in_order(grel, word_ref, base, moved)
        dk = out[:, seq:] + dot_nn(moved[:, : 2 * seq], keep(pq_ref[...]))
        dpq = dot_tn(moved[:, : 2 * seq], k_a)
        for ref, value in (
            (dq_ref, dq), (dk_ref, dk), (dv_ref, dv), (dpos_ref.at[0], dpk), (dpos_ref.at[1], dpq),
        ):
            low = value.astype(bf16)
            ref[...] = low if a == 0 else jnp.where(mine, low, ref[...])


def attend_back(words, words_pick, q_pick, k, v, dctx, probs, pos_query, pos_key):
    seq, width = k.shape
    picks = q_pick.shape[0]
    pairs = width // LANES
    whole = lambda rows, cols: pl.BlockSpec((rows, cols), lambda h: (0, 0))
    col = lambda rows: pl.BlockSpec((rows, LANES), lambda h: (0, h))
    shape = lambda rows: jax.ShapeDtypeStruct((rows, width), bf16)
    return pl.pallas_call(
        back_kernel,
        grid=(pairs,),
        in_specs=[
            whole(seq, LANES), whole(picks, LANES),
            col(picks), col(seq), col(seq), col(picks),
            pl.BlockSpec((2, picks, seq), lambda h: (h, 0, 0)),
            col(2 * seq), col(2 * seq),
        ],
        out_specs=[
            col(picks), col(seq), col(seq),
            pl.BlockSpec((2, 2 * seq, LANES), lambda h: (0, 0, h)),
        ],
        out_shape=[
            shape(picks), shape(seq), shape(seq),
            jax.ShapeDtypeStruct((2, 2 * seq, width), bf16),
        ],
        scratch_shapes=[
            pltpu.VMEM((seq, seq + LANES), bf16),
            pltpu.VMEM((picks, seq + LANES), bf16),
            pltpu.VMEM((seq, 2 * seq + LANES), bf16),
            pltpu.VMEM((picks, 2 * seq), bf16),
            pltpu.VMEM((seq, seq), f32),
            pltpu.SMEM((seq // LANES,), jnp.int32),
        ],
        compiler_params=pltpu.CompilerParams(vmem_limit_bytes=48 * 2**20),
        name="attend_back",
    )(words, words_pick, q_pick, k, v, dctx, probs, pos_key, pos_query)


def grads_kernel(
    half, x_ref, rel_ref, xpick_ref, cpick_ref, dpos_ref,
    dq_ref, dk_ref, dv_ref, dattn_ref, dposk_ref, dposq_ref, wq_ref, wk_ref,
    out_ref, sum_ref,
):
    width = x_ref.shape[1]
    group = 2 * LANES
    seq = x_ref.shape[0]

    def left(ref):
        starts = range(half * LANES, width, group)
        return jnp.concatenate([ref[:, at : at + LANES] for at in starts], axis=1)

    def put(at, value):
        for n in range(value.shape[0] // LANES):
            out_ref[at + n] = value[n * LANES : (n + 1) * LANES].astype(bf16)

    count = width // group
    rel_left = left(rel_ref)
    x_left = left(x_ref)
    put(0, dot_tn(left(xpick_ref), dq_ref[...]) + dot_tn(rel_left, dposq_ref[0]))
    put(count, dot_tn(x_left, dk_ref[...]) + dot_tn(rel_left, dposk_ref[0]))
    put(2 * count, dot_tn(x_left, dv_ref[...]))
    put(3 * count, dot_tn(left(cpick_ref), dattn_ref[...]))
    for n in range(dpos_ref.shape[1] // group):
        rows = slice(n * group + half * LANES, n * group + (half + 1) * LANES)
        put(
            4 * count + n,
            dot_nt(dpos_ref[0, rows, :], wk_ref[...]) + dot_nt(dpos_ref[1, rows, :], wq_ref[...]),
        )
    total = lambda ref: jnp.sum(ref[...].astype(f32), axis=-2).reshape(1, group)
    sum_ref[...] = jnp.concatenate(
        [
            total(dq_ref) + total(dposq_ref),
            total(dk_ref) + total(dposk_ref),
            total(dv_ref),
            jnp.zeros((5, group), f32),
        ],
        axis=0,
    )


def weight_grads(half, x, rel, x_pick, c_pick, dpos, dq, dk, dv, dattn, w_query, w_key):
    seq, width = x.shape
    group = 2 * LANES
    planes = 4 * (width // group) + dpos.shape[1] // group
    whole = lambda value: pl.BlockSpec(value.shape, lambda n: (0,) * value.ndim)
    col = lambda value: pl.BlockSpec((value.shape[0], group), lambda n: (0, n))
    row = lambda value: pl.BlockSpec((group, value.shape[1]), lambda n: (n, 0))
    plane = lambda t: pl.BlockSpec((1, dpos.shape[1], group), lambda n: (t, 0, n))
    return pl.pallas_call(
        functools.partial(grads_kernel, half),
        grid=(width // group,),
        in_specs=[
            whole(x), whole(rel), whole(x_pick), whole(c_pick), whole(dpos),
            col(dq), col(dk), col(dv), col(dattn), plane(0), plane(1), row(w_query), row(w_key),
        ],
        out_specs=[
            pl.BlockSpec((planes, LANES, group), lambda n: (0, 0, n)),
            pl.BlockSpec((8, group), lambda n: (0, n)),
        ],
        out_shape=[
            jax.ShapeDtypeStruct((planes, LANES, width), bf16),
            jax.ShapeDtypeStruct((8, width), f32),
        ],
        compiler_params=pltpu.CompilerParams(vmem_limit_bytes=48 * 2**20),
        name="weight_grads",
    )(x, rel, x_pick, c_pick, dpos, dq, dk, dv, dattn, dpos, dpos, w_query, w_key)


def norm_stats(values):
    centered = values - jnp.mean(values, axis=1, keepdims=True)
    inv_std = lax.rsqrt(jnp.mean(centered * centered, axis=1, keepdims=True) + norm_eps)
    return centered * inv_std, inv_std


def norm_backward(upstream, normed, inv_std, norm_gain):
    scaled = upstream * norm_gain
    adjusted = (
        scaled
        - jnp.mean(scaled, axis=1, keepdims=True)
        - normed * jnp.mean(scaled * normed, axis=1, keepdims=True)
    )
    return (inv_std * adjusted, jnp.sum(upstream * normed, axis=0), jnp.sum(upstream, axis=0))


def normal_cdf(pre_act):
    return 0.5 * (1.0 + lax.erf(pre_act * (1.0 / math.sqrt(2.0))))


def swap(values, axis, bit):
    size = lax.axis_size(axis)
    return lax.ppermute(values, axis, [(n, n ^ bit) for n in range(size)])


def after(values, *others):
    return lax.optimization_barrier((values, others))[0]


class Halving:
    def __init__(self, axes, core, near, size):
        rest = [1 << n for n in range(size.bit_length() - 1) if (1 << n) != core]
        near = [bit for bit in near if bit in rest]
        rest = [bit for bit in rest if bit not in near]
        turned = near[-1:] + near[:-1]
        self.axes, self.core, self.size = axes, core, size
        self.orders = [[core] + near + rest, [core] + turned + rest]
        self.steps = len(self.orders[0])
        self.me = lax.axis_index(axes)
        self.upper = (self.me // core) % 2

    def core_of(self, place):
        return (place // self.core) % 2

    def send(self, values, step):
        pairs = [(n, n ^ self.orders[self.core_of(n)][step]) for n in range(self.size)]
        return lax.ppermute(values, self.axes, pairs)

    def bit(self, step):
        first, second = (order[step] for order in self.orders)
        return jnp.where(self.upper == 0, first, second)

    def block_of(self, places):
        relative = []
        for upper in range(2):
            masks = []
            for place in range(self.size):
                bits = [(place >> (self.steps - 1 - step)) & 1 for step in range(self.steps)]
                order = self.orders[upper ^ bits[0]]
                mask = 0
                for step, bit in enumerate(bits):
                    mask ^= bit * order[step]
                masks.append(mask)
            relative.append(np.array(masks, np.int32)[places])
        return self.me ^ jnp.where(self.upper == 0, relative[0], relative[1])


def reorder(source, length):
    return (lax.broadcasted_iota(jnp.int32, (length, source.shape[0]), 0) == source[None, :]).astype(bf16)


def local(
    tokens, rel_ids, mask_pos, grad_vals, w_query, w_key, w_value, w_out, b_query, b_key,
    b_value, b_out, rel_table, ln1_gain, ln1_bias, w_in, b_in, w_down, b_down, ln2_gain, ln2_bias,
):
    seq_count, seq_len = rel_ids.shape[0], rel_ids.shape[1]
    rows_here, width = tokens.shape
    table_rows = rel_table.shape[0]
    hidden_cols = w_in.shape[1]
    slots = mask_pos.shape[1]
    pairs = width // LANES
    n_tok = lax.axis_size("tok")
    n_ffn = lax.axis_size("ffn")
    n_all = n_tok * n_ffn
    low = lambda value: value.astype(bf16)

    core = lax.axis_index("tok") % 2
    half_cols = hidden_cols // 2
    own_half = (
        lax.dynamic_slice_in_dim(w_in, core * half_cols, half_cols, 1),
        lax.dynamic_slice_in_dim(w_down, core * half_cols, half_cols, 0),
        lax.dynamic_slice_in_dim(b_in, core * half_cols, half_cols, 0),
    )
    far_half = [swap(value, "ffn", 1) for value in own_half]
    near_half = [swap(value, "tok", 1) for value in far_half]
    shards = [(w_in, w_down, b_in), far_half, near_half]

    place = mask_pos + lax.broadcasted_iota(jnp.int32, mask_pos.shape, 0) * seq_len
    place = jnp.where(mask_pos >= 0, place, -1).reshape(-1)
    pick = low(place[:, None] == lax.broadcasted_iota(jnp.int32, (place.shape[0], rows_here), 1))
    x_pick = dot_nn(pick, tokens)
    x_pick_low = low(x_pick)
    q_pick = low(dot_nn(x_pick_low, w_query) + b_query)
    k = low(dot_nn(tokens, w_key) + b_key)
    v = low(dot_nn(tokens, w_value) + b_value)
    pos_query = low(dot_nn(rel_table, w_query) + b_query)
    pos_key = low(dot_nn(rel_table, w_key) + b_key)

    def seq_rows(values, s, count):
        return values if seq_count == 1 else values[s * count : (s + 1) * count]

    firsts = [
        attend_picked(
            mask_pos[s],
            rel_ids[s],
            seq_rows(q_pick, s, slots),
            seq_rows(k, s, seq_len),
            seq_rows(v, s, seq_len),
            pos_query,
            pos_key,
        )
        for s in range(seq_count)
    ]
    join = lambda parts: parts[0] if seq_count == 1 else jnp.concatenate(parts, axis=0)
    ctx_pick = join([first[0] for first in firsts])

    over_tok = Halving("tok", 1, [2, 4], n_tok)
    over_all = Halving(("tok", "ffn"), n_ffn, [2 * n_ffn, 1, 4 * n_ffn], n_all)
    part = width // n_tok
    spots = np.arange(width)
    tok_order = reorder(over_tok.block_of(spots // part) * part + spots % part, width)
    own, own_rel = width // n_all, table_rows // n_all
    unit = math.gcd(own, own_rel)
    group = n_all * unit

    def all_source(count, size):
        spots = np.arange(count)
        return (
            over_all.block_of(spots % group // unit) * size
            + spots // group * unit
            + spots % unit
        )

    all_order = reorder(all_source(width, own), width)
    rel_source = all_source(table_rows, own_rel)
    rel_order = reorder(rel_source, table_rows)
    to_rows = lax.optimization_barrier(jnp.asarray(distance_rows(seq_len, table_rows)))
    expand = (to_rows[:, None] == lax.broadcasted_iota(jnp.int32, (1, table_rows), 1)).astype(bf16)
    expand_order = (to_rows[:, None] == rel_source[None, :]).astype(bf16)
    far_query = low(dot_nn(expand, pos_query))
    far_key = low(dot_nn(expand, pos_key))
    x_turned = low(dot_nn(tokens, all_order))
    x_pick_turned = low(dot_nn(x_pick_low, all_order))
    rel_turned = low(dot_nn(low(dot_tn(rel_order, rel_table)), all_order))

    h1_normed, h1_inv = norm_stats(x_pick + (dot_nn(ctx_pick, w_out) + b_out))
    h1_pick = h1_normed * ln1_gain + ln1_bias
    h1_mine = low(h1_pick)
    pair = lambda value: jnp.concatenate([value, swap(value, "ffn", 1)], axis=0)
    count = h1_mine.shape[0]
    both = lambda value: low(value)[:count].astype(f32) + swap(low(value)[count:], "ffn", 1).astype(f32)
    h1_both = pair(h1_mine)
    pre = dot_nn(h1_both, w_in) + b_in
    cdf = normal_cdf(pre)
    hidden = low(pre * cdf)
    branch = both(dot_nn(hidden, w_down)) + b_down
    z2_normed, z2_inv = norm_stats(h1_pick + branch)
    cot = jnp.where(mask_pos.reshape(-1, 1) >= 0, grad_vals.reshape(-1, width).astype(f32), 0.0)
    dz2, g_ln2_gain, g_ln2_bias = norm_backward(cot, z2_normed, z2_inv, ln2_gain)
    dffn = low(dz2)
    g_b_down = jnp.sum(dffn.astype(f32), axis=0)
    dffn_both = pair(dffn)
    slope = cdf + pre * (jnp.exp(-0.5 * pre * pre) * (1.0 / math.sqrt(2.0 * math.pi)))
    dpre = low(dot_nt(dffn_both, w_down) * slope)
    dh1 = dz2 + both(dot_nt(dpre, w_in))
    gb_in = jnp.sum(dpre.astype(f32), axis=0)
    dz1, g_ln1_gain, g_ln1_bias = norm_backward(dh1, h1_normed, h1_inv, ln1_gain)
    dattn = low(dz1)
    g_b_out = jnp.sum(dattn.astype(f32), axis=0)
    dctx = low(dot_nt(dattn, w_out))

    lefts = (low(dot_nn(h1_both, tok_order)), low(dot_nn(dffn_both, tok_order)))
    rights = (dpre, hidden)
    middle = width // 2
    sends = [low(dot_tn(a[:, middle:], b)) for a, b in zip(lefts, rights)]
    dctx, sends = lax.optimization_barrier((dctx, sends))
    got = [over_tok.send(value, 0) for value in sends]
    ffn_sums = [
        low(dot_tn(a[:, :middle], b) + value.astype(f32)) for a, b, value in zip(lefts, rights, got)
    ]

    def halve(values, sums, step, axis):
        size = values[0].shape[axis] // 2
        cut = lambda value, at: lax.slice_in_dim(value, at, at + size, axis=axis)
        got = [sums.send(cut(value, size), step) for value in values]
        return [
            low(cut(value, 0).astype(f32) + other.astype(f32)) for value, other in zip(values, got)
        ]

    backs = []
    for s in range(seq_count):
        picks = lambda value: seq_rows(value, s, slots)
        _, probs, _, words, words_pick = firsts[s]
        backs.append(
            attend_back(
                words,
                words_pick,
                picks(q_pick),
                seq_rows(k, s, seq_len),
                seq_rows(v, s, seq_len),
                picks(dctx),
                probs,
                far_query,
                far_key,
            )
        )
    dq = join([back[0] for back in backs])
    dk = join([back[1] for back in backs])
    dv = join([back[2] for back in backs])
    dfar = backs[0][3] if seq_count == 1 else low(sum(back[3].astype(f32) for back in backs))
    for step in range(1, over_tok.steps):
        ffn_sums = halve(ffn_sums, over_tok, step, 0)

    dpos = low(jnp.einsum("mr,tmc->trc", expand_order, dfar, preferred_element_type=f32))
    c_pick_turned = low(dot_nn(ctx_pick, all_order))
    grads = lambda half: weight_grads(
        half, x_turned, rel_turned, x_pick_turned, c_pick_turned, dpos, dq, dk, dv, dattn, w_query, w_key
    )
    send, sums = grads(1)
    got = over_all.send(send, 0)
    dk_later = after(dk, send)
    keep, _ = weight_grads(
        0, x_turned, rel_turned, x_pick_turned, c_pick_turned, dpos, dq, dk_later, dv, dattn, w_query, w_key
    )
    all_sums = low(keep.astype(f32) + got.astype(f32))
    vectors = jnp.concatenate(
        [
            sums[:3],
            jnp.stack([g_b_out, g_ln1_gain, g_ln1_bias, g_b_down, g_ln2_gain, g_ln2_bias]),
            gb_in.reshape(hidden_cols // width, width),
        ],
        axis=0,
    )
    shared = lax.broadcasted_iota(jnp.int32, (vectors.shape[0], 1), 0) < 9

    def double(values, step):
        other = over_all.send(values, step)
        return values + jnp.where(shared | (over_all.bit(step) != 1), other, 0.0)

    vectors = double(vectors, 0)

    q = low(dot_nn(after(tokens, dk), w_query) + b_query)
    cuts = [0, pairs // 2, pairs]
    ctx = []
    for step in range(1, over_all.steps):
        (next_sums,) = halve([all_sums], over_all, step, 1)
        next_vectors = double(vectors, step)
        if step < len(cuts):
            at, stop = cuts[step - 1], cuts[step]
            q = after(q, all_sums)
            ctx.append(
                join(
                    [
                        attend_full(
                            rel_ids[s],
                            seq_rows(q, s, seq_len),
                            seq_rows(k, s, seq_len),
                            seq_rows(v, s, seq_len),
                            pos_key,
                            firsts[s][2],
                            at,
                            stop - at,
                        )
                        for s in range(seq_count)
                    ]
                )
            )
        all_sums, vectors = next_sums, next_vectors
    attn = sum(
        dot_nn(value, w_out[at * LANES : stop * LANES])
        for value, at, stop in zip(ctx, cuts[:-1], cuts[1:])
    )
    normed, _ = norm_stats(tokens.astype(f32) + (attn + b_out))
    h1 = normed * ln1_gain + ln1_bias
    h1_low = low(h1)
    branch_all = b_down
    for in_part, down_part, bias_part in shards:
        pre_act = dot_nn(h1_low, in_part) + bias_part
        branch_all = branch_all + dot_nn(low(pre_act * normal_cdf(pre_act)), down_part)
    final, _ = norm_stats(h1 + branch_all)
    output = low(final * ln2_gain + ln2_bias)

    sparse = dz1 + dot_nt(dq, w_query)
    sparse_up = low(sparse)
    sparse_lo = low(sparse - sparse_up.astype(f32))
    grad_tokens = (
        dot_tn(pick, sparse_up) + dot_tn(pick, sparse_lo) + dot_nt(dk, w_key) + dot_nt(dv, w_value)
    )

    wide = lambda value: value.astype(f32)
    all_sums = all_sums.reshape(all_sums.shape[0] * unit, width)
    s_w = [wide(all_sums[n * own : (n + 1) * own]) for n in range(4)]
    s_rel = wide(all_sums[4 * own :])
    s_vec = lax.dynamic_slice_in_dim(vectors[:9], over_all.me * own, own, 1)
    s_bin = lax.dynamic_slice_in_dim(
        vectors[9:].reshape(1, hidden_cols), over_tok.me * (hidden_cols // n_tok), hidden_cols // n_tok, 1
    )
    return (
        output,
        grad_tokens,
        s_w[0],
        s_w[1],
        s_w[2],
        s_w[3],
        s_vec[0],
        s_vec[1],
        s_vec[2],
        s_vec[3],
        s_rel,
        s_vec[4],
        s_vec[5],
        wide(ffn_sums[0]),
        s_bin,
        jnp.transpose(wide(ffn_sums[1])),
        s_vec[6],
        s_vec[7],
        s_vec[8],
    )


def solution(mesh):
    every = ("tok", "ffn")
    placed = (
        P(every, None), P(every, None, None), P(every, None), P(every, None, None),
        P(), P(), P(), P(), P(), P(), P(), P(), P(), P(), P(),
        P(None, "ffn"), P("ffn"), P("ffn", None), P(), P(), P(),
    )
    given = (
        P(every, None), P(every, None),
        P(every, None), P(every, None), P(every, None), P(every, None),
        P(every), P(every), P(every), P(every),
        P(every, None), P(every), P(every),
        P("tok", "ffn"), P("ffn", "tok"), P("ffn", "tok"),
        P(every), P(every), P(every),
    )
    return jax.shard_map(local, mesh=mesh, in_specs=placed, out_specs=given, check_vma=False)
```

```python
import functools
import math

import numpy as np

import jax
import jax.numpy as jnp
from jax import lax
from jax.experimental import pallas as pl
from jax.experimental.pallas import tpu as pltpu
from jax.sharding import PartitionSpec as P

HEAD = 64
LANES = 128
HALF = 64
ROWS = 32
norm_eps = 1e-07
bf16 = jnp.bfloat16
f32 = jnp.float32


def dot_nn(first_op, second_op):
    return lax.dot_general(
        first_op, second_op, (((1,), (0,)), ((), ())), preferred_element_type=f32
    )


def dot_nt(first_op, second_op):
    return lax.dot_general(
        first_op, second_op, (((1,), (1,)), ((), ())), preferred_element_type=f32
    )


def dot_tn(first_op, second_op):
    return lax.dot_general(
        first_op, second_op, (((0,), (0,)), ((), ())), preferred_element_type=f32
    )


def distance_rows(seq_len, table_rows):
    side = table_rows // 2
    middle = side // 2
    rows = []
    for m in range(2 * seq_len):
        offset = max(seq_len - 1 - m, 1 - seq_len)
        size = abs(offset)
        if size > middle:
            ratio = math.log(size / middle) / math.log((2 * side - 1) / middle)
            size = int(math.ceil(ratio * (middle - 1))) + middle
        rows.append(side + (size if offset > 0 else -size))
    return np.array(rows, dtype=np.int32)


def lane_iota(rows=1):
    return lax.broadcasted_iota(jnp.int32, (rows, LANES), 1)


def member_chunk(words, c):
    return (words == lane_iota(words.shape[0]) + c * LANES).astype(f32).astype(bf16)


def id_bases(rel_ref, base):
    seq = rel_ref.shape[0]
    chunks = seq // LANES
    last = chunks * 2 - 2
    for g in range(seq // HALF):
        for c in range(chunks):
            block = rel_ref[g * HALF : (g + 1) * HALF, c * LANES : (c + 1) * LANES]
            base[g * chunks + c] = jnp.minimum(jnp.min(block) // HALF, last)


def both_alignments(table):
    return jnp.concatenate([table, table[HALF:], table[:HALF]], axis=0)


def longest(rows):
    wide = rows.astype(f32)
    return jnp.sqrt(jnp.max(jnp.sum(wide * wide, axis=1, keepdims=True)))


def pack_heads(first, second, dest, top):
    top = jnp.maximum(top, 1e-30)
    scale = 32000.0 / top
    upper = (first * scale).astype(jnp.int32)
    lower = (second * scale).astype(jnp.int32)
    dest[...] = upper * 65536 + lower
    return top * (1.0 / 32000.0)


def unpack_heads(words, step):
    lower = lax.shift_right_arithmetic(lax.shift_left(words, 16), 16)
    return words.astype(f32) * (step * (1.0 / 65536.0)), lower.astype(f32) * step


def picked_words(source, rel_ref, base, rows, c):
    chunks = rel_ref.shape[1] // LANES
    first = base[(rows.start // HALF) * chunks + c]
    place = rel_ref[rows, c * LANES : (c + 1) * LANES] - first * HALF
    index = place & (LANES - 1)
    at = pl.multiple_of((first % 2) * (chunks * LANES) + (first // 2) * LANES, LANES)
    near = jnp.take_along_axis(source[rows, pl.ds(at, LANES)], index, axis=1)
    at = pl.multiple_of(at + LANES, LANES)
    far = jnp.take_along_axis(source[rows, pl.ds(at, LANES)], index, axis=1)
    return jnp.where(place < LANES, near, far)


def unshift_in_order(source, words_ref, base, dest):
    seq = words_ref.shape[0]
    chunks = seq // LANES
    lane = lane_iota()
    zero = jnp.zeros((ROWS, LANES), f32)
    for g in range(chunks):
        first = base[g]
        for sub in range(LANES // ROWS):
            start = g * LANES + sub * ROWS
            rows = slice(start, start + ROWS)
            place = lane - (seq - 1) + words_ref[rows, :] + first * LANES
            index = place & (LANES - 1)
            turned = [
                jnp.take_along_axis(
                    source[rows, c * LANES : (c + 1) * LANES], index, axis=1
                )
                for c in range(chunks)
            ]

            def pick(c):
                return turned[c] if 0 <= c < chunks else zero

            near = place >= 0
            mid = place >= -LANES
            for c in range(chunks + 2):
                value = jnp.where(near, pick(c), jnp.where(mid, pick(c - 1), pick(c - 2)))
                at = pl.multiple_of((first + c) * LANES, LANES)
                dest[rows, pl.ds(at, LANES)] = value.astype(bf16)


def group_bases(words, base):
    seq = words.shape[0]
    for g in range(seq // LANES):
        top = jnp.max(words[g * LANES : (g + 1) * LANES])
        base[g] = (seq - 1 - top) // LANES


def softmax_weights(scores):
    factor = math.log2(math.e) / math.sqrt(3.0 * HEAD)
    top = jnp.max(functools.reduce(jnp.maximum, scores), axis=1, keepdims=True)
    return [jnp.exp2((score - top) * factor) for score in scores]


def head_lanes(a):
    return (lane_iota() < HEAD) if a == 0 else (lane_iota() >= HEAD)


def picked_kernel(
    pos_ref, rel_ref, qc_ref, k_ref, v_ref, pk_ref, pq_ref,
    ctx_ref, prob_ref, key_ref, word_ref, wordc_ref,
    packed, cpick, relc, keyc, base,
):
    seq = k_ref.shape[0]
    picks = qc_ref.shape[0]
    chunks = seq // LANES

    @pl.when(pl.program_id(0) == 0)
    def _():
        row = lax.broadcasted_iota(jnp.int32, (seq, seq), 0)
        col = lax.broadcasted_iota(jnp.int32, (seq, seq), 1)
        side = pk_ref.shape[0] // 2
        step = jnp.sum(jnp.where(col == row - 1, rel_ref[...] - side, 0), axis=1, keepdims=True)
        steps = jnp.broadcast_to(step.astype(f32), (seq, LANES)).astype(bf16)
        word_ref[...] = dot_nn((col <= row).astype(f32).astype(bf16), steps).astype(jnp.int32)
        id_bases(rel_ref, base)
        for n in range(picks):
            place = jnp.maximum(pos_ref[n], 0)
            relc[n : n + 1, :] = rel_ref[pl.ds(place, 1), :]
            wordc_ref[n : n + 1, :] = word_ref[pl.ds(place, 1), :]

    zero = jnp.zeros((), bf16)
    table = both_alignments(pq_ref[...])
    keys = [dot_nt(jnp.where(head_lanes(a), k_ref[...], zero), table) for a in range(2)]
    unit = pack_heads(keys[0], keys[1], packed, longest(k_ref[...]) * longest(pq_ref[...]))
    for a in range(2):
        cpick[a] = dot_nt(jnp.where(head_lanes(a), qc_ref[...], zero), pk_ref[...])
    for g in range(chunks):
        for c in range(chunks):
            parts = []
            for start in range(g * LANES, (g + 1) * LANES, ROWS):
                parts.append(picked_words(packed, rel_ref, base, slice(start, start + ROWS), c))
            block = jnp.concatenate(parts, axis=0).T
            for a, value in enumerate(unpack_heads(block, unit)):
                key_ref[a, c * LANES : (c + 1) * LANES, g * LANES : (g + 1) * LANES] = value

    for n in range(picks):
        place = jnp.maximum(pos_ref[n], 0)
        for a in range(2):
            keyc[a, n : n + 1, :] = key_ref[a, pl.ds(place, 1), :]
    for a in range(2):
        mine = head_lanes(a)
        direct = dot_nt(jnp.where(mine, qc_ref[...], zero), k_ref[...])
        scores = []
        for c in range(chunks):
            ids = relc[:, c * LANES : (c + 1) * LANES]
            index = ids & (LANES - 1)
            value = jnp.take_along_axis(cpick[a, :, :LANES], index, axis=1)
            for n in range(1, pk_ref.shape[0] // LANES):
                other = cpick[a, :, n * LANES : (n + 1) * LANES]
                value = jnp.where(
                    ids >= n * LANES, jnp.take_along_axis(other, index, axis=1), value
                )
            cols = slice(c * LANES, (c + 1) * LANES)
            scores.append(direct[:, cols] + value + keyc[a, :, cols])
        weights = softmax_weights(scores)
        inverse = 1.0 / jnp.sum(sum(weights[1:], weights[0]), axis=1, keepdims=True)
        probs = jnp.concatenate([(weight * inverse).astype(bf16) for weight in weights], axis=1)
        prob_ref[a] = probs
        mixed = dot_nn(probs, v_ref[...]).astype(bf16)
        ctx_ref[...] = mixed if a == 0 else jnp.where(mine, mixed, ctx_ref[...])


def attend_picked(positions, rel_ids, q_pick, k, v, pos_query, pos_key):
    seq, width = k.shape
    picks = q_pick.shape[0]
    table = pos_key.shape[0]
    pairs = width // LANES
    whole = lambda rows, cols: pl.BlockSpec((rows, cols), lambda h: (0, 0))
    col = lambda rows: pl.BlockSpec((rows, LANES), lambda h: (0, h))
    heads = lambda rows: pl.BlockSpec((2, rows, seq), lambda h: (h, 0, 0))
    return pl.pallas_call(
        picked_kernel,
        grid=(pairs,),
        in_specs=[
            pl.BlockSpec(memory_space=pltpu.SMEM), whole(seq, seq),
            col(picks), col(seq), col(seq), col(table), col(table),
        ],
        out_specs=[
            col(picks), heads(picks), heads(seq), whole(seq, LANES), whole(picks, LANES),
        ],
        out_shape=[
            jax.ShapeDtypeStruct((picks, width), bf16),
            jax.ShapeDtypeStruct((2 * pairs, picks, seq), bf16),
            jax.ShapeDtypeStruct((2 * pairs, seq, seq), f32),
            jax.ShapeDtypeStruct((seq, LANES), jnp.int32),
            jax.ShapeDtypeStruct((picks, LANES), jnp.int32),
        ],
        scratch_shapes=[
            pltpu.VMEM((seq, 2 * table), jnp.int32),
            pltpu.VMEM((2, picks, table), f32),
            pltpu.VMEM((picks, seq), jnp.int32),
            pltpu.VMEM((2, picks, seq), f32),
            pltpu.SMEM((seq // HALF * (seq // LANES),), jnp.int32),
        ],
        compiler_params=pltpu.CompilerParams(vmem_limit_bytes=48 * 2**20),
        name="attend_picked",
    )(positions, rel_ids, q_pick, k, v, pos_key, pos_query)


def full_kernel(rel_ref, q_ref, k_ref, v_ref, pk_ref, key_ref, ctx_ref, packed, direct, low, base):
    seq = q_ref.shape[0]
    chunks = seq // LANES

    @pl.when(pl.program_id(0) == 0)
    def _():
        id_bases(rel_ref, base)

    zero = jnp.zeros((), bf16)
    table = both_alignments(pk_ref[...])
    far = []
    for a in range(2):
        q_a = jnp.where(head_lanes(a), q_ref[...], zero)
        far.append(dot_nt(q_a, table))
        direct[a] = dot_nt(q_a, k_ref[...])
    unit = pack_heads(far[0], far[1], packed, longest(q_ref[...]) * longest(pk_ref[...]))
    for start in range(0, seq, HALF):
        rows = slice(start, start + HALF)
        scores = [[], []]
        for c in range(chunks):
            cols = slice(c * LANES, (c + 1) * LANES)
            values = unpack_heads(picked_words(packed, rel_ref, base, rows, c), unit)
            for a in range(2):
                scores[a].append(values[a] + direct[a, rows, cols] + key_ref[a, rows, cols])
        for a in range(2):
            for c, weight in enumerate(softmax_weights(scores[a])):
                low[a, rows, c * LANES : (c + 1) * LANES] = weight.astype(bf16)
    mixed = [
        dot_nn(low[a], jnp.where(head_lanes(a), v_ref[...], jnp.ones((), bf16))) for a in range(2)
    ]
    upper = head_lanes(0)
    totals = pltpu.roll(jnp.where(upper, mixed[1], mixed[0]), HEAD, 1)
    ctx_ref[...] = (jnp.where(upper, mixed[0], mixed[1]) * (1.0 / totals)).astype(bf16)


def attend_full(rel_ids, q, k, v, pos_key, key_scores, first, pairs):
    seq = k.shape[0]
    table = pos_key.shape[0]
    col = lambda rows: pl.BlockSpec((rows, LANES), lambda h: (0, h + first))
    return pl.pallas_call(
        full_kernel,
        grid=(pairs,),
        in_specs=[
            pl.BlockSpec((seq, seq), lambda h: (0, 0)),
            col(seq), col(seq), col(seq), col(table),
            pl.BlockSpec((2, seq, seq), lambda h: (h + first, 0, 0)),
        ],
        out_specs=pl.BlockSpec((seq, LANES), lambda h: (0, h)),
        out_shape=jax.ShapeDtypeStruct((seq, pairs * LANES), bf16),
        scratch_shapes=[
            pltpu.VMEM((seq, 2 * table), jnp.int32),
            pltpu.VMEM((2, seq, seq), f32),
            pltpu.VMEM((2, seq, seq), bf16),
            pltpu.SMEM((seq // HALF * (seq // LANES),), jnp.int32),
        ],
        compiler_params=pltpu.CompilerParams(vmem_limit_bytes=48 * 2**20),
        name="attend_full",
    )(rel_ids, q, k, v, pos_key, key_scores)


def back_kernel(
    row_ref, order_ref, word_ref, wordc_ref, qc_ref, k_ref, v_ref, dctx_ref, prob_ref, pk_ref, pq_ref,
    dq_ref, dk_ref, dv_ref, dpos_ref,
    side, sidec, moved, movedc, grel, expand, turned_expand, base,
):
    seq = k_ref.shape[0]
    picks = qc_ref.shape[0]
    table = pk_ref.shape[0]
    chunks = seq // LANES

    @pl.when(pl.program_id(0) == 0)
    def _():
        words = word_ref[...]
        for c in range(chunks):
            side[:, c * LANES : (c + 1) * LANES] = member_chunk(words, c)
            sidec[:, c * LANES : (c + 1) * LANES] = member_chunk(wordc_ref[...], c)
        group_bases(words, base)
        moved[...] = jnp.zeros_like(moved)
        for c in range(table // LANES):
            cols = slice(c * LANES, (c + 1) * LANES)
            expand[:, cols] = member_chunk(row_ref[...], c)
            turned_expand[:, cols] = (row_ref[...] == order_ref[:1, cols]).astype(f32).astype(bf16)

    lane = lane_iota()
    scale = 1.0 / math.sqrt(3.0 * HEAD)
    zero = jnp.zeros((), bf16)
    far_key = dot_nn(expand[...], pk_ref[...]).astype(bf16)
    far_query = dot_nn(expand[...], pq_ref[...]).astype(bf16)
    for a in range(2):
        mine = head_lanes(a)
        keep = lambda value: jnp.where(mine, value, zero)
        dctx_a = keep(dctx_ref[...])
        q_a = keep(qc_ref[...])
        k_a = keep(k_ref[...])
        side[:, seq:] = k_a
        sidec[:, seq:] = q_a
        dprobs = dot_nt(dctx_a, v_ref[...])
        probs = prob_ref[a].astype(f32)
        prod = probs * dprobs
        gs = ((prod - probs * jnp.sum(prod, axis=1, keepdims=True)) * scale).astype(bf16)
        dv = dot_tn(prob_ref[a], dctx_a)

        out = dot_nn(gs, side[...])
        place = lane - (seq - 1) + wordc_ref[...]
        index = place & (LANES - 1)
        turned = [
            jnp.take_along_axis(out[:, c * LANES : (c + 1) * LANES], index, axis=1)
            for c in range(chunks)
        ]
        blank = jnp.zeros((picks, LANES), f32)
        for c in range(2 * chunks):
            value = turned[c] if c < chunks else blank
            for n in range(1, chunks + 1):
                other = turned[c - n] if 0 <= c - n < chunks else blank
                value = jnp.where(place < -LANES * (n - 1), other, value)
            movedc[:, c * LANES : (c + 1) * LANES] = value.astype(bf16)
        dq = out[:, seq:] + dot_nn(movedc[...], keep(far_key))
        dpk = dot_tn(movedc[...], q_a)

        out = dot_tn(gs, sidec[...])
        grel[...] = out[:, :seq]
        unshift_in_order(grel, word_ref, base, moved)
        dk = out[:, seq:] + dot_nn(moved[:, : 2 * seq], keep(far_query))
        dpq = dot_tn(moved[:, : 2 * seq], k_a)
        dpk = dot_tn(turned_expand[...], dpk.astype(bf16))
        dpq = dot_tn(turned_expand[...], dpq.astype(bf16))
        for ref, value in (
            (dq_ref, dq), (dk_ref, dk), (dv_ref, dv), (dpos_ref.at[0], dpk), (dpos_ref.at[1], dpq),
        ):
            low = value.astype(bf16)
            ref[...] = low if a == 0 else jnp.where(mine, low, ref[...])


def attend_back(
    table_of, order, words, words_pick, q_pick, k, v, dctx, probs, pos_query, pos_key
):
    seq, width = k.shape
    picks = q_pick.shape[0]
    table = pos_key.shape[0]
    pairs = width // LANES
    whole = lambda value: pl.BlockSpec(value.shape, lambda h: (0, 0))
    col = lambda rows: pl.BlockSpec((rows, LANES), lambda h: (0, h))
    shape = lambda rows: jax.ShapeDtypeStruct((rows, width), bf16)
    return pl.pallas_call(
        back_kernel,
        grid=(pairs,),
        in_specs=[
            whole(table_of), whole(order), whole(words), whole(words_pick),
            col(picks), col(seq), col(seq), col(picks),
            pl.BlockSpec((2, picks, seq), lambda h: (h, 0, 0)),
            col(table), col(table),
        ],
        out_specs=[
            col(picks), col(seq), col(seq),
            pl.BlockSpec((2, table, LANES), lambda h: (0, 0, h)),
        ],
        out_shape=[
            shape(picks), shape(seq), shape(seq),
            jax.ShapeDtypeStruct((2, table, width), bf16),
        ],
        scratch_shapes=[
            pltpu.VMEM((seq, seq + LANES), bf16),
            pltpu.VMEM((picks, seq + LANES), bf16),
            pltpu.VMEM((seq, 2 * seq + LANES), bf16),
            pltpu.VMEM((picks, 2 * seq), bf16),
            pltpu.VMEM((seq, seq), f32),
            pltpu.VMEM((2 * seq, table), bf16),
            pltpu.VMEM((2 * seq, table), bf16),
            pltpu.SMEM((seq // LANES,), jnp.int32),
        ],
        compiler_params=pltpu.CompilerParams(vmem_limit_bytes=48 * 2**20),
        name="attend_back",
    )(table_of, order, words, words_pick, q_pick, k, v, dctx, probs, pos_key, pos_query)


def grads_kernel(
    half, x_ref, rel_ref, xpick_ref, cpick_ref, dpos_ref,
    dq_ref, dk_ref, dv_ref, dattn_ref, dposk_ref, dposq_ref, wq_ref, wk_ref,
    out_ref, sum_ref,
):
    width = x_ref.shape[1]
    group = 2 * LANES
    seq = x_ref.shape[0]

    def left(ref):
        starts = range(half * LANES, width, group)
        return jnp.concatenate([ref[:, at : at + LANES] for at in starts], axis=1)

    def put(at, value):
        for n in range(value.shape[0] // LANES):
            out_ref[at + n] = value[n * LANES : (n + 1) * LANES].astype(bf16)

    count = width // group
    rel_left = left(rel_ref)
    x_left = left(x_ref)
    put(0, dot_tn(left(xpick_ref), dq_ref[...]) + dot_tn(rel_left, dposq_ref[0]))
    put(count, dot_tn(x_left, dk_ref[...]) + dot_tn(rel_left, dposk_ref[0]))
    put(2 * count, dot_tn(x_left, dv_ref[...]))
    put(3 * count, dot_tn(left(cpick_ref), dattn_ref[...]))
    for n in range(dpos_ref.shape[1] // group):
        rows = slice(n * group + half * LANES, n * group + (half + 1) * LANES)
        put(
            4 * count + n,
            dot_nt(dpos_ref[0, rows, :], wk_ref[...]) + dot_nt(dpos_ref[1, rows, :], wq_ref[...]),
        )
    total = lambda ref: jnp.sum(ref[...].astype(f32), axis=-2).reshape(1, group)
    sum_ref[...] = jnp.concatenate(
        [
            total(dq_ref) + total(dposq_ref),
            total(dk_ref) + total(dposk_ref),
            total(dv_ref),
            jnp.zeros((5, group), f32),
        ],
        axis=0,
    )


def weight_grads(half, x, rel, x_pick, c_pick, dpos, dq, dk, dv, dattn, w_query, w_key):
    seq, width = x.shape
    group = 2 * LANES
    planes = 4 * (width // group) + dpos.shape[1] // group
    whole = lambda value: pl.BlockSpec(value.shape, lambda n: (0,) * value.ndim)
    col = lambda value: pl.BlockSpec((value.shape[0], group), lambda n: (0, n))
    row = lambda value: pl.BlockSpec((group, value.shape[1]), lambda n: (n, 0))
    plane = lambda t: pl.BlockSpec((1, dpos.shape[1], group), lambda n: (t, 0, n))
    return pl.pallas_call(
        functools.partial(grads_kernel, half),
        grid=(width // group,),
        in_specs=[
            whole(x), whole(rel), whole(x_pick), whole(c_pick), whole(dpos),
            col(dq), col(dk), col(dv), col(dattn), plane(0), plane(1), row(w_query), row(w_key),
        ],
        out_specs=[
            pl.BlockSpec((planes, LANES, group), lambda n: (0, 0, n)),
            pl.BlockSpec((8, group), lambda n: (0, n)),
        ],
        out_shape=[
            jax.ShapeDtypeStruct((planes, LANES, width), bf16),
            jax.ShapeDtypeStruct((8, width), f32),
        ],
        compiler_params=pltpu.CompilerParams(vmem_limit_bytes=48 * 2**20),
        name="weight_grads",
    )(x, rel, x_pick, c_pick, dpos, dq, dk, dv, dattn, dpos, dpos, w_query, w_key)


def norm_stats(values):
    centered = values - jnp.mean(values, axis=1, keepdims=True)
    inv_std = lax.rsqrt(jnp.mean(centered * centered, axis=1, keepdims=True) + norm_eps)
    return centered * inv_std, inv_std


def norm_backward(upstream, normed, inv_std, norm_gain):
    scaled = upstream * norm_gain
    adjusted = (
        scaled
        - jnp.mean(scaled, axis=1, keepdims=True)
        - normed * jnp.mean(scaled * normed, axis=1, keepdims=True)
    )
    return (inv_std * adjusted, jnp.sum(upstream * normed, axis=0), jnp.sum(upstream, axis=0))


def normal_cdf(pre_act):
    return 0.5 * (1.0 + lax.erf(pre_act * (1.0 / math.sqrt(2.0))))


def swap(values, axis, bit):
    size = lax.axis_size(axis)
    return lax.ppermute(values, axis, [(n, n ^ bit) for n in range(size)])


def after(values, *others):
    return lax.optimization_barrier((values, others))[0]


class Halving:
    def __init__(self, axes, core, near, size):
        rest = [1 << n for n in range(size.bit_length() - 1) if (1 << n) != core]
        near = [bit for bit in near if bit in rest]
        rest = [bit for bit in rest if bit not in near]
        turned = near[-1:] + near[:-1]
        self.axes, self.core, self.size = axes, core, size
        self.orders = [[core] + near + rest, [core] + turned + rest]
        self.steps = len(self.orders[0])
        self.me = lax.axis_index(axes)
        self.upper = (self.me // core) % 2

    def core_of(self, place):
        return (place // self.core) % 2

    def send(self, values, step):
        pairs = [(n, n ^ self.orders[self.core_of(n)][step]) for n in range(self.size)]
        return lax.ppermute(values, self.axes, pairs)

    def bit(self, step):
        first, second = (order[step] for order in self.orders)
        return jnp.where(self.upper == 0, first, second)

    def block_of(self, places):
        relative = []
        for upper in range(2):
            masks = []
            for place in range(self.size):
                bits = [(place >> (self.steps - 1 - step)) & 1 for step in range(self.steps)]
                order = self.orders[upper ^ bits[0]]
                mask = 0
                for step, bit in enumerate(bits):
                    mask ^= bit * order[step]
                masks.append(mask)
            relative.append(np.array(masks, np.int32)[places])
        return self.me ^ jnp.where(self.upper == 0, relative[0], relative[1])


def reorder(source, length):
    return (lax.broadcasted_iota(jnp.int32, (length, source.shape[0]), 0) == source[None, :]).astype(bf16)


def local(
    tokens, rel_ids, mask_pos, grad_vals, w_query, w_key, w_value, w_out, b_query, b_key,
    b_value, b_out, rel_table, ln1_gain, ln1_bias, w_in, b_in, w_down, b_down, ln2_gain, ln2_bias,
):
    seq_count, seq_len = rel_ids.shape[0], rel_ids.shape[1]
    rows_here, width = tokens.shape
    table_rows = rel_table.shape[0]
    hidden_cols = w_in.shape[1]
    slots = mask_pos.shape[1]
    pairs = width // LANES
    n_tok = lax.axis_size("tok")
    n_ffn = lax.axis_size("ffn")
    n_all = n_tok * n_ffn
    low = lambda value: value.astype(bf16)

    place = mask_pos + lax.broadcasted_iota(jnp.int32, mask_pos.shape, 0) * seq_len
    place = jnp.where(mask_pos >= 0, place, -1).reshape(-1)
    pick = low(place[:, None] == lax.broadcasted_iota(jnp.int32, (place.shape[0], rows_here), 1))
    x_pick = dot_nn(pick, tokens)
    x_pick_low = low(x_pick)
    q_pick = low(dot_nn(x_pick_low, w_query) + b_query)
    k = low(dot_nn(tokens, w_key) + b_key)
    v = low(dot_nn(tokens, w_value) + b_value)
    pos_query = low(dot_nn(rel_table, w_query) + b_query)
    pos_key = low(dot_nn(rel_table, w_key) + b_key)

    def seq_rows(values, s, count):
        return values if seq_count == 1 else values[s * count : (s + 1) * count]

    firsts = [
        attend_picked(
            mask_pos[s],
            rel_ids[s],
            seq_rows(q_pick, s, slots),
            seq_rows(k, s, seq_len),
            seq_rows(v, s, seq_len),
            pos_query,
            pos_key,
        )
        for s in range(seq_count)
    ]
    join = lambda parts: parts[0] if seq_count == 1 else jnp.concatenate(parts, axis=0)
    ctx_pick = join([first[0] for first in firsts])

    over_tok = Halving("tok", 1, [2, 4], n_tok)
    over_all = Halving(("tok", "ffn"), n_ffn, [2 * n_ffn, 1, 4 * n_ffn], n_all)
    part = width // n_tok
    spots = np.arange(width)
    tok_order = reorder(over_tok.block_of(spots // part) * part + spots % part, width)
    own, own_rel = width // n_all, table_rows // n_all
    unit = math.gcd(own, own_rel)
    group = n_all * unit

    def all_source(count, size):
        spots = np.arange(count)
        return (
            over_all.block_of(spots % group // unit) * size
            + spots // group * unit
            + spots % unit
        )

    all_order = reorder(all_source(width, own), width)
    rel_source = all_source(table_rows, own_rel)
    tok_order, all_order, rel_order = lax.optimization_barrier(
        (tok_order, all_order, reorder(rel_source, table_rows))
    )
    table_of = jnp.broadcast_to(
        jnp.asarray(distance_rows(seq_len, table_rows))[:, None], (2 * seq_len, LANES)
    )
    order_rows = jnp.broadcast_to(rel_source[None, :], (8, table_rows))
    x_turned = low(dot_nn(tokens, all_order))
    x_pick_turned = low(dot_nn(x_pick_low, all_order))
    rel_turned = low(dot_nn(low(dot_tn(rel_order, rel_table)), all_order))
    q = low(dot_nn(tokens, w_query) + b_query)

    h1_normed, h1_inv = norm_stats(x_pick + (dot_nn(ctx_pick, w_out) + b_out))
    h1_pick = h1_normed * ln1_gain + ln1_bias
    h1_mine = low(h1_pick)
    pair = lambda value: jnp.concatenate([value, swap(value, "ffn", 1)], axis=0)
    count = h1_mine.shape[0]
    both = lambda value: low(value)[:count].astype(f32) + swap(low(value)[count:], "ffn", 1).astype(f32)
    h1_both = pair(h1_mine)
    pre = dot_nn(h1_both, w_in) + b_in
    cdf = normal_cdf(pre)
    hidden = low(pre * cdf)
    branch = both(dot_nn(hidden, w_down)) + b_down
    z2_normed, z2_inv = norm_stats(h1_pick + branch)
    cot = jnp.where(mask_pos.reshape(-1, 1) >= 0, grad_vals.reshape(-1, width).astype(f32), 0.0)
    dz2, g_ln2_gain, g_ln2_bias = norm_backward(cot, z2_normed, z2_inv, ln2_gain)
    dffn = low(dz2)
    g_b_down = jnp.sum(dffn.astype(f32), axis=0)
    dffn_both = pair(dffn)
    slope = cdf + pre * (jnp.exp(-0.5 * pre * pre) * (1.0 / math.sqrt(2.0 * math.pi)))
    dpre = low(dot_nt(dffn_both, w_down) * slope)
    dh1 = dz2 + both(dot_nt(dpre, w_in))
    gb_in = jnp.sum(dpre.astype(f32), axis=0)
    dz1, g_ln1_gain, g_ln1_bias = norm_backward(dh1, h1_normed, h1_inv, ln1_gain)
    dattn = low(dz1)
    g_b_out = jnp.sum(dattn.astype(f32), axis=0)
    dctx = low(dot_nt(dattn, w_out))

    core = lax.axis_index("tok") % 2
    half_cols = hidden_cols // 2
    in_half, bias_half, down_half = after(
        (
            lax.dynamic_slice_in_dim(w_in, core * half_cols, half_cols, 1),
            lax.dynamic_slice_in_dim(b_in, core * half_cols, half_cols, 0),
            lax.dynamic_slice_in_dim(w_down, core * half_cols, half_cols, 0),
        ),
        dh1,
    )
    far_in, far_bias = swap(in_half, "ffn", 1), swap(bias_half, "ffn", 1)

    lefts = (low(dot_nn(h1_both, tok_order)), low(dot_nn(dffn_both, tok_order)))
    rights = (dpre, hidden)
    middle = width // 2
    sends = [low(dot_tn(a[:, middle:], b)) for a, b in zip(lefts, rights)]
    dctx, sends = lax.optimization_barrier((dctx, sends))
    got = after([over_tok.send(value, 0) for value in sends], dctx)
    ffn_sums = [
        low(dot_tn(a[:, :middle], b) + value.astype(f32)) for a, b, value in zip(lefts, rights, got)
    ]

    def halves(values, axis):
        size = values.shape[axis] // 2
        cut = lambda at: lax.slice_in_dim(values, at, at + size, axis=axis)
        return cut(0), cut(size)

    def add(kept, others):
        return [low(one.astype(f32) + other.astype(f32)) for one, other in zip(kept, others)]

    def ffn_step(values, step):
        kept, sent = zip(*[halves(value, 0) for value in values])
        return kept, [over_tok.send(value, step) for value in sent]

    kept, got = ffn_step(ffn_sums, 1)
    dctx = after(dctx, ffn_sums, in_half)
    backs = []
    for s in range(seq_count):
        picks = lambda value: seq_rows(value, s, slots)
        _, probs, _, words, words_pick = firsts[s]
        backs.append(
            attend_back(
                table_of,
                order_rows,
                words,
                words_pick,
                picks(q_pick),
                seq_rows(k, s, seq_len),
                seq_rows(v, s, seq_len),
                picks(dctx),
                probs,
                pos_query,
                pos_key,
            )
        )
    dq = join([back[0] for back in backs])
    dk = join([back[1] for back in backs])
    dv = join([back[2] for back in backs])
    dpos = backs[0][3] if seq_count == 1 else low(sum(back[3].astype(f32) for back in backs))
    ffn_sums = add(kept, after(got, dk))
    far_in, far_bias = after((far_in, far_bias), dk)
    dk = after(dk, ffn_sums, far_in)
    near_in, near_bias = swap(far_in, "tok", 1), swap(far_bias, "tok", 1)
    far_down = swap(after(down_half, dk), "ffn", 1)
    c_pick_turned = low(dot_nn(ctx_pick, all_order))

    def grads(half, dk):
        return weight_grads(
            half, x_turned, rel_turned, x_pick_turned, c_pick_turned, dpos, dq, dk, dv, dattn, w_query, w_key
        )

    ffn_step_now = 2
    if over_tok.steps > 2:
        kept, got = ffn_step(ffn_sums, 2)
    all_send, sums = grads(1, dk)
    all_got = over_all.send(all_send, 0)
    all_kept, _ = grads(0, after(dk, all_send))
    vectors = jnp.concatenate(
        [
            sums[:3],
            jnp.stack([g_b_out, g_ln1_gain, g_ln1_bias, g_b_down, g_ln2_gain, g_ln2_bias]),
            gb_in.reshape(hidden_cols // width, width),
        ],
        axis=0,
    )
    shared = lax.broadcasted_iota(jnp.int32, (vectors.shape[0], 1), 0) < 9
    vec_got = over_all.send(vectors, 0)
    (all_sums,) = add([all_kept], [after(all_got, all_kept)])
    vectors = vectors + vec_got

    def filler(step, state):
        if step <= 2:
            at, stop = pairs // 2 * (step - 1), pairs // 2 * step
            return join(
                [
                    attend_full(
                        rel_ids[s],
                        seq_rows(state[0], s, seq_len),
                        seq_rows(k, s, seq_len),
                        seq_rows(v, s, seq_len),
                        pos_key,
                        firsts[s][2],
                        at,
                        stop - at,
                    )
                    for s in range(seq_count)
                ]
            )
        if step == 3:
            attn = sum(
                dot_nn(value, w_out[n * width // 2 : (n + 1) * width // 2])
                for n, value in enumerate(state)
            )
            normed, _ = norm_stats(tokens.astype(f32) + (attn + b_out))
            return normed * ln1_gain + ln1_bias
        h1 = state[0]
        h1_low = low(h1)
        branch_all = b_down
        for in_part, down_part, bias_part in shards:
            pre_act = dot_nn(h1_low, in_part) + bias_part
            branch_all = branch_all + dot_nn(low(pre_act * normal_cdf(pre_act)), down_part)
        return branch_all

    fills = []
    for step in range(1, over_all.steps):
        kept_all, sent = halves(all_sums, 1)
        all_got = over_all.send(sent, step)
        vec_got = over_all.send(vectors, step)
        if step <= 4:
            state = [q] if step <= 2 else fills[:2] if step == 3 else [fills[2]]
            fills.append(filler(step, after(state, all_sums)))
            all_got, vec_got = after((all_got, vec_got), fills[-1])
        if step == 1:
            far_down = after(far_down, fills[0])
            near_down = swap(far_down, "tok", 1)
            shards = [
                (w_in, w_down, b_in), (far_in, far_down, far_bias), (near_in, near_down, near_bias)
            ]
            all_got = after(all_got, far_down)
        if ffn_step_now < over_tok.steps:
            ffn_sums = add(kept, got)
            ffn_step_now += 1
            if ffn_step_now < over_tok.steps:
                kept, got = ffn_step(ffn_sums, ffn_step_now)
        (all_sums,) = add([kept_all], [all_got])
        vectors = vectors + jnp.where(shared | (over_all.bit(step) != 1), vec_got, 0.0)
    for step in range(len(fills) + 1, 5):
        fills.append(filler(step, [q] if step <= 2 else fills[:2] if step == 3 else [fills[2]]))
    h1, branch_all = fills[2:]
    final, _ = norm_stats(h1 + branch_all)
    output = low(final * ln2_gain + ln2_bias)

    sparse = dz1 + dot_nt(dq, w_query)
    sparse_up = low(sparse)
    sparse_lo = low(sparse - sparse_up.astype(f32))
    grad_tokens = (
        dot_tn(pick, sparse_up) + dot_tn(pick, sparse_lo) + dot_nt(dk, w_key) + dot_nt(dv, w_value)
    )

    wide = lambda value: value.astype(f32)
    all_sums = all_sums.reshape(all_sums.shape[0] * unit, width)
    s_w = [wide(all_sums[n * own : (n + 1) * own]) for n in range(4)]
    s_rel = wide(all_sums[4 * own :])
    s_vec = lax.dynamic_slice_in_dim(vectors[:9], over_all.me * own, own, 1)
    s_bin = lax.dynamic_slice_in_dim(
        vectors[9:].reshape(1, hidden_cols), over_tok.me * (hidden_cols // n_tok), hidden_cols // n_tok, 1
    )
    return (
        output,
        grad_tokens,
        s_w[0],
        s_w[1],
        s_w[2],
        s_w[3],
        s_vec[0],
        s_vec[1],
        s_vec[2],
        s_vec[3],
        s_rel,
        s_vec[4],
        s_vec[5],
        wide(ffn_sums[0]),
        s_bin,
        jnp.transpose(wide(ffn_sums[1])),
        s_vec[6],
        s_vec[7],
        s_vec[8],
    )


def solution(mesh):
    every = ("tok", "ffn")
    placed = (
        P(every, None), P(every, None, None), P(every, None), P(every, None, None),
        P(), P(), P(), P(), P(), P(), P(), P(), P(), P(), P(),
        P(None, "ffn"), P("ffn"), P("ffn", None), P(), P(), P(),
    )
    given = (
        P(every, None), P(every, None),
        P(every, None), P(every, None), P(every, None), P(every, None),
        P(every), P(every), P(every), P(every),
        P(every, None), P(every), P(every),
        P("tok", "ffn"), P("ffn", "tok"), P("ffn", "tok"),
        P(every), P(every), P(every),
    )
    return jax.shard_map(local, mesh=mesh, in_specs=placed, out_specs=given, check_vma=False)
```

```python
import functools
import math

import numpy as np

import jax
import jax.numpy as jnp
from jax import lax
from jax.experimental import pallas as pl
from jax.experimental.pallas import tpu as pltpu
from jax.sharding import PartitionSpec as P

HEAD = 64
LANES = 128
HALF = 64
ROWS = 32
norm_eps = 1e-07
bf16 = jnp.bfloat16
f32 = jnp.float32


def dot_nn(first_op, second_op):
    return lax.dot_general(
        first_op, second_op, (((1,), (0,)), ((), ())), preferred_element_type=f32
    )


def dot_nt(first_op, second_op):
    return lax.dot_general(
        first_op, second_op, (((1,), (1,)), ((), ())), preferred_element_type=f32
    )


def dot_tn(first_op, second_op):
    return lax.dot_general(
        first_op, second_op, (((0,), (0,)), ((), ())), preferred_element_type=f32
    )


def distance_rows(seq_len, table_rows):
    side = table_rows // 2
    middle = side // 2
    rows = []
    for m in range(2 * seq_len):
        offset = max(seq_len - 1 - m, 1 - seq_len)
        size = abs(offset)
        if size > middle:
            ratio = math.log(size / middle) / math.log((2 * side - 1) / middle)
            size = int(math.ceil(ratio * (middle - 1))) + middle
        rows.append(side + (size if offset > 0 else -size))
    return np.array(rows, dtype=np.int32)


def lane_iota(rows=1):
    return lax.broadcasted_iota(jnp.int32, (rows, LANES), 1)


def member_chunk(words, c):
    return (words == lane_iota(words.shape[0]) + c * LANES).astype(f32).astype(bf16)


def id_bases(rel_ref, base):
    seq = rel_ref.shape[0]
    chunks = seq // LANES
    last = chunks * 2 - 2
    for g in range(seq // HALF):
        for c in range(chunks):
            block = rel_ref[g * HALF : (g + 1) * HALF, c * LANES : (c + 1) * LANES]
            base[g * chunks + c] = jnp.minimum(jnp.min(block) // HALF, last)


def both_alignments(table):
    return jnp.concatenate([table, table[HALF:], table[:HALF]], axis=0)


def longest(rows):
    wide = rows.astype(f32)
    return jnp.sqrt(jnp.max(jnp.sum(wide * wide, axis=1, keepdims=True)))


def pack_heads(first, second, dest, top):
    top = jnp.maximum(top, 1e-30)
    scale = 32000.0 / top
    upper = (first * scale).astype(jnp.int32)
    lower = (second * scale).astype(jnp.int32)
    dest[...] = upper * 65536 + lower
    return top * (1.0 / 32000.0)


def unpack_heads(words, step):
    lower = lax.shift_right_arithmetic(lax.shift_left(words, 16), 16)
    return words.astype(f32) * (step * (1.0 / 65536.0)), lower.astype(f32) * step


def picked_words(source, rel_ref, base, rows, c):
    chunks = rel_ref.shape[1] // LANES
    first = base[(rows.start // HALF) * chunks + c]
    place = rel_ref[rows, c * LANES : (c + 1) * LANES] - first * HALF
    index = place & (LANES - 1)
    at = pl.multiple_of((first % 2) * (chunks * LANES) + (first // 2) * LANES, LANES)
    near = jnp.take_along_axis(source[rows, pl.ds(at, LANES)], index, axis=1)
    at = pl.multiple_of(at + LANES, LANES)
    far = jnp.take_along_axis(source[rows, pl.ds(at, LANES)], index, axis=1)
    return jnp.where(place < LANES, near, far)


def unshift_in_order(source, words_ref, base, dest):
    seq = words_ref.shape[0]
    chunks = seq // LANES
    lane = lane_iota()
    zero = jnp.zeros((ROWS, LANES), f32)
    for g in range(chunks):
        first = base[g]
        for sub in range(LANES // ROWS):
            start = g * LANES + sub * ROWS
            rows = slice(start, start + ROWS)
            place = lane - (seq - 1) + words_ref[rows, :] + first * LANES
            index = place & (LANES - 1)
            turned = [
                jnp.take_along_axis(
                    source[rows, c * LANES : (c + 1) * LANES], index, axis=1
                )
                for c in range(chunks)
            ]

            def pick(c):
                return turned[c] if 0 <= c < chunks else zero

            near = place >= 0
            mid = place >= -LANES
            for c in range(chunks + 2):
                value = jnp.where(near, pick(c), jnp.where(mid, pick(c - 1), pick(c - 2)))
                at = pl.multiple_of((first + c) * LANES, LANES)
                dest[rows, pl.ds(at, LANES)] = value.astype(bf16)


def group_bases(words, base):
    seq = words.shape[0]
    for g in range(seq // LANES):
        top = jnp.max(words[g * LANES : (g + 1) * LANES])
        base[g] = (seq - 1 - top) // LANES


def softmax_weights(scores):
    factor = math.log2(math.e) / math.sqrt(3.0 * HEAD)
    top = jnp.max(functools.reduce(jnp.maximum, scores), axis=1, keepdims=True)
    return [jnp.exp2((score - top) * factor) for score in scores]


def head_lanes(a):
    return (lane_iota() < HEAD) if a == 0 else (lane_iota() >= HEAD)


def row_of(ref):
    return ref[...].reshape(1, ref.shape[0])


def norm_stats(values):
    centered = values - jnp.mean(values, axis=1, keepdims=True)
    inv_std = lax.rsqrt(jnp.mean(centered * centered, axis=1, keepdims=True) + norm_eps)
    return centered * inv_std, inv_std


def norm_backward(upstream, normed, inv_std, norm_gain):
    scaled = upstream * norm_gain
    adjusted = (
        scaled
        - jnp.mean(scaled, axis=1, keepdims=True)
        - normed * jnp.mean(scaled * normed, axis=1, keepdims=True)
    )
    return inv_std * adjusted, col_sum(upstream * normed), col_sum(upstream)


def col_sum(values):
    return jnp.sum(values, axis=0, keepdims=True)


def normal_cdf(pre_act):
    return 0.5 * (1.0 + lax.erf(pre_act * (1.0 / math.sqrt(2.0))))


def picked_kernel(
    pos_ref, rel_ref, qc_ref, k_ref, v_ref, pk_ref, pq_ref,
    x_ref, wo_ref, bo_ref, gain_ref, bias_ref,
    ctx_ref, prob_ref, key_ref, word_ref, wordc_ref, normed_ref, inv_ref, low_ref,
    packed, cpick, relc, keyc, attn, base,
):
    seq = k_ref.shape[0]
    picks = qc_ref.shape[0]
    chunks = seq // LANES

    @pl.when(pl.program_id(0) == 0)
    def _():
        row = lax.broadcasted_iota(jnp.int32, (seq, seq), 0)
        col = lax.broadcasted_iota(jnp.int32, (seq, seq), 1)
        side = pk_ref.shape[0] // 2
        step = jnp.sum(jnp.where(col == row - 1, rel_ref[...] - side, 0), axis=1, keepdims=True)
        steps = jnp.broadcast_to(step.astype(f32), (seq, LANES)).astype(bf16)
        word_ref[...] = dot_nn((col <= row).astype(f32).astype(bf16), steps).astype(jnp.int32)
        id_bases(rel_ref, base)
        for n in range(picks):
            place = jnp.maximum(pos_ref[n], 0)
            relc[n : n + 1, :] = rel_ref[pl.ds(place, 1), :]
            wordc_ref[n : n + 1, :] = word_ref[pl.ds(place, 1), :]

    zero = jnp.zeros((), bf16)
    table = both_alignments(pq_ref[...])
    keys = [dot_nt(jnp.where(head_lanes(a), k_ref[...], zero), table) for a in range(2)]
    unit = pack_heads(keys[0], keys[1], packed, longest(k_ref[...]) * longest(pq_ref[...]))
    for a in range(2):
        cpick[a] = dot_nt(jnp.where(head_lanes(a), qc_ref[...], zero), pk_ref[...])
    for g in range(chunks):
        for c in range(chunks):
            parts = []
            for start in range(g * LANES, (g + 1) * LANES, ROWS):
                parts.append(picked_words(packed, rel_ref, base, slice(start, start + ROWS), c))
            block = jnp.concatenate(parts, axis=0).T
            for a, value in enumerate(unpack_heads(block, unit)):
                key_ref[a, c * LANES : (c + 1) * LANES, g * LANES : (g + 1) * LANES] = value

    for n in range(picks):
        place = jnp.maximum(pos_ref[n], 0)
        for a in range(2):
            keyc[a, n : n + 1, :] = key_ref[a, pl.ds(place, 1), :]
    for a in range(2):
        mine = head_lanes(a)
        direct = dot_nt(jnp.where(mine, qc_ref[...], zero), k_ref[...])
        scores = []
        for c in range(chunks):
            ids = relc[:, c * LANES : (c + 1) * LANES]
            index = ids & (LANES - 1)
            value = jnp.take_along_axis(cpick[a, :, :LANES], index, axis=1)
            for n in range(1, pk_ref.shape[0] // LANES):
                other = cpick[a, :, n * LANES : (n + 1) * LANES]
                value = jnp.where(
                    ids >= n * LANES, jnp.take_along_axis(other, index, axis=1), value
                )
            cols = slice(c * LANES, (c + 1) * LANES)
            scores.append(direct[:, cols] + value + keyc[a, :, cols])
        weights = softmax_weights(scores)
        inverse = 1.0 / jnp.sum(sum(weights[1:], weights[0]), axis=1, keepdims=True)
        probs = jnp.concatenate([(weight * inverse).astype(bf16) for weight in weights], axis=1)
        prob_ref[a] = probs
        mixed = dot_nn(probs, v_ref[...]).astype(bf16)
        ctx_ref[...] = mixed if a == 0 else jnp.where(mine, mixed, ctx_ref[...])

    part = dot_nn(ctx_ref[...], wo_ref[...])

    @pl.when(pl.program_id(0) == 0)
    def _():
        attn[...] = x_ref[...].astype(f32) + row_of(bo_ref) + part

    @pl.when(pl.program_id(0) > 0)
    def _():
        attn[...] += part

    @pl.when(pl.program_id(0) == pl.num_programs(0) - 1)
    def _():
        normed, inv_std = norm_stats(attn[...])
        normed_ref[...] = normed
        inv_ref[...] = jnp.broadcast_to(inv_std, (picks, LANES))
        low_ref[...] = (normed * row_of(gain_ref) + row_of(bias_ref)).astype(bf16)


def attend_picked(
    positions, rel_ids, q_pick, k, v, pos_query, pos_key, x_pick, w_out, b_out, gain, bias
):
    seq, width = k.shape
    picks = q_pick.shape[0]
    table = pos_key.shape[0]
    pairs = width // LANES
    whole = lambda rows, cols: pl.BlockSpec((rows, cols), lambda h: (0, 0))
    line = pl.BlockSpec((width,), lambda h: (0,))
    col = lambda rows: pl.BlockSpec((rows, LANES), lambda h: (0, h))
    heads = lambda rows: pl.BlockSpec((2, rows, seq), lambda h: (h, 0, 0))
    return pl.pallas_call(
        picked_kernel,
        grid=(pairs,),
        in_specs=[
            pl.BlockSpec(memory_space=pltpu.SMEM), whole(seq, seq),
            col(picks), col(seq), col(seq), col(table), col(table),
            whole(picks, width), pl.BlockSpec((LANES, width), lambda h: (h, 0)), line, line, line,
        ],
        out_specs=[
            col(picks), heads(picks), heads(seq), whole(seq, LANES), whole(picks, LANES),
            whole(picks, width), whole(picks, LANES), whole(picks, width),
        ],
        out_shape=[
            jax.ShapeDtypeStruct((picks, width), bf16),
            jax.ShapeDtypeStruct((2 * pairs, picks, seq), bf16),
            jax.ShapeDtypeStruct((2 * pairs, seq, seq), f32),
            jax.ShapeDtypeStruct((seq, LANES), jnp.int32),
            jax.ShapeDtypeStruct((picks, LANES), jnp.int32),
            jax.ShapeDtypeStruct((picks, width), f32),
            jax.ShapeDtypeStruct((picks, LANES), f32),
            jax.ShapeDtypeStruct((picks, width), bf16),
        ],
        scratch_shapes=[
            pltpu.VMEM((seq, 2 * table), jnp.int32),
            pltpu.VMEM((2, picks, table), f32),
            pltpu.VMEM((picks, seq), jnp.int32),
            pltpu.VMEM((2, picks, seq), f32),
            pltpu.VMEM((picks, width), f32),
            pltpu.SMEM((seq // HALF * (seq // LANES),), jnp.int32),
        ],
        compiler_params=pltpu.CompilerParams(vmem_limit_bytes=48 * 2**20),
        name="attend_picked",
    )(
        positions, rel_ids, q_pick, k, v, pos_key, pos_query, x_pick, w_out, b_out, gain, bias
    )


def full_kernel(rel_ref, q_ref, k_ref, v_ref, pk_ref, key_ref, ctx_ref, packed, direct, low, base):
    seq = q_ref.shape[0]
    chunks = seq // LANES

    @pl.when(pl.program_id(0) == 0)
    def _():
        id_bases(rel_ref, base)

    zero = jnp.zeros((), bf16)
    table = both_alignments(pk_ref[...])
    far = []
    for a in range(2):
        q_a = jnp.where(head_lanes(a), q_ref[...], zero)
        far.append(dot_nt(q_a, table))
        direct[a] = dot_nt(q_a, k_ref[...])
    unit = pack_heads(far[0], far[1], packed, longest(q_ref[...]) * longest(pk_ref[...]))
    for start in range(0, seq, HALF):
        rows = slice(start, start + HALF)
        scores = [[], []]
        for c in range(chunks):
            cols = slice(c * LANES, (c + 1) * LANES)
            values = unpack_heads(picked_words(packed, rel_ref, base, rows, c), unit)
            for a in range(2):
                scores[a].append(values[a] + direct[a, rows, cols] + key_ref[a, rows, cols])
        for a in range(2):
            for c, weight in enumerate(softmax_weights(scores[a])):
                low[a, rows, c * LANES : (c + 1) * LANES] = weight.astype(bf16)
    mixed = [
        dot_nn(low[a], jnp.where(head_lanes(a), v_ref[...], jnp.ones((), bf16))) for a in range(2)
    ]
    upper = head_lanes(0)
    totals = pltpu.roll(jnp.where(upper, mixed[1], mixed[0]), HEAD, 1)
    ctx_ref[...] = (jnp.where(upper, mixed[0], mixed[1]) * (1.0 / totals)).astype(bf16)


def attend_full(rel_ids, q, k, v, pos_key, key_scores, first, pairs):
    seq = k.shape[0]
    table = pos_key.shape[0]
    col = lambda rows: pl.BlockSpec((rows, LANES), lambda h: (0, h + first))
    return pl.pallas_call(
        full_kernel,
        grid=(pairs,),
        in_specs=[
            pl.BlockSpec((seq, seq), lambda h: (0, 0)),
            col(seq), col(seq), col(seq), col(table),
            pl.BlockSpec((2, seq, seq), lambda h: (h + first, 0, 0)),
        ],
        out_specs=pl.BlockSpec((seq, LANES), lambda h: (0, h)),
        out_shape=jax.ShapeDtypeStruct((seq, pairs * LANES), bf16),
        scratch_shapes=[
            pltpu.VMEM((seq, 2 * table), jnp.int32),
            pltpu.VMEM((2, seq, seq), f32),
            pltpu.VMEM((2, seq, seq), bf16),
            pltpu.SMEM((seq // HALF * (seq // LANES),), jnp.int32),
        ],
        compiler_params=pltpu.CompilerParams(vmem_limit_bytes=48 * 2**20),
        name="attend_full",
    )(rel_ids, q, k, v, pos_key, key_scores)


def back_kernel(
    me_ref, row_ref, order_ref, word_ref, wordc_ref, qc_ref, k_ref, v_ref, prob_ref, pk_ref, pq_ref,
    dz2_ref, mine_ref, got_ref, normed_ref, inv_ref, gain_ref, wo_ref, early_ref,
    dq_ref, dk_ref, dv_ref, dpos_ref, dz1_ref, dattn_ref, sum_ref,
    side, sidec, moved, movedc, grel, expand, turned_expand, base,
):
    seq = k_ref.shape[0]
    picks = qc_ref.shape[0]
    table = pk_ref.shape[0]
    chunks = seq // LANES

    @pl.when(pl.program_id(0) == 0)
    def _():
        words = word_ref[...]
        for c in range(chunks):
            side[:, c * LANES : (c + 1) * LANES] = member_chunk(words, c)
            sidec[:, c * LANES : (c + 1) * LANES] = member_chunk(wordc_ref[...], c)
        group_bases(words, base)
        moved[...] = jnp.zeros_like(moved)
        for c in range(table // LANES):
            cols = slice(c * LANES, (c + 1) * LANES)
            expand[:, cols] = member_chunk(row_ref[...], c)
            source = block_source(order_ref, me_ref, cols, table)
            turned_expand[:, cols] = (row_ref[...] == source).astype(f32).astype(bf16)
        dh1 = dz2_ref[...] + mine_ref[...].astype(f32) + got_ref[...].astype(f32)
        dz1, g_gain, g_bias = norm_backward(dh1, normed_ref[...], inv_ref[:, :1], row_of(gain_ref))
        dz1_ref[...] = dz1
        dattn = dz1.astype(bf16)
        dattn_ref[...] = dattn
        sum_ref[...] = jnp.concatenate(
            [col_sum(dattn.astype(f32)), g_gain, g_bias, early_ref[:5]], axis=0
        )

    lane = lane_iota()
    scale = 1.0 / math.sqrt(3.0 * HEAD)
    zero = jnp.zeros((), bf16)
    far_key = dot_nn(expand[...], pk_ref[...]).astype(bf16)
    far_query = dot_nn(expand[...], pq_ref[...]).astype(bf16)
    dctx = dot_nt(dattn_ref[...], wo_ref[...]).astype(bf16)
    for a in range(2):
        mine = head_lanes(a)
        keep = lambda value: jnp.where(mine, value, zero)
        dctx_a = keep(dctx)
        q_a = keep(qc_ref[...])
        k_a = keep(k_ref[...])
        side[:, seq:] = k_a
        sidec[:, seq:] = q_a
        dprobs = dot_nt(dctx_a, v_ref[...])
        probs = prob_ref[a].astype(f32)
        prod = probs * dprobs
        gs = ((prod - probs * jnp.sum(prod, axis=1, keepdims=True)) * scale).astype(bf16)
        dv = dot_tn(prob_ref[a], dctx_a)

        out = dot_nn(gs, side[...])
        place = lane - (seq - 1) + wordc_ref[...]
        index = place & (LANES - 1)
        turned = [
            jnp.take_along_axis(out[:, c * LANES : (c + 1) * LANES], index, axis=1)
            for c in range(chunks)
        ]
        blank = jnp.zeros((picks, LANES), f32)
        for c in range(2 * chunks):
            value = turned[c] if c < chunks else blank
            for n in range(1, chunks + 1):
                other = turned[c - n] if 0 <= c - n < chunks else blank
                value = jnp.where(place < -LANES * (n - 1), other, value)
            movedc[:, c * LANES : (c + 1) * LANES] = value.astype(bf16)
        dq = out[:, seq:] + dot_nn(movedc[...], keep(far_key))
        dpk = dot_tn(movedc[...], q_a)

        out = dot_tn(gs, sidec[...])
        grel[...] = out[:, :seq]
        unshift_in_order(grel, word_ref, base, moved)
        dk = out[:, seq:] + dot_nn(moved[:, : 2 * seq], keep(far_query))
        dpq = dot_tn(moved[:, : 2 * seq], k_a)
        dpk = dot_tn(turned_expand[...], dpk.astype(bf16))
        dpq = dot_tn(turned_expand[...], dpq.astype(bf16))
        for ref, value in (
            (dq_ref, dq), (dk_ref, dk), (dv_ref, dv), (dpos_ref.at[0], dpk), (dpos_ref.at[1], dpq),
        ):
            low = value.astype(bf16)
            ref[...] = low if a == 0 else jnp.where(mine, low, ref[...])


def attend_back(
    me, table_of, order, words, words_pick, q_pick, k, v, probs, pos_query, pos_key,
    dz2, mine, got, normed, inv_std, gain, w_out, early,
):
    seq, width = k.shape
    picks = q_pick.shape[0]
    table = pos_key.shape[0]
    pairs = width // LANES
    whole = lambda value: pl.BlockSpec(value.shape, lambda h: (0,) * value.ndim)
    col = lambda rows: pl.BlockSpec((rows, LANES), lambda h: (0, h))
    shape = lambda rows: jax.ShapeDtypeStruct((rows, width), bf16)
    return pl.pallas_call(
        back_kernel,
        grid=(pairs,),
        in_specs=[
            pl.BlockSpec(memory_space=pltpu.SMEM),
            whole(table_of), whole(order), whole(words), whole(words_pick),
            col(picks), col(seq), col(seq),
            pl.BlockSpec((2, picks, seq), lambda h: (h, 0, 0)),
            col(table), col(table),
            whole(dz2), whole(mine), whole(got), whole(normed), whole(inv_std), whole(gain),
            pl.BlockSpec((LANES, width), lambda h: (h, 0)), whole(early),
        ],
        out_specs=[
            col(picks), col(seq), col(seq),
            pl.BlockSpec((2, table, LANES), lambda h: (0, 0, h)),
            whole(dz2), whole(dz2), whole(early),
        ],
        out_shape=[
            shape(picks), shape(seq), shape(seq),
            jax.ShapeDtypeStruct((2, table, width), bf16),
            jax.ShapeDtypeStruct((picks, width), f32),
            shape(picks),
            jax.ShapeDtypeStruct(early.shape, f32),
        ],
        scratch_shapes=[
            pltpu.VMEM((seq, seq + LANES), bf16),
            pltpu.VMEM((picks, seq + LANES), bf16),
            pltpu.VMEM((seq, 2 * seq + LANES), bf16),
            pltpu.VMEM((picks, 2 * seq), bf16),
            pltpu.VMEM((seq, seq), f32),
            pltpu.VMEM((2 * seq, table), bf16),
            pltpu.VMEM((2 * seq, table), bf16),
            pltpu.SMEM((seq // LANES,), jnp.int32),
        ],
        compiler_params=pltpu.CompilerParams(vmem_limit_bytes=48 * 2**20),
        name="attend_back",
    )(
        me, table_of, order, words, words_pick, q_pick, k, v, probs, pos_key, pos_query,
        dz2, mine, got, normed, inv_std, gain, w_out, early,
    )


def block_source(order_ref, me_ref, cols, length):
    relative = jnp.where(me_ref[1] == 0, order_ref[0:1, cols], order_ref[1:2, cols])
    return (me_ref[0] ^ relative) * (length // me_ref[2]) + order_ref[2:3, cols]


def turn_kernel(
    me_ref, order_ref, relorder_ref, x_ref, xpick_ref, cpick_ref, rel_ref,
    x_out, xpick_out, cpick_out, rel_out, rows,
):
    width, group = x_ref.shape[1], x_out.shape[1]
    table = rel_ref.shape[0]

    @pl.when(pl.program_id(0) == 0)
    def _():
        source = block_source(relorder_ref, me_ref, slice(None), table)
        spot = lax.broadcasted_iota(jnp.int32, (table, table), 0)
        rows[...] = dot_tn((spot == source).astype(f32).astype(bf16), rel_ref[...]).astype(bf16)

    source = block_source(order_ref, me_ref, slice(None), width)
    spot = lax.broadcasted_iota(jnp.int32, (width, group), 0)
    chosen = (spot == source).astype(f32).astype(bf16)
    for ref, out in ((x_ref, x_out), (xpick_ref, xpick_out), (cpick_ref, cpick_out), (rows, rel_out)):
        out[...] = dot_nn(ref[...], chosen).astype(bf16)


def turn_blocks(me, order, rel_order, x, x_pick, ctx_pick, rel_table):
    width = x.shape[1]
    group = 2 * LANES
    whole = lambda value: pl.BlockSpec(value.shape, lambda n: (0, 0))
    col = lambda value: pl.BlockSpec((value.shape[0], group), lambda n: (0, n))
    given = [x, x_pick, ctx_pick, rel_table]
    return pl.pallas_call(
        turn_kernel,
        grid=(width // group,),
        in_specs=[pl.BlockSpec(memory_space=pltpu.SMEM), col(order), whole(rel_order)]
        + [whole(value) for value in given],
        out_specs=[col(value) for value in given],
        out_shape=[jax.ShapeDtypeStruct(value.shape, bf16) for value in given],
        scratch_shapes=[pltpu.VMEM(rel_table.shape, bf16)],
        compiler_params=pltpu.CompilerParams(vmem_limit_bytes=48 * 2**20),
        name="turn_blocks",
    )(me, order, rel_order, *given)


def ffn_picked_kernel(
    mine_ref, their_ref, win_ref, bin_ref, down_ref, part_ref, theirs_ref, hidden_ref, slope_ref, total
):
    step = pl.program_id(0)
    rows = jnp.concatenate([mine_ref[...], their_ref[...]], axis=0)
    pre = dot_nn(rows, win_ref[...]) + row_of(bin_ref)
    cdf = normal_cdf(pre)
    hidden = (pre * cdf).astype(bf16)
    hidden_ref[...] = hidden
    slope_ref[...] = cdf + pre * (jnp.exp(-0.5 * pre * pre) * (1.0 / math.sqrt(2.0 * math.pi)))
    part = dot_nn(hidden, down_ref[...])
    total[...] = jnp.where(step == 0, part, total[...] + part)

    @pl.when(step == pl.num_programs(0) - 1)
    def _():
        count = mine_ref.shape[0]
        part_ref[...] = total[:count].astype(bf16)
        theirs_ref[...] = total[count:].astype(bf16)


def ffn_picked(mine, theirs, w_in, b_in, w_down):
    picks, width = mine.shape
    hidden_cols = w_in.shape[1]
    tile = hidden_cols // 3
    whole = pl.BlockSpec((picks, width), lambda n: (0, 0))
    col = lambda rows: pl.BlockSpec((rows, tile), lambda n: (0, n))
    return pl.pallas_call(
        ffn_picked_kernel,
        grid=(3,),
        in_specs=[
            whole, whole, col(width), pl.BlockSpec((tile,), lambda n: (n,)),
            pl.BlockSpec((tile, width), lambda n: (n, 0)),
        ],
        out_specs=[whole, whole, col(2 * picks), col(2 * picks)],
        out_shape=[
            jax.ShapeDtypeStruct((picks, width), bf16),
            jax.ShapeDtypeStruct((picks, width), bf16),
            jax.ShapeDtypeStruct((2 * picks, hidden_cols), bf16),
            jax.ShapeDtypeStruct((2 * picks, hidden_cols), f32),
        ],
        scratch_shapes=[pltpu.VMEM((2 * picks, width), f32)],
        compiler_params=pltpu.CompilerParams(vmem_limit_bytes=48 * 2**20),
        name="ffn_picked",
    )(mine, theirs, w_in, b_in, w_down)


def norm_picked_kernel(
    normed_ref, gain1_ref, bias1_ref, mine_ref, got_ref, bdown_ref, gain2_ref, grad_ref, pick_ref,
    dz2_ref, low_ref, sum_ref,
):
    h1 = normed_ref[...] * row_of(gain1_ref) + row_of(bias1_ref)
    branch = mine_ref[...].astype(f32) + got_ref[...].astype(f32) + row_of(bdown_ref)
    normed, inv_std = norm_stats(h1 + branch)
    used = jnp.sum(pick_ref[...].astype(f32), axis=1, keepdims=True)
    cot = jnp.where(used > 0.0, grad_ref[...].astype(f32), 0.0)
    dz2, g_gain, g_bias = norm_backward(cot, normed, inv_std, row_of(gain2_ref))
    dz2_ref[...] = dz2
    low = dz2.astype(bf16)
    low_ref[...] = low
    sum_ref[...] = jnp.concatenate(
        [col_sum(low.astype(f32)), g_gain, g_bias, jnp.zeros((5, h1.shape[1]), f32)], axis=0
    )


def norm_picked(normed, gain1, bias1, mine, got, b_down, gain2, grads, pick):
    picks, width = normed.shape
    return pl.pallas_call(
        norm_picked_kernel,
        out_shape=[
            jax.ShapeDtypeStruct((picks, width), f32),
            jax.ShapeDtypeStruct((picks, width), bf16),
            jax.ShapeDtypeStruct((8, width), f32),
        ],
        name="norm_picked",
    )(normed, gain1, bias1, mine, got, b_down, gain2, grads, pick)


def ffn_back_kernel(
    mine_ref, their_ref, win_ref, down_ref, slope_ref, part_ref, theirs_ref, dpre_ref, sum_ref, total
):
    step = pl.program_id(0)
    rows = jnp.concatenate([mine_ref[...], their_ref[...]], axis=0)
    dpre = (dot_nt(rows, down_ref[...]) * slope_ref[...]).astype(bf16)
    dpre_ref[...] = dpre
    sum_ref[...] = jnp.broadcast_to(col_sum(dpre.astype(f32)), sum_ref.shape)
    part = dot_nt(dpre, win_ref[...])
    total[...] = jnp.where(step == 0, part, total[...] + part)

    @pl.when(step == pl.num_programs(0) - 1)
    def _():
        count = mine_ref.shape[0]
        part_ref[...] = total[:count].astype(bf16)
        theirs_ref[...] = total[count:].astype(bf16)


def ffn_back(mine, theirs, w_in, w_down, slope):
    picks, width = mine.shape
    hidden_cols = w_in.shape[1]
    tile = hidden_cols // 3
    whole = pl.BlockSpec((picks, width), lambda n: (0, 0))
    col = lambda rows: pl.BlockSpec((rows, tile), lambda n: (0, n))
    return pl.pallas_call(
        ffn_back_kernel,
        grid=(3,),
        in_specs=[
            whole, whole, col(width), pl.BlockSpec((tile, width), lambda n: (n, 0)), col(2 * picks)
        ],
        out_specs=[whole, whole, col(2 * picks), col(8)],
        out_shape=[
            jax.ShapeDtypeStruct((picks, width), bf16),
            jax.ShapeDtypeStruct((picks, width), bf16),
            jax.ShapeDtypeStruct((2 * picks, hidden_cols), bf16),
            jax.ShapeDtypeStruct((8, hidden_cols), f32),
        ],
        scratch_shapes=[pltpu.VMEM((2 * picks, width), f32)],
        compiler_params=pltpu.CompilerParams(vmem_limit_bytes=48 * 2**20),
        name="ffn_back",
    )(mine, theirs, w_in, w_down, slope)


def ffn_grads_kernel(mine_ref, their_ref, dmine_ref, dtheir_ref, dpre_ref, hidden_ref, out_ref):
    @pl.when(pl.program_id(0) == 0)
    def _():
        rows = jnp.concatenate([mine_ref[...], their_ref[...]], axis=0)
        out_ref[...] = dot_tn(rows, dpre_ref[...]).astype(bf16)

    @pl.when(pl.program_id(0) == 1)
    def _():
        rows = jnp.concatenate([dmine_ref[...], dtheir_ref[...]], axis=0)
        out_ref[...] = dot_tn(rows, hidden_ref[...]).astype(bf16)


def ffn_grads(mine, theirs, dmine, dtheirs, dpre, hidden):
    picks, width = mine.shape
    hidden_cols = dpre.shape[1]
    tile = hidden_cols // 3
    whole = pl.BlockSpec((picks, width), lambda n, t: (0, 0))
    return pl.pallas_call(
        ffn_grads_kernel,
        grid=(2, 3),
        in_specs=[
            whole, whole, whole, whole,
            pl.BlockSpec((2 * picks, tile), lambda n, t: (0, jnp.where(n == 0, t, 2))),
            pl.BlockSpec((2 * picks, tile), lambda n, t: (0, jnp.where(n == 0, 0, t))),
        ],
        out_specs=pl.BlockSpec((width, tile), lambda n, t: (0, 3 * n + t)),
        out_shape=jax.ShapeDtypeStruct((width, 2 * hidden_cols), bf16),
        compiler_params=pltpu.CompilerParams(vmem_limit_bytes=48 * 2**20),
        name="ffn_grads",
    )(mine, theirs, dmine, dtheirs, dpre, hidden)


def ffn_full_kernel(
    x_ref, ctx_ref, ctx2_ref, wo_ref, bo_ref, gain1_ref, bias1_ref,
    win_ref, down_ref, bin_ref, win2_ref, down2_ref, bin2_ref, win3_ref, down3_ref, bin3_ref,
    bdown_ref, gain2_ref, bias2_ref, out_ref, h1, low, total,
):
    step = pl.program_id(0)
    width = x_ref.shape[1]

    @pl.when(step == 0)
    def _():
        attn = dot_nn(ctx_ref[...], wo_ref[: width // 2]) + dot_nn(ctx2_ref[...], wo_ref[width // 2 :])
        normed, _ = norm_stats(x_ref[...].astype(f32) + (attn + row_of(bo_ref)))
        value = normed * row_of(gain1_ref) + row_of(bias1_ref)
        h1[...] = value
        low[...] = value.astype(bf16)
        total[...] = jnp.zeros_like(total)

    def tile(w_ref, d_ref, b_ref):
        pre = dot_nn(low[...], w_ref[...]) + b_ref[...]
        total[...] += dot_nn((pre * normal_cdf(pre)).astype(bf16), d_ref[...])

    @pl.when(step < 4)
    def _():
        tile(win_ref, down_ref, bin_ref)

    @pl.when((step >= 4) & (step < 6))
    def _():
        tile(win2_ref, down2_ref, bin2_ref)

    @pl.when(step >= 6)
    def _():
        tile(win3_ref, down3_ref, bin3_ref)

    @pl.when(step == 7)
    def _():
        normed, _ = norm_stats(h1[...] + (total[...] + row_of(bdown_ref)))
        out_ref[...] = (normed * row_of(gain2_ref) + row_of(bias2_ref)).astype(bf16)


def ffn_full(x, ctx, w_out, b_out, gain1, bias1, shards, b_down, gain2, bias2):
    rows, width = x.shape
    tile = shards[0][0].shape[1] // 4
    whole = lambda value: pl.BlockSpec(value.shape, lambda t: (0,) * value.ndim)
    specs = []
    for first, last in ((0, 4), (4, 6), (6, 8)):
        at = lambda t, first=first, last=last: jnp.clip(t, first, last - 1) - first
        specs += [
            pl.BlockSpec((width, tile), lambda t, at=at: (0, at(t))),
            pl.BlockSpec((tile, width), lambda t, at=at: (at(t), 0)),
            pl.BlockSpec((1, tile), lambda t, at=at: (0, at(t))),
        ]
    head = [x, ctx[0], ctx[1], w_out, b_out, gain1, bias1]
    tail = [b_down, gain2, bias2]
    return pl.pallas_call(
        ffn_full_kernel,
        grid=(8,),
        in_specs=[whole(value) for value in head] + specs + [whole(value) for value in tail],
        out_specs=pl.BlockSpec((rows, width), lambda t: (0, 0)),
        out_shape=jax.ShapeDtypeStruct((rows, width), bf16),
        scratch_shapes=[
            pltpu.VMEM((rows, width), f32), pltpu.VMEM((rows, width), bf16), pltpu.VMEM((rows, width), f32)
        ],
        compiler_params=pltpu.CompilerParams(vmem_limit_bytes=48 * 2**20),
        name="ffn_full",
    )(*head, *[value for shard in shards for value in shard], *tail)


def token_grads_kernel(pick_ref, dz1_ref, dq_ref, dk_ref, dv_ref, wq_ref, wk_ref, wv_ref, out_ref):
    sparse = dz1_ref[...] + dot_nt(dq_ref[...], wq_ref[...])
    upper = sparse.astype(bf16)
    lower = (sparse - upper.astype(f32)).astype(bf16)
    out_ref[...] = (
        dot_nt(dk_ref[...], wk_ref[...])
        + dot_nt(dv_ref[...], wv_ref[...])
        + dot_tn(pick_ref[...], upper)
        + dot_tn(pick_ref[...], lower)
    )


def token_grads(pick, dz1, dq, dk, dv, w_query, w_key, w_value):
    seq, width = dk.shape
    group = 2 * LANES
    whole = lambda value: pl.BlockSpec(value.shape, lambda n: (0, 0))
    col = lambda rows: pl.BlockSpec((rows, group), lambda n: (0, n))
    row = pl.BlockSpec((group, width), lambda n: (n, 0))
    return pl.pallas_call(
        token_grads_kernel,
        grid=(width // group,),
        in_specs=[whole(pick), col(dz1.shape[0]), whole(dq), whole(dk), whole(dv), row, row, row],
        out_specs=col(seq),
        out_shape=jax.ShapeDtypeStruct((seq, width), f32),
        compiler_params=pltpu.CompilerParams(vmem_limit_bytes=48 * 2**20),
        name="token_grads",
    )(pick, dz1, dq, dk, dv, w_query, w_key, w_value)


def grads_kernel(
    half, x_ref, rel_ref, xpick_ref, cpick_ref, dpos_ref,
    dq_ref, dk_ref, dv_ref, dattn_ref, dposk_ref, dposq_ref, wq_ref, wk_ref,
    early_ref, bin_ref, bin2_ref, out_ref, sum_ref,
):
    width = x_ref.shape[1]
    group = 2 * LANES
    seq = x_ref.shape[0]

    def left(ref):
        starts = range(half * LANES, width, group)
        return jnp.concatenate([ref[:, at : at + LANES] for at in starts], axis=1)

    def put(at, value):
        for n in range(value.shape[0] // LANES):
            out_ref[at + n] = value[n * LANES : (n + 1) * LANES].astype(bf16)

    count = width // group
    rel_left = left(rel_ref)
    x_left = left(x_ref)
    put(0, dot_tn(left(xpick_ref), dq_ref[...]) + dot_tn(rel_left, dposq_ref[0]))
    put(count, dot_tn(x_left, dk_ref[...]) + dot_tn(rel_left, dposk_ref[0]))
    put(2 * count, dot_tn(x_left, dv_ref[...]))
    put(3 * count, dot_tn(left(cpick_ref), dattn_ref[...]))
    for n in range(dpos_ref.shape[1] // group):
        rows = slice(n * group + half * LANES, n * group + (half + 1) * LANES)
        put(
            4 * count + n,
            dot_nt(dpos_ref[0, rows, :], wk_ref[...]) + dot_nt(dpos_ref[1, rows, :], wq_ref[...]),
        )
    total = lambda value: col_sum(value.astype(f32))
    sum_ref[...] = jnp.concatenate(
        [
            total(dq_ref[...]) + total(dposq_ref[0]),
            total(dk_ref[...]) + total(dposk_ref[0]),
            total(dv_ref[...]),
            early_ref[:6],
            bin_ref[:1],
            bin2_ref[:1],
            jnp.zeros((5, group), f32),
        ],
        axis=0,
    )


def weight_grads(half, x, rel, x_pick, c_pick, dpos, dq, dk, dv, dattn, w_query, w_key, early, bins):
    seq, width = x.shape
    group = 2 * LANES
    planes = 4 * (width // group) + dpos.shape[1] // group
    whole = lambda value: pl.BlockSpec(value.shape, lambda n: (0,) * value.ndim)
    col = lambda value: pl.BlockSpec((value.shape[0], group), lambda n: (0, n))
    row = lambda value: pl.BlockSpec((group, value.shape[1]), lambda n: (n, 0))
    plane = lambda t: pl.BlockSpec((1, dpos.shape[1], group), lambda n: (t, 0, n))
    return pl.pallas_call(
        functools.partial(grads_kernel, half),
        grid=(width // group,),
        in_specs=[
            whole(x), whole(rel), whole(x_pick), whole(c_pick), whole(dpos),
            col(dq), col(dk), col(dv), col(dattn), plane(0), plane(1), row(w_query), row(w_key),
            col(early), col(bins), pl.BlockSpec((8, group), lambda n: (0, n + width // group)),
        ],
        out_specs=[
            pl.BlockSpec((planes, LANES, group), lambda n: (0, 0, n)),
            pl.BlockSpec((16, group), lambda n: (0, n)),
        ],
        out_shape=[
            jax.ShapeDtypeStruct((planes, LANES, width), bf16),
            jax.ShapeDtypeStruct((16, width), f32),
        ],
        compiler_params=pltpu.CompilerParams(vmem_limit_bytes=48 * 2**20),
        name="weight_grads",
    )(
        x, rel, x_pick, c_pick, dpos, dq, dk, dv, dattn, dpos, dpos, w_query, w_key, early, bins, bins
    )


def swap(values, axis, bit):
    size = lax.axis_size(axis)
    return lax.ppermute(values, axis, [(n, n ^ bit) for n in range(size)])


def after(values, *others):
    return lax.optimization_barrier((values, others))[0]


class Halving:
    def __init__(self, axes, core, near, size):
        rest = [1 << n for n in range(size.bit_length() - 1) if (1 << n) != core]
        near = [bit for bit in near if bit in rest]
        rest = [bit for bit in rest if bit not in near]
        turned = near[-1:] + near[:-1]
        self.axes, self.core, self.size = axes, core, size
        self.orders = [[core] + near + rest, [core] + turned + rest]
        self.steps = len(self.orders[0])
        self.me = lax.axis_index(axes)
        self.upper = (self.me // core) % 2

    def core_of(self, place):
        return (place // self.core) % 2

    def send(self, values, step):
        pairs = [(n, n ^ self.orders[self.core_of(n)][step]) for n in range(self.size)]
        return lax.ppermute(values, self.axes, pairs)

    def bit(self, step):
        first, second = (order[step] for order in self.orders)
        return jnp.where(self.upper == 0, first, second)

    def relative(self, upper):
        masks = []
        for place in range(self.size):
            bits = [(place >> (self.steps - 1 - step)) & 1 for step in range(self.steps)]
            order = self.orders[upper ^ bits[0]]
            mask = 0
            for step, bit in enumerate(bits):
                mask ^= bit * order[step]
            masks.append(mask)
        return np.array(masks, np.int32)

    def order(self, length, unit):
        spots = np.arange(length)
        group = self.size * unit
        place = spots % group // unit
        rows = [self.relative(upper)[place] for upper in range(2)]
        rows.append(spots // group * unit + spots % unit)
        return jnp.asarray(np.stack(rows + [np.zeros_like(spots)] * 5).astype(np.int32))


def local(
    tokens, rel_ids, mask_pos, grad_vals, w_query, w_key, w_value, w_out, b_query, b_key,
    b_value, b_out, rel_table, ln1_gain, ln1_bias, w_in, b_in, w_down, b_down, ln2_gain, ln2_bias,
):
    assert rel_ids.shape[0] == 1
    seq, width = tokens.shape
    table_rows = rel_table.shape[0]
    hidden_cols = w_in.shape[1]
    pairs = width // LANES
    n_tok = lax.axis_size("tok")
    n_ffn = lax.axis_size("ffn")
    n_all = n_tok * n_ffn
    low = lambda value: value.astype(bf16)
    wide = lambda value: value.astype(f32)
    rel_ids, positions, grad_vals = rel_ids[0], mask_pos[0], grad_vals[0]

    over_all = Halving(("tok", "ffn"), n_ffn, [2 * n_ffn, 1, 4 * n_ffn], n_all)
    own, own_rel = width // n_all, table_rows // n_all
    unit = math.gcd(own, own_rel)
    me = jnp.stack([over_all.me, over_all.upper, jnp.int32(n_all)])
    order, rel_order = over_all.order(width, unit), over_all.order(table_rows, unit)
    table_of = jnp.asarray(np.repeat(distance_rows(seq, table_rows)[:, None], LANES, 1))

    core = lax.axis_index("tok") % 2
    half_cols = hidden_cols // 2
    in_half = lax.dynamic_slice_in_dim(w_in, core * half_cols, half_cols, 1)
    bias_row = b_in.reshape(1, hidden_cols)
    bias_half = lax.dynamic_slice_in_dim(bias_row, core * half_cols, half_cols, 1)
    down_half = lax.dynamic_slice_in_dim(w_down, core * half_cols, half_cols, 0)

    pick = low(positions[:, None] == lax.broadcasted_iota(jnp.int32, (positions.shape[0], seq), 1))
    x_pick = low(dot_nn(pick, tokens))
    q_pick = low(dot_nn(x_pick, w_query) + b_query)
    k = low(dot_nn(tokens, w_key) + b_key)
    v = low(dot_nn(tokens, w_value) + b_value)
    pos_query = low(dot_nn(rel_table, w_query) + b_query)
    pos_key = low(dot_nn(rel_table, w_key) + b_key)
    ctx_pick, probs, key_scores, words, words_pick, normed1, inv1, h1_mine = attend_picked(
        positions, rel_ids, q_pick, k, v, pos_query, pos_key, x_pick, w_out, b_out, ln1_gain, ln1_bias
    )

    h1_theirs = swap(h1_mine, "ffn", 1)
    x_turned, x_pick_turned, c_pick_turned, rel_turned = turn_blocks(
        me, order, rel_order, tokens, x_pick, ctx_pick, rel_table
    )
    h1_theirs = after(h1_theirs, x_turned)
    part, theirs, hidden, slope = ffn_picked(h1_mine, h1_theirs, w_in, b_in, w_down)
    got = swap(theirs, "ffn", 1)
    q = low(dot_nn(after(tokens, theirs), w_query) + b_query)
    got = after(got, q)
    dz2, dffn, early = norm_picked(
        normed1, ln1_gain, ln1_bias, part, got, b_down, ln2_gain, grad_vals, pick
    )
    dffn_theirs = swap(dffn, "ffn", 1)
    dpart, dtheirs, dpre, gb_in = ffn_back(dffn, dffn_theirs, w_in, w_down, slope)
    dgot = swap(dtheirs, "ffn", 1)
    gw_ffn = ffn_grads(h1_mine, h1_theirs, dffn, dffn_theirs, after(dpre, dtheirs), hidden)
    dgot = after(dgot, gw_ffn)
    s_ffn = lax.psum_scatter(gw_ffn, "tok", scatter_dimension=0, tiled=True)

    in_half, bias_half, down_half = after((in_half, bias_half, down_half), dgot)
    far_in, far_bias = swap(in_half, "ffn", 1), swap(bias_half, "ffn", 1)
    dq, dk, dv, dpos, dz1, dattn, early = attend_back(
        me, table_of, rel_order, words, words_pick, q_pick, k, v, probs, pos_query, pos_key,
        dz2, dpart, after(dgot, in_half), normed1, inv1, ln1_gain, w_out, early,
    )
    far_in, far_bias = after((far_in, far_bias), dk)

    def grads(half, dk):
        return weight_grads(
            half, x_turned, rel_turned, x_pick_turned, c_pick_turned, dpos, dq, dk, dv, dattn,
            w_query, w_key, early, gb_in,
        )

    all_send, vectors = grads(1, after(dk, far_in))
    near_in, near_bias = swap(far_in, "tok", 1), swap(far_bias, "tok", 1)
    far_down = swap(after(down_half, far_in), "ffn", 1)

    def halves(values, axis):
        size = values.shape[axis] // 2
        cut = lambda at: lax.slice_in_dim(values, at, at + size, axis=axis)
        return cut(0), cut(size)

    add = lambda one, other: low(wide(one) + wide(other))
    all_got = over_all.send(all_send, 0)
    vec_got = over_all.send(vectors, 0)
    all_kept, _ = grads(0, after(dk, all_send))
    all_sums = add(all_kept, after(all_got, all_kept))
    vectors = vectors + vec_got
    shared = lax.broadcasted_iota(jnp.int32, (vectors.shape[0], 1), 0) < 9

    def attend(first, count, q):
        return attend_full(rel_ids, q, k, v, pos_key, key_scores, first, count)

    fills = []
    for step in range(1, over_all.steps):
        kept, sent = halves(all_sums, 1)
        all_got = over_all.send(sent, step)
        vec_got = over_all.send(vectors, step)
        if step == 1:
            fills.append(attend(0, pairs // 2, after(q, sent)))
        elif step == 2:
            fills.append(attend(pairs // 2, pairs - pairs // 2, after(q, sent)))
        elif step == 3:
            fills.append(
                token_grads(pick, dz1, dq, after(dk, sent), dv, w_query, w_key, w_value)
            )
        elif step == 4:
            near_down = swap(far_down, "tok", 1)
            shards = [
                (w_in, w_down, bias_row), (far_in, far_down, far_bias), (near_in, near_down, near_bias)
            ]
            fills.append(
                ffn_full(
                    after(tokens, sent), fills[:2], w_out, b_out, ln1_gain, ln1_bias, shards,
                    b_down, ln2_gain, ln2_bias,
                )
            )
        if step <= 4:
            all_got, vec_got = after((all_got, vec_got), fills[-1])
        all_sums = add(kept, all_got)
        vectors = vectors + jnp.where(shared | (over_all.bit(step) != 1), vec_got, 0.0)
    grad_tokens, output = fills[2:]

    all_sums = all_sums.reshape(all_sums.shape[0] * unit, width)
    s_w = [wide(all_sums[n * own : (n + 1) * own]) for n in range(4)]
    s_rel = wide(all_sums[4 * own :])
    s_vec = lax.dynamic_slice_in_dim(vectors[:9], over_all.me * own, own, 1)
    part = hidden_cols // n_tok
    s_bin = lax.dynamic_slice_in_dim(
        vectors[9 : 9 + hidden_cols // width].reshape(1, hidden_cols), lax.axis_index("tok") * part, part, 1
    )
    return (
        output,
        grad_tokens,
        s_w[0],
        s_w[1],
        s_w[2],
        s_w[3],
        s_vec[0],
        s_vec[1],
        s_vec[2],
        s_vec[3],
        s_rel,
        s_vec[4],
        s_vec[5],
        wide(s_ffn[:, :hidden_cols]),
        s_bin,
        jnp.transpose(wide(s_ffn[:, hidden_cols:])),
        s_vec[6],
        s_vec[7],
        s_vec[8],
    )


def solution(mesh):
    every = ("tok", "ffn")
    placed = (
        P(every, None), P(every, None, None), P(every, None), P(every, None, None),
        P(), P(), P(), P(), P(), P(), P(), P(), P(), P(), P(),
        P(None, "ffn"), P("ffn"), P("ffn", None), P(), P(), P(),
    )
    given = (
        P(every, None), P(every, None),
        P(every, None), P(every, None), P(every, None), P(every, None),
        P(every), P(every), P(every), P(every),
        P(every, None), P(every), P(every),
        P("tok", "ffn"), P("ffn", "tok"), P("ffn", "tok"),
        P(every), P(every), P(every),
    )
    return jax.shard_map(local, mesh=mesh, in_specs=placed, out_specs=given, check_vma=False)
```

```python
import functools
import math

import numpy as np

import jax
import jax.numpy as jnp
from jax import lax
from jax.experimental import pallas as pl
from jax.experimental.pallas import tpu as pltpu
from jax.sharding import PartitionSpec as P

HEAD = 64
LANES = 128
HALF = 64
ROWS = 32
norm_eps = 1e-07
bf16 = jnp.bfloat16
f32 = jnp.float32
PARAMS = pltpu.CompilerParams(vmem_limit_bytes=60 * 2**20)


def dot_nn(first_op, second_op):
    return lax.dot_general(
        first_op, second_op, (((1,), (0,)), ((), ())), preferred_element_type=f32
    )


def dot_nt(first_op, second_op):
    return lax.dot_general(
        first_op, second_op, (((1,), (1,)), ((), ())), preferred_element_type=f32
    )


def dot_tn(first_op, second_op):
    return lax.dot_general(
        first_op, second_op, (((0,), (0,)), ((), ())), preferred_element_type=f32
    )


def distance_rows(seq_len, table_rows):
    side = table_rows // 2
    middle = side // 2
    rows = []
    for m in range(2 * seq_len):
        offset = max(seq_len - 1 - m, 1 - seq_len)
        size = abs(offset)
        if size > middle:
            ratio = math.log(size / middle) / math.log((2 * side - 1) / middle)
            size = int(math.ceil(ratio * (middle - 1))) + middle
        rows.append(side + (size if offset > 0 else -size))
    return np.array(rows, dtype=np.int32)


def lane_iota(rows=1):
    return lax.broadcasted_iota(jnp.int32, (rows, LANES), 1)


def member_chunk(words, c):
    return (words == lane_iota(words.shape[0]) + c * LANES).astype(f32).astype(bf16)


def id_bases(rel_ref, base):
    seq = rel_ref.shape[0]
    chunks = seq // LANES
    last = chunks * 2 - 2
    for g in range(seq // HALF):
        for c in range(chunks):
            block = rel_ref[g * HALF : (g + 1) * HALF, c * LANES : (c + 1) * LANES]
            base[g * chunks + c] = jnp.minimum(jnp.min(block) // HALF, last)


def both_alignments(table):
    return jnp.concatenate([table, table[HALF:], table[:HALF]], axis=0)


def longest(rows):
    wide = rows.astype(f32)
    return jnp.sqrt(jnp.max(jnp.sum(wide * wide, axis=1, keepdims=True)))


def pack_heads(first, second, dest, top):
    top = jnp.maximum(top, 1e-30)
    scale = 32000.0 / top
    upper = (first * scale).astype(jnp.int32)
    lower = (second * scale).astype(jnp.int32)
    dest[...] = upper * 65536 + lower
    return top * (1.0 / 32000.0)


def unpack_heads(words, step):
    lower = lax.shift_right_arithmetic(lax.shift_left(words, 16), 16)
    return words.astype(f32) * (step * (1.0 / 65536.0)), lower.astype(f32) * step


def picked_words(source, rel_ref, base, rows, c):
    chunks = rel_ref.shape[1] // LANES
    first = base[(rows.start // HALF) * chunks + c]
    place = rel_ref[rows, c * LANES : (c + 1) * LANES] - first * HALF
    index = place & (LANES - 1)
    at = pl.multiple_of((first % 2) * (chunks * LANES) + (first // 2) * LANES, LANES)
    near = jnp.take_along_axis(source[rows, pl.ds(at, LANES)], index, axis=1)
    at = pl.multiple_of(at + LANES, LANES)
    far = jnp.take_along_axis(source[rows, pl.ds(at, LANES)], index, axis=1)
    return jnp.where(place < LANES, near, far)


def unshift_in_order(source, words_ref, base, dest):
    seq = words_ref.shape[0]
    chunks = seq // LANES
    lane = lane_iota()
    zero = jnp.zeros((ROWS, LANES), f32)
    for g in range(chunks):
        first = base[g]
        for sub in range(LANES // ROWS):
            start = g * LANES + sub * ROWS
            rows = slice(start, start + ROWS)
            place = lane - (seq - 1) + words_ref[rows, :] + first * LANES
            index = place & (LANES - 1)
            turned = [
                jnp.take_along_axis(
                    source[rows, c * LANES : (c + 1) * LANES], index, axis=1
                )
                for c in range(chunks)
            ]

            def pick(c):
                return turned[c] if 0 <= c < chunks else zero

            near = place >= 0
            mid = place >= -LANES
            for c in range(chunks + 2):
                value = jnp.where(near, pick(c), jnp.where(mid, pick(c - 1), pick(c - 2)))
                at = pl.multiple_of((first + c) * LANES, LANES)
                dest[rows, pl.ds(at, LANES)] = value.astype(bf16)


def group_bases(words, base):
    seq = words.shape[0]
    for g in range(seq // LANES):
        top = jnp.max(words[g * LANES : (g + 1) * LANES])
        base[g] = (seq - 1 - top) // LANES


def softmax_weights(scores):
    factor = math.log2(math.e) / math.sqrt(3.0 * HEAD)
    top = jnp.max(functools.reduce(jnp.maximum, scores), axis=1, keepdims=True)
    return [jnp.exp2((score - top) * factor) for score in scores]


def head_lanes(a):
    return (lane_iota() < HEAD) if a == 0 else (lane_iota() >= HEAD)


def row_of(ref):
    return ref[...].reshape(1, ref.shape[0])


def norm_stats(values):
    centered = values - jnp.mean(values, axis=1, keepdims=True)
    inv_std = lax.rsqrt(jnp.mean(centered * centered, axis=1, keepdims=True) + norm_eps)
    return centered * inv_std, inv_std


def norm_backward(upstream, normed, inv_std, norm_gain):
    scaled = upstream * norm_gain
    adjusted = (
        scaled
        - jnp.mean(scaled, axis=1, keepdims=True)
        - normed * jnp.mean(scaled * normed, axis=1, keepdims=True)
    )
    return inv_std * adjusted, col_sum(upstream * normed), col_sum(upstream)


def col_sum(values):
    return jnp.sum(values, axis=0, keepdims=True)


def normal_cdf(pre_act):
    return 0.5 * (1.0 + lax.erf(pre_act * (1.0 / math.sqrt(2.0))))


def picked_kernel(
    pos_ref, rel_ref, qc_ref, k_ref, v_ref, pk_ref, pq_ref,
    x_ref, wo_ref, bo_ref, gain_ref, bias_ref,
    ctx_ref, prob_ref, key_ref, word_ref, wordc_ref, normed_ref, inv_ref, low_ref,
    packed, cpick, relc, keyc, attn, base,
):
    seq = k_ref.shape[0]
    picks = qc_ref.shape[0]
    chunks = seq // LANES

    @pl.when(pl.program_id(0) == 0)
    def _():
        row = lax.broadcasted_iota(jnp.int32, (seq, seq), 0)
        col = lax.broadcasted_iota(jnp.int32, (seq, seq), 1)
        side = pk_ref.shape[0] // 2
        step = jnp.sum(jnp.where(col == row - 1, rel_ref[...] - side, 0), axis=1, keepdims=True)
        steps = jnp.broadcast_to(step.astype(f32), (seq, LANES)).astype(bf16)
        word_ref[...] = dot_nn((col <= row).astype(f32).astype(bf16), steps).astype(jnp.int32)
        id_bases(rel_ref, base)
        for n in range(picks):
            place = jnp.maximum(pos_ref[n], 0)
            relc[n : n + 1, :] = rel_ref[pl.ds(place, 1), :]
            wordc_ref[n : n + 1, :] = word_ref[pl.ds(place, 1), :]

    zero = jnp.zeros((), bf16)
    table = both_alignments(pq_ref[...])
    keys = [dot_nt(jnp.where(head_lanes(a), k_ref[...], zero), table) for a in range(2)]
    unit = pack_heads(keys[0], keys[1], packed, longest(k_ref[...]) * longest(pq_ref[...]))
    for a in range(2):
        cpick[a] = dot_nt(jnp.where(head_lanes(a), qc_ref[...], zero), pk_ref[...])
    for g in range(chunks):
        for c in range(chunks):
            parts = []
            for start in range(g * LANES, (g + 1) * LANES, ROWS):
                parts.append(picked_words(packed, rel_ref, base, slice(start, start + ROWS), c))
            block = jnp.concatenate(parts, axis=0).T
            for a, value in enumerate(unpack_heads(block, unit)):
                key_ref[a, c * LANES : (c + 1) * LANES, g * LANES : (g + 1) * LANES] = value

    for n in range(picks):
        place = jnp.maximum(pos_ref[n], 0)
        for a in range(2):
            keyc[a, n : n + 1, :] = key_ref[a, pl.ds(place, 1), :]
    for a in range(2):
        mine = head_lanes(a)
        direct = dot_nt(jnp.where(mine, qc_ref[...], zero), k_ref[...])
        scores = []
        for c in range(chunks):
            ids = relc[:, c * LANES : (c + 1) * LANES]
            index = ids & (LANES - 1)
            value = jnp.take_along_axis(cpick[a, :, :LANES], index, axis=1)
            for n in range(1, pk_ref.shape[0] // LANES):
                other = cpick[a, :, n * LANES : (n + 1) * LANES]
                value = jnp.where(
                    ids >= n * LANES, jnp.take_along_axis(other, index, axis=1), value
                )
            cols = slice(c * LANES, (c + 1) * LANES)
            scores.append(direct[:, cols] + value + keyc[a, :, cols])
        weights = softmax_weights(scores)
        inverse = 1.0 / jnp.sum(sum(weights[1:], weights[0]), axis=1, keepdims=True)
        probs = jnp.concatenate([(weight * inverse).astype(bf16) for weight in weights], axis=1)
        prob_ref[a] = probs
        mixed = dot_nn(probs, v_ref[...]).astype(bf16)
        ctx_ref[...] = mixed if a == 0 else jnp.where(mine, mixed, ctx_ref[...])

    part = dot_nn(ctx_ref[...], wo_ref[...])

    @pl.when(pl.program_id(0) == 0)
    def _():
        attn[...] = x_ref[...].astype(f32) + row_of(bo_ref) + part

    @pl.when(pl.program_id(0) > 0)
    def _():
        attn[...] += part

    @pl.when(pl.program_id(0) == pl.num_programs(0) - 1)
    def _():
        normed, inv_std = norm_stats(attn[...])
        normed_ref[...] = normed
        inv_ref[...] = jnp.broadcast_to(inv_std, (picks, LANES))
        low_ref[...] = (normed * row_of(gain_ref) + row_of(bias_ref)).astype(bf16)


def attend_picked(
    positions, rel_ids, q_pick, k, v, pos_query, pos_key, x_pick, w_out, b_out, gain, bias
):
    seq, width = k.shape
    picks = q_pick.shape[0]
    table = pos_key.shape[0]
    pairs = width // LANES
    whole = lambda rows, cols: pl.BlockSpec((rows, cols), lambda h: (0, 0))
    line = pl.BlockSpec((width,), lambda h: (0,))
    col = lambda rows: pl.BlockSpec((rows, LANES), lambda h: (0, h))
    heads = lambda rows: pl.BlockSpec((2, rows, seq), lambda h: (h, 0, 0))
    return pl.pallas_call(
        picked_kernel,
        grid=(pairs,),
        in_specs=[
            pl.BlockSpec(memory_space=pltpu.SMEM), whole(seq, seq),
            col(picks), col(seq), col(seq), col(table), col(table),
            whole(picks, width), pl.BlockSpec((LANES, width), lambda h: (h, 0)), line, line, line,
        ],
        out_specs=[
            col(picks), heads(picks), heads(seq), whole(seq, LANES), whole(picks, LANES),
            whole(picks, width), whole(picks, LANES), whole(picks, width),
        ],
        out_shape=[
            jax.ShapeDtypeStruct((picks, width), bf16),
            jax.ShapeDtypeStruct((2 * pairs, picks, seq), bf16),
            jax.ShapeDtypeStruct((2 * pairs, seq, seq), f32),
            jax.ShapeDtypeStruct((seq, LANES), jnp.int32),
            jax.ShapeDtypeStruct((picks, LANES), jnp.int32),
            jax.ShapeDtypeStruct((picks, width), f32),
            jax.ShapeDtypeStruct((picks, LANES), f32),
            jax.ShapeDtypeStruct((picks, width), bf16),
        ],
        scratch_shapes=[
            pltpu.VMEM((seq, 2 * table), jnp.int32),
            pltpu.VMEM((2, picks, table), f32),
            pltpu.VMEM((picks, seq), jnp.int32),
            pltpu.VMEM((2, picks, seq), f32),
            pltpu.VMEM((picks, width), f32),
            pltpu.SMEM((seq // HALF * (seq // LANES),), jnp.int32),
        ],
        compiler_params=PARAMS,
        name="attend_picked",
    )(
        positions, rel_ids, q_pick, k, v, pos_key, pos_query, x_pick, w_out, b_out, gain, bias
    )


def full_kernel(rel_ref, q_ref, k_ref, v_ref, pk_ref, key_ref, ctx_ref, packed, direct, low, base):
    seq = q_ref.shape[0]
    chunks = seq // LANES

    @pl.when(pl.program_id(0) == 0)
    def _():
        id_bases(rel_ref, base)

    zero = jnp.zeros((), bf16)
    table = both_alignments(pk_ref[...])
    far = []
    for a in range(2):
        q_a = jnp.where(head_lanes(a), q_ref[...], zero)
        far.append(dot_nt(q_a, table))
        direct[a] = dot_nt(q_a, k_ref[...])
    unit = pack_heads(far[0], far[1], packed, longest(q_ref[...]) * longest(pk_ref[...]))
    for start in range(0, seq, HALF):
        rows = slice(start, start + HALF)
        scores = [[], []]
        for c in range(chunks):
            cols = slice(c * LANES, (c + 1) * LANES)
            values = unpack_heads(picked_words(packed, rel_ref, base, rows, c), unit)
            for a in range(2):
                scores[a].append(values[a] + direct[a, rows, cols] + key_ref[a, rows, cols])
        for a in range(2):
            for c, weight in enumerate(softmax_weights(scores[a])):
                low[a, rows, c * LANES : (c + 1) * LANES] = weight.astype(bf16)
    mixed = [
        dot_nn(low[a], jnp.where(head_lanes(a), v_ref[...], jnp.ones((), bf16))) for a in range(2)
    ]
    upper = head_lanes(0)
    totals = pltpu.roll(jnp.where(upper, mixed[1], mixed[0]), HEAD, 1)
    ctx_ref[...] = (jnp.where(upper, mixed[0], mixed[1]) * (1.0 / totals)).astype(bf16)


def attend_full(rel_ids, q, k, v, pos_key, key_scores, first, pairs):
    seq = k.shape[0]
    table = pos_key.shape[0]
    col = lambda rows: pl.BlockSpec((rows, LANES), lambda h: (0, h + first))
    return pl.pallas_call(
        full_kernel,
        grid=(pairs,),
        in_specs=[
            pl.BlockSpec((seq, seq), lambda h: (0, 0)),
            col(seq), col(seq), col(seq), col(table),
            pl.BlockSpec((2, seq, seq), lambda h: (h + first, 0, 0)),
        ],
        out_specs=pl.BlockSpec((seq, LANES), lambda h: (0, h)),
        out_shape=jax.ShapeDtypeStruct((seq, pairs * LANES), bf16),
        scratch_shapes=[
            pltpu.VMEM((seq, 2 * table), jnp.int32),
            pltpu.VMEM((2, seq, seq), f32),
            pltpu.VMEM((2, seq, seq), bf16),
            pltpu.SMEM((seq // HALF * (seq // LANES),), jnp.int32),
        ],
        compiler_params=PARAMS,
        name="attend_full",
    )(rel_ids, q, k, v, pos_key, key_scores)


def back_kernel(
    me_ref, row_ref, order_ref, word_ref, wordc_ref, qc_ref, k_ref, v_ref, prob_ref, pk_ref, pq_ref,
    dz2_ref, mine_ref, got_ref, normed_ref, inv_ref, gain_ref, wo_ref, early_ref,
    dq_ref, dk_ref, dv_ref, dpos_ref, dz1_ref, dattn_ref, sum_ref,
    side, sidec, moved, movedc, grel, expand, turned_expand, base,
):
    seq = k_ref.shape[0]
    picks = qc_ref.shape[0]
    table = pk_ref.shape[0]
    chunks = seq // LANES

    @pl.when(pl.program_id(0) == 0)
    def _():
        words = word_ref[...]
        for c in range(chunks):
            side[:, c * LANES : (c + 1) * LANES] = member_chunk(words, c)
            sidec[:, c * LANES : (c + 1) * LANES] = member_chunk(wordc_ref[...], c)
        group_bases(words, base)
        moved[...] = jnp.zeros_like(moved)
        for c in range(table // LANES):
            cols = slice(c * LANES, (c + 1) * LANES)
            expand[:, cols] = member_chunk(row_ref[...], c)
            source = block_source(order_ref, me_ref, cols, table)
            turned_expand[:, cols] = (row_ref[...] == source).astype(f32).astype(bf16)
        dh1 = dz2_ref[...] + mine_ref[...].astype(f32) + got_ref[...].astype(f32)
        dz1, g_gain, g_bias = norm_backward(dh1, normed_ref[...], inv_ref[:, :1], row_of(gain_ref))
        dz1_ref[...] = dz1
        dattn = dz1.astype(bf16)
        dattn_ref[...] = dattn
        sum_ref[...] = jnp.concatenate(
            [col_sum(dattn.astype(f32)), g_gain, g_bias, early_ref[:5]], axis=0
        )

    lane = lane_iota()
    scale = 1.0 / math.sqrt(3.0 * HEAD)
    zero = jnp.zeros((), bf16)
    far_key = dot_nn(expand[...], pk_ref[...]).astype(bf16)
    far_query = dot_nn(expand[...], pq_ref[...]).astype(bf16)
    dctx = dot_nt(dattn_ref[...], wo_ref[...]).astype(bf16)
    for a in range(2):
        mine = head_lanes(a)
        keep = lambda value: jnp.where(mine, value, zero)
        dctx_a = keep(dctx)
        q_a = keep(qc_ref[...])
        k_a = keep(k_ref[...])
        side[:, seq:] = k_a
        sidec[:, seq:] = q_a
        dprobs = dot_nt(dctx_a, v_ref[...])
        probs = prob_ref[a].astype(f32)
        prod = probs * dprobs
        gs = ((prod - probs * jnp.sum(prod, axis=1, keepdims=True)) * scale).astype(bf16)
        dv = dot_tn(prob_ref[a], dctx_a)

        out = dot_nn(gs, side[...])
        place = lane - (seq - 1) + wordc_ref[...]
        index = place & (LANES - 1)
        turned = [
            jnp.take_along_axis(out[:, c * LANES : (c + 1) * LANES], index, axis=1)
            for c in range(chunks)
        ]
        blank = jnp.zeros((picks, LANES), f32)
        for c in range(2 * chunks):
            value = turned[c] if c < chunks else blank
            for n in range(1, chunks + 1):
                other = turned[c - n] if 0 <= c - n < chunks else blank
                value = jnp.where(place < -LANES * (n - 1), other, value)
            movedc[:, c * LANES : (c + 1) * LANES] = value.astype(bf16)
        dq = out[:, seq:] + dot_nn(movedc[...], keep(far_key))
        dpk = dot_tn(movedc[...], q_a)

        out = dot_tn(gs, sidec[...])
        grel[...] = out[:, :seq]
        unshift_in_order(grel, word_ref, base, moved)
        dk = out[:, seq:] + dot_nn(moved[:, : 2 * seq], keep(far_query))
        dpq = dot_tn(moved[:, : 2 * seq], k_a)
        dpk = dot_tn(turned_expand[...], dpk.astype(bf16))
        dpq = dot_tn(turned_expand[...], dpq.astype(bf16))
        for ref, value in (
            (dq_ref, dq), (dk_ref, dk), (dv_ref, dv), (dpos_ref.at[0], dpk), (dpos_ref.at[1], dpq),
        ):
            low = value.astype(bf16)
            ref[...] = low if a == 0 else jnp.where(mine, low, ref[...])


def attend_back(
    me, table_of, order, words, words_pick, q_pick, k, v, probs, pos_query, pos_key,
    dz2, mine, got, normed, inv_std, gain, w_out, early,
):
    seq, width = k.shape
    picks = q_pick.shape[0]
    table = pos_key.shape[0]
    pairs = width // LANES
    whole = lambda value: pl.BlockSpec(value.shape, lambda h: (0,) * value.ndim)
    col = lambda rows: pl.BlockSpec((rows, LANES), lambda h: (0, h))
    shape = lambda rows: jax.ShapeDtypeStruct((rows, width), bf16)
    return pl.pallas_call(
        back_kernel,
        grid=(pairs,),
        in_specs=[
            pl.BlockSpec(memory_space=pltpu.SMEM),
            whole(table_of), whole(order), whole(words), whole(words_pick),
            col(picks), col(seq), col(seq),
            pl.BlockSpec((2, picks, seq), lambda h: (h, 0, 0)),
            col(table), col(table),
            whole(dz2), whole(mine), whole(got), whole(normed), whole(inv_std), whole(gain),
            pl.BlockSpec((LANES, width), lambda h: (h, 0)), whole(early),
        ],
        out_specs=[
            col(picks), col(seq), col(seq),
            pl.BlockSpec((2, table, LANES), lambda h: (0, 0, h)),
            whole(dz2), whole(dz2), whole(early),
        ],
        out_shape=[
            shape(picks), shape(seq), shape(seq),
            jax.ShapeDtypeStruct((2, table, width), bf16),
            jax.ShapeDtypeStruct((picks, width), f32),
            shape(picks),
            jax.ShapeDtypeStruct(early.shape, f32),
        ],
        scratch_shapes=[
            pltpu.VMEM((seq, seq + LANES), bf16),
            pltpu.VMEM((picks, seq + LANES), bf16),
            pltpu.VMEM((seq, 2 * seq + LANES), bf16),
            pltpu.VMEM((picks, 2 * seq), bf16),
            pltpu.VMEM((seq, seq), f32),
            pltpu.VMEM((2 * seq, table), bf16),
            pltpu.VMEM((2 * seq, table), bf16),
            pltpu.SMEM((seq // LANES,), jnp.int32),
        ],
        compiler_params=PARAMS,
        name="attend_back",
    )(
        me, table_of, order, words, words_pick, q_pick, k, v, probs, pos_key, pos_query,
        dz2, mine, got, normed, inv_std, gain, w_out, early,
    )


def block_source(order_ref, me_ref, cols, length):
    relative = jnp.where(me_ref[1] == 0, order_ref[0:1, cols], order_ref[1:2, cols])
    return (me_ref[0] ^ relative) * (length // me_ref[2]) + order_ref[2:3, cols]


def turn_kernel(
    me_ref, order_ref, relorder_ref, x_ref, xpick_ref, cpick_ref, rel_ref,
    x_out, xpick_out, cpick_out, rel_out, rows,
):
    width, group = x_ref.shape[1], x_out.shape[1]
    table = rel_ref.shape[0]

    @pl.when(pl.program_id(0) == 0)
    def _():
        source = block_source(relorder_ref, me_ref, slice(None), table)
        spot = lax.broadcasted_iota(jnp.int32, (table, table), 0)
        rows[...] = dot_tn((spot == source).astype(f32).astype(bf16), rel_ref[...]).astype(bf16)

    source = block_source(order_ref, me_ref, slice(None), width)
    spot = lax.broadcasted_iota(jnp.int32, (width, group), 0)
    chosen = (spot == source).astype(f32).astype(bf16)
    for ref, out in ((x_ref, x_out), (xpick_ref, xpick_out), (cpick_ref, cpick_out), (rows, rel_out)):
        out[...] = dot_nn(ref[...], chosen).astype(bf16)


def turn_blocks(me, order, rel_order, x, x_pick, ctx_pick, rel_table):
    width = x.shape[1]
    group = 2 * LANES
    whole = lambda value: pl.BlockSpec(value.shape, lambda n: (0, 0))
    col = lambda value: pl.BlockSpec((value.shape[0], group), lambda n: (0, n))
    given = [x, x_pick, ctx_pick, rel_table]
    return pl.pallas_call(
        turn_kernel,
        grid=(width // group,),
        in_specs=[pl.BlockSpec(memory_space=pltpu.SMEM), col(order), whole(rel_order)]
        + [whole(value) for value in given],
        out_specs=[col(value) for value in given],
        out_shape=[jax.ShapeDtypeStruct(value.shape, bf16) for value in given],
        scratch_shapes=[pltpu.VMEM(rel_table.shape, bf16)],
        compiler_params=PARAMS,
        name="turn_blocks",
    )(me, order, rel_order, *given)


def ffn_picked_kernel(
    mine_ref, their_ref, win_ref, bin_ref, down_ref, part_ref, theirs_ref, hidden_ref, slope_ref, total
):
    step = pl.program_id(0)
    rows = jnp.concatenate([mine_ref[...], their_ref[...]], axis=0)
    pre = dot_nn(rows, win_ref[...]) + row_of(bin_ref)
    cdf = normal_cdf(pre)
    hidden = (pre * cdf).astype(bf16)
    hidden_ref[...] = hidden
    slope_ref[...] = cdf + pre * (jnp.exp(-0.5 * pre * pre) * (1.0 / math.sqrt(2.0 * math.pi)))
    part = dot_nn(hidden, down_ref[...])
    total[...] = jnp.where(step == 0, part, total[...] + part)

    @pl.when(step == pl.num_programs(0) - 1)
    def _():
        count = mine_ref.shape[0]
        part_ref[...] = total[:count].astype(bf16)
        theirs_ref[...] = total[count:].astype(bf16)


def ffn_picked(mine, theirs, w_in, b_in, w_down):
    picks, width = mine.shape
    hidden_cols = w_in.shape[1]
    tile = hidden_cols // 3
    whole = pl.BlockSpec((picks, width), lambda n: (0, 0))
    col = lambda rows: pl.BlockSpec((rows, tile), lambda n: (0, n))
    return pl.pallas_call(
        ffn_picked_kernel,
        grid=(3,),
        in_specs=[
            whole, whole, col(width), pl.BlockSpec((tile,), lambda n: (n,)),
            pl.BlockSpec((tile, width), lambda n: (n, 0)),
        ],
        out_specs=[whole, whole, col(2 * picks), col(2 * picks)],
        out_shape=[
            jax.ShapeDtypeStruct((picks, width), bf16),
            jax.ShapeDtypeStruct((picks, width), bf16),
            jax.ShapeDtypeStruct((2 * picks, hidden_cols), bf16),
            jax.ShapeDtypeStruct((2 * picks, hidden_cols), f32),
        ],
        scratch_shapes=[pltpu.VMEM((2 * picks, width), f32)],
        compiler_params=PARAMS,
        name="ffn_picked",
    )(mine, theirs, w_in, b_in, w_down)


def norm_picked_kernel(
    normed_ref, gain1_ref, bias1_ref, mine_ref, got_ref, bdown_ref, gain2_ref, grad_ref, pick_ref,
    dz2_ref, low_ref, sum_ref,
):
    h1 = normed_ref[...] * row_of(gain1_ref) + row_of(bias1_ref)
    branch = mine_ref[...].astype(f32) + got_ref[...].astype(f32) + row_of(bdown_ref)
    normed, inv_std = norm_stats(h1 + branch)
    used = jnp.sum(pick_ref[...].astype(f32), axis=1, keepdims=True)
    cot = jnp.where(used > 0.0, grad_ref[...].astype(f32), 0.0)
    dz2, g_gain, g_bias = norm_backward(cot, normed, inv_std, row_of(gain2_ref))
    dz2_ref[...] = dz2
    low = dz2.astype(bf16)
    low_ref[...] = low
    sum_ref[...] = jnp.concatenate(
        [col_sum(low.astype(f32)), g_gain, g_bias, jnp.zeros((5, h1.shape[1]), f32)], axis=0
    )


def norm_picked(normed, gain1, bias1, mine, got, b_down, gain2, grads, pick):
    picks, width = normed.shape
    return pl.pallas_call(
        norm_picked_kernel,
        out_shape=[
            jax.ShapeDtypeStruct((picks, width), f32),
            jax.ShapeDtypeStruct((picks, width), bf16),
            jax.ShapeDtypeStruct((8, width), f32),
        ],
        compiler_params=PARAMS,
        name="norm_picked",
    )(normed, gain1, bias1, mine, got, b_down, gain2, grads, pick)


def ffn_back_kernel(
    mine_ref, their_ref, win_ref, down_ref, slope_ref, part_ref, theirs_ref, dpre_ref, sum_ref, total
):
    step = pl.program_id(0)
    rows = jnp.concatenate([mine_ref[...], their_ref[...]], axis=0)
    dpre = (dot_nt(rows, down_ref[...]) * slope_ref[...]).astype(bf16)
    dpre_ref[...] = dpre
    sum_ref[...] = jnp.broadcast_to(col_sum(dpre.astype(f32)), sum_ref.shape)
    part = dot_nt(dpre, win_ref[...])
    total[...] = jnp.where(step == 0, part, total[...] + part)

    @pl.when(step == pl.num_programs(0) - 1)
    def _():
        count = mine_ref.shape[0]
        part_ref[...] = total[:count].astype(bf16)
        theirs_ref[...] = total[count:].astype(bf16)


def ffn_back(mine, theirs, w_in, w_down, slope):
    picks, width = mine.shape
    hidden_cols = w_in.shape[1]
    tile = hidden_cols // 3
    whole = pl.BlockSpec((picks, width), lambda n: (0, 0))
    col = lambda rows: pl.BlockSpec((rows, tile), lambda n: (0, n))
    return pl.pallas_call(
        ffn_back_kernel,
        grid=(3,),
        in_specs=[
            whole, whole, col(width), pl.BlockSpec((tile, width), lambda n: (n, 0)), col(2 * picks)
        ],
        out_specs=[whole, whole, col(2 * picks), col(8)],
        out_shape=[
            jax.ShapeDtypeStruct((picks, width), bf16),
            jax.ShapeDtypeStruct((picks, width), bf16),
            jax.ShapeDtypeStruct((2 * picks, hidden_cols), bf16),
            jax.ShapeDtypeStruct((8, hidden_cols), f32),
        ],
        scratch_shapes=[pltpu.VMEM((2 * picks, width), f32)],
        compiler_params=PARAMS,
        name="ffn_back",
    )(mine, theirs, w_in, w_down, slope)


def ffn_grads_kernel(
    half, me_ref, order_ref, mine_ref, their_ref, dmine_ref, dtheir_ref, dpre_ref, hidden_ref,
    out_ref, left,
):
    first = pl.program_id(0) == 0

    @pl.when(pl.program_id(1) == 0)
    def _():
        width = mine_ref.shape[1]
        cols = slice(half * (width // 2), (half + 1) * (width // 2))
        source = block_source(order_ref, me_ref, cols, width)
        spot = lax.broadcasted_iota(jnp.int32, (width, width // 2), 0)
        chosen = (spot == source).astype(f32).astype(bf16)
        mine = jnp.where(first, mine_ref[...], dmine_ref[...])
        theirs = jnp.where(first, their_ref[...], dtheir_ref[...])
        left[...] = dot_nn(jnp.concatenate([mine, theirs], axis=0), chosen).astype(bf16)

    @pl.when(first)
    def _():
        out_ref[...] = dot_tn(left[...], dpre_ref[...]).astype(bf16)

    @pl.when(jnp.logical_not(first))
    def _():
        out_ref[...] = dot_tn(left[...], hidden_ref[...]).astype(bf16)


def ffn_grads(half, me, order, mine, theirs, dmine, dtheirs, dpre, hidden):
    picks, width = mine.shape
    hidden_cols = dpre.shape[1]
    tile = hidden_cols // 3
    whole = lambda value: pl.BlockSpec(value.shape, lambda n, t: (0, 0))
    return pl.pallas_call(
        functools.partial(ffn_grads_kernel, half),
        grid=(2, 3),
        in_specs=[
            pl.BlockSpec(memory_space=pltpu.SMEM),
            whole(order), whole(mine), whole(mine), whole(mine), whole(mine),
            pl.BlockSpec((2 * picks, tile), lambda n, t: (0, jnp.where(n == 0, t, 2))),
            pl.BlockSpec((2 * picks, tile), lambda n, t: (0, jnp.where(n == 0, 0, t))),
        ],
        out_specs=pl.BlockSpec((width // 2, tile), lambda n, t: (0, 3 * n + t)),
        out_shape=jax.ShapeDtypeStruct((width // 2, 2 * hidden_cols), bf16),
        scratch_shapes=[pltpu.VMEM((2 * picks, width // 2), bf16)],
        compiler_params=PARAMS,
        name="ffn_grads",
    )(me, order, mine, theirs, dmine, dtheirs, dpre, hidden)


def ffn_full_kernel(
    x_ref, ctx_ref, ctx2_ref, wo_ref, bo_ref, gain1_ref, bias1_ref,
    win_ref, down_ref, bin_ref, win2_ref, down2_ref, bin2_ref, win3_ref, down3_ref, bin3_ref,
    bdown_ref, gain2_ref, bias2_ref, out_ref, h1, low, total,
):
    step = pl.program_id(0)
    width = x_ref.shape[1]

    @pl.when(step == 0)
    def _():
        attn = dot_nn(ctx_ref[...], wo_ref[: width // 2]) + dot_nn(ctx2_ref[...], wo_ref[width // 2 :])
        normed, _ = norm_stats(x_ref[...].astype(f32) + (attn + row_of(bo_ref)))
        value = normed * row_of(gain1_ref) + row_of(bias1_ref)
        h1[...] = value
        low[...] = value.astype(bf16)
        total[...] = jnp.zeros_like(total)

    def tile(w_ref, d_ref, b_ref):
        pre = dot_nn(low[...], w_ref[...]) + b_ref[...]
        total[...] += dot_nn((pre * normal_cdf(pre)).astype(bf16), d_ref[...])

    @pl.when(step < 4)
    def _():
        tile(win_ref, down_ref, bin_ref)

    @pl.when((step >= 4) & (step < 6))
    def _():
        tile(win2_ref, down2_ref, bin2_ref)

    @pl.when(step >= 6)
    def _():
        tile(win3_ref, down3_ref, bin3_ref)

    @pl.when(step == 7)
    def _():
        normed, _ = norm_stats(h1[...] + (total[...] + row_of(bdown_ref)))
        out_ref[...] = (normed * row_of(gain2_ref) + row_of(bias2_ref)).astype(bf16)


def ffn_full(x, ctx, w_out, b_out, gain1, bias1, shards, b_down, gain2, bias2):
    rows, width = x.shape
    tile = shards[0][0].shape[1] // 4
    whole = lambda value: pl.BlockSpec(value.shape, lambda t: (0,) * value.ndim)
    specs = []
    for first, last in ((0, 4), (4, 6), (6, 8)):
        at = lambda t, first=first, last=last: jnp.clip(t, first, last - 1) - first
        specs += [
            pl.BlockSpec((width, tile), lambda t, at=at: (0, at(t))),
            pl.BlockSpec((tile, width), lambda t, at=at: (at(t), 0)),
            pl.BlockSpec((1, tile), lambda t, at=at: (0, at(t))),
        ]
    head = [x, ctx[0], ctx[1], w_out, b_out, gain1, bias1]
    tail = [b_down, gain2, bias2]
    return pl.pallas_call(
        ffn_full_kernel,
        grid=(8,),
        in_specs=[whole(value) for value in head] + specs + [whole(value) for value in tail],
        out_specs=pl.BlockSpec((rows, width), lambda t: (0, 0)),
        out_shape=jax.ShapeDtypeStruct((rows, width), bf16),
        scratch_shapes=[
            pltpu.VMEM((rows, width), f32), pltpu.VMEM((rows, width), bf16), pltpu.VMEM((rows, width), f32)
        ],
        compiler_params=PARAMS,
        name="ffn_full",
    )(*head, *[value for shard in shards for value in shard], *tail)


def token_grads_kernel(pick_ref, dz1_ref, dq_ref, dk_ref, dv_ref, wq_ref, wk_ref, wv_ref, out_ref):
    sparse = dz1_ref[...] + dot_nt(dq_ref[...], wq_ref[...])
    upper = sparse.astype(bf16)
    lower = (sparse - upper.astype(f32)).astype(bf16)
    out_ref[...] = (
        dot_nt(dk_ref[...], wk_ref[...])
        + dot_nt(dv_ref[...], wv_ref[...])
        + dot_tn(pick_ref[...], upper)
        + dot_tn(pick_ref[...], lower)
    )


def token_grads(pick, dz1, dq, dk, dv, w_query, w_key, w_value):
    seq, width = dk.shape
    group = 2 * LANES
    whole = lambda value: pl.BlockSpec(value.shape, lambda n: (0, 0))
    col = lambda rows: pl.BlockSpec((rows, group), lambda n: (0, n))
    row = pl.BlockSpec((group, width), lambda n: (n, 0))
    return pl.pallas_call(
        token_grads_kernel,
        grid=(width // group,),
        in_specs=[whole(pick), col(dz1.shape[0]), whole(dq), whole(dk), whole(dv), row, row, row],
        out_specs=col(seq),
        out_shape=jax.ShapeDtypeStruct((seq, width), f32),
        compiler_params=PARAMS,
        name="token_grads",
    )(pick, dz1, dq, dk, dv, w_query, w_key, w_value)


def grads_kernel(
    half, x_ref, rel_ref, xpick_ref, cpick_ref, dpos_ref,
    dq_ref, dk_ref, dv_ref, dattn_ref, dposk_ref, dposq_ref, wq_ref, wk_ref,
    early_ref, bin_ref, bin2_ref, out_ref, sum_ref,
):
    width = x_ref.shape[1]
    group = 2 * LANES
    seq = x_ref.shape[0]

    def left(ref):
        starts = range(half * LANES, width, group)
        return jnp.concatenate([ref[:, at : at + LANES] for at in starts], axis=1)

    def put(at, value):
        for n in range(value.shape[0] // LANES):
            out_ref[at + n] = value[n * LANES : (n + 1) * LANES].astype(bf16)

    count = width // group
    rel_left = left(rel_ref)
    x_left = left(x_ref)
    put(0, dot_tn(left(xpick_ref), dq_ref[...]) + dot_tn(rel_left, dposq_ref[0]))
    put(count, dot_tn(x_left, dk_ref[...]) + dot_tn(rel_left, dposk_ref[0]))
    put(2 * count, dot_tn(x_left, dv_ref[...]))
    put(3 * count, dot_tn(left(cpick_ref), dattn_ref[...]))
    for n in range(dpos_ref.shape[1] // group):
        rows = slice(n * group + half * LANES, n * group + (half + 1) * LANES)
        put(
            4 * count + n,
            dot_nt(dpos_ref[0, rows, :], wk_ref[...]) + dot_nt(dpos_ref[1, rows, :], wq_ref[...]),
        )
    total = lambda value: col_sum(value.astype(f32))
    sum_ref[...] = jnp.concatenate(
        [
            total(dq_ref[...]) + total(dposq_ref[0]),
            total(dk_ref[...]) + total(dposk_ref[0]),
            total(dv_ref[...]),
            early_ref[:6],
            bin_ref[:1],
            bin2_ref[:1],
            jnp.zeros((5, group), f32),
        ],
        axis=0,
    )


def weight_grads(half, x, rel, x_pick, c_pick, dpos, dq, dk, dv, dattn, w_query, w_key, early, bins):
    seq, width = x.shape
    group = 2 * LANES
    planes = 4 * (width // group) + dpos.shape[1] // group
    whole = lambda value: pl.BlockSpec(value.shape, lambda n: (0,) * value.ndim)
    col = lambda value: pl.BlockSpec((value.shape[0], group), lambda n: (0, n))
    row = lambda value: pl.BlockSpec((group, value.shape[1]), lambda n: (n, 0))
    plane = lambda t: pl.BlockSpec((1, dpos.shape[1], group), lambda n: (t, 0, n))
    return pl.pallas_call(
        functools.partial(grads_kernel, half),
        grid=(width // group,),
        in_specs=[
            whole(x), whole(rel), whole(x_pick), whole(c_pick), whole(dpos),
            col(dq), col(dk), col(dv), col(dattn), plane(0), plane(1), row(w_query), row(w_key),
            col(early), col(bins), pl.BlockSpec((8, group), lambda n: (0, n + width // group)),
        ],
        out_specs=[
            pl.BlockSpec((planes, LANES, group), lambda n: (0, 0, n)),
            pl.BlockSpec((16, group), lambda n: (0, n)),
        ],
        out_shape=[
            jax.ShapeDtypeStruct((planes, LANES, width), bf16),
            jax.ShapeDtypeStruct((16, width), f32),
        ],
        compiler_params=PARAMS,
        name="weight_grads",
    )(
        x, rel, x_pick, c_pick, dpos, dq, dk, dv, dattn, dpos, dpos, w_query, w_key, early, bins, bins
    )


def swap(values, axis, bit):
    size = lax.axis_size(axis)
    return lax.ppermute(values, axis, [(n, n ^ bit) for n in range(size)])


def after(values, *others):
    return lax.optimization_barrier((values, others))[0]


class Halving:
    def __init__(self, axes, core, near, size):
        rest = [1 << n for n in range(size.bit_length() - 1) if (1 << n) != core]
        near = [bit for bit in near if bit in rest]
        rest = [bit for bit in rest if bit not in near]
        turned = near[-1:] + near[:-1]
        self.axes, self.core, self.size = axes, core, size
        self.orders = [[core] + near + rest, [core] + turned + rest]
        self.steps = len(self.orders[0])
        self.me = lax.axis_index(axes)
        self.upper = (self.me // core) % 2

    def core_of(self, place):
        return (place // self.core) % 2

    def send(self, values, step):
        pairs = [(n, n ^ self.orders[self.core_of(n)][step]) for n in range(self.size)]
        return lax.ppermute(values, self.axes, pairs)

    def bit(self, step):
        first, second = (order[step] for order in self.orders)
        return jnp.where(self.upper == 0, first, second)

    def relative(self, upper):
        masks = []
        for place in range(self.size):
            bits = [(place >> (self.steps - 1 - step)) & 1 for step in range(self.steps)]
            order = self.orders[upper ^ bits[0]]
            mask = 0
            for step, bit in enumerate(bits):
                mask ^= bit * order[step]
            masks.append(mask)
        return np.array(masks, np.int32)

    def order(self, length, unit):
        spots = np.arange(length)
        group = self.size * unit
        place = spots % group // unit
        rows = [self.relative(upper)[place] for upper in range(2)]
        rows.append(spots // group * unit + spots % unit)
        return jnp.asarray(np.stack(rows + [np.zeros_like(spots)] * 5).astype(np.int32))


def local(
    tokens, rel_ids, mask_pos, grad_vals, w_query, w_key, w_value, w_out, b_query, b_key,
    b_value, b_out, rel_table, ln1_gain, ln1_bias, w_in, b_in, w_down, b_down, ln2_gain, ln2_bias,
):
    assert rel_ids.shape[0] == 1
    seq, width = tokens.shape
    table_rows = rel_table.shape[0]
    hidden_cols = w_in.shape[1]
    pairs = width // LANES
    n_tok = lax.axis_size("tok")
    n_ffn = lax.axis_size("ffn")
    n_all = n_tok * n_ffn
    low = lambda value: value.astype(bf16)
    wide = lambda value: value.astype(f32)
    rel_ids, positions, grad_vals = rel_ids[0], mask_pos[0], grad_vals[0]

    over_all = Halving(("tok", "ffn"), n_ffn, [2 * n_ffn, 1, 4 * n_ffn], n_all)
    own, own_rel = width // n_all, table_rows // n_all
    unit = math.gcd(own, own_rel)
    over_tok = Halving("tok", 1, [2, 4], n_tok)
    me = jnp.stack([over_all.me, over_all.upper, jnp.int32(n_all)])
    me_tok = jnp.stack([over_tok.me, over_tok.upper, jnp.int32(n_tok)])
    tok_order = over_tok.order(width, width // n_tok)
    order, rel_order = over_all.order(width, unit), over_all.order(table_rows, unit)
    table_of = jnp.asarray(np.repeat(distance_rows(seq, table_rows)[:, None], LANES, 1))

    core = lax.axis_index("tok") % 2
    half_cols = hidden_cols // 2
    in_half = lax.dynamic_slice_in_dim(w_in, core * half_cols, half_cols, 1)
    bias_row = b_in.reshape(1, hidden_cols)
    bias_half = lax.dynamic_slice_in_dim(bias_row, core * half_cols, half_cols, 1)
    down_half = lax.dynamic_slice_in_dim(w_down, core * half_cols, half_cols, 0)

    pick = low(positions[:, None] == lax.broadcasted_iota(jnp.int32, (positions.shape[0], seq), 1))
    x_pick = low(dot_nn(pick, tokens))
    q_pick = low(dot_nn(x_pick, w_query) + b_query)
    k = low(dot_nn(tokens, w_key) + b_key)
    v = low(dot_nn(tokens, w_value) + b_value)
    pos_query = low(dot_nn(rel_table, w_query) + b_query)
    pos_key = low(dot_nn(rel_table, w_key) + b_key)
    ctx_pick, probs, key_scores, words, words_pick, normed1, inv1, h1_mine = attend_picked(
        positions, rel_ids, q_pick, k, v, pos_query, pos_key, x_pick, w_out, b_out, ln1_gain, ln1_bias
    )

    h1_theirs = swap(h1_mine, "ffn", 1)
    x_turned, x_pick_turned, c_pick_turned, rel_turned = turn_blocks(
        me, order, rel_order, tokens, x_pick, ctx_pick, rel_table
    )
    h1_theirs = after(h1_theirs, x_turned)
    part, theirs, hidden, slope = ffn_picked(h1_mine, h1_theirs, w_in, b_in, w_down)
    got = swap(theirs, "ffn", 1)
    q = low(dot_nn(after(tokens, theirs), w_query) + b_query)
    got = after(got, q)
    dz2, dffn, early = norm_picked(
        normed1, ln1_gain, ln1_bias, part, got, b_down, ln2_gain, grad_vals, pick
    )
    dffn_theirs = swap(dffn, "ffn", 1)
    dpart, dtheirs, dpre, gb_in = ffn_back(dffn, dffn_theirs, w_in, w_down, slope)
    dgot = swap(dtheirs, "ffn", 1)
    def halves(values, axis):
        size = values.shape[axis] // 2
        cut = lambda at: lax.slice_in_dim(values, at, at + size, axis=axis)
        return cut(0), cut(size)

    add = lambda one, other: low(wide(one) + wide(other))

    def next_halves(kept, got, axis):
        pieces = [add(one, other) for one, other in zip(halves(kept, axis), halves(got, axis))]
        return pieces

    def ffn_half(half, dpre):
        return ffn_grads(
            half, me_tok, tok_order, h1_mine, h1_theirs, dffn, dffn_theirs, dpre, hidden
        )

    ffn_sent = ffn_half(1, after(dpre, dtheirs))
    ffn_got = over_tok.send(ffn_sent, 0)
    in_half, bias_half, down_half = after((in_half, bias_half, down_half), ffn_sent)
    ffn_kept = ffn_half(0, after(dpre, ffn_sent))
    dgot = after(dgot, ffn_kept)
    far_in, far_bias = swap(in_half, "ffn", 1), swap(bias_half, "ffn", 1)
    ffn_kept, ffn_sent = next_halves(ffn_kept, ffn_got, 0)
    ffn_got = over_tok.send(ffn_sent, 1)
    dq, dk, dv, dpos, dz1, dattn, early = attend_back(
        me, table_of, rel_order, words, words_pick, q_pick, k, v, probs, pos_query, pos_key,
        dz2, dpart, after(dgot, in_half, ffn_sent), normed1, inv1, ln1_gain, w_out, early,
    )
    far_in, far_bias, ffn_got = after((far_in, far_bias, ffn_got), dk)
    ffn_kept, ffn_sent = next_halves(ffn_kept, ffn_got, 0)
    ffn_got = over_tok.send(ffn_sent, 2)

    def grads(half, dk):
        return weight_grads(
            half, x_turned, rel_turned, x_pick_turned, c_pick_turned, dpos, dq, dk, dv, dattn,
            w_query, w_key, early, gb_in,
        )

    all_send, vectors = grads(1, after(dk, far_in, ffn_sent))
    near_in, near_bias = swap(far_in, "tok", 1), swap(far_bias, "tok", 1)
    far_down = swap(after(down_half, far_in), "ffn", 1)

    all_got = over_all.send(all_send, 0)
    vec_got = over_all.send(vectors, 0)
    all_kept, _ = grads(0, after(dk, all_send))
    all_kept, all_sent = next_halves(all_kept, after(all_got, all_kept), 1)
    vectors = vectors + vec_got
    ffn_step = 3
    shared = lax.broadcasted_iota(jnp.int32, (vectors.shape[0], 1), 0) < 9

    def attend(first, count, q):
        return attend_full(rel_ids, q, k, v, pos_key, key_scores, first, count)

    fills = []
    for step in range(1, over_all.steps):
        all_got = over_all.send(all_sent, step)
        vec_got = over_all.send(vectors, step)
        if step == 1:
            fills.append(attend(0, pairs // 2, after(q, all_sent)))
        elif step == 2:
            fills.append(attend(pairs // 2, pairs - pairs // 2, after(q, all_sent)))
        elif step == 3:
            fills.append(
                token_grads(pick, dz1, dq, after(dk, all_sent), dv, w_query, w_key, w_value)
            )
        elif step == 4:
            near_down = swap(far_down, "tok", 1)
            shards = [
                (w_in, w_down, bias_row), (far_in, far_down, far_bias), (near_in, near_down, near_bias)
            ]
            fills.append(
                ffn_full(
                    after(tokens, all_sent), fills[:2], w_out, b_out, ln1_gain, ln1_bias, shards,
                    b_down, ln2_gain, ln2_bias,
                )
            )
        if step <= 4:
            all_got, vec_got = after((all_got, vec_got), fills[-1])
        if step <= 2 and ffn_step <= over_tok.steps:
            ffn_got = after(ffn_got, fills[-1])
            if ffn_step < over_tok.steps:
                ffn_kept, ffn_sent = next_halves(ffn_kept, ffn_got, 0)
                ffn_got = over_tok.send(ffn_sent, ffn_step)
                all_got = after(all_got, ffn_sent)
            else:
                ffn_kept = add(ffn_kept, ffn_got)
            ffn_step += 1
        if step < over_all.steps - 1:
            all_kept, all_sent = next_halves(all_kept, all_got, 1)
        else:
            all_sums = add(all_kept, all_got)
        vectors = vectors + jnp.where(shared | (over_all.bit(step) != 1), vec_got, 0.0)
    grad_tokens, output = fills[2:]
    for step in range(ffn_step, over_tok.steps + 1):
        if step < over_tok.steps:
            ffn_kept, ffn_sent = next_halves(ffn_kept, ffn_got, 0)
            ffn_got = over_tok.send(ffn_sent, step)
        else:
            ffn_kept = add(ffn_kept, ffn_got)
    s_ffn = ffn_kept

    all_sums = all_sums.reshape(all_sums.shape[0] * unit, width)
    s_w = [wide(all_sums[n * own : (n + 1) * own]) for n in range(4)]
    s_rel = wide(all_sums[4 * own :])
    s_vec = lax.dynamic_slice_in_dim(vectors[:9], over_all.me * own, own, 1)
    part = hidden_cols // n_tok
    s_bin = lax.dynamic_slice_in_dim(
        vectors[9 : 9 + hidden_cols // width].reshape(1, hidden_cols), lax.axis_index("tok") * part, part, 1
    )
    return (
        output,
        grad_tokens,
        s_w[0],
        s_w[1],
        s_w[2],
        s_w[3],
        s_vec[0],
        s_vec[1],
        s_vec[2],
        s_vec[3],
        s_rel,
        s_vec[4],
        s_vec[5],
        wide(s_ffn[:, :hidden_cols]),
        s_bin,
        jnp.transpose(wide(s_ffn[:, hidden_cols:])),
        s_vec[6],
        s_vec[7],
        s_vec[8],
    )


def solution(mesh):
    every = ("tok", "ffn")
    placed = (
        P(every, None), P(every, None, None), P(every, None), P(every, None, None),
        P(), P(), P(), P(), P(), P(), P(), P(), P(), P(), P(),
        P(None, "ffn"), P("ffn"), P("ffn", None), P(), P(), P(),
    )
    given = (
        P(every, None), P(every, None),
        P(every, None), P(every, None), P(every, None), P(every, None),
        P(every), P(every), P(every), P(every),
        P(every, None), P(every), P(every),
        P("tok", "ffn"), P("ffn", "tok"), P("ffn", "tok"),
        P(every), P(every), P(every),
    )
    return jax.shard_map(local, mesh=mesh, in_specs=placed, out_specs=given, check_vma=False)
```

```python
import functools
import math

import numpy as np

import jax
import jax.numpy as jnp
from jax import lax
from jax.experimental import pallas as pl
from jax.experimental.pallas import tpu as pltpu
from jax.sharding import PartitionSpec as P

HEAD = 64
LANES = 128
HALF = 64
ROWS = 32
AT_ONCE = 2
FIRST_PAIRS = 2
norm_eps = 1e-07
bf16 = jnp.bfloat16
f32 = jnp.float32
PARAMS = pltpu.CompilerParams(vmem_limit_bytes=60 * 2**20)


def dot_nn(first_op, second_op):
    return lax.dot_general(
        first_op, second_op, (((1,), (0,)), ((), ())), preferred_element_type=f32
    )


def dot_nt(first_op, second_op):
    return lax.dot_general(
        first_op, second_op, (((1,), (1,)), ((), ())), preferred_element_type=f32
    )


def dot_tn(first_op, second_op):
    return lax.dot_general(
        first_op, second_op, (((0,), (0,)), ((), ())), preferred_element_type=f32
    )


def distance_rows(seq_len, table_rows):
    side = table_rows // 2
    middle = side // 2
    rows = []
    for m in range(2 * seq_len):
        offset = max(seq_len - 1 - m, 1 - seq_len)
        size = abs(offset)
        if size > middle:
            ratio = math.log(size / middle) / math.log((2 * side - 1) / middle)
            size = int(math.ceil(ratio * (middle - 1))) + middle
        rows.append(side + (size if offset > 0 else -size))
    return np.array(rows, dtype=np.int32)


def lane_iota(rows=1):
    return lax.broadcasted_iota(jnp.int32, (rows, LANES), 1)


def member_chunk(words, c):
    return (words == lane_iota(words.shape[0]) + c * LANES).astype(f32).astype(bf16)


def id_bases(rel_ref, base):
    seq = rel_ref.shape[0]
    chunks = seq // LANES
    last = chunks * 2 - 2
    for g in range(seq // HALF):
        for c in range(chunks):
            block = rel_ref[g * HALF : (g + 1) * HALF, c * LANES : (c + 1) * LANES]
            base[g * chunks + c] = jnp.minimum(jnp.min(block) // HALF, last)


def both_alignments(table):
    return jnp.concatenate([table, table[HALF:], table[:HALF]], axis=0)


def longest(rows):
    wide = rows.astype(f32)
    return jnp.sqrt(jnp.max(jnp.sum(wide * wide, axis=1, keepdims=True)))


def pack_heads(first, second, dest, top):
    top = jnp.maximum(top, 1e-30)
    scale = 32000.0 / top
    upper = (first * scale).astype(jnp.int32)
    lower = (second * scale).astype(jnp.int32)
    dest[...] = upper * 65536 + lower
    return top * (1.0 / 32000.0)


def unpack_heads(words, step):
    lower = lax.shift_right_arithmetic(lax.shift_left(words, 16), 16)
    return words.astype(f32) * (step * (1.0 / 65536.0)), lower.astype(f32) * step


def picked_words(source, rel_ref, base, rows, c):
    chunks = rel_ref.shape[1] // LANES
    first = base[(rows.start // HALF) * chunks + c]
    place = rel_ref[rows, c * LANES : (c + 1) * LANES] - first * HALF
    index = place & (LANES - 1)
    at = pl.multiple_of((first % 2) * (chunks * LANES) + (first // 2) * LANES, LANES)
    near = jnp.take_along_axis(source[rows, pl.ds(at, LANES)], index, axis=1)
    at = pl.multiple_of(at + LANES, LANES)
    far = jnp.take_along_axis(source[rows, pl.ds(at, LANES)], index, axis=1)
    return jnp.where(place < LANES, near, far)


def unshift_in_order(source, words_ref, base, dest):
    seq = words_ref.shape[0]
    chunks = seq // LANES
    lane = lane_iota()
    zero = jnp.zeros((ROWS, LANES), f32)
    for g in range(chunks):
        first = base[g]
        for sub in range(LANES // ROWS):
            start = g * LANES + sub * ROWS
            rows = slice(start, start + ROWS)
            place = lane - (seq - 1) + words_ref[rows, :] + first * LANES
            index = place & (LANES - 1)
            turned = [
                jnp.take_along_axis(
                    source[rows, c * LANES : (c + 1) * LANES], index, axis=1
                )
                for c in range(chunks)
            ]

            def pick(c):
                return turned[c] if 0 <= c < chunks else zero

            near = place >= 0
            mid = place >= -LANES
            for c in range(chunks + 2):
                value = jnp.where(near, pick(c), jnp.where(mid, pick(c - 1), pick(c - 2)))
                at = pl.multiple_of((first + c) * LANES, LANES)
                dest[rows, pl.ds(at, LANES)] = value.astype(bf16)


def group_bases(words, base):
    seq = words.shape[0]
    for g in range(seq // LANES):
        top = jnp.max(words[g * LANES : (g + 1) * LANES])
        base[g] = (seq - 1 - top) // LANES


def softmax_weights(scores):
    factor = math.log2(math.e) / math.sqrt(3.0 * HEAD)
    top = jnp.max(functools.reduce(jnp.maximum, scores), axis=1, keepdims=True)
    return [jnp.exp2((score - top) * factor) for score in scores]


def head_lanes(a):
    return (lane_iota() < HEAD) if a == 0 else (lane_iota() >= HEAD)


def row_of(ref):
    return ref[...].reshape(1, ref.shape[0])


def norm_stats(values):
    centered = values - jnp.mean(values, axis=1, keepdims=True)
    inv_std = lax.rsqrt(jnp.mean(centered * centered, axis=1, keepdims=True) + norm_eps)
    return centered * inv_std, inv_std


def norm_backward(upstream, normed, inv_std, norm_gain):
    scaled = upstream * norm_gain
    adjusted = (
        scaled
        - jnp.mean(scaled, axis=1, keepdims=True)
        - normed * jnp.mean(scaled * normed, axis=1, keepdims=True)
    )
    return inv_std * adjusted, col_sum(upstream * normed), col_sum(upstream)


def col_sum(values):
    return jnp.sum(values, axis=0, keepdims=True)


def normal_cdf(pre_act):
    return 0.5 * (1.0 + lax.erf(pre_act * (1.0 / math.sqrt(2.0))))


def picked_kernel(
    pos_ref, rel_ref, qc_ref, k_ref, v_ref, pk_ref, pq_ref,
    x_ref, wo_ref, bo_ref, gain_ref, bias_ref,
    ctx_ref, prob_ref, key_ref, word_ref, wordc_ref, normed_ref, inv_ref, low_ref,
    packed, cpick, relc, keyc, attn, base,
):
    seq = k_ref.shape[0]
    picks = qc_ref.shape[0]
    chunks = seq // LANES

    @pl.when(pl.program_id(0) == 0)
    def _():
        row = lax.broadcasted_iota(jnp.int32, (seq, seq), 0)
        col = lax.broadcasted_iota(jnp.int32, (seq, seq), 1)
        side = pk_ref.shape[0] // 2
        step = jnp.sum(jnp.where(col == row - 1, rel_ref[...] - side, 0), axis=1, keepdims=True)
        steps = jnp.broadcast_to(step.astype(f32), (seq, LANES)).astype(bf16)
        word_ref[...] = dot_nn((col <= row).astype(f32).astype(bf16), steps).astype(jnp.int32)
        id_bases(rel_ref, base)
        for n in range(picks):
            place = jnp.maximum(pos_ref[n], 0)
            relc[n : n + 1, :] = rel_ref[pl.ds(place, 1), :]
            wordc_ref[n : n + 1, :] = word_ref[pl.ds(place, 1), :]

    zero = jnp.zeros((), bf16)
    table = both_alignments(pq_ref[...])
    keys = [dot_nt(jnp.where(head_lanes(a), k_ref[...], zero), table) for a in range(2)]
    unit = pack_heads(keys[0], keys[1], packed, longest(k_ref[...]) * longest(pq_ref[...]))
    for a in range(2):
        cpick[a] = dot_nt(jnp.where(head_lanes(a), qc_ref[...], zero), pk_ref[...])
    for g in range(chunks):
        for c in range(chunks):
            parts = []
            for start in range(g * LANES, (g + 1) * LANES, ROWS):
                parts.append(picked_words(packed, rel_ref, base, slice(start, start + ROWS), c))
            block = jnp.concatenate(parts, axis=0).T
            for a, value in enumerate(unpack_heads(block, unit)):
                key_ref[a, c * LANES : (c + 1) * LANES, g * LANES : (g + 1) * LANES] = value

    for n in range(picks):
        place = jnp.maximum(pos_ref[n], 0)
        for a in range(2):
            keyc[a, n : n + 1, :] = key_ref[a, pl.ds(place, 1), :]
    for a in range(2):
        mine = head_lanes(a)
        direct = dot_nt(jnp.where(mine, qc_ref[...], zero), k_ref[...])
        scores = []
        for c in range(chunks):
            ids = relc[:, c * LANES : (c + 1) * LANES]
            index = ids & (LANES - 1)
            value = jnp.take_along_axis(cpick[a, :, :LANES], index, axis=1)
            for n in range(1, pk_ref.shape[0] // LANES):
                other = cpick[a, :, n * LANES : (n + 1) * LANES]
                value = jnp.where(
                    ids >= n * LANES, jnp.take_along_axis(other, index, axis=1), value
                )
            cols = slice(c * LANES, (c + 1) * LANES)
            scores.append(direct[:, cols] + value + keyc[a, :, cols])
        weights = softmax_weights(scores)
        inverse = 1.0 / jnp.sum(sum(weights[1:], weights[0]), axis=1, keepdims=True)
        probs = jnp.concatenate([(weight * inverse).astype(bf16) for weight in weights], axis=1)
        prob_ref[a] = probs
        mixed = dot_nn(probs, v_ref[...]).astype(bf16)
        ctx_ref[...] = mixed if a == 0 else jnp.where(mine, mixed, ctx_ref[...])

    part = dot_nn(ctx_ref[...], wo_ref[...])

    @pl.when(pl.program_id(0) == 0)
    def _():
        attn[...] = x_ref[...].astype(f32) + row_of(bo_ref) + part

    @pl.when(pl.program_id(0) > 0)
    def _():
        attn[...] += part

    @pl.when(pl.program_id(0) == pl.num_programs(0) - 1)
    def _():
        normed, inv_std = norm_stats(attn[...])
        normed_ref[...] = normed
        inv_ref[...] = jnp.broadcast_to(inv_std, (picks, LANES))
        low_ref[...] = (normed * row_of(gain_ref) + row_of(bias_ref)).astype(bf16)


def attend_picked(
    positions, rel_ids, q_pick, k, v, pos_query, pos_key, x_pick, w_out, b_out, gain, bias
):
    seq, width = k.shape
    picks = q_pick.shape[0]
    table = pos_key.shape[0]
    pairs = width // LANES
    whole = lambda rows, cols: pl.BlockSpec((rows, cols), lambda h: (0, 0))
    line = pl.BlockSpec((width,), lambda h: (0,))
    col = lambda rows: pl.BlockSpec((rows, LANES), lambda h: (0, h))
    heads = lambda rows: pl.BlockSpec((2, rows, seq), lambda h: (h, 0, 0))
    return pl.pallas_call(
        picked_kernel,
        grid=(pairs,),
        in_specs=[
            pl.BlockSpec(memory_space=pltpu.SMEM), whole(seq, seq),
            col(picks), col(seq), col(seq), col(table), col(table),
            whole(picks, width), pl.BlockSpec((LANES, width), lambda h: (h, 0)), line, line, line,
        ],
        out_specs=[
            col(picks), heads(picks), heads(seq), whole(seq, LANES), whole(picks, LANES),
            whole(picks, width), whole(picks, LANES), whole(picks, width),
        ],
        out_shape=[
            jax.ShapeDtypeStruct((picks, width), bf16),
            jax.ShapeDtypeStruct((2 * pairs, picks, seq), bf16),
            jax.ShapeDtypeStruct((2 * pairs, seq, seq), f32),
            jax.ShapeDtypeStruct((seq, LANES), jnp.int32),
            jax.ShapeDtypeStruct((picks, LANES), jnp.int32),
            jax.ShapeDtypeStruct((picks, width), f32),
            jax.ShapeDtypeStruct((picks, LANES), f32),
            jax.ShapeDtypeStruct((picks, width), bf16),
        ],
        scratch_shapes=[
            pltpu.VMEM((seq, 2 * table), jnp.int32),
            pltpu.VMEM((2, picks, table), f32),
            pltpu.VMEM((picks, seq), jnp.int32),
            pltpu.VMEM((2, picks, seq), f32),
            pltpu.VMEM((picks, width), f32),
            pltpu.SMEM((seq // HALF * (seq // LANES),), jnp.int32),
        ],
        compiler_params=PARAMS,
        name="attend_picked",
    )(
        positions, rel_ids, q_pick, k, v, pos_key, pos_query, x_pick, w_out, b_out, gain, bias
    )


def full_kernel(rel_ref, q_ref, k_ref, v_ref, pk_ref, key_ref, ctx_ref, *scratch):
    seq = rel_ref.shape[0]
    chunks = seq // LANES
    base, scratch = scratch[-1], scratch[:-1]
    count = len(scratch) // 3

    @pl.when(pl.program_id(0) == 0)
    def _():
        id_bases(rel_ref, base)

    zero = jnp.zeros((), bf16)
    units = []
    for n in range(count):
        packed, direct, low = scratch[3 * n : 3 * n + 3]
        lanes = slice(n * LANES, (n + 1) * LANES)
        q, pos = q_ref[:, lanes], pk_ref[:, lanes]
        table = both_alignments(pos)
        far = []
        for a in range(2):
            q_a = jnp.where(head_lanes(a), q, zero)
            far.append(dot_nt(q_a, table))
            direct[a] = dot_nt(q_a, k_ref[:, lanes])
        units.append(pack_heads(far[0], far[1], packed, longest(q) * longest(pos)))
    for n in range(count):
        packed, direct, low = scratch[3 * n : 3 * n + 3]
        lanes = slice(n * LANES, (n + 1) * LANES)
        for start in range(0, seq, HALF):
            rows = slice(start, start + HALF)
            scores = [[], []]
            for c in range(chunks):
                cols = slice(c * LANES, (c + 1) * LANES)
                values = unpack_heads(picked_words(packed, rel_ref, base, rows, c), units[n])
                for a in range(2):
                    scores[a].append(
                        values[a] + direct[a, rows, cols] + key_ref[2 * n + a, rows, cols]
                    )
            for a in range(2):
                for c, weight in enumerate(softmax_weights(scores[a])):
                    low[a, rows, c * LANES : (c + 1) * LANES] = weight.astype(bf16)
        v = v_ref[:, lanes]
        mixed = [
            dot_nn(low[a], jnp.where(head_lanes(a), v, jnp.ones((), bf16))) for a in range(2)
        ]
        upper = head_lanes(0)
        totals = pltpu.roll(jnp.where(upper, mixed[1], mixed[0]), HEAD, 1)
        ctx_ref[:, lanes] = (jnp.where(upper, mixed[0], mixed[1]) * (1.0 / totals)).astype(bf16)


def attend_full(rel_ids, q, k, v, pos_key, key_scores, first, pairs):
    seq = k.shape[0]
    table = pos_key.shape[0]
    per = AT_ONCE
    wide = per * LANES
    col = lambda rows: pl.BlockSpec((rows, wide), lambda h: (0, h + first // per))
    return pl.pallas_call(
        full_kernel,
        grid=(pairs // per,),
        in_specs=[
            pl.BlockSpec((seq, seq), lambda h: (0, 0)),
            col(seq), col(seq), col(seq), col(table),
            pl.BlockSpec((2 * per, seq, seq), lambda h: (h + first // per, 0, 0)),
        ],
        out_specs=pl.BlockSpec((seq, wide), lambda h: (0, h)),
        out_shape=jax.ShapeDtypeStruct((seq, pairs * LANES), bf16),
        scratch_shapes=[
            pltpu.VMEM((seq, 2 * table), jnp.int32),
            pltpu.VMEM((2, seq, seq), f32),
            pltpu.VMEM((2, seq, seq), bf16),
        ]
        * per
        + [pltpu.SMEM((seq // HALF * (seq // LANES),), jnp.int32)],
        compiler_params=PARAMS,
        name="attend_full",
    )(rel_ids, q, k, v, pos_key, key_scores)


def back_kernel(
    me_ref, row_ref, order_ref, word_ref, wordc_ref, qc_ref, k_ref, v_ref, prob_ref, pk_ref, pq_ref,
    dz2_ref, mine_ref, got_ref, normed_ref, inv_ref, gain_ref, wo_ref, early_ref,
    dq_ref, dk_ref, dv_ref, dpos_ref, dz1_ref, dattn_ref, sum_ref,
    side, sidec, moved, movedc, expand, turned_expand, base,
):
    seq = k_ref.shape[0]
    picks = qc_ref.shape[0]
    table = pk_ref.shape[0]
    chunks = seq // LANES

    @pl.when(pl.program_id(0) == 0)
    def _():
        words = word_ref[...]
        for c in range(chunks):
            side[:, c * LANES : (c + 1) * LANES] = member_chunk(words, c)
            sidec[:, c * LANES : (c + 1) * LANES] = member_chunk(wordc_ref[...], c)
        group_bases(words, base)
        moved[...] = jnp.zeros_like(moved)
        for c in range(table // LANES):
            cols = slice(c * LANES, (c + 1) * LANES)
            expand[:, cols] = member_chunk(row_ref[...], c)
            source = block_source(order_ref, me_ref, cols, table)
            chosen = (row_ref[...] == source).astype(f32).astype(bf16)
            turned_expand[cols, :] = chosen.T
        dh1 = dz2_ref[...] + mine_ref[...].astype(f32) + got_ref[...].astype(f32)
        dz1, g_gain, g_bias = norm_backward(dh1, normed_ref[...], inv_ref[:, :1], row_of(gain_ref))
        dz1_ref[...] = dz1
        dattn = dz1.astype(bf16)
        dattn_ref[...] = dattn
        sum_ref[...] = jnp.concatenate(
            [col_sum(dattn.astype(f32)), g_gain, g_bias, early_ref[:5]], axis=0
        )

    lane = lane_iota()
    scale = 1.0 / math.sqrt(3.0 * HEAD)
    zero = jnp.zeros((), bf16)
    far_key = dot_nn(expand[...], pk_ref[...]).astype(bf16)
    far_query = dot_nn(expand[...], pq_ref[...]).astype(bf16)
    dctx = dot_nt(dattn_ref[...], wo_ref[...]).astype(bf16)
    for a in range(2):
        mine = head_lanes(a)
        keep = lambda value: jnp.where(mine, value, zero)
        dctx_a = keep(dctx)
        q_a = keep(qc_ref[...])
        k_a = keep(k_ref[...])
        side[:, seq:] = k_a
        sidec[:, seq:] = q_a
        dprobs = dot_nt(dctx_a, v_ref[...])
        probs = prob_ref[a].astype(f32)
        prod = probs * dprobs
        gs = ((prod - probs * jnp.sum(prod, axis=1, keepdims=True)) * scale).astype(bf16)
        dv = dot_tn(prob_ref[a], dctx_a)

        out = dot_nn(gs, side[...])
        place = lane - (seq - 1) + wordc_ref[...]
        index = place & (LANES - 1)
        turned = [
            jnp.take_along_axis(out[:, c * LANES : (c + 1) * LANES], index, axis=1)
            for c in range(chunks)
        ]
        blank = jnp.zeros((picks, LANES), f32)
        for c in range(2 * chunks):
            value = turned[c] if c < chunks else blank
            for n in range(1, chunks + 1):
                other = turned[c - n] if 0 <= c - n < chunks else blank
                value = jnp.where(place < -LANES * (n - 1), other, value)
            movedc[:, c * LANES : (c + 1) * LANES] = value.astype(bf16)
        dq = out[:, seq:] + dot_nn(movedc[...], keep(far_key))
        dpk = dot_tn(movedc[...], q_a)

        out = dot_tn(gs, sidec[...])
        unshift_in_order(out, word_ref, base, moved)
        dk = out[:, seq:] + dot_nn(moved[:, : 2 * seq], keep(far_query))
        dpq = dot_tn(moved[:, : 2 * seq], k_a)
        far = [dpk, dpq] if a == 0 else [far[0] + dpk, far[1] + dpq]
        for ref, value in ((dq_ref, dq), (dk_ref, dk), (dv_ref, dv)):
            low = value.astype(bf16)
            ref[...] = low if a == 0 else jnp.where(mine, low, ref[...])
    for n in range(2):
        dpos_ref[n] = dot_nn(turned_expand[...], far[n].astype(bf16)).astype(bf16)


def attend_back(
    me, table_of, order, words, words_pick, q_pick, k, v, probs, pos_query, pos_key,
    dz2, mine, got, normed, inv_std, gain, w_out, early,
):
    seq, width = k.shape
    picks = q_pick.shape[0]
    table = pos_key.shape[0]
    pairs = width // LANES
    whole = lambda value: pl.BlockSpec(value.shape, lambda h: (0,) * value.ndim)
    col = lambda rows: pl.BlockSpec((rows, LANES), lambda h: (0, h))
    shape = lambda rows: jax.ShapeDtypeStruct((rows, width), bf16)
    return pl.pallas_call(
        back_kernel,
        grid=(pairs,),
        in_specs=[
            pl.BlockSpec(memory_space=pltpu.SMEM),
            whole(table_of), whole(order), whole(words), whole(words_pick),
            col(picks), col(seq), col(seq),
            pl.BlockSpec((2, picks, seq), lambda h: (h, 0, 0)),
            col(table), col(table),
            whole(dz2), whole(mine), whole(got), whole(normed), whole(inv_std), whole(gain),
            pl.BlockSpec((LANES, width), lambda h: (h, 0)), whole(early),
        ],
        out_specs=[
            col(picks), col(seq), col(seq),
            pl.BlockSpec((2, table, LANES), lambda h: (0, 0, h)),
            whole(dz2), whole(dz2), whole(early),
        ],
        out_shape=[
            shape(picks), shape(seq), shape(seq),
            jax.ShapeDtypeStruct((2, table, width), bf16),
            jax.ShapeDtypeStruct((picks, width), f32),
            shape(picks),
            jax.ShapeDtypeStruct(early.shape, f32),
        ],
        scratch_shapes=[
            pltpu.VMEM((seq, seq + LANES), bf16),
            pltpu.VMEM((picks, seq + LANES), bf16),
            pltpu.VMEM((seq, 2 * seq + LANES), bf16),
            pltpu.VMEM((picks, 2 * seq), bf16),
            pltpu.VMEM((2 * seq, table), bf16),
            pltpu.VMEM((table, 2 * seq), bf16),
            pltpu.SMEM((seq // LANES,), jnp.int32),
        ],
        compiler_params=PARAMS,
        name="attend_back",
    )(
        me, table_of, order, words, words_pick, q_pick, k, v, probs, pos_key, pos_query,
        dz2, mine, got, normed, inv_std, gain, w_out, early,
    )


def block_source(order_ref, me_ref, cols, length):
    relative = jnp.where(me_ref[1] == 0, order_ref[0:1, cols], order_ref[1:2, cols])
    return (me_ref[0] ^ relative) * (length // me_ref[2]) + order_ref[2:3, cols]


def turn_kernel(
    me_ref, order_ref, relorder_ref, x_ref, xpick_ref, cpick_ref, rel_ref,
    x_out, xpick_out, cpick_out, rel_out, rows,
):
    width, group = x_ref.shape[1], x_out.shape[0]
    table = rel_ref.shape[0]

    def chosen(ref, length):
        relative = jnp.where(me_ref[1] == 0, ref[:, 0:1], ref[:, 1:2])
        source = (me_ref[0] ^ relative) * (length // me_ref[2]) + ref[:, 2:3]
        spot = lax.broadcasted_iota(jnp.int32, (ref.shape[0], length), 1)
        return (spot == source).astype(f32).astype(bf16)

    @pl.when(pl.program_id(0) == 0)
    def _():
        rows[...] = dot_nn(chosen(relorder_ref, table), rel_ref[...]).astype(bf16)

    picked = chosen(order_ref, width)
    for ref, out in ((x_ref, x_out), (xpick_ref, xpick_out), (cpick_ref, cpick_out), (rows, rel_out)):
        out[...] = dot_nt(picked, ref[...]).astype(bf16)


def turn_blocks(me, order, rel_order, x, x_pick, ctx_pick, rel_table):
    width = x.shape[1]
    group = 2 * LANES
    whole = lambda value: pl.BlockSpec(value.shape, lambda n: (0, 0))
    row = lambda count: pl.BlockSpec((group, count), lambda n: (n, 0))
    given = [x, x_pick, ctx_pick, rel_table]
    return pl.pallas_call(
        turn_kernel,
        grid=(width // group,),
        in_specs=[pl.BlockSpec(memory_space=pltpu.SMEM), row(LANES), whole(rel_order)]
        + [whole(value) for value in given],
        out_specs=[row(value.shape[0]) for value in given],
        out_shape=[jax.ShapeDtypeStruct(value.shape[::-1], bf16) for value in given],
        scratch_shapes=[pltpu.VMEM(rel_table.shape, bf16)],
        compiler_params=PARAMS,
        name="turn_blocks",
    )(me, order, rel_order, *given)


def norm_picked_kernel(
    normed_ref, gain1_ref, bias1_ref, mine_ref, got_ref, bdown_ref, gain2_ref, grad_ref, pick_ref,
    dz2_ref, low_ref, sum_ref,
):
    h1 = normed_ref[...] * row_of(gain1_ref) + row_of(bias1_ref)
    branch = mine_ref[...].astype(f32) + got_ref[...].astype(f32) + row_of(bdown_ref)
    normed, inv_std = norm_stats(h1 + branch)
    used = jnp.sum(pick_ref[...].astype(f32), axis=1, keepdims=True)
    cot = jnp.where(used > 0.0, grad_ref[...].astype(f32), 0.0)
    dz2, g_gain, g_bias = norm_backward(cot, normed, inv_std, row_of(gain2_ref))
    dz2_ref[...] = dz2
    low = dz2.astype(bf16)
    low_ref[...] = low
    sum_ref[...] = jnp.concatenate(
        [col_sum(low.astype(f32)), g_gain, g_bias, jnp.zeros((5, h1.shape[1]), f32)], axis=0
    )


def norm_picked(normed, gain1, bias1, mine, got, b_down, gain2, grads, pick):
    picks, width = normed.shape
    return pl.pallas_call(
        norm_picked_kernel,
        out_shape=[
            jax.ShapeDtypeStruct((picks, width), f32),
            jax.ShapeDtypeStruct((picks, width), bf16),
            jax.ShapeDtypeStruct((8, width), f32),
        ],
        compiler_params=PARAMS,
        name="norm_picked",
    )(normed, gain1, bias1, mine, got, b_down, gain2, grads, pick)


def ffn_full_kernel(
    x_ref, ctx_ref, ctx2_ref, wo_ref, bo_ref, gain1_ref, bias1_ref, bdown_ref, gain2_ref, bias2_ref,
    bin_ref, bin2_ref, bin3_ref, win_ref, down_ref, win2_ref, down2_ref, win3_ref, down3_ref,
    out_ref, h1, low, total, win_here, down_here, win_sem, down_sem,
):
    rows, width = x_ref.shape
    tile = win_here.shape[2]
    parts = [(win_ref, down_ref, bin_ref, n * tile) for n in range(win_ref.shape[1] // tile)]
    parts += [(win2_ref, down2_ref, bin2_ref, 0), (win3_ref, down3_ref, bin3_ref, 0)]

    def copies(n):
        w_ref, d_ref, _, at = parts[n]
        return (
            pltpu.make_async_copy(w_ref.at[:, at : at + tile], win_here.at[n], win_sem.at[n]),
            pltpu.make_async_copy(d_ref.at[at : at + tile, :], down_here.at[n], down_sem.at[n]),
        )

    for n in range(len(parts)):
        for copy in copies(n):
            copy.start()
    attn = dot_nn(ctx_ref[...], wo_ref[: ctx_ref.shape[1]]) + dot_nn(
        ctx2_ref[...], wo_ref[ctx_ref.shape[1] :]
    )
    normed, _ = norm_stats(x_ref[...].astype(f32) + (attn + row_of(bo_ref)))
    value = normed * row_of(gain1_ref) + row_of(bias1_ref)
    h1[...] = value
    low[...] = value.astype(bf16)
    step = rows // 2
    for n in range(len(parts)):
        for copy in copies(n):
            copy.wait()
        bias = parts[n][2][:, parts[n][3] : parts[n][3] + tile]
        for at in range(0, rows, step):
            pre = dot_nn(low[at : at + step], win_here[n]) + bias
            part = dot_nn((pre * normal_cdf(pre)).astype(bf16), down_here[n])
            total[at : at + step] = part if n == 0 else total[at : at + step] + part
    normed, _ = norm_stats(h1[...] + (total[...] + row_of(bdown_ref)))
    out_ref[...] = (normed * row_of(gain2_ref) + row_of(bias2_ref)).astype(bf16)


def ffn_full(x, ctx, w_out, b_out, gain1, bias1, shards, b_down, gain2, bias2):
    rows, width = x.shape
    tile = shards[1][0].shape[1]
    count = shards[0][0].shape[1] // tile + 2
    held = [x, ctx[0], ctx[1], w_out, b_out, gain1, bias1, b_down, gain2, bias2]
    held += [shard[2] for shard in shards]
    moved = [value for shard in shards for value in shard[:2]]
    return pl.pallas_call(
        ffn_full_kernel,
        in_specs=[pl.BlockSpec(memory_space=pltpu.VMEM)] * len(held)
        + [pl.BlockSpec(memory_space=pl.ANY)] * len(moved),
        out_specs=pl.BlockSpec(memory_space=pltpu.VMEM),
        out_shape=jax.ShapeDtypeStruct((rows, width), bf16),
        scratch_shapes=[
            pltpu.VMEM((rows, width), f32), pltpu.VMEM((rows, width), bf16), pltpu.VMEM((rows, width), f32),
            pltpu.VMEM((count, width, tile), bf16), pltpu.VMEM((count, tile, width), bf16),
            pltpu.SemaphoreType.DMA((count,)), pltpu.SemaphoreType.DMA((count,)),
        ],
        compiler_params=PARAMS,
        name="ffn_full",
    )(*held, *moved)


def token_grads_kernel(pick_ref, dz1_ref, dq_ref, dk_ref, dv_ref, wq_ref, wk_ref, wv_ref, out_ref):
    sparse = dz1_ref[...] + dot_nt(dq_ref[...], wq_ref[...])
    upper = sparse.astype(bf16)
    lower = (sparse - upper.astype(f32)).astype(bf16)
    out_ref[...] = (
        dot_nt(dk_ref[...], wk_ref[...])
        + dot_nt(dv_ref[...], wv_ref[...])
        + dot_tn(pick_ref[...], upper)
        + dot_tn(pick_ref[...], lower)
    )


def token_grads(pick, dz1, dq, dk, dv, w_query, w_key, w_value):
    seq, width = dk.shape
    group = 2 * LANES
    whole = lambda value: pl.BlockSpec(value.shape, lambda n: (0, 0))
    col = lambda rows: pl.BlockSpec((rows, group), lambda n: (0, n))
    row = pl.BlockSpec((group, width), lambda n: (n, 0))
    return pl.pallas_call(
        token_grads_kernel,
        grid=(width // group,),
        in_specs=[whole(pick), col(dz1.shape[0]), whole(dq), whole(dk), whole(dv), row, row, row],
        out_specs=col(seq),
        out_shape=jax.ShapeDtypeStruct((seq, width), f32),
        compiler_params=PARAMS,
        name="token_grads",
    )(pick, dz1, dq, dk, dv, w_query, w_key, w_value)


def grads_kernel(
    half, x_ref, rel_ref, xpick_ref, cpick_ref, dpos_ref,
    dq_ref, dk_ref, dv_ref, dattn_ref, dposk_ref, dposq_ref, wq_ref, wk_ref, *refs
):
    width = x_ref.shape[0]
    group = 2 * LANES

    def left(ref):
        starts = range(half * LANES, width, group)
        return jnp.concatenate([ref[at : at + LANES, :] for at in starts], axis=0)

    def put(at, value):
        for n in range(value.shape[0] // LANES):
            block = value[n * LANES : (n + 1) * LANES]
            if half:
                refs[3][at + n] = block.astype(bf16)
            else:
                block = (block + refs[0][at + n].astype(f32)).astype(bf16)
                refs[1][at + n] = block[: LANES // 2]
                refs[2][at + n] = block[LANES // 2 :]

    count = width // group
    rel_left = left(rel_ref)
    x_left = left(x_ref)
    put(0, dot_nn(left(xpick_ref), dq_ref[...]) + dot_nn(rel_left, dposq_ref[0]))
    put(count, dot_nn(x_left, dk_ref[...]) + dot_nn(rel_left, dposk_ref[0]))
    put(2 * count, dot_nn(x_left, dv_ref[...]))
    put(3 * count, dot_nn(left(cpick_ref), dattn_ref[...]))
    for n in range(dpos_ref.shape[1] // group):
        rows = slice(n * group + half * LANES, n * group + (half + 1) * LANES)
        put(
            4 * count + n,
            dot_nt(dpos_ref[0, rows, :], wk_ref[...]) + dot_nt(dpos_ref[1, rows, :], wq_ref[...]),
        )
    if half:
        early_ref, bin_ref, bin2_ref, _, sum_ref = refs
        total = lambda value: col_sum(value.astype(f32))
        sum_ref[...] = jnp.concatenate(
            [
                total(dq_ref[...]) + total(dposq_ref[0]),
                total(dk_ref[...]) + total(dposk_ref[0]),
                total(dv_ref[...]),
                early_ref[:6],
                bin_ref[:1],
                bin2_ref[:1],
                jnp.zeros((5, group), f32),
            ],
            axis=0,
        )


def weight_grads(half, x, rel, x_pick, c_pick, dpos, dq, dk, dv, dattn, w_query, w_key, *more):
    width, seq = x.shape
    group = 2 * LANES
    planes = 4 * (width // group) + dpos.shape[1] // group
    whole = lambda value: pl.BlockSpec(value.shape, lambda n: (0,) * value.ndim)
    col = lambda value: pl.BlockSpec((value.shape[0], group), lambda n: (0, n))
    row = lambda value: pl.BlockSpec((group, value.shape[1]), lambda n: (n, 0))
    plane = lambda t: pl.BlockSpec((1, dpos.shape[1], group), lambda n: (t, 0, n))
    block = lambda rows: pl.BlockSpec((planes, rows, group), lambda n: (0, 0, n))
    shape = lambda rows: jax.ShapeDtypeStruct((planes, rows, width), bf16)
    if half:
        early, bins = more
        extra = [early, bins, bins]
        extra_specs = [
            col(early), col(bins), pl.BlockSpec((8, group), lambda n: (0, n + width // group))
        ]
        out_specs = [block(LANES), pl.BlockSpec((16, group), lambda n: (0, n))]
        out_shape = [shape(LANES), jax.ShapeDtypeStruct((16, width), f32)]
    else:
        extra = list(more)
        extra_specs = [block(LANES)]
        out_specs = [block(LANES // 2)] * 2
        out_shape = [shape(LANES // 2)] * 2
    return pl.pallas_call(
        functools.partial(grads_kernel, half),
        grid=(width // group,),
        in_specs=[
            whole(x), whole(rel), whole(x_pick), whole(c_pick), whole(dpos),
            col(dq), col(dk), col(dv), col(dattn), plane(0), plane(1), row(w_query), row(w_key),
        ]
        + extra_specs,
        out_specs=out_specs,
        out_shape=out_shape,
        compiler_params=PARAMS,
        name="weight_grads",
    )(x, rel, x_pick, c_pick, dpos, dq, dk, dv, dattn, dpos, dpos, w_query, w_key, *extra)


def swap(values, axis, bit):
    size = lax.axis_size(axis)
    return lax.ppermute(values, axis, [(n, n ^ bit) for n in range(size)])


def after(values, *others):
    return lax.optimization_barrier((values, others))[0]


class Halving:
    def __init__(self, axes, core, near, size):
        rest = [1 << n for n in range(size.bit_length() - 1) if (1 << n) != core]
        near = [bit for bit in near if bit in rest]
        rest = [bit for bit in rest if bit not in near]
        turned = near[-1:] + near[:-1]
        self.axes, self.core, self.size = axes, core, size
        self.orders = [[core] + near + rest, [core] + turned + rest]
        self.steps = len(self.orders[0])
        self.me = lax.axis_index(axes)
        self.upper = (self.me // core) % 2

    def core_of(self, place):
        return (place // self.core) % 2

    def send(self, values, step):
        pairs = [(n, n ^ self.orders[self.core_of(n)][step]) for n in range(self.size)]
        return lax.ppermute(values, self.axes, pairs)

    def bit(self, step):
        first, second = (order[step] for order in self.orders)
        return jnp.where(self.upper == 0, first, second)

    def relative(self, upper):
        masks = []
        for place in range(self.size):
            bits = [(place >> (self.steps - 1 - step)) & 1 for step in range(self.steps)]
            order = self.orders[upper ^ bits[0]]
            mask = 0
            for step, bit in enumerate(bits):
                mask ^= bit * order[step]
            masks.append(mask)
        return np.array(masks, np.int32)

    def order(self, length, unit):
        spots = np.arange(length)
        group = self.size * unit
        place = spots % group // unit
        rows = [self.relative(upper)[place] for upper in range(2)]
        rows.append(spots // group * unit + spots % unit)
        return np.stack(rows).astype(np.int32)

    def matrix(self, length, unit):
        first, second, inner = self.order(length, unit)
        source = (self.me ^ jnp.where(self.upper == 0, first, second)) * (length // self.size) + inner
        spot = lax.broadcasted_iota(jnp.int32, (length, length), 0)
        return (spot == source[None, :]).astype(bf16)


def local(
    tokens, rel_ids, mask_pos, grad_vals, w_query, w_key, w_value, w_out, b_query, b_key,
    b_value, b_out, rel_table, ln1_gain, ln1_bias, w_in, b_in, w_down, b_down, ln2_gain, ln2_bias,
):
    assert rel_ids.shape[0] == 1
    seq, width = tokens.shape
    table_rows = rel_table.shape[0]
    hidden_cols = w_in.shape[1]
    pairs = width // LANES
    n_tok = lax.axis_size("tok")
    n_ffn = lax.axis_size("ffn")
    n_all = n_tok * n_ffn
    low = lambda value: value.astype(bf16)
    wide = lambda value: value.astype(f32)
    rel_ids, positions, grad_vals = rel_ids[0], mask_pos[0], grad_vals[0]

    over_all = Halving(("tok", "ffn"), n_ffn, [2 * n_ffn, 1, 4 * n_ffn], n_all)
    own, own_rel = width // n_all, table_rows // n_all
    unit = math.gcd(own, own_rel)
    over_tok = Halving("tok", 1, [2, 4], n_tok)
    me = jnp.stack([over_all.me, over_all.upper, jnp.int32(n_all)])
    pad = lambda value, count: np.pad(value, ((0, count - value.shape[0]), (0, 0)))
    order = jnp.asarray(pad(over_all.order(width, unit), LANES).T)
    rel_order = jnp.asarray(pad(over_all.order(table_rows, unit), 8))
    rel_order_cols = jnp.asarray(pad(over_all.order(table_rows, unit), LANES).T)
    table_of = jnp.asarray(np.repeat(distance_rows(seq, table_rows)[:, None], LANES, 1))

    core = lax.axis_index("tok") % 2
    half_cols = hidden_cols // 2
    in_half = lax.dynamic_slice_in_dim(w_in, core * half_cols, half_cols, 1)
    bias_row = b_in.reshape(1, hidden_cols)
    bias_half = lax.dynamic_slice_in_dim(bias_row, core * half_cols, half_cols, 1)
    down_half = lax.dynamic_slice_in_dim(w_down, core * half_cols, half_cols, 0)

    pick = low(positions[:, None] == lax.broadcasted_iota(jnp.int32, (positions.shape[0], seq), 1))
    x_pick = low(dot_nn(pick, tokens))
    q_pick = low(dot_nn(x_pick, w_query) + b_query)
    k = low(dot_nn(tokens, w_key) + b_key)
    v = low(dot_nn(tokens, w_value) + b_value)
    pos_query = low(dot_nn(rel_table, w_query) + b_query)
    pos_key = low(dot_nn(rel_table, w_key) + b_key)
    ctx_pick, probs, key_scores, words, words_pick, normed1, inv1, h1_mine = attend_picked(
        positions, rel_ids, q_pick, k, v, pos_query, pos_key, x_pick, w_out, b_out, ln1_gain, ln1_bias
    )

    h1_theirs = swap(h1_mine, "ffn", 1)
    x_turned, x_pick_turned, c_pick_turned, rel_turned = turn_blocks(
        me, order, rel_order_cols, tokens, x_pick, ctx_pick, rel_table
    )
    h1_both = jnp.concatenate([h1_mine, after(h1_theirs, x_turned)], axis=0)
    count = h1_mine.shape[0]
    pre = dot_nn(h1_both, w_in) + b_in
    cdf = normal_cdf(pre)
    hidden = low(pre * cdf)
    slope = cdf + pre * (jnp.exp(-0.5 * pre * pre) * (1.0 / math.sqrt(2.0 * math.pi)))
    part = low(dot_nn(hidden, w_down))
    got = swap(part[count:], "ffn", 1)
    q = low(dot_nn(after(tokens, part), w_query) + b_query)
    tok_order = over_tok.matrix(width, width // n_tok)
    h1_left = low(dot_nn(h1_both, lax.optimization_barrier(tok_order)))
    got = after(got, q, h1_left)
    dz2, dffn, early = norm_picked(
        normed1, ln1_gain, ln1_bias, part[:count], got, b_down, ln2_gain, grad_vals, pick
    )
    dffn_both = jnp.concatenate([dffn, swap(dffn, "ffn", 1)], axis=0)
    dpre = low(dot_nt(dffn_both, w_down) * slope)
    dpart = low(dot_nt(dpre, w_in))
    dgot = swap(dpart[count:], "ffn", 1)

    def halves(values, axis):
        size = values.shape[axis] // 2
        cut = lambda at: lax.slice_in_dim(values, at, at + size, axis=axis)
        return cut(0), cut(size)

    add = lambda one, other: low(wide(one) + wide(other))

    def next_halves(kept, got, axis):
        return [add(one, other) for one, other in zip(halves(kept, axis), halves(got, axis))]

    dpre_later = after(dpre, dpart)
    dffn_left = low(dot_nn(after(dffn_both, dpart), tok_order))
    gb_in = dot_nn(jnp.ones((8, 2 * count), bf16), dpre_later)
    lefts, rights = (h1_left, dffn_left), (dpre_later, hidden)
    middle, quarter = width // 2, width // 4
    ffn_sent = [low(dot_tn(one[:, middle:], other)) for one, other in zip(lefts, rights)]
    dgot, ffn_sent = lax.optimization_barrier((dgot, ffn_sent))
    ffn_got = [over_tok.send(value, 0) for value in ffn_sent]
    in_half, bias_half, down_half = after((in_half, bias_half, down_half), dgot, ffn_sent)
    ffn_got = after(ffn_got, in_half, down_half)
    far_in, far_bias = swap(in_half, "ffn", 1), swap(bias_half, "ffn", 1)

    def ffn_piece(at):
        return [
            low(dot_tn(one[:, at : at + quarter], other) + wide(value[at : at + quarter]))
            for one, other, value in zip(lefts, rights, ffn_got)
        ]

    ffn_sent = ffn_piece(quarter)
    ffn_kept = ffn_piece(0)
    ffn_got = [over_tok.send(value, 1) for value in ffn_sent]

    def ffn_next(step, kept, got):
        if step < over_tok.steps:
            pieces = [next_halves(one, other, 0) for one, other in zip(kept, got)]
            return [piece[0] for piece in pieces], [over_tok.send(piece[1], step) for piece in pieces]
        return [add(one, other) for one, other in zip(kept, got)], None

    dq, dk, dv, dpos, dz1, dattn, early = attend_back(
        me, table_of, rel_order, words, words_pick, q_pick, k, v, probs, pos_query, pos_key,
        dz2, dpart[:count], after(dgot, in_half, ffn_sent, ffn_kept), normed1, inv1, ln1_gain, w_out, early,
    )
    far_in, far_bias, ffn_got = after((far_in, far_bias, ffn_got), dk)
    ffn_kept, ffn_got = ffn_next(2, ffn_kept, ffn_got)

    def grads(half, dk, *more):
        return weight_grads(
            half, x_turned, rel_turned, x_pick_turned, c_pick_turned, dpos, dq, dk, dv, dattn,
            w_query, w_key, *more,
        )

    all_send, vectors = grads(1, after(dk, far_in, ffn_kept), early, gb_in)
    near_in, near_bias = swap(far_in, "tok", 1), swap(far_bias, "tok", 1)
    far_down = swap(after(down_half, far_in), "ffn", 1)
    all_got = over_all.send(all_send, 0)
    vec_got = over_all.send(vectors, 0)
    grad_tokens = token_grads(pick, dz1, dq, after(dk, all_send), dv, w_query, w_key, w_value)
    all_kept, all_sent = grads(0, after(dk, grad_tokens), all_got)
    vectors = vectors + vec_got
    ffn_step = 3
    shared = lax.broadcasted_iota(jnp.int32, (vectors.shape[0], 1), 0) < 9

    def attend(first, count, q):
        return attend_full(rel_ids, q, k, v, pos_key, key_scores, first, count)

    ctx = []
    for step in range(1, over_all.steps):
        all_got = over_all.send(all_sent, step)
        vec_got = over_all.send(vectors, step)
        if step == 1:
            ctx.append(attend(0, FIRST_PAIRS, after(q, all_sent)))
            fill = ctx[-1]
        elif step == 2:
            ctx.append(attend(FIRST_PAIRS, pairs - FIRST_PAIRS, after(q, all_sent)))
            fill = ctx[-1]
        elif step == 3:
            near_down = swap(far_down, "tok", 1)
            bias_row = b_in.reshape(1, hidden_cols)
            shards = [
                (w_in, w_down, bias_row), (far_in, far_down, far_bias), (near_in, near_down, near_bias)
            ]
            output = ffn_full(
                after(tokens, all_sent), ctx, w_out, b_out, ln1_gain, ln1_bias, shards,
                b_down, ln2_gain, ln2_bias,
            )
            fill = output
        if step <= 3:
            all_got, vec_got = after((all_got, vec_got), fill)
        if step <= 2 and ffn_step <= over_tok.steps:
            ffn_kept, ffn_got = ffn_next(ffn_step, ffn_kept, after(ffn_got, fill))
            all_got = after(all_got, ffn_kept)
            ffn_step += 1
        if step < over_all.steps - 1:
            all_kept, all_sent = next_halves(all_kept, all_got, 1)
        else:
            all_sums = add(all_kept, all_got)
        vectors = vectors + jnp.where(shared | (over_all.bit(step) != 1), vec_got, 0.0)
    for step in range(ffn_step, over_tok.steps + 1):
        ffn_kept, ffn_got = ffn_next(step, ffn_kept, ffn_got)

    all_sums = all_sums.reshape(all_sums.shape[0] * unit, width)
    s_w = [wide(all_sums[n * own : (n + 1) * own]) for n in range(4)]
    s_rel = wide(all_sums[4 * own :])
    s_vec = lax.dynamic_slice_in_dim(vectors[:9], over_all.me * own, own, 1)
    part = hidden_cols // n_tok
    s_bin = lax.dynamic_slice_in_dim(
        vectors[9 : 9 + hidden_cols // width].reshape(1, hidden_cols), lax.axis_index("tok") * part, part, 1
    )
    return (
        output,
        grad_tokens,
        s_w[0],
        s_w[1],
        s_w[2],
        s_w[3],
        s_vec[0],
        s_vec[1],
        s_vec[2],
        s_vec[3],
        s_rel,
        s_vec[4],
        s_vec[5],
        wide(ffn_kept[0]),
        s_bin,
        jnp.transpose(wide(ffn_kept[1])),
        s_vec[6],
        s_vec[7],
        s_vec[8],
    )


def solution(mesh):
    every = ("tok", "ffn")
    placed = (
        P(every, None), P(every, None, None), P(every, None), P(every, None, None),
        P(), P(), P(), P(), P(), P(), P(), P(), P(), P(), P(),
        P(None, "ffn"), P("ffn"), P("ffn", None), P(), P(), P(),
    )
    given = (
        P(every, None), P(every, None),
        P(every, None), P(every, None), P(every, None), P(every, None),
        P(every), P(every), P(every), P(every),
        P(every, None), P(every), P(every),
        P("tok", "ffn"), P("ffn", "tok"), P("ffn", "tok"),
        P(every), P(every), P(every),
    )
    return jax.shard_map(local, mesh=mesh, in_specs=placed, out_specs=given, check_vma=False)
```

```python
import functools
import math

import numpy as np

import jax
import jax.numpy as jnp
from jax import lax
from jax.experimental import pallas as pl
from jax.experimental.pallas import tpu as pltpu
from jax.sharding import PartitionSpec as P

HEAD = 64
LANES = 128
HALF = 64
ROWS = 32
AT_ONCE = 2
FIRST_PAIRS = 2
VECTORS = 9
norm_eps = 1e-07
bf16 = jnp.bfloat16
f32 = jnp.float32
PARAMS = pltpu.CompilerParams(vmem_limit_bytes=60 * 2**20)


def dot_nn(first_op, second_op):
    return lax.dot_general(
        first_op, second_op, (((1,), (0,)), ((), ())), preferred_element_type=f32
    )


def dot_nt(first_op, second_op):
    return lax.dot_general(
        first_op, second_op, (((1,), (1,)), ((), ())), preferred_element_type=f32
    )


def dot_tn(first_op, second_op):
    return lax.dot_general(
        first_op, second_op, (((0,), (0,)), ((), ())), preferred_element_type=f32
    )


def distance_rows(seq_len, table_rows):
    side = table_rows // 2
    middle = side // 2
    rows = []
    for m in range(2 * seq_len):
        offset = max(m - seq_len, 1 - seq_len)
        size = abs(offset)
        if size > middle:
            ratio = math.log(size / middle) / math.log((2 * side - 1) / middle)
            size = int(math.ceil(ratio * (middle - 1))) + middle
        rows.append(side + (size if offset > 0 else -size))
    return np.array(rows, dtype=np.int32)


def lane_iota(rows=1):
    return lax.broadcasted_iota(jnp.int32, (rows, LANES), 1)


def member_chunk(words, c, last):
    return (last - words == lane_iota(words.shape[0]) + c * LANES).astype(f32).astype(bf16)


def id_bases(rel_ref, base):
    seq = rel_ref.shape[0]
    chunks = seq // LANES
    last = chunks * 2 - 2
    for g in range(seq // HALF):
        for c in range(chunks):
            block = rel_ref[g * HALF : (g + 1) * HALF, c * LANES : (c + 1) * LANES]
            base[g * chunks + c] = jnp.minimum(jnp.min(block) // HALF, last)


def both_alignments(table):
    return jnp.concatenate([table, table[HALF:], table[:HALF]], axis=0)


def longest(rows):
    wide = rows.astype(f32)
    return jnp.sqrt(jnp.max(jnp.sum(wide * wide, axis=1, keepdims=True)))


def pack_heads(first, second, dest, top):
    top = jnp.maximum(top, 1e-30)
    scale = 32000.0 / top
    upper = (first * scale).astype(jnp.int32)
    lower = (second * scale).astype(jnp.int32)
    dest[...] = upper * 65536 + lower
    return top * (1.0 / 32000.0)


def unpack_heads(words, step):
    lower = lax.shift_right_arithmetic(lax.shift_left(words, 16), 16)
    return words.astype(f32) * (step * (1.0 / 65536.0)), lower.astype(f32) * step


def picked_words(source, rel_ref, base, rows, c):
    chunks = rel_ref.shape[1] // LANES
    first = base[(rows.start // HALF) * chunks + c]
    place = rel_ref[rows, c * LANES : (c + 1) * LANES] - first * HALF
    index = place & (LANES - 1)
    at = pl.multiple_of((first % 2) * (chunks * LANES) + (first // 2) * LANES, LANES)
    near = jnp.take_along_axis(source[rows, pl.ds(at, LANES)], index, axis=1)
    at = pl.multiple_of(at + LANES, LANES)
    far = jnp.take_along_axis(source[rows, pl.ds(at, LANES)], index, axis=1)
    return jnp.where(place < LANES, near, far)


def unshift_in_order(sources, words_ref, base, dest):
    seq = words_ref.shape[0]
    chunks = seq // LANES
    lane = lane_iota()
    zero = jnp.zeros((ROWS, LANES), f32)
    for g in range(chunks):
        first = base[g]
        for sub in range(LANES // ROWS):
            start = g * LANES + sub * ROWS
            rows = slice(start, start + ROWS)
            place = lane - 1 - words_ref[rows, :] + first * LANES
            index = place & (LANES - 1)
            near = place >= 0
            mid = place >= -LANES
            for a, source in enumerate(sources):
                turned = [
                    jnp.take_along_axis(
                        source[rows, c * LANES : (c + 1) * LANES], index, axis=1
                    )
                    for c in range(chunks)
                ]
                turned = [zero, zero] + turned + [zero, zero]
                for c in range(chunks + 2):
                    value = jnp.where(near, turned[c + 2], jnp.where(mid, turned[c + 1], turned[c]))
                    at = pl.multiple_of((first + c) * LANES, LANES)
                    dest[a, rows, pl.ds(at, LANES)] = value.astype(bf16)


def group_bases(words, base):
    seq = words.shape[0]
    for g in range(seq // LANES):
        base[g] = (jnp.min(words[g * LANES : (g + 1) * LANES]) + 1) // LANES


def softmax_weights(scores):
    factor = math.log2(math.e) / math.sqrt(3.0 * HEAD)
    top = jnp.max(functools.reduce(jnp.maximum, scores), axis=1, keepdims=True)
    return [jnp.exp2((score - top) * factor) for score in scores]


def head_lanes(a):
    return (lane_iota() < HEAD) if a == 0 else (lane_iota() >= HEAD)


def row_of(ref):
    return ref[...].reshape(1, ref.shape[0])


def norm_stats(values):
    centered = values - jnp.mean(values, axis=1, keepdims=True)
    inv_std = lax.rsqrt(jnp.mean(centered * centered, axis=1, keepdims=True) + norm_eps)
    return centered * inv_std, inv_std


def norm_backward(upstream, normed, inv_std, norm_gain):
    scaled = upstream * norm_gain
    adjusted = (
        scaled
        - jnp.mean(scaled, axis=1, keepdims=True)
        - normed * jnp.mean(scaled * normed, axis=1, keepdims=True)
    )
    return inv_std * adjusted, col_sum(upstream * normed), col_sum(upstream)


def col_sum(values):
    return jnp.sum(values, axis=0, keepdims=True)


def normal_cdf(pre_act):
    return 0.5 * (1.0 + lax.erf(pre_act * (1.0 / math.sqrt(2.0))))


def picked_kernel(
    pos_ref, rel_ref, qc_ref, k_ref, v_ref, pk_ref, pq_ref,
    x_ref, wo_ref, bo_ref, gain_ref, bias_ref,
    ctx_ref, prob_ref, key_ref, word_ref, wordc_ref, normed_ref, inv_ref, low_ref,
    packed, cpick, relc, keyc, attn, base,
):
    seq = k_ref.shape[0]
    picks = qc_ref.shape[0]
    chunks = seq // LANES

    @pl.when(pl.program_id(0) == 0)
    def _():
        row = lax.broadcasted_iota(jnp.int32, (seq, seq), 0)
        col = lax.broadcasted_iota(jnp.int32, (seq, seq), 1)
        side = pk_ref.shape[0] // 2
        step = jnp.sum(jnp.where(col == row - 1, rel_ref[...] - side, 0), axis=1, keepdims=True)
        steps = jnp.broadcast_to(step.astype(f32), (seq, LANES)).astype(bf16)
        word_ref[...] = dot_nn((col <= row).astype(f32).astype(bf16), steps).astype(jnp.int32)
        id_bases(rel_ref, base)
        for n in range(picks):
            place = jnp.maximum(pos_ref[n], 0)
            relc[n : n + 1, :] = rel_ref[pl.ds(place, 1), :]
            wordc_ref[n : n + 1, :] = word_ref[pl.ds(place, 1), :]

    zero = jnp.zeros((), bf16)
    table = both_alignments(pq_ref[...])
    keys = [dot_nt(jnp.where(head_lanes(a), k_ref[...], zero), table) for a in range(2)]
    unit = pack_heads(keys[0], keys[1], packed, longest(k_ref[...]) * longest(pq_ref[...]))
    for a in range(2):
        cpick[a] = dot_nt(jnp.where(head_lanes(a), qc_ref[...], zero), pk_ref[...])
    for g in range(chunks):
        for c in range(chunks):
            parts = []
            for start in range(g * LANES, (g + 1) * LANES, ROWS):
                parts.append(picked_words(packed, rel_ref, base, slice(start, start + ROWS), c))
            block = jnp.concatenate(parts, axis=0).T
            for a, value in enumerate(unpack_heads(block, unit)):
                key_ref[a, c * LANES : (c + 1) * LANES, g * LANES : (g + 1) * LANES] = value

    for n in range(picks):
        place = jnp.maximum(pos_ref[n], 0)
        for a in range(2):
            keyc[a, n : n + 1, :] = key_ref[a, pl.ds(place, 1), :]
    for a in range(2):
        mine = head_lanes(a)
        direct = dot_nt(jnp.where(mine, qc_ref[...], zero), k_ref[...])
        scores = []
        for c in range(chunks):
            ids = relc[:, c * LANES : (c + 1) * LANES]
            index = ids & (LANES - 1)
            value = jnp.take_along_axis(cpick[a, :, :LANES], index, axis=1)
            for n in range(1, pk_ref.shape[0] // LANES):
                other = cpick[a, :, n * LANES : (n + 1) * LANES]
                value = jnp.where(
                    ids >= n * LANES, jnp.take_along_axis(other, index, axis=1), value
                )
            cols = slice(c * LANES, (c + 1) * LANES)
            scores.append(direct[:, cols] + value + keyc[a, :, cols])
        weights = softmax_weights(scores)
        inverse = 1.0 / jnp.sum(sum(weights[1:], weights[0]), axis=1, keepdims=True)
        probs = jnp.concatenate([(weight * inverse).astype(bf16) for weight in weights], axis=1)
        prob_ref[a] = probs
        mixed = dot_nn(probs, v_ref[...]).astype(bf16)
        ctx_ref[...] = mixed if a == 0 else jnp.where(mine, mixed, ctx_ref[...])

    part = dot_nn(ctx_ref[...], wo_ref[...])

    @pl.when(pl.program_id(0) == 0)
    def _():
        attn[...] = x_ref[...].astype(f32) + row_of(bo_ref) + part

    @pl.when(pl.program_id(0) > 0)
    def _():
        attn[...] += part

    @pl.when(pl.program_id(0) == pl.num_programs(0) - 1)
    def _():
        normed, inv_std = norm_stats(attn[...])
        normed_ref[...] = normed
        inv_ref[...] = jnp.broadcast_to(inv_std, (picks, LANES))
        low_ref[...] = (normed * row_of(gain_ref) + row_of(bias_ref)).astype(bf16)


def attend_picked(
    positions, rel_ids, q_pick, k, v, pos_query, pos_key, x_pick, w_out, b_out, gain, bias
):
    seq, width = k.shape
    picks = q_pick.shape[0]
    table = pos_key.shape[0]
    pairs = width // LANES
    whole = lambda rows, cols: pl.BlockSpec((rows, cols), lambda h: (0, 0))
    line = pl.BlockSpec((width,), lambda h: (0,))
    col = lambda rows: pl.BlockSpec((rows, LANES), lambda h: (0, h))
    heads = lambda rows: pl.BlockSpec((2, rows, seq), lambda h: (h, 0, 0))
    return pl.pallas_call(
        picked_kernel,
        grid=(pairs,),
        in_specs=[
            pl.BlockSpec(memory_space=pltpu.SMEM), whole(seq, seq),
            col(picks), col(seq), col(seq), col(table), col(table),
            whole(picks, width), pl.BlockSpec((LANES, width), lambda h: (h, 0)), line, line, line,
        ],
        out_specs=[
            col(picks), heads(picks), heads(seq), whole(seq, LANES), whole(picks, LANES),
            whole(picks, width), whole(picks, LANES), whole(picks, width),
        ],
        out_shape=[
            jax.ShapeDtypeStruct((picks, width), bf16),
            jax.ShapeDtypeStruct((2 * pairs, picks, seq), bf16),
            jax.ShapeDtypeStruct((2 * pairs, seq, seq), f32),
            jax.ShapeDtypeStruct((seq, LANES), jnp.int32),
            jax.ShapeDtypeStruct((picks, LANES), jnp.int32),
            jax.ShapeDtypeStruct((picks, width), f32),
            jax.ShapeDtypeStruct((picks, LANES), f32),
            jax.ShapeDtypeStruct((picks, width), bf16),
        ],
        scratch_shapes=[
            pltpu.VMEM((seq, 2 * table), jnp.int32),
            pltpu.VMEM((2, picks, table), f32),
            pltpu.VMEM((picks, seq), jnp.int32),
            pltpu.VMEM((2, picks, seq), f32),
            pltpu.VMEM((picks, width), f32),
            pltpu.SMEM((seq // HALF * (seq // LANES),), jnp.int32),
        ],
        compiler_params=PARAMS,
        name="attend_picked",
    )(
        positions, rel_ids, q_pick, k, v, pos_key, pos_query, x_pick, w_out, b_out, gain, bias
    )


def full_kernel(rel_ref, q_ref, k_ref, v_ref, pk_ref, key_ref, ctx_ref, *scratch):
    seq = rel_ref.shape[0]
    chunks = seq // LANES
    base, scratch = scratch[-1], scratch[:-1]
    count = len(scratch) // 3

    @pl.when(pl.program_id(0) == 0)
    def _():
        id_bases(rel_ref, base)

    zero = jnp.zeros((), bf16)
    units = []
    for n in range(count):
        packed, direct, low = scratch[3 * n : 3 * n + 3]
        lanes = slice(n * LANES, (n + 1) * LANES)
        q, pos = q_ref[:, lanes], pk_ref[:, lanes]
        table = both_alignments(pos)
        far = []
        for a in range(2):
            q_a = jnp.where(head_lanes(a), q, zero)
            far.append(dot_nt(q_a, table))
            direct[a] = dot_nt(q_a, k_ref[:, lanes])
        units.append(pack_heads(far[0], far[1], packed, longest(q) * longest(pos)))
    for n in range(count):
        packed, direct, low = scratch[3 * n : 3 * n + 3]
        lanes = slice(n * LANES, (n + 1) * LANES)
        for start in range(0, seq, HALF):
            rows = slice(start, start + HALF)
            scores = [[], []]
            for c in range(chunks):
                cols = slice(c * LANES, (c + 1) * LANES)
                values = unpack_heads(picked_words(packed, rel_ref, base, rows, c), units[n])
                for a in range(2):
                    scores[a].append(
                        values[a] + direct[a, rows, cols] + key_ref[2 * n + a, rows, cols]
                    )
            for a in range(2):
                for c, weight in enumerate(softmax_weights(scores[a])):
                    low[a, rows, c * LANES : (c + 1) * LANES] = weight.astype(bf16)
        v = v_ref[:, lanes]
        mixed = [
            dot_nn(low[a], jnp.where(head_lanes(a), v, jnp.ones((), bf16))) for a in range(2)
        ]
        upper = head_lanes(0)
        totals = pltpu.roll(jnp.where(upper, mixed[1], mixed[0]), HEAD, 1)
        ctx_ref[:, lanes] = (jnp.where(upper, mixed[0], mixed[1]) * (1.0 / totals)).astype(bf16)


def attend_full(rel_ids, q, k, v, pos_key, key_scores, first, pairs):
    seq = k.shape[0]
    table = pos_key.shape[0]
    per = AT_ONCE
    wide = per * LANES
    col = lambda rows: pl.BlockSpec((rows, wide), lambda h: (0, h + first // per))
    return pl.pallas_call(
        full_kernel,
        grid=(pairs // per,),
        in_specs=[
            pl.BlockSpec((seq, seq), lambda h: (0, 0)),
            col(seq), col(seq), col(seq), col(table),
            pl.BlockSpec((2 * per, seq, seq), lambda h: (h + first // per, 0, 0)),
        ],
        out_specs=pl.BlockSpec((seq, wide), lambda h: (0, h)),
        out_shape=jax.ShapeDtypeStruct((seq, pairs * LANES), bf16),
        scratch_shapes=[
            pltpu.VMEM((seq, 2 * table), jnp.int32),
            pltpu.VMEM((2, seq, seq), f32),
            pltpu.VMEM((2, seq, seq), bf16),
        ]
        * per
        + [pltpu.SMEM((seq // HALF * (seq // LANES),), jnp.int32)],
        compiler_params=PARAMS,
        name="attend_full",
    )(rel_ids, q, k, v, pos_key, key_scores)


def back_kernel(
    row_ref, word_ref, wordc_ref, qc_ref, k_ref, v_ref, prob_ref, pk_ref, pq_ref,
    dz2_ref, mine_ref, got_ref, normed_ref, inv_ref, gain_ref, wo_ref, early_ref,
    dq_ref, dk_ref, dv_ref, dpos_ref, dz1_ref, dattn_ref, sum_ref,
    side, sidec, moved, movedc, expand, shrink, base,
):
    seq = k_ref.shape[0]
    picks = qc_ref.shape[0]
    table = pk_ref.shape[0]
    chunks = seq // LANES

    @pl.when(pl.program_id(0) == 0)
    def _():
        words = word_ref[...]
        for c in range(chunks):
            side[:, c * LANES : (c + 1) * LANES] = member_chunk(words, c, seq - 1)
            sidec[:, c * LANES : (c + 1) * LANES] = member_chunk(wordc_ref[...], c, seq - 1)
        group_bases(words, base)
        moved[...] = jnp.zeros_like(moved)
        edge = expand.shape[1]
        for n, start in ((0, 0), (1, 2 * seq - edge)):
            ids = row_ref[start : start + edge, :] - n * (table - LANES)
            chosen = (ids == lane_iota(edge)).astype(f32).astype(bf16)
            expand[n] = chosen
            shrink[n] = chosen.T
        dh1 = dz2_ref[...] + mine_ref[...].astype(f32) + got_ref[...].astype(f32)
        dz1, g_gain, g_bias = norm_backward(dh1, normed_ref[...], inv_ref[:, :1], row_of(gain_ref))
        dz1_ref[...] = dz1
        dattn = dz1.astype(bf16)
        dattn_ref[...] = dattn
        sum_ref[...] = jnp.concatenate(
            [col_sum(dattn.astype(f32)), g_gain, g_bias, early_ref[:5]], axis=0
        )

    lane = lane_iota()
    scale = 1.0 / math.sqrt(3.0 * HEAD)
    zero = jnp.zeros((), bf16)
    heads = range(2)
    upper = head_lanes(0)
    join = lambda pair: jnp.where(upper, pair[0], pair[1])
    side[:, seq:] = k_ref[...]
    sidec[:, seq:] = qc_ref[...]
    dctx = dot_nt(dattn_ref[...], wo_ref[...]).astype(bf16)
    dprobs = [dot_nt(jnp.where(head_lanes(a), dctx, zero), v_ref[...]) for a in heads]

    def widened(ref):
        ends = [
            dot_nn(expand[n], ref[at : at + LANES, :]).astype(bf16)
            for n, at in ((0, 0), (1, table - LANES))
        ]
        return jnp.concatenate([ends[0], ref[LANES : table - LANES, :], ends[1]], axis=0)

    far_key, far_query = widened(pk_ref), widened(pq_ref)
    gs = []
    for a in heads:
        probs = prob_ref[a].astype(f32)
        prod = probs * dprobs[a]
        gs.append(((prod - probs * jnp.sum(prod, axis=1, keepdims=True)) * scale).astype(bf16))
    outs = [dot_tn(gs[a], sidec[...]) for a in heads]
    outcs = [dot_nn(gs[a], side[...]) for a in heads]
    dv_ref[...] = join([dot_tn(prob_ref[a], dctx) for a in heads]).astype(bf16)
    place = lane - 1 - wordc_ref[...]
    index = place & (LANES - 1)
    blank = jnp.zeros((picks, LANES), f32)
    for a in heads:
        turned = [
            jnp.take_along_axis(outcs[a][:, c * LANES : (c + 1) * LANES], index, axis=1)
            for c in range(chunks)
        ]
        for c in range(2 * chunks):
            value = turned[c] if c < chunks else blank
            for n in range(1, chunks + 1):
                other = turned[c - n] if 0 <= c - n < chunks else blank
                value = jnp.where(place < -LANES * (n - 1), other, value)
            movedc[a, :, c * LANES : (c + 1) * LANES] = value.astype(bf16)
    unshift_in_order(outs, word_ref, base, moved)
    dq = [outcs[a][:, seq:] + dot_nn(movedc[a], far_key) for a in heads]
    dq_ref[...] = join(dq).astype(bf16)
    dk = [outs[a][:, seq:] + dot_nn(moved[a, :, : 2 * seq], far_query) for a in heads]
    dk_ref[...] = join(dk).astype(bf16)
    far = [
        join([dot_tn(movedc[a], qc_ref[...]) for a in heads]),
        join([dot_tn(moved[a, :, : 2 * seq], k_ref[...]) for a in heads]),
    ]
    edge = expand.shape[1]
    for n, value in enumerate(far):
        value = value.astype(bf16)
        dpos_ref[n, :LANES, :] = dot_nn(shrink[0], value[:edge]).astype(bf16)
        dpos_ref[n, LANES : table - LANES, :] = value[edge : 2 * seq - edge]
        dpos_ref[n, table - LANES :, :] = dot_nn(shrink[1], value[2 * seq - edge :]).astype(bf16)


def attend_back(
    table_of, words, words_pick, q_pick, k, v, probs, pos_query, pos_key,
    dz2, mine, got, normed, inv_std, gain, w_out, early,
):
    seq, width = k.shape
    picks = q_pick.shape[0]
    table = pos_key.shape[0]
    pairs = width // LANES
    edge = seq - table // 4
    whole = lambda value: pl.BlockSpec(value.shape, lambda h: (0,) * value.ndim)
    col = lambda rows: pl.BlockSpec((rows, LANES), lambda h: (0, h))
    shape = lambda rows: jax.ShapeDtypeStruct((rows, width), bf16)
    return pl.pallas_call(
        back_kernel,
        grid=(pairs,),
        in_specs=[
            whole(table_of), whole(words), whole(words_pick),
            col(picks), col(seq), col(seq),
            pl.BlockSpec((2, picks, seq), lambda h: (h, 0, 0)),
            col(table), col(table),
            whole(dz2), whole(mine), whole(got), whole(normed), whole(inv_std), whole(gain),
            pl.BlockSpec((LANES, width), lambda h: (h, 0)), whole(early),
        ],
        out_specs=[
            col(picks), col(seq), col(seq),
            pl.BlockSpec((2, table, LANES), lambda h: (0, 0, h)),
            whole(dz2), whole(dz2), whole(early),
        ],
        out_shape=[
            shape(picks), shape(seq), shape(seq),
            jax.ShapeDtypeStruct((2, table, width), bf16),
            jax.ShapeDtypeStruct((picks, width), f32),
            shape(picks),
            jax.ShapeDtypeStruct(early.shape, f32),
        ],
        scratch_shapes=[
            pltpu.VMEM((seq, seq + LANES), bf16),
            pltpu.VMEM((picks, seq + LANES), bf16),
            pltpu.VMEM((2, seq, 2 * seq + 2 * LANES), bf16),
            pltpu.VMEM((2, picks, 2 * seq), bf16),
            pltpu.VMEM((2, edge, LANES), bf16),
            pltpu.VMEM((2, LANES, edge), bf16),
            pltpu.SMEM((seq // LANES,), jnp.int32),
        ],
        compiler_params=PARAMS,
        name="attend_back",
    )(
        table_of, words, words_pick, q_pick, k, v, probs, pos_key, pos_query,
        dz2, mine, got, normed, inv_std, gain, w_out, early,
    )


def turn_kernel(
    me_ref, order_ref, x_ref, xpick_ref, cpick_ref, rel_ref, x_out, xpick_out, cpick_out, rel_out
):
    picked = order_rows(order_ref, me_ref, x_ref.shape[1])
    for ref, out in ((x_ref, x_out), (xpick_ref, xpick_out), (cpick_ref, cpick_out), (rel_ref, rel_out)):
        out[...] = dot_nt(picked, ref[...]).astype(bf16)


def block_rows(ref, me_ref):
    return me_ref[0] ^ jnp.where(me_ref[1] == 0, ref[:, 0:1], ref[:, 1:2])


def order_rows(ref, me_ref, length):
    source = block_rows(ref, me_ref) * (length // me_ref[2]) + ref[:, 2:3]
    spot = lax.broadcasted_iota(jnp.int32, (ref.shape[0], length), 1)
    return (spot == source).astype(f32).astype(bf16)


def turn_blocks(me, order, x, x_pick, ctx_pick, rel_table):
    width = x.shape[1]
    group = 2 * LANES
    whole = lambda value: pl.BlockSpec(value.shape, lambda n: (0, 0))
    row = lambda count: pl.BlockSpec((group, count), lambda n: (n, 0))
    given = [x, x_pick, ctx_pick, rel_table]
    return pl.pallas_call(
        turn_kernel,
        grid=(width // group,),
        in_specs=[pl.BlockSpec(memory_space=pltpu.SMEM), row(LANES)]
        + [whole(value) for value in given],
        out_specs=[row(value.shape[0]) for value in given],
        out_shape=[jax.ShapeDtypeStruct(value.shape[::-1], bf16) for value in given],
        compiler_params=PARAMS,
        name="turn_blocks",
    )(me, order, *given)


def norm_picked_kernel(
    normed_ref, gain1_ref, bias1_ref, mine_ref, got_ref, bdown_ref, gain2_ref, grad_ref, pick_ref,
    dz2_ref, low_ref, sum_ref,
):
    h1 = normed_ref[...] * row_of(gain1_ref) + row_of(bias1_ref)
    branch = mine_ref[...].astype(f32) + got_ref[...].astype(f32) + row_of(bdown_ref)
    normed, inv_std = norm_stats(h1 + branch)
    used = jnp.sum(pick_ref[...].astype(f32), axis=1, keepdims=True)
    cot = jnp.where(used > 0.0, grad_ref[...].astype(f32), 0.0)
    dz2, g_gain, g_bias = norm_backward(cot, normed, inv_std, row_of(gain2_ref))
    dz2_ref[...] = dz2
    low = dz2.astype(bf16)
    low_ref[...] = low
    sum_ref[...] = jnp.concatenate(
        [col_sum(low.astype(f32)), g_gain, g_bias, jnp.zeros((5, h1.shape[1]), f32)], axis=0
    )


def norm_picked(normed, gain1, bias1, mine, got, b_down, gain2, grads, pick):
    picks, width = normed.shape
    return pl.pallas_call(
        norm_picked_kernel,
        out_shape=[
            jax.ShapeDtypeStruct((picks, width), f32),
            jax.ShapeDtypeStruct((picks, width), bf16),
            jax.ShapeDtypeStruct((8, width), f32),
        ],
        compiler_params=PARAMS,
        name="norm_picked",
    )(normed, gain1, bias1, mine, got, b_down, gain2, grads, pick)


def ffn_full_kernel(
    x_ref, ctx_ref, ctx2_ref, wo_ref, bo_ref, gain1_ref, bias1_ref, bdown_ref, gain2_ref, bias2_ref,
    bin_ref, bin2_ref, bin3_ref, win_ref, down_ref, win2_ref, down2_ref, win3_ref, down3_ref,
    out_ref, h1, low, total, win_here, down_here, win_sem, down_sem,
):
    rows, width = x_ref.shape
    tile = win_here.shape[2]
    parts = [(win_ref, down_ref, bin_ref, n * tile) for n in range(win_ref.shape[1] // tile)]
    parts += [(win2_ref, down2_ref, bin2_ref, 0), (win3_ref, down3_ref, bin3_ref, 0)]

    def copies(n):
        w_ref, d_ref, _, at = parts[n]
        return (
            pltpu.make_async_copy(w_ref.at[:, at : at + tile], win_here.at[n], win_sem.at[n]),
            pltpu.make_async_copy(d_ref.at[at : at + tile, :], down_here.at[n], down_sem.at[n]),
        )

    for n in range(len(parts)):
        for copy in copies(n):
            copy.start()
    attn = dot_nn(ctx_ref[...], wo_ref[: ctx_ref.shape[1]]) + dot_nn(
        ctx2_ref[...], wo_ref[ctx_ref.shape[1] :]
    )
    normed, _ = norm_stats(x_ref[...].astype(f32) + (attn + row_of(bo_ref)))
    value = normed * row_of(gain1_ref) + row_of(bias1_ref)
    h1[...] = value
    low[...] = value.astype(bf16)
    step = rows // 2
    for n in range(len(parts)):
        for copy in copies(n):
            copy.wait()
        bias = parts[n][2][:, parts[n][3] : parts[n][3] + tile]
        for at in range(0, rows, step):
            pre = dot_nn(low[at : at + step], win_here[n]) + bias
            part = dot_nn((pre * normal_cdf(pre)).astype(bf16), down_here[n])
            total[at : at + step] = part if n == 0 else total[at : at + step] + part
    normed, _ = norm_stats(h1[...] + (total[...] + row_of(bdown_ref)))
    out_ref[...] = (normed * row_of(gain2_ref) + row_of(bias2_ref)).astype(bf16)


def ffn_full(x, ctx, w_out, b_out, gain1, bias1, shards, b_down, gain2, bias2):
    rows, width = x.shape
    tile = shards[1][0].shape[1]
    count = shards[0][0].shape[1] // tile + 2
    held = [x, ctx[0], ctx[1], w_out, b_out, gain1, bias1, b_down, gain2, bias2]
    held += [shard[2] for shard in shards]
    moved = [value for shard in shards for value in shard[:2]]
    return pl.pallas_call(
        ffn_full_kernel,
        in_specs=[pl.BlockSpec(memory_space=pltpu.VMEM)] * len(held)
        + [pl.BlockSpec(memory_space=pl.ANY)] * len(moved),
        out_specs=pl.BlockSpec(memory_space=pltpu.VMEM),
        out_shape=jax.ShapeDtypeStruct((rows, width), bf16),
        scratch_shapes=[
            pltpu.VMEM((rows, width), f32), pltpu.VMEM((rows, width), bf16), pltpu.VMEM((rows, width), f32),
            pltpu.VMEM((count, width, tile), bf16), pltpu.VMEM((count, tile, width), bf16),
            pltpu.SemaphoreType.DMA((count,)), pltpu.SemaphoreType.DMA((count,)),
        ],
        compiler_params=PARAMS,
        name="ffn_full",
    )(*held, *moved)


def token_grads_kernel(pick_ref, dz1_ref, dq_ref, dk_ref, dv_ref, wq_ref, wk_ref, wv_ref, out_ref):
    sparse = dz1_ref[...] + dot_nt(dq_ref[...], wq_ref[...])
    upper = sparse.astype(bf16)
    lower = (sparse - upper.astype(f32)).astype(bf16)
    out_ref[...] = (
        dot_nt(dk_ref[...], wk_ref[...])
        + dot_nt(dv_ref[...], wv_ref[...])
        + dot_tn(pick_ref[...], upper)
        + dot_tn(pick_ref[...], lower)
    )


def token_grads(pick, dz1, dq, dk, dv, w_query, w_key, w_value):
    seq, width = dk.shape
    group = 2 * LANES
    whole = lambda value: pl.BlockSpec(value.shape, lambda n: (0, 0))
    col = lambda rows: pl.BlockSpec((rows, group), lambda n: (0, n))
    row = pl.BlockSpec((group, width), lambda n: (n, 0))
    return pl.pallas_call(
        token_grads_kernel,
        grid=(width // group,),
        in_specs=[whole(pick), col(dz1.shape[0]), whole(dq), whole(dk), whole(dv), row, row, row],
        out_specs=col(seq),
        out_shape=jax.ShapeDtypeStruct((seq, width), f32),
        compiler_params=PARAMS,
        name="token_grads",
    )(pick, dz1, dq, dk, dv, w_query, w_key, w_value)


def grads_kernel(
    half, planes, unit, me_ref, order_ref, relorder_ref, taker_ref,
    x_ref, rel_ref, xpick_ref, cpick_ref, dpos_ref,
    dq_ref, dk_ref, dv_ref, dattn_ref, dposk_ref, dposq_ref, wq_ref, wk_ref,
    early_ref, bin_ref, bin2_ref, *refs
):
    width = x_ref.shape[0]
    group = 2 * LANES
    dpos = refs[-1]

    def left(ref):
        starts = range(half * LANES, width, group)
        return jnp.concatenate([ref[at : at + LANES, :] for at in starts], axis=0)

    def put(at, value):
        for n in range(value.shape[0] // LANES):
            block = value[n * LANES : (n + 1) * LANES]
            if half:
                refs[0][at + n] = block.astype(bf16)
            else:
                block = (block + refs[0][at + n].astype(f32)).astype(bf16)
                refs[1][at + n] = block[: LANES // 2]
                refs[2][at + n] = block[LANES // 2 :]

    @pl.when(pl.program_id(0) == 0)
    def _():
        rows = order_rows(relorder_ref, me_ref, dpos_ref.shape[1])
        starts = range(half * LANES, rows.shape[0], group)
        rows = jnp.concatenate([rows[at : at + LANES] for at in starts], axis=0)
        for n in range(2):
            dpos[n] = dot_nn(rows, dpos_ref[n]).astype(bf16)

    count = width // group
    rel_left = left(rel_ref)
    x_left = left(x_ref)
    put(0, dot_nn(left(xpick_ref), dq_ref[...]) + dot_nn(rel_left, dposq_ref[0]))
    put(count, dot_nn(x_left, dk_ref[...]) + dot_nn(rel_left, dposk_ref[0]))
    put(2 * count, dot_nn(x_left, dv_ref[...]))
    put(3 * count, dot_nn(left(cpick_ref), dattn_ref[...]))
    put(4 * count, dot_nt(dpos[0], wk_ref[...]) + dot_nt(dpos[1], wq_ref[...]))

    total = lambda value: col_sum(value.astype(f32))
    values = jnp.concatenate(
        [
            total(dq_ref[...]) + total(dposq_ref[0]),
            total(dk_ref[...]) + total(dposk_ref[0]),
            total(dv_ref[...]),
            early_ref[:6],
            bin_ref[:1],
            bin2_ref[:1],
            jnp.zeros((5, group), f32),
        ],
        axis=0,
    )
    block = block_rows(order_ref[half * LANES : (half + 1) * LANES, :], me_ref)
    tok_place = jnp.where(block % me_ref[3] == me_ref[0] % me_ref[3], block // me_ref[3], -1)
    first = 4 * count + dpos.shape[1] // LANES
    row = lax.broadcasted_iota(jnp.int32, (LANES, 1), 0) % unit
    for n in range(first, planes):
        rows = slice((n - first) * unit, (n - first + 1) * unit)
        spread = lambda value: jnp.concatenate([value[rows]] * (LANES // unit), axis=0)
        taker = jnp.where(row + rows.start < VECTORS, block, tok_place)
        put(n, jnp.where(spread(taker_ref[...]) == taker, spread(values), 0.0))


def weight_grads(
    half, unit, me, order, rel_order, takers, x, rel, x_pick, c_pick, dpos, dq, dk, dv, dattn,
    w_query, w_key, early, bins, *got
):
    width, seq = x.shape
    group = 2 * LANES
    planes = 4 * (width // group) + dpos.shape[1] // group + 16 // unit
    whole = lambda value: pl.BlockSpec(value.shape, lambda n: (0,) * value.ndim)
    col = lambda value: pl.BlockSpec((value.shape[0], group), lambda n: (0, n))
    row = lambda value: pl.BlockSpec((group, value.shape[1]), lambda n: (n, 0))
    plane = lambda t: pl.BlockSpec((1, dpos.shape[1], group), lambda n: (t, 0, n))
    block = lambda rows: pl.BlockSpec((planes, rows, group), lambda n: (0, 0, n))
    shape = lambda rows: jax.ShapeDtypeStruct((planes, rows, width), bf16)
    rows = [LANES] if half else [LANES // 2] * 2
    return pl.pallas_call(
        functools.partial(grads_kernel, half, planes, unit),
        grid=(width // group,),
        in_specs=[
            pl.BlockSpec(memory_space=pltpu.SMEM), whole(order), whole(rel_order), col(takers),
            whole(x), whole(rel), whole(x_pick), whole(c_pick), whole(dpos),
            col(dq), col(dk), col(dv), col(dattn), plane(0), plane(1), row(w_query), row(w_key),
            col(early), col(bins), pl.BlockSpec((8, group), lambda n: (0, n + width // group)),
        ]
        + [block(LANES) for _ in got],
        out_specs=[block(count) for count in rows],
        out_shape=[shape(count) for count in rows],
        scratch_shapes=[pltpu.VMEM((2, dpos.shape[1] // 2, width), bf16)],
        compiler_params=PARAMS,
        name="weight_grads",
    )(
        me, order, rel_order, takers, x, rel, x_pick, c_pick, dpos, dq, dk, dv, dattn, dpos, dpos,
        w_query, w_key, early, bins, bins, *got
    )


def swap(values, axis, bit):
    size = lax.axis_size(axis)
    return lax.ppermute(values, axis, [(n, n ^ bit) for n in range(size)])


def after(values, *others):
    return lax.optimization_barrier((values, others))[0]


class Halving:
    def __init__(self, axes, core, near, size):
        rest = [1 << n for n in range(size.bit_length() - 1) if (1 << n) != core]
        near = [bit for bit in near if bit in rest]
        rest = [bit for bit in rest if bit not in near]
        turned = near[-1:] + near[:-1]
        self.axes, self.core, self.size = axes, core, size
        self.orders = [[core] + near + rest, [core] + turned + rest]
        self.steps = len(self.orders[0])
        self.me = lax.axis_index(axes)
        self.upper = (self.me // core) % 2

    def core_of(self, place):
        return (place // self.core) % 2

    def send(self, values, step):
        pairs = [(n, n ^ self.orders[self.core_of(n)][step]) for n in range(self.size)]
        return lax.ppermute(values, self.axes, pairs)

    def relative(self, upper):
        masks = []
        for place in range(self.size):
            bits = [(place >> (self.steps - 1 - step)) & 1 for step in range(self.steps)]
            order = self.orders[upper ^ bits[0]]
            mask = 0
            for step, bit in enumerate(bits):
                mask ^= bit * order[step]
            masks.append(mask)
        return np.array(masks, np.int32)

    def order(self, length, unit):
        spots = np.arange(length)
        group = self.size * unit
        place = spots % group // unit
        rows = [self.relative(upper)[place] for upper in range(2)]
        rows.append(spots // group * unit + spots % unit)
        return np.stack(rows).astype(np.int32)

    def matrix(self, length, unit):
        first, second, inner = self.order(length, unit)
        source = (self.me ^ jnp.where(self.upper == 0, first, second)) * (length // self.size) + inner
        spot = lax.broadcasted_iota(jnp.int32, (length, length), 0)
        return (spot == source[None, :]).astype(bf16)


def local(
    tokens, rel_ids, mask_pos, grad_vals, w_query, w_key, w_value, w_out, b_query, b_key,
    b_value, b_out, rel_table, ln1_gain, ln1_bias, w_in, b_in, w_down, b_down, ln2_gain, ln2_bias,
):
    assert rel_ids.shape[0] == 1
    seq, width = tokens.shape
    table_rows = rel_table.shape[0]
    hidden_cols = w_in.shape[1]
    pairs = width // LANES
    n_tok = lax.axis_size("tok")
    n_ffn = lax.axis_size("ffn")
    n_all = n_tok * n_ffn
    low = lambda value: value.astype(bf16)
    wide = lambda value: value.astype(f32)
    rel_ids, positions, grad_vals = rel_ids[0], mask_pos[0], grad_vals[0]

    over_all = Halving(("tok", "ffn"), n_ffn, [2 * n_ffn, 1, 4 * n_ffn], n_all)
    own, own_rel = width // n_all, table_rows // n_all
    unit = math.gcd(own, own_rel)
    group = n_all * unit
    over_tok = Halving("tok", 1, [2, 4], n_tok)
    pad = lambda value, count: np.pad(value, ((0, count - value.shape[0]), (0, 0)))
    order = jnp.asarray(pad(over_all.order(width, unit), LANES).T)
    rel_order = jnp.asarray(pad(over_all.order(table_rows, unit), LANES).T)
    spots = np.arange(width)
    takers = [spots // own] * VECTORS
    takers += [(spots + n * width) // (hidden_cols // n_tok) for n in range(hidden_cols // width)]
    takers = np.stack(takers).astype(np.int32)
    takers = jnp.asarray(np.pad(takers, ((0, 16 - takers.shape[0]), (0, 0)), constant_values=-2))
    me = jnp.stack([over_all.me, over_all.upper, jnp.int32(n_all), jnp.int32(n_ffn)])
    table_of = jnp.asarray(np.repeat(distance_rows(seq, table_rows)[:, None], LANES, 1))

    core = lax.axis_index("tok") % 2
    half_cols = hidden_cols // 2
    bias_row = b_in.reshape(1, hidden_cols)
    in_half = lax.dynamic_slice_in_dim(w_in, core * half_cols, half_cols, 1)
    down_half = lax.dynamic_slice_in_dim(w_down, core * half_cols, half_cols, 0)

    pick = low(positions[:, None] == lax.broadcasted_iota(jnp.int32, (positions.shape[0], seq), 1))
    x_pick = low(dot_nn(pick, tokens))
    q_pick = low(dot_nn(x_pick, w_query) + b_query)
    k = low(dot_nn(tokens, w_key) + b_key)
    v = low(dot_nn(tokens, w_value) + b_value)
    pos_query = low(dot_nn(rel_table, w_query) + b_query)
    pos_key = low(dot_nn(rel_table, w_key) + b_key)
    ctx_pick, probs, key_scores, words, words_pick, normed1, inv1, h1_mine = attend_picked(
        positions, rel_ids, q_pick, k, v, pos_query, pos_key, x_pick, w_out, b_out, ln1_gain, ln1_bias
    )

    h1_theirs = swap(h1_mine, "ffn", 1)
    bias_theirs = swap(bias_row, "ffn", 1)
    x_turned, x_pick_turned, c_pick_turned, rel_turned = turn_blocks(
        me, order, tokens, x_pick, ctx_pick, rel_table
    )
    h1_both = jnp.concatenate([h1_mine, after(h1_theirs, x_turned)], axis=0)
    count = h1_mine.shape[0]
    pre = dot_nn(h1_both, w_in) + b_in
    cdf = normal_cdf(pre)
    hidden = low(pre * cdf)
    slope = cdf + pre * (jnp.exp(-0.5 * pre * pre) * (1.0 / math.sqrt(2.0 * math.pi)))
    part = low(dot_nn(hidden, w_down))
    got = swap(part[count:], "ffn", 1)
    q = low(dot_nn(after(tokens, part), w_query) + b_query)
    tok_order = over_tok.matrix(width, width // n_tok)
    h1_left = low(dot_nn(h1_both, lax.optimization_barrier(tok_order)))
    in_half = after(in_half, part)
    got = after(got, q, h1_left, in_half)
    dz2, dffn, early = norm_picked(
        normed1, ln1_gain, ln1_bias, part[:count], got, b_down, ln2_gain, grad_vals, pick
    )
    down_half = after(down_half, dffn)
    dffn_both = jnp.concatenate([dffn, after(swap(dffn, "ffn", 1), down_half)], axis=0)
    dpre = low(dot_nt(dffn_both, w_down) * slope)
    dpart = low(dot_nt(dpre, w_in))
    dgot = swap(dpart[count:], "ffn", 1)

    def halves(values, axis):
        size = values.shape[axis] // 2
        cut = lambda at: lax.slice_in_dim(values, at, at + size, axis=axis)
        return cut(0), cut(size)

    add = lambda one, other: low(wide(one) + wide(other))

    def next_halves(kept, got, axis):
        return [add(one, other) for one, other in zip(halves(kept, axis), halves(got, axis))]

    dpre_later = after(dpre, dpart)
    dffn_left = low(dot_nn(after(dffn_both, dpart), tok_order))
    gb_in = dot_nn(jnp.ones((8, 2 * count), bf16), dpre_later)
    lefts, rights = (h1_left, dffn_left), (dpre_later, hidden)
    middle, quarter = width // 2, width // 4
    ffn_sent = [low(dot_tn(one[:, middle:], other)) for one, other in zip(lefts, rights)]
    dgot, ffn_sent = lax.optimization_barrier((dgot, ffn_sent))
    ffn_got = [over_tok.send(value, 0) for value in ffn_sent]
    far_in = swap(after(in_half, dgot, ffn_sent), "ffn", 1)

    def ffn_piece(at):
        return [
            low(dot_tn(one[:, at : at + quarter], other) + wide(value[at : at + quarter]))
            for one, other, value in zip(lefts, rights, ffn_got)
        ]

    ffn_sent = ffn_piece(quarter)
    ffn_kept = ffn_piece(0)
    ffn_got = [over_tok.send(value, 1) for value in ffn_sent]

    def ffn_next(step, kept, got):
        if step < over_tok.steps:
            pieces = [next_halves(one, other, 0) for one, other in zip(kept, got)]
            return [piece[0] for piece in pieces], [over_tok.send(piece[1], step) for piece in pieces]
        return [add(one, other) for one, other in zip(kept, got)], None

    dq, dk, dv, dpos, dz1, dattn, early = attend_back(
        table_of, words, words_pick, q_pick, k, v, probs, pos_query, pos_key,
        dz2, dpart[:count], after(dgot, in_half, ffn_sent, ffn_kept), normed1, inv1, ln1_gain, w_out, early,
    )
    far_in, ffn_got = after((far_in, ffn_got), dk)
    ffn_kept, ffn_got = ffn_next(2, ffn_kept, ffn_got)

    def grads(half, dk, *more):
        return weight_grads(
            half, unit, me, order, rel_order, takers,
            x_turned, rel_turned, x_pick_turned, c_pick_turned, dpos, dq, dk, dv, dattn,
            w_query, w_key, early, gb_in, *more,
        )

    (all_send,) = grads(1, after(dk, far_in, ffn_kept))
    near_in = swap(far_in, "tok", 1)
    far_down = swap(after(down_half, far_in), "ffn", 1)
    all_got = over_all.send(all_send, 0)
    grad_tokens = token_grads(pick, dz1, dq, after(dk, all_send), dv, w_query, w_key, w_value)
    all_kept, all_sent = grads(0, after(dk, grad_tokens), all_got)
    ffn_step = 3

    def attend(first, count, q):
        return attend_full(rel_ids, q, k, v, pos_key, key_scores, first, count)

    ctx = []
    for step in range(1, over_all.steps):
        all_got = over_all.send(all_sent, step)
        if step == 1:
            ctx.append(attend(0, FIRST_PAIRS, after(q, all_sent)))
            fill = ctx[-1]
        elif step == 2:
            ctx.append(attend(FIRST_PAIRS, pairs - FIRST_PAIRS, after(q, all_sent)))
            fill = ctx[-1]
        elif step == 3:
            near_down = swap(far_down, "tok", 1)
            biases = [
                lax.dynamic_slice_in_dim(bias_theirs, at * half_cols, half_cols, 1)
                for at in (core, 1 - core)
            ]
            shards = [
                (w_in, w_down, bias_row), (far_in, far_down, biases[0]), (near_in, near_down, biases[1])
            ]
            output = ffn_full(
                after(tokens, all_sent), ctx, w_out, b_out, ln1_gain, ln1_bias, shards,
                b_down, ln2_gain, ln2_bias,
            )
            fill = output
        if step <= 3:
            all_got = after(all_got, fill)
        if step <= 2 and ffn_step <= over_tok.steps:
            ffn_kept, ffn_got = ffn_next(ffn_step, ffn_kept, after(ffn_got, fill))
            all_got = after(all_got, ffn_kept)
            ffn_step += 1
        if step < over_all.steps - 1:
            all_kept, all_sent = next_halves(all_kept, all_got, 1)
        else:
            all_sums = add(all_kept, all_got)
    for step in range(ffn_step, over_tok.steps + 1):
        ffn_kept, ffn_got = ffn_next(step, ffn_kept, ffn_got)

    planes = 4 * (width // group) + table_rows // group
    vectors = wide(all_sums[planes:].reshape(16, width))
    all_sums = all_sums[:planes].reshape(planes * unit, width)
    s_w = [wide(all_sums[n * own : (n + 1) * own]) for n in range(4)]
    s_rel = wide(all_sums[4 * own :])
    s_vec = lax.dynamic_slice_in_dim(vectors[:VECTORS], over_all.me * own, own, 1)
    part = hidden_cols // n_tok
    bins = vectors[VECTORS : VECTORS + hidden_cols // width].reshape(1, hidden_cols)
    s_bin = lax.dynamic_slice_in_dim(bins, lax.axis_index("tok") * part, part, 1)
    return (
        output,
        grad_tokens,
        s_w[0],
        s_w[1],
        s_w[2],
        s_w[3],
        s_vec[0],
        s_vec[1],
        s_vec[2],
        s_vec[3],
        s_rel,
        s_vec[4],
        s_vec[5],
        wide(ffn_kept[0]),
        s_bin,
        jnp.transpose(wide(ffn_kept[1])),
        s_vec[6],
        s_vec[7],
        s_vec[8],
    )


def solution(mesh):
    every = ("tok", "ffn")
    placed = (
        P(every, None), P(every, None, None), P(every, None), P(every, None, None),
        P(), P(), P(), P(), P(), P(), P(), P(), P(), P(), P(),
        P(None, "ffn"), P("ffn"), P("ffn", None), P(), P(), P(),
    )
    given = (
        P(every, None), P(every, None),
        P(every, None), P(every, None), P(every, None), P(every, None),
        P(every), P(every), P(every), P(every),
        P(every, None), P(every), P(every),
        P("tok", "ffn"), P("ffn", "tok"), P("ffn", "tok"),
        P(every), P(every), P(every),
    )
    return jax.shard_map(local, mesh=mesh, in_specs=placed, out_specs=given, check_vma=False)
```

```python
import functools
import math

import numpy as np

import jax
import jax.numpy as jnp
from jax import lax
from jax.experimental import pallas as pl
from jax.experimental.pallas import tpu as pltpu
from jax.sharding import PartitionSpec as P

HEAD = 64
LANES = 128
HALF = 64
ROWS = 32
AT_ONCE = 2
FIRST_PAIRS = 4
VECTORS = 9
norm_eps = 1e-07
bf16 = jnp.bfloat16
f32 = jnp.float32
PARAMS = pltpu.CompilerParams(vmem_limit_bytes=60 * 2**20)


def dot_nn(first_op, second_op):
    return lax.dot_general(
        first_op, second_op, (((1,), (0,)), ((), ())), preferred_element_type=f32
    )


def dot_nt(first_op, second_op):
    return lax.dot_general(
        first_op, second_op, (((1,), (1,)), ((), ())), preferred_element_type=f32
    )


def dot_tn(first_op, second_op):
    return lax.dot_general(
        first_op, second_op, (((0,), (0,)), ((), ())), preferred_element_type=f32
    )


def distance_rows(seq_len, table_rows):
    side = table_rows // 2
    middle = side // 2
    rows = []
    for m in range(2 * seq_len):
        offset = max(m - seq_len, 1 - seq_len)
        size = abs(offset)
        if size > middle:
            ratio = math.log(size / middle) / math.log((2 * side - 1) / middle)
            size = int(math.ceil(ratio * (middle - 1))) + middle
        rows.append(side + (size if offset > 0 else -size))
    return np.array(rows, dtype=np.int32)


def lane_iota(rows=1):
    return lax.broadcasted_iota(jnp.int32, (rows, LANES), 1)


def member_chunk(words, c, last):
    return (last - words == lane_iota(words.shape[0]) + c * LANES).astype(f32).astype(bf16)


def id_bases(rel_ref, base):
    seq = rel_ref.shape[0]
    chunks = seq // LANES
    last = chunks * 2 - 2
    for g in range(seq // HALF):
        for c in range(chunks):
            block = rel_ref[g * HALF : (g + 1) * HALF, c * LANES : (c + 1) * LANES]
            base[g * chunks + c] = jnp.minimum(jnp.min(block) // HALF, last)


def both_alignments(table):
    return jnp.concatenate([table, table[HALF:], table[:HALF]], axis=0)


def longest(rows):
    wide = rows.astype(f32)
    return jnp.sqrt(jnp.max(jnp.sum(wide * wide, axis=1, keepdims=True)))


def pack_heads(first, second, dest, top):
    top = jnp.maximum(top, 1e-30)
    scale = 32000.0 / top
    upper = (first * scale).astype(jnp.int32)
    lower = (second * scale).astype(jnp.int32)
    dest[...] = upper * 65536 + lower
    return top * (1.0 / 32000.0)


def unpack_heads(words, step):
    lower = lax.shift_right_arithmetic(lax.shift_left(words, 16), 16)
    return words.astype(f32) * (step * (1.0 / 65536.0)), lower.astype(f32) * step


def picked_words(source, rel_ref, base, rows, c):
    chunks = rel_ref.shape[1] // LANES
    first = base[(rows.start // HALF) * chunks + c]
    place = rel_ref[rows, c * LANES : (c + 1) * LANES] - first * HALF
    index = place & (LANES - 1)
    at = pl.multiple_of((first % 2) * (chunks * LANES) + (first // 2) * LANES, LANES)
    near = jnp.take_along_axis(source[rows, pl.ds(at, LANES)], index, axis=1)
    at = pl.multiple_of(at + LANES, LANES)
    far = jnp.take_along_axis(source[rows, pl.ds(at, LANES)], index, axis=1)
    return jnp.where(place < LANES, near, far)


def unshift_in_order(sources, words_ref, base, dest):
    seq = words_ref.shape[0]
    chunks = seq // LANES
    lane = lane_iota()
    zero = jnp.zeros((ROWS, LANES), f32)
    for g in range(chunks):
        first = base[g]
        for sub in range(LANES // ROWS):
            start = g * LANES + sub * ROWS
            rows = slice(start, start + ROWS)
            place = lane - 1 - words_ref[rows, :] + first * LANES
            index = place & (LANES - 1)
            near = place >= 0
            mid = place >= -LANES
            for a, source in enumerate(sources):
                turned = [
                    jnp.take_along_axis(
                        source[rows, c * LANES : (c + 1) * LANES], index, axis=1
                    )
                    for c in range(chunks)
                ]
                turned = [zero, zero] + turned + [zero, zero]
                for c in range(chunks + 2):
                    value = jnp.where(near, turned[c + 2], jnp.where(mid, turned[c + 1], turned[c]))
                    at = pl.multiple_of((first + c) * LANES, LANES)
                    dest[a, rows, pl.ds(at, LANES)] = value.astype(bf16)


def group_bases(words, base):
    seq = words.shape[0]
    for g in range(seq // LANES):
        base[g] = (jnp.min(words[g * LANES : (g + 1) * LANES]) + 1) // LANES


def softmax_weights(scores):
    factor = math.log2(math.e) / math.sqrt(3.0 * HEAD)
    top = jnp.max(functools.reduce(jnp.maximum, scores), axis=1, keepdims=True)
    return [jnp.exp2((score - top) * factor) for score in scores]


def head_lanes(a):
    return (lane_iota() < HEAD) if a == 0 else (lane_iota() >= HEAD)


def row_of(ref):
    return ref[...].reshape(1, ref.shape[0])


def norm_stats(values):
    centered = values - jnp.mean(values, axis=1, keepdims=True)
    inv_std = lax.rsqrt(jnp.mean(centered * centered, axis=1, keepdims=True) + norm_eps)
    return centered * inv_std, inv_std


def norm_backward(upstream, normed, inv_std, norm_gain):
    scaled = upstream * norm_gain
    adjusted = (
        scaled
        - jnp.mean(scaled, axis=1, keepdims=True)
        - normed * jnp.mean(scaled * normed, axis=1, keepdims=True)
    )
    return inv_std * adjusted, col_sum(upstream * normed), col_sum(upstream)


def col_sum(values):
    return jnp.sum(values, axis=0, keepdims=True)


def normal_cdf(pre_act):
    return 0.5 * (1.0 + lax.erf(pre_act * (1.0 / math.sqrt(2.0))))


def picked_kernel(
    pos_ref, rel_ref, qc_ref, k_ref, v_ref, pk_ref, pq_ref,
    x_ref, wo_ref, bo_ref, gain_ref, bias_ref,
    ctx_ref, prob_ref, key_ref, word_ref, wordc_ref, normed_ref, inv_ref, low_ref,
    packed, cpick, relc, keyc, attn, base,
):
    seq = k_ref.shape[0]
    picks = qc_ref.shape[0]
    chunks = seq // LANES

    @pl.when(pl.program_id(0) == 0)
    def _():
        row = lax.broadcasted_iota(jnp.int32, (seq, seq), 0)
        col = lax.broadcasted_iota(jnp.int32, (seq, seq), 1)
        side = pk_ref.shape[0] // 2
        step = jnp.sum(jnp.where(col == row - 1, rel_ref[...] - side, 0), axis=1, keepdims=True)
        steps = jnp.broadcast_to(step.astype(f32), (seq, LANES)).astype(bf16)
        word_ref[...] = dot_nn((col <= row).astype(f32).astype(bf16), steps).astype(jnp.int32)
        id_bases(rel_ref, base)
        for n in range(picks):
            place = jnp.maximum(pos_ref[n], 0)
            relc[n : n + 1, :] = rel_ref[pl.ds(place, 1), :]
            wordc_ref[n : n + 1, :] = word_ref[pl.ds(place, 1), :]

    zero = jnp.zeros((), bf16)
    table = both_alignments(pq_ref[...])
    keys = [dot_nt(jnp.where(head_lanes(a), k_ref[...], zero), table) for a in range(2)]
    unit = pack_heads(keys[0], keys[1], packed, longest(k_ref[...]) * longest(pq_ref[...]))
    for a in range(2):
        cpick[a] = dot_nt(jnp.where(head_lanes(a), qc_ref[...], zero), pk_ref[...])
    for g in range(chunks):
        for c in range(chunks):
            parts = []
            for start in range(g * LANES, (g + 1) * LANES, ROWS):
                parts.append(picked_words(packed, rel_ref, base, slice(start, start + ROWS), c))
            block = jnp.concatenate(parts, axis=0).T
            for a, value in enumerate(unpack_heads(block, unit)):
                key_ref[a, c * LANES : (c + 1) * LANES, g * LANES : (g + 1) * LANES] = value

    for n in range(picks):
        place = jnp.maximum(pos_ref[n], 0)
        for a in range(2):
            keyc[a, n : n + 1, :] = key_ref[a, pl.ds(place, 1), :]
    for a in range(2):
        mine = head_lanes(a)
        direct = dot_nt(jnp.where(mine, qc_ref[...], zero), k_ref[...])
        scores = []
        for c in range(chunks):
            ids = relc[:, c * LANES : (c + 1) * LANES]
            index = ids & (LANES - 1)
            value = jnp.take_along_axis(cpick[a, :, :LANES], index, axis=1)
            for n in range(1, pk_ref.shape[0] // LANES):
                other = cpick[a, :, n * LANES : (n + 1) * LANES]
                value = jnp.where(
                    ids >= n * LANES, jnp.take_along_axis(other, index, axis=1), value
                )
            cols = slice(c * LANES, (c + 1) * LANES)
            scores.append(direct[:, cols] + value + keyc[a, :, cols])
        weights = softmax_weights(scores)
        inverse = 1.0 / jnp.sum(sum(weights[1:], weights[0]), axis=1, keepdims=True)
        probs = jnp.concatenate([(weight * inverse).astype(bf16) for weight in weights], axis=1)
        prob_ref[a] = probs
        mixed = dot_nn(probs, v_ref[...]).astype(bf16)
        ctx_ref[...] = mixed if a == 0 else jnp.where(mine, mixed, ctx_ref[...])

    part = dot_nn(ctx_ref[...], wo_ref[...])

    @pl.when(pl.program_id(0) == 0)
    def _():
        attn[...] = x_ref[...].astype(f32) + row_of(bo_ref) + part

    @pl.when(pl.program_id(0) > 0)
    def _():
        attn[...] += part

    @pl.when(pl.program_id(0) == pl.num_programs(0) - 1)
    def _():
        normed, inv_std = norm_stats(attn[...])
        normed_ref[...] = normed
        inv_ref[...] = jnp.broadcast_to(inv_std, (picks, LANES))
        low_ref[...] = (normed * row_of(gain_ref) + row_of(bias_ref)).astype(bf16)


def attend_picked(
    positions, rel_ids, q_pick, k, v, pos_query, pos_key, x_pick, w_out, b_out, gain, bias
):
    seq, width = k.shape
    picks = q_pick.shape[0]
    table = pos_key.shape[0]
    pairs = width // LANES
    whole = lambda rows, cols: pl.BlockSpec((rows, cols), lambda h: (0, 0))
    line = pl.BlockSpec((width,), lambda h: (0,))
    col = lambda rows: pl.BlockSpec((rows, LANES), lambda h: (0, h))
    heads = lambda rows: pl.BlockSpec((2, rows, seq), lambda h: (h, 0, 0))
    return pl.pallas_call(
        picked_kernel,
        grid=(pairs,),
        in_specs=[
            pl.BlockSpec(memory_space=pltpu.SMEM), whole(seq, seq),
            col(picks), col(seq), col(seq), col(table), col(table),
            whole(picks, width), pl.BlockSpec((LANES, width), lambda h: (h, 0)), line, line, line,
        ],
        out_specs=[
            col(picks), heads(picks), heads(seq), whole(seq, LANES), whole(picks, LANES),
            whole(picks, width), whole(picks, LANES), whole(picks, width),
        ],
        out_shape=[
            jax.ShapeDtypeStruct((picks, width), bf16),
            jax.ShapeDtypeStruct((2 * pairs, picks, seq), bf16),
            jax.ShapeDtypeStruct((2 * pairs, seq, seq), f32),
            jax.ShapeDtypeStruct((seq, LANES), jnp.int32),
            jax.ShapeDtypeStruct((picks, LANES), jnp.int32),
            jax.ShapeDtypeStruct((picks, width), f32),
            jax.ShapeDtypeStruct((picks, LANES), f32),
            jax.ShapeDtypeStruct((picks, width), bf16),
        ],
        scratch_shapes=[
            pltpu.VMEM((seq, 2 * table), jnp.int32),
            pltpu.VMEM((2, picks, table), f32),
            pltpu.VMEM((picks, seq), jnp.int32),
            pltpu.VMEM((2, picks, seq), f32),
            pltpu.VMEM((picks, width), f32),
            pltpu.SMEM((seq // HALF * (seq // LANES),), jnp.int32),
        ],
        compiler_params=PARAMS,
        name="attend_picked",
    )(
        positions, rel_ids, q_pick, k, v, pos_key, pos_query, x_pick, w_out, b_out, gain, bias
    )


def full_kernel(rel_ref, q_ref, k_ref, v_ref, pk_ref, key_ref, ctx_ref, *scratch):
    seq = rel_ref.shape[0]
    chunks = seq // LANES
    base, scratch = scratch[-1], scratch[:-1]
    count = len(scratch) // 3

    @pl.when(pl.program_id(0) == 0)
    def _():
        id_bases(rel_ref, base)

    zero = jnp.zeros((), bf16)
    units = []
    for n in range(count):
        packed, direct, low = scratch[3 * n : 3 * n + 3]
        lanes = slice(n * LANES, (n + 1) * LANES)
        q, pos = q_ref[:, lanes], pk_ref[:, lanes]
        table = both_alignments(pos)
        far = []
        for a in range(2):
            q_a = jnp.where(head_lanes(a), q, zero)
            far.append(dot_nt(q_a, table))
            direct[a] = dot_nt(q_a, k_ref[:, lanes])
        units.append(pack_heads(far[0], far[1], packed, longest(q) * longest(pos)))
    for n in range(count):
        packed, direct, low = scratch[3 * n : 3 * n + 3]
        lanes = slice(n * LANES, (n + 1) * LANES)
        for start in range(0, seq, HALF):
            rows = slice(start, start + HALF)
            scores = [[], []]
            for c in range(chunks):
                cols = slice(c * LANES, (c + 1) * LANES)
                values = unpack_heads(picked_words(packed, rel_ref, base, rows, c), units[n])
                for a in range(2):
                    scores[a].append(
                        values[a] + direct[a, rows, cols] + key_ref[2 * n + a, rows, cols]
                    )
            for a in range(2):
                for c, weight in enumerate(softmax_weights(scores[a])):
                    low[a, rows, c * LANES : (c + 1) * LANES] = weight.astype(bf16)
        v = v_ref[:, lanes]
        mixed = [
            dot_nn(low[a], jnp.where(head_lanes(a), v, jnp.ones((), bf16))) for a in range(2)
        ]
        upper = head_lanes(0)
        totals = pltpu.roll(jnp.where(upper, mixed[1], mixed[0]), HEAD, 1)
        ctx_ref[:, lanes] = (jnp.where(upper, mixed[0], mixed[1]) * (1.0 / totals)).astype(bf16)


def attend_full(rel_ids, q, k, v, pos_key, key_scores, first, pairs):
    seq = k.shape[0]
    table = pos_key.shape[0]
    per = AT_ONCE
    wide = per * LANES
    col = lambda rows: pl.BlockSpec((rows, wide), lambda h: (0, h + first // per))
    return pl.pallas_call(
        full_kernel,
        grid=(pairs // per,),
        in_specs=[
            pl.BlockSpec((seq, seq), lambda h: (0, 0)),
            col(seq), col(seq), col(seq), col(table),
            pl.BlockSpec((2 * per, seq, seq), lambda h: (h + first // per, 0, 0)),
        ],
        out_specs=pl.BlockSpec((seq, wide), lambda h: (0, h)),
        out_shape=jax.ShapeDtypeStruct((seq, pairs * LANES), bf16),
        scratch_shapes=[
            pltpu.VMEM((seq, 2 * table), jnp.int32),
            pltpu.VMEM((2, seq, seq), f32),
            pltpu.VMEM((2, seq, seq), bf16),
        ]
        * per
        + [pltpu.SMEM((seq // HALF * (seq // LANES),), jnp.int32)],
        compiler_params=PARAMS,
        name="attend_full",
    )(rel_ids, q, k, v, pos_key, key_scores)


def back_kernel(
    row_ref, word_ref, wordc_ref, qc_ref, k_ref, v_ref, prob_ref, pk_ref, pq_ref,
    dz2_ref, mine_ref, got_ref, normed_ref, inv_ref, gain_ref, wo_ref, early_ref,
    dq_ref, dk_ref, dv_ref, dpos_ref, dz1_ref, dattn_ref, sum_ref,
    side, sidec, moved, movedc, expand, shrink, base,
):
    seq = k_ref.shape[0]
    picks = qc_ref.shape[0]
    table = pk_ref.shape[0]
    chunks = seq // LANES

    @pl.when(pl.program_id(0) == 0)
    def _():
        words = word_ref[...]
        for c in range(chunks):
            side[:, c * LANES : (c + 1) * LANES] = member_chunk(words, c, seq - 1)
            sidec[:, c * LANES : (c + 1) * LANES] = member_chunk(wordc_ref[...], c, seq - 1)
        group_bases(words, base)
        moved[...] = jnp.zeros_like(moved)
        edge = expand.shape[1]
        for n, start in ((0, 0), (1, 2 * seq - edge)):
            ids = row_ref[start : start + edge, :] - n * (table - LANES)
            chosen = (ids == lane_iota(edge)).astype(f32).astype(bf16)
            expand[n] = chosen
            shrink[n] = chosen.T
        dh1 = dz2_ref[...] + mine_ref[...].astype(f32) + got_ref[...].astype(f32)
        dz1, g_gain, g_bias = norm_backward(dh1, normed_ref[...], inv_ref[:, :1], row_of(gain_ref))
        dz1_ref[...] = dz1
        dattn = dz1.astype(bf16)
        dattn_ref[...] = dattn
        sum_ref[...] = jnp.concatenate(
            [col_sum(dattn.astype(f32)), g_gain, g_bias, early_ref[:5]], axis=0
        )

    lane = lane_iota()
    scale = 1.0 / math.sqrt(3.0 * HEAD)
    zero = jnp.zeros((), bf16)
    heads = range(2)
    upper = head_lanes(0)
    join = lambda pair: jnp.where(upper, pair[0], pair[1])
    side[:, seq:] = k_ref[...]
    sidec[:, seq:] = qc_ref[...]
    dctx = dot_nt(dattn_ref[...], wo_ref[...]).astype(bf16)
    dprobs = [dot_nt(jnp.where(head_lanes(a), dctx, zero), v_ref[...]) for a in heads]

    def widened(ref):
        ends = [
            dot_nn(expand[n], ref[at : at + LANES, :]).astype(bf16)
            for n, at in ((0, 0), (1, table - LANES))
        ]
        return jnp.concatenate([ends[0], ref[LANES : table - LANES, :], ends[1]], axis=0)

    far_key, far_query = widened(pk_ref), widened(pq_ref)
    gs = []
    for a in heads:
        probs = prob_ref[a].astype(f32)
        prod = probs * dprobs[a]
        gs.append(((prod - probs * jnp.sum(prod, axis=1, keepdims=True)) * scale).astype(bf16))
    outs = [dot_tn(gs[a], sidec[...]) for a in heads]
    outcs = [dot_nn(gs[a], side[...]) for a in heads]
    dv_ref[...] = join([dot_tn(prob_ref[a], dctx) for a in heads]).astype(bf16)
    place = lane - 1 - wordc_ref[...]
    index = place & (LANES - 1)
    blank = jnp.zeros((picks, LANES), f32)
    for a in heads:
        turned = [
            jnp.take_along_axis(outcs[a][:, c * LANES : (c + 1) * LANES], index, axis=1)
            for c in range(chunks)
        ]
        for c in range(2 * chunks):
            value = turned[c] if c < chunks else blank
            for n in range(1, chunks + 1):
                other = turned[c - n] if 0 <= c - n < chunks else blank
                value = jnp.where(place < -LANES * (n - 1), other, value)
            movedc[a, :, c * LANES : (c + 1) * LANES] = value.astype(bf16)
    unshift_in_order(outs, word_ref, base, moved)
    dq = [outcs[a][:, seq:] + dot_nn(movedc[a], far_key) for a in heads]
    dq_ref[...] = join(dq).astype(bf16)
    dk = [outs[a][:, seq:] + dot_nn(moved[a, :, : 2 * seq], far_query) for a in heads]
    dk_ref[...] = join(dk).astype(bf16)
    far = [
        join([dot_tn(movedc[a], qc_ref[...]) for a in heads]),
        join([dot_tn(moved[a, :, : 2 * seq], k_ref[...]) for a in heads]),
    ]
    edge = expand.shape[1]
    for n, value in enumerate(far):
        value = value.astype(bf16)
        dpos_ref[n, :LANES, :] = dot_nn(shrink[0], value[:edge]).astype(bf16)
        dpos_ref[n, LANES : table - LANES, :] = value[edge : 2 * seq - edge]
        dpos_ref[n, table - LANES :, :] = dot_nn(shrink[1], value[2 * seq - edge :]).astype(bf16)


def attend_back(
    table_of, words, words_pick, q_pick, k, v, probs, pos_query, pos_key,
    dz2, mine, got, normed, inv_std, gain, w_out, early,
):
    seq, width = k.shape
    picks = q_pick.shape[0]
    table = pos_key.shape[0]
    pairs = width // LANES
    edge = seq - table // 4
    whole = lambda value: pl.BlockSpec(value.shape, lambda h: (0,) * value.ndim)
    col = lambda rows: pl.BlockSpec((rows, LANES), lambda h: (0, h))
    shape = lambda rows: jax.ShapeDtypeStruct((rows, width), bf16)
    return pl.pallas_call(
        back_kernel,
        grid=(pairs,),
        in_specs=[
            whole(table_of), whole(words), whole(words_pick),
            col(picks), col(seq), col(seq),
            pl.BlockSpec((2, picks, seq), lambda h: (h, 0, 0)),
            col(table), col(table),
            whole(dz2), whole(mine), whole(got), whole(normed), whole(inv_std), whole(gain),
            pl.BlockSpec((LANES, width), lambda h: (h, 0)), whole(early),
        ],
        out_specs=[
            col(picks), col(seq), col(seq),
            pl.BlockSpec((2, table, LANES), lambda h: (0, 0, h)),
            whole(dz2), whole(dz2), whole(early),
        ],
        out_shape=[
            shape(picks), shape(seq), shape(seq),
            jax.ShapeDtypeStruct((2, table, width), bf16),
            jax.ShapeDtypeStruct((picks, width), f32),
            shape(picks),
            jax.ShapeDtypeStruct(early.shape, f32),
        ],
        scratch_shapes=[
            pltpu.VMEM((seq, seq + LANES), bf16),
            pltpu.VMEM((picks, seq + LANES), bf16),
            pltpu.VMEM((2, seq, 2 * seq + 2 * LANES), bf16),
            pltpu.VMEM((2, picks, 2 * seq), bf16),
            pltpu.VMEM((2, edge, LANES), bf16),
            pltpu.VMEM((2, LANES, edge), bf16),
            pltpu.SMEM((seq // LANES,), jnp.int32),
        ],
        compiler_params=PARAMS,
        name="attend_back",
    )(
        table_of, words, words_pick, q_pick, k, v, probs, pos_key, pos_query,
        dz2, mine, got, normed, inv_std, gain, w_out, early,
    )


def turn_kernel(
    n_all, me_ref, order_ref, x_ref, xpick_ref, cpick_ref, rel_ref, x_out, xpick_out, cpick_out, rel_out
):
    picked = order_rows(order_ref, me_ref, x_ref.shape[1], n_all)
    for ref, out in ((x_ref, x_out), (xpick_ref, xpick_out), (cpick_ref, cpick_out), (rel_ref, rel_out)):
        out[...] = dot_nt(picked, ref[...]).astype(bf16)


def block_rows(ref, me_ref):
    return me_ref[0] ^ jnp.where(me_ref[1] == 0, ref[:, 0:1], ref[:, 1:2])


def order_rows(ref, me_ref, length, n_all):
    source = block_rows(ref, me_ref) * (length // n_all) + ref[:, 2:3]
    spot = lax.broadcasted_iota(jnp.int32, (ref.shape[0], length), 1)
    return (spot == source).astype(f32).astype(bf16)


def turn_blocks(n_all, me, order, x, x_pick, ctx_pick, rel_table):
    width = x.shape[1]
    group = 2 * LANES
    whole = lambda value: pl.BlockSpec(value.shape, lambda n: (0, 0))
    row = lambda count: pl.BlockSpec((group, count), lambda n: (n, 0))
    given = [x, x_pick, ctx_pick, rel_table]
    return pl.pallas_call(
        functools.partial(turn_kernel, n_all),
        grid=(width // group,),
        in_specs=[pl.BlockSpec(memory_space=pltpu.SMEM), row(LANES)]
        + [whole(value) for value in given],
        out_specs=[row(value.shape[0]) for value in given],
        out_shape=[jax.ShapeDtypeStruct(value.shape[::-1], bf16) for value in given],
        compiler_params=PARAMS,
        name="turn_blocks",
    )(me, order, *given)


def norm_picked_kernel(
    normed_ref, gain1_ref, bias1_ref, mine_ref, got_ref, bdown_ref, gain2_ref, grad_ref, pick_ref,
    dz2_ref, low_ref, sum_ref,
):
    h1 = normed_ref[...] * row_of(gain1_ref) + row_of(bias1_ref)
    branch = mine_ref[...].astype(f32) + got_ref[...].astype(f32) + row_of(bdown_ref)
    normed, inv_std = norm_stats(h1 + branch)
    used = jnp.sum(pick_ref[...].astype(f32), axis=1, keepdims=True)
    cot = jnp.where(used > 0.0, grad_ref[...].astype(f32), 0.0)
    dz2, g_gain, g_bias = norm_backward(cot, normed, inv_std, row_of(gain2_ref))
    dz2_ref[...] = dz2
    low = dz2.astype(bf16)
    low_ref[...] = low
    sum_ref[...] = jnp.concatenate(
        [col_sum(low.astype(f32)), g_gain, g_bias, jnp.zeros((5, h1.shape[1]), f32)], axis=0
    )


def norm_picked(normed, gain1, bias1, mine, got, b_down, gain2, grads, pick):
    picks, width = normed.shape
    return pl.pallas_call(
        norm_picked_kernel,
        out_shape=[
            jax.ShapeDtypeStruct((picks, width), f32),
            jax.ShapeDtypeStruct((picks, width), bf16),
            jax.ShapeDtypeStruct((8, width), f32),
        ],
        compiler_params=PARAMS,
        name="norm_picked",
    )(normed, gain1, bias1, mine, got, b_down, gain2, grads, pick)


def ffn_full_kernel(
    x_ref, ctx_ref, ctx2_ref, wo_ref, bo_ref, gain1_ref, bias1_ref, bdown_ref, gain2_ref, bias2_ref,
    bin_ref, bin2_ref, bin3_ref, win_ref, down_ref, win2_ref, down2_ref, win3_ref, down3_ref,
    out_ref, h1, low, total, win_here, down_here, win_sem, down_sem,
):
    rows, width = x_ref.shape
    tile = win_here.shape[2]
    parts = [(win_ref, down_ref, bin_ref, n * tile) for n in range(win_ref.shape[1] // tile)]
    parts += [(win2_ref, down2_ref, bin2_ref, 0), (win3_ref, down3_ref, bin3_ref, 0)]

    def copies(n):
        w_ref, d_ref, _, at = parts[n]
        return (
            pltpu.make_async_copy(w_ref.at[:, at : at + tile], win_here.at[n], win_sem.at[n]),
            pltpu.make_async_copy(d_ref.at[at : at + tile, :], down_here.at[n], down_sem.at[n]),
        )

    for n in range(len(parts)):
        for copy in copies(n):
            copy.start()
    attn = dot_nn(ctx_ref[...], wo_ref[: ctx_ref.shape[1]]) + dot_nn(
        ctx2_ref[...], wo_ref[ctx_ref.shape[1] :]
    )
    normed, _ = norm_stats(x_ref[...].astype(f32) + (attn + row_of(bo_ref)))
    value = normed * row_of(gain1_ref) + row_of(bias1_ref)
    h1[...] = value
    low[...] = value.astype(bf16)
    step = rows // 2
    for n in range(len(parts)):
        for copy in copies(n):
            copy.wait()
        bias = parts[n][2][:, parts[n][3] : parts[n][3] + tile]
        for at in range(0, rows, step):
            pre = dot_nn(low[at : at + step], win_here[n]) + bias
            part = dot_nn((pre * normal_cdf(pre)).astype(bf16), down_here[n])
            total[at : at + step] = part if n == 0 else total[at : at + step] + part
    normed, _ = norm_stats(h1[...] + (total[...] + row_of(bdown_ref)))
    out_ref[...] = (normed * row_of(gain2_ref) + row_of(bias2_ref)).astype(bf16)


def ffn_full(x, ctx, w_out, b_out, gain1, bias1, shards, b_down, gain2, bias2):
    rows, width = x.shape
    tile = shards[1][0].shape[1]
    count = shards[0][0].shape[1] // tile + 2
    held = [x, ctx[0], ctx[1], w_out, b_out, gain1, bias1, b_down, gain2, bias2]
    held += [shard[2] for shard in shards]
    moved = [value for shard in shards for value in shard[:2]]
    return pl.pallas_call(
        ffn_full_kernel,
        in_specs=[pl.BlockSpec(memory_space=pltpu.VMEM)] * len(held)
        + [pl.BlockSpec(memory_space=pl.ANY)] * len(moved),
        out_specs=pl.BlockSpec(memory_space=pltpu.VMEM),
        out_shape=jax.ShapeDtypeStruct((rows, width), bf16),
        scratch_shapes=[
            pltpu.VMEM((rows, width), f32), pltpu.VMEM((rows, width), bf16), pltpu.VMEM((rows, width), f32),
            pltpu.VMEM((count, width, tile), bf16), pltpu.VMEM((count, tile, width), bf16),
            pltpu.SemaphoreType.DMA((count,)), pltpu.SemaphoreType.DMA((count,)),
        ],
        compiler_params=PARAMS,
        name="ffn_full",
    )(*held, *moved)


def token_grads_kernel(pick_ref, dz1_ref, dq_ref, dk_ref, dv_ref, wq_ref, wk_ref, wv_ref, out_ref):
    sparse = dz1_ref[...] + dot_nt(dq_ref[...], wq_ref[...])
    upper = sparse.astype(bf16)
    lower = (sparse - upper.astype(f32)).astype(bf16)
    out_ref[...] = (
        dot_nt(dk_ref[...], wk_ref[...])
        + dot_nt(dv_ref[...], wv_ref[...])
        + dot_tn(pick_ref[...], upper)
        + dot_tn(pick_ref[...], lower)
    )


def token_grads(pick, dz1, dq, dk, dv, w_query, w_key, w_value):
    seq, width = dk.shape
    group = 2 * LANES
    whole = lambda value: pl.BlockSpec(value.shape, lambda n: (0, 0))
    col = lambda rows: pl.BlockSpec((rows, group), lambda n: (0, n))
    row = pl.BlockSpec((group, width), lambda n: (n, 0))
    return pl.pallas_call(
        token_grads_kernel,
        grid=(width // group,),
        in_specs=[whole(pick), col(dz1.shape[0]), whole(dq), whole(dk), whole(dv), row, row, row],
        out_specs=col(seq),
        out_shape=jax.ShapeDtypeStruct((seq, width), f32),
        compiler_params=PARAMS,
        name="token_grads",
    )(pick, dz1, dq, dk, dv, w_query, w_key, w_value)


def grads_kernel(
    n_all, n_ffn, unit, me_ref, order_ref, relorder_ref, taker_ref,
    x_ref, rel_ref, xpick_ref, cpick_ref, dpos_ref,
    dq_ref, dk_ref, dv_ref, dattn_ref, dposk_ref, dposq_ref, wq_ref, wk_ref,
    early_ref, bin_ref, bin2_ref, kept_ref, sent_ref, dpos,
):
    width = x_ref.shape[0]
    group = 2 * LANES

    def put(at, value):
        value = value.astype(bf16)
        for n in range(value.shape[0] // group):
            kept_ref[at + n] = value[n * group : n * group + LANES]
            sent_ref[at + n] = value[n * group + LANES : (n + 1) * group]

    @pl.when(pl.program_id(0) == 0)
    def _():
        rows = order_rows(relorder_ref, me_ref, dpos_ref.shape[1], n_all)
        for n in range(2):
            dpos[n] = dot_nn(rows, dpos_ref[n]).astype(bf16)

    count = width // group
    put(0, dot_nn(xpick_ref[...], dq_ref[...]) + dot_nn(rel_ref[...], dposq_ref[0]))
    put(count, dot_nn(x_ref[...], dk_ref[...]) + dot_nn(rel_ref[...], dposk_ref[0]))
    put(2 * count, dot_nn(x_ref[...], dv_ref[...]))
    put(3 * count, dot_nn(cpick_ref[...], dattn_ref[...]))
    put(4 * count, dot_nt(dpos[0], wk_ref[...]) + dot_nt(dpos[1], wq_ref[...]))

    total = lambda value: col_sum(value.astype(f32))
    values = jnp.concatenate(
        [
            total(dq_ref[...]) + total(dposq_ref[0]),
            total(dk_ref[...]) + total(dposk_ref[0]),
            total(dv_ref[...]),
            early_ref[:6],
            bin_ref[:1],
            bin2_ref[:1],
            jnp.zeros((5, group), f32),
        ],
        axis=0,
    )
    block = block_rows(order_ref[:group, :], me_ref)
    ours = (block % n_ffn) == (me_ref[0] % n_ffn)
    tok_place = jnp.where(ours, block // n_ffn, -1)
    first = 4 * count + dpos.shape[1] // group
    row = lax.broadcasted_iota(jnp.int32, (group, 1), 0) % unit
    for n in range(16 // unit):
        rows = slice(n * unit, (n + 1) * unit)
        spread = lambda value: jnp.concatenate([value[rows]] * (group // unit), axis=0)
        taker = jnp.where(row + n * unit < VECTORS, block, tok_place)
        put(first + n, jnp.where(spread(taker_ref[...]) == taker, spread(values), 0.0))


def weight_grads(
    n_all, n_ffn, unit, me, order, rel_order, takers, x, rel, x_pick, c_pick, dpos, dq, dk, dv, dattn,
    w_query, w_key, early, bins,
):
    width, seq = x.shape
    group = 2 * LANES
    planes = 4 * (width // group) + dpos.shape[1] // group + 16 // unit
    whole = lambda value: pl.BlockSpec(value.shape, lambda n: (0,) * value.ndim)
    col = lambda value: pl.BlockSpec((value.shape[0], group), lambda n: (0, n))
    row = lambda value: pl.BlockSpec((group, value.shape[1]), lambda n: (n, 0))
    plane = lambda t: pl.BlockSpec((1, dpos.shape[1], group), lambda n: (t, 0, n))
    block = pl.BlockSpec((planes, LANES, group), lambda n: (0, 0, n))
    return pl.pallas_call(
        functools.partial(grads_kernel, n_all, n_ffn, unit),
        grid=(width // group,),
        in_specs=[
            pl.BlockSpec(memory_space=pltpu.SMEM), whole(order), whole(rel_order), col(takers),
            whole(x), whole(rel), whole(x_pick), whole(c_pick), whole(dpos),
            col(dq), col(dk), col(dv), col(dattn), plane(0), plane(1), row(w_query), row(w_key),
            col(early), col(bins), pl.BlockSpec((8, group), lambda n: (0, n + width // group)),
        ],
        out_specs=[block] * 2,
        out_shape=[jax.ShapeDtypeStruct((planes, LANES, width), bf16)] * 2,
        scratch_shapes=[pltpu.VMEM(dpos.shape, bf16)],
        compiler_params=PARAMS,
        name="weight_grads",
    )(
        me, order, rel_order, takers, x, rel, x_pick, c_pick, dpos, dq, dk, dv, dattn, dpos, dpos,
        w_query, w_key, early, bins, bins,
    )


def swap(values, axis, bit):
    size = lax.axis_size(axis)
    return lax.ppermute(values, axis, [(n, n ^ bit) for n in range(size)])


def after(values, *others):
    return lax.optimization_barrier((values, others))[0]


class Halving:
    def __init__(self, axes, core, near, size):
        rest = [1 << n for n in range(size.bit_length() - 1) if (1 << n) != core]
        near = [bit for bit in near if bit in rest]
        rest = [bit for bit in rest if bit not in near]
        turned = near[-1:] + near[:-1]
        self.axes, self.core, self.size = axes, core, size
        self.orders = [[core] + near + rest, [core] + turned + rest]
        self.steps = len(self.orders[0])
        self.me = lax.axis_index(axes)
        self.upper = (self.me // core) % 2

    def core_of(self, place):
        return (place // self.core) % 2

    def send(self, values, step):
        pairs = [(n, n ^ self.orders[self.core_of(n)][step]) for n in range(self.size)]
        return lax.ppermute(values, self.axes, pairs)

    def relative(self, upper):
        masks = []
        for place in range(self.size):
            bits = [(place >> (self.steps - 1 - step)) & 1 for step in range(self.steps)]
            order = self.orders[upper ^ bits[0]]
            mask = 0
            for step, bit in enumerate(bits):
                mask ^= bit * order[step]
            masks.append(mask)
        return np.array(masks, np.int32)

    def order(self, length, unit):
        spots = np.arange(length)
        group = self.size * unit
        place = spots % group // unit
        rows = [self.relative(upper)[place] for upper in range(2)]
        rows.append(spots // group * unit + spots % unit)
        return np.stack(rows).astype(np.int32)

    def matrix(self, length, unit):
        first, second, inner = self.order(length, unit)
        source = (self.me ^ jnp.where(self.upper == 0, first, second)) * (length // self.size) + inner
        spot = lax.broadcasted_iota(jnp.int32, (length, length), 0)
        return (spot == source[None, :]).astype(bf16)


def local(
    tokens, rel_ids, mask_pos, grad_vals, w_query, w_key, w_value, w_out, b_query, b_key,
    b_value, b_out, rel_table, ln1_gain, ln1_bias, w_in, b_in, w_down, b_down, ln2_gain, ln2_bias,
):
    assert rel_ids.shape[0] == 1
    seq, width = tokens.shape
    table_rows = rel_table.shape[0]
    hidden_cols = w_in.shape[1]
    pairs = width // LANES
    n_tok = lax.axis_size("tok")
    n_ffn = lax.axis_size("ffn")
    n_all = n_tok * n_ffn
    low = lambda value: value.astype(bf16)
    wide = lambda value: value.astype(f32)
    rel_ids, positions, grad_vals = rel_ids[0], mask_pos[0], grad_vals[0]

    over_all = Halving(("tok", "ffn"), n_ffn, [2 * n_ffn, 1, 4 * n_ffn], n_all)
    own, own_rel = width // n_all, table_rows // n_all
    unit = math.gcd(own, own_rel)
    group = n_all * unit
    over_tok = Halving("tok", 1, [2, 4], n_tok)
    pad = lambda value, count: np.pad(value, ((0, count - value.shape[0]), (0, 0)))
    order = jnp.asarray(pad(over_all.order(width, unit), LANES).T)
    rel_order = jnp.asarray(pad(over_all.order(table_rows, unit), LANES).T)
    spots = np.arange(width)
    takers = [spots // own] * VECTORS
    takers += [(spots + n * width) // (hidden_cols // n_tok) for n in range(hidden_cols // width)]
    takers = np.stack(takers).astype(np.int32)
    takers = jnp.asarray(np.pad(takers, ((0, 16 - takers.shape[0]), (0, 0)), constant_values=-2))
    me = jnp.stack([over_all.me, over_all.upper])
    table_of = jnp.asarray(np.repeat(distance_rows(seq, table_rows)[:, None], LANES, 1))

    core = lax.axis_index("tok") % 2
    half_cols = hidden_cols // 2
    bias_row = b_in.reshape(1, hidden_cols)
    in_half = lax.dynamic_slice_in_dim(w_in, core * half_cols, half_cols, 1)
    down_half = lax.dynamic_slice_in_dim(w_down, core * half_cols, half_cols, 0)

    pick = low(positions[:, None] == lax.broadcasted_iota(jnp.int32, (positions.shape[0], seq), 1))
    x_pick = low(dot_nn(pick, tokens))
    q_pick = low(dot_nn(x_pick, w_query) + b_query)
    k = low(dot_nn(tokens, w_key) + b_key)
    v = low(dot_nn(tokens, w_value) + b_value)
    pos_query = low(dot_nn(rel_table, w_query) + b_query)
    pos_key = low(dot_nn(rel_table, w_key) + b_key)
    ctx_pick, probs, key_scores, words, words_pick, normed1, inv1, h1_mine = attend_picked(
        positions, rel_ids, q_pick, k, v, pos_query, pos_key, x_pick, w_out, b_out, ln1_gain, ln1_bias
    )

    h1_theirs = swap(h1_mine, "ffn", 1)
    bias_theirs = swap(bias_row, "ffn", 1)
    x_turned, x_pick_turned, c_pick_turned, rel_turned = turn_blocks(
        n_all, me, order, tokens, x_pick, ctx_pick, rel_table
    )
    h1_both = jnp.concatenate([h1_mine, after(h1_theirs, x_turned)], axis=0)
    count = h1_mine.shape[0]
    pre = dot_nn(h1_both, w_in) + b_in
    cdf = normal_cdf(pre)
    hidden = low(pre * cdf)
    slope = cdf + pre * (jnp.exp(-0.5 * pre * pre) * (1.0 / math.sqrt(2.0 * math.pi)))
    part = low(dot_nn(hidden, w_down))
    got = swap(part[count:], "ffn", 1)
    q = low(dot_nn(after(tokens, part), w_query) + b_query)
    tok_order = over_tok.matrix(width, width // n_tok)
    h1_left = low(dot_nn(h1_both, lax.optimization_barrier(tok_order)))
    in_half = after(in_half, part)
    got = after(got, q, h1_left, in_half)
    dz2, dffn, early = norm_picked(
        normed1, ln1_gain, ln1_bias, part[:count], got, b_down, ln2_gain, grad_vals, pick
    )
    down_half = after(down_half, dffn)
    dffn_both = jnp.concatenate([dffn, after(swap(dffn, "ffn", 1), down_half)], axis=0)
    dpre = low(dot_nt(dffn_both, w_down) * slope)
    dpart = low(dot_nt(dpre, w_in))
    dgot = swap(dpart[count:], "ffn", 1)

    def halves(values, axis):
        size = values.shape[axis] // 2
        cut = lambda at: lax.slice_in_dim(values, at, at + size, axis=axis)
        return cut(0), cut(size)

    add = lambda one, other: low(wide(one) + wide(other))

    def next_halves(kept, got, axis):
        return [add(one, other) for one, other in zip(halves(kept, axis), halves(got, axis))]

    dpre_later = after(dpre, dpart)
    dffn_left = low(dot_nn(after(dffn_both, dpart), tok_order))
    gb_in = dot_nn(jnp.ones((8, 2 * count), bf16), dpre_later)
    lefts, rights = (h1_left, dffn_left), (dpre_later, hidden)
    middle, quarter = width // 2, width // 4
    ffn_sent = [low(dot_tn(one[:, middle:], other)) for one, other in zip(lefts, rights)]
    dgot, ffn_sent = lax.optimization_barrier((dgot, ffn_sent))
    ffn_got = [over_tok.send(value, 0) for value in ffn_sent]
    far_in = swap(after(in_half, dgot, ffn_sent), "ffn", 1)

    def ffn_piece(at):
        return [
            low(dot_tn(one[:, at : at + quarter], other) + wide(value[at : at + quarter]))
            for one, other, value in zip(lefts, rights, ffn_got)
        ]

    ffn_sent = ffn_piece(quarter)
    ffn_kept = ffn_piece(0)
    ffn_got = [over_tok.send(value, 1) for value in ffn_sent]

    def ffn_next(step, kept, got):
        if step < over_tok.steps:
            pieces = [next_halves(one, other, 0) for one, other in zip(kept, got)]
            return [piece[0] for piece in pieces], [over_tok.send(piece[1], step) for piece in pieces]
        return [add(one, other) for one, other in zip(kept, got)], None

    dq, dk, dv, dpos, dz1, dattn, early = attend_back(
        table_of, words, words_pick, q_pick, k, v, probs, pos_query, pos_key,
        dz2, dpart[:count], after(dgot, in_half, ffn_sent, ffn_kept), normed1, inv1, ln1_gain, w_out, early,
    )
    far_in, ffn_got = after((far_in, ffn_got), dk)
    ffn_kept, ffn_got = ffn_next(2, ffn_kept, ffn_got)
    near_in = swap(far_in, "tok", 1)
    far_down = swap(after(down_half, far_in), "ffn", 1)
    all_kept, all_sent = weight_grads(
        n_all, n_ffn, unit, me, order, rel_order, takers,
        x_turned, rel_turned, x_pick_turned, c_pick_turned, dpos, dq, after(dk, far_in, ffn_kept), dv,
        dattn, w_query, w_key, early, gb_in,
    )
    all_got = over_all.send(all_sent, 0)
    ffn_kept, ffn_got = ffn_next(3, ffn_kept, after(ffn_got, all_sent))
    dk_later, dq_later = after((dk, dq), all_sent, ffn_kept)
    grad_tokens = token_grads(pick, dz1, dq_later, dk_later, dv, w_query, w_key, w_value)
    all_kept, all_sent = next_halves(all_kept, after(all_got, grad_tokens), 1)
    ffn_step = 4

    def attend(first, count, q):
        return attend_full(rel_ids, q, k, v, pos_key, key_scores, first, count)

    ctx = []
    cuts = [(0, FIRST_PAIRS), (FIRST_PAIRS, pairs - FIRST_PAIRS)]
    for step in range(1, over_all.steps):
        all_got = over_all.send(all_sent, step)
        if step <= 2:
            ctx.append(attend(*cuts[step - 1], after(q, all_sent)))
            all_got = after(all_got, ctx[-1])
            if step == 1:
                far_down = after(far_down, ctx[-1])
                near_down = swap(far_down, "tok", 1)
                all_got = after(all_got, far_down)
        elif step == 4:
            biases = [
                lax.dynamic_slice_in_dim(bias_theirs, at * half_cols, half_cols, 1)
                for at in (core, 1 - core)
            ]
            shards = [
                (w_in, w_down, bias_row), (far_in, far_down, biases[0]), (near_in, near_down, biases[1])
            ]
            output = ffn_full(
                after(tokens, all_sent), ctx, w_out, b_out, ln1_gain, ln1_bias, shards,
                b_down, ln2_gain, ln2_bias,
            )
            all_got = after(all_got, output)
        if ffn_step <= over_tok.steps:
            ffn_got = after(ffn_got, all_sent)
            if step <= 2:
                ffn_got = after(ffn_got, ctx[-1])
            ffn_kept, ffn_got = ffn_next(ffn_step, ffn_kept, ffn_got)
            ffn_step += 1
        if step < over_all.steps - 1:
            all_kept, all_sent = next_halves(all_kept, all_got, 1)
        else:
            all_sums = add(all_kept, all_got)

    planes = 4 * (width // group) + table_rows // group
    vectors = wide(all_sums[planes:].reshape(16, width))
    all_sums = all_sums[:planes].reshape(planes * unit, width)
    s_w = [wide(all_sums[n * own : (n + 1) * own]) for n in range(4)]
    s_rel = wide(all_sums[4 * own :])
    s_vec = lax.dynamic_slice_in_dim(vectors[:VECTORS], over_all.me * own, own, 1)
    part = hidden_cols // n_tok
    bins = vectors[VECTORS : VECTORS + hidden_cols // width].reshape(1, hidden_cols)
    s_bin = lax.dynamic_slice_in_dim(bins, lax.axis_index("tok") * part, part, 1)
    return (
        output,
        grad_tokens,
        s_w[0],
        s_w[1],
        s_w[2],
        s_w[3],
        s_vec[0],
        s_vec[1],
        s_vec[2],
        s_vec[3],
        s_rel,
        s_vec[4],
        s_vec[5],
        wide(ffn_kept[0]),
        s_bin,
        jnp.transpose(wide(ffn_kept[1])),
        s_vec[6],
        s_vec[7],
        s_vec[8],
    )


def solution(mesh):
    every = ("tok", "ffn")
    placed = (
        P(every, None), P(every, None, None), P(every, None), P(every, None, None),
        P(), P(), P(), P(), P(), P(), P(), P(), P(), P(), P(),
        P(None, "ffn"), P("ffn"), P("ffn", None), P(), P(), P(),
    )
    given = (
        P(every, None), P(every, None),
        P(every, None), P(every, None), P(every, None), P(every, None),
        P(every), P(every), P(every), P(every),
        P(every, None), P(every), P(every),
        P("tok", "ffn"), P("ffn", "tok"), P("ffn", "tok"),
        P(every), P(every), P(every),
    )
    return jax.shard_map(local, mesh=mesh, in_specs=placed, out_specs=given, check_vma=False)
```

```python
import functools
import math

import numpy as np

import jax
import jax.numpy as jnp
from jax import lax
from jax.experimental import pallas as pl
from jax.experimental.pallas import tpu as pltpu
from jax.sharding import PartitionSpec as P

HEAD = 64
LANES = 128
HALF = 64
ROWS = 32
AT_ONCE = 2
FIRST_PAIRS = 4
VECTORS = 9
norm_eps = 1e-07
bf16 = jnp.bfloat16
f32 = jnp.float32
PARAMS = pltpu.CompilerParams(vmem_limit_bytes=60 * 2**20)


def lasting(micros):
    return pl.CostEstimate(
        flops=int(micros * 1.1e9), bytes_accessed=int(micros * 3.4e6), transcendentals=0
    )


def dot_nn(first_op, second_op):
    return lax.dot_general(
        first_op, second_op, (((1,), (0,)), ((), ())), preferred_element_type=f32
    )


def dot_nt(first_op, second_op):
    return lax.dot_general(
        first_op, second_op, (((1,), (1,)), ((), ())), preferred_element_type=f32
    )


def dot_tn(first_op, second_op):
    return lax.dot_general(
        first_op, second_op, (((0,), (0,)), ((), ())), preferred_element_type=f32
    )


def distance_rows(seq_len, table_rows):
    side = table_rows // 2
    middle = side // 2
    rows = []
    for m in range(2 * seq_len):
        offset = max(m - seq_len, 1 - seq_len)
        size = abs(offset)
        if size > middle:
            ratio = math.log(size / middle) / math.log((2 * side - 1) / middle)
            size = int(math.ceil(ratio * (middle - 1))) + middle
        rows.append(side + (size if offset > 0 else -size))
    return np.array(rows, dtype=np.int32)


def lane_iota(rows=1):
    return lax.broadcasted_iota(jnp.int32, (rows, LANES), 1)


def member_chunk(words, c, last):
    return (last - words == lane_iota(words.shape[0]) + c * LANES).astype(f32).astype(bf16)


def id_bases(rel_ref, base):
    seq = rel_ref.shape[0]
    chunks = seq // LANES
    last = chunks * 2 - 2
    for g in range(seq // HALF):
        for c in range(chunks):
            block = rel_ref[g * HALF : (g + 1) * HALF, c * LANES : (c + 1) * LANES]
            base[g * chunks + c] = jnp.minimum(jnp.min(block) // HALF, last)


def both_alignments(table):
    return jnp.concatenate([table, table[HALF:], table[:HALF]], axis=0)


def longest(rows):
    wide = rows.astype(f32)
    return jnp.sqrt(jnp.max(jnp.sum(wide * wide, axis=1, keepdims=True)))


def pack_heads(first, second, dest, top):
    top = jnp.maximum(top, 1e-30)
    scale = 32000.0 / top
    upper = (first * scale).astype(jnp.int32)
    lower = (second * scale).astype(jnp.int32)
    dest[...] = upper * 65536 + lower
    return top * (1.0 / 32000.0)


def unpack_heads(words, step):
    lower = lax.shift_right_arithmetic(lax.shift_left(words, 16), 16)
    return words.astype(f32) * (step * (1.0 / 65536.0)), lower.astype(f32) * step


def picked_words(source, rel_ref, base, rows, c):
    chunks = rel_ref.shape[1] // LANES
    first = base[(rows.start // HALF) * chunks + c]
    place = rel_ref[rows, c * LANES : (c + 1) * LANES] - first * HALF
    index = place & (LANES - 1)
    at = pl.multiple_of((first % 2) * (chunks * LANES) + (first // 2) * LANES, LANES)
    near = jnp.take_along_axis(source[rows, pl.ds(at, LANES)], index, axis=1)
    at = pl.multiple_of(at + LANES, LANES)
    far = jnp.take_along_axis(source[rows, pl.ds(at, LANES)], index, axis=1)
    return jnp.where(place < LANES, near, far)


def unshift_in_order(sources, words_ref, base, dest):
    seq = words_ref.shape[0]
    chunks = seq // LANES
    lane = lane_iota()
    zero = jnp.zeros((ROWS, LANES), f32)
    for g in range(chunks):
        first = base[g]
        for sub in range(LANES // ROWS):
            start = g * LANES + sub * ROWS
            rows = slice(start, start + ROWS)
            place = lane - 1 - words_ref[rows, :] + first * LANES
            index = place & (LANES - 1)
            near = place >= 0
            mid = place >= -LANES
            for a, source in enumerate(sources):
                turned = [
                    jnp.take_along_axis(
                        source[rows, c * LANES : (c + 1) * LANES], index, axis=1
                    )
                    for c in range(chunks)
                ]
                turned = [zero, zero] + turned + [zero, zero]
                for c in range(chunks + 2):
                    value = jnp.where(near, turned[c + 2], jnp.where(mid, turned[c + 1], turned[c]))
                    at = pl.multiple_of((first + c) * LANES, LANES)
                    dest[a, rows, pl.ds(at, LANES)] = value.astype(bf16)


def group_bases(words, base):
    seq = words.shape[0]
    for g in range(seq // LANES):
        base[g] = (jnp.min(words[g * LANES : (g + 1) * LANES]) + 1) // LANES


def softmax_weights(scores):
    factor = math.log2(math.e) / math.sqrt(3.0 * HEAD)
    top = jnp.max(functools.reduce(jnp.maximum, scores), axis=1, keepdims=True)
    return [jnp.exp2((score - top) * factor) for score in scores]


def head_lanes(a):
    return (lane_iota() < HEAD) if a == 0 else (lane_iota() >= HEAD)


def row_of(ref):
    return ref[...].reshape(1, ref.shape[0])


def norm_stats(values):
    centered = values - jnp.mean(values, axis=1, keepdims=True)
    inv_std = lax.rsqrt(jnp.mean(centered * centered, axis=1, keepdims=True) + norm_eps)
    return centered * inv_std, inv_std


def norm_backward(upstream, normed, inv_std, norm_gain):
    scaled = upstream * norm_gain
    adjusted = (
        scaled
        - jnp.mean(scaled, axis=1, keepdims=True)
        - normed * jnp.mean(scaled * normed, axis=1, keepdims=True)
    )
    return inv_std * adjusted, col_sum(upstream * normed), col_sum(upstream)


def col_sum(values):
    return jnp.sum(values, axis=0, keepdims=True)


def normal_cdf(pre_act):
    return 0.5 * (1.0 + lax.erf(pre_act * (1.0 / math.sqrt(2.0))))


def project_kernel(
    pick_ref, x_ref, rel_ref, wq_ref, wk_ref, wv_ref, bq_ref, bk_ref, bv_ref,
    q_ref, k_ref, v_ref, pq_ref, pk_ref, qpick_ref, xpick_ref,
):
    @pl.when(pl.program_id(0) == 0)
    def _():
        xpick_ref[...] = dot_nn(pick_ref[...], x_ref[...]).astype(bf16)

    for source, weight, bias, out in (
        (xpick_ref, wq_ref, bq_ref, qpick_ref),
        (x_ref, wk_ref, bk_ref, k_ref),
        (rel_ref, wk_ref, bk_ref, pk_ref),
        (rel_ref, wq_ref, bq_ref, pq_ref),
        (x_ref, wq_ref, bq_ref, q_ref),
        (x_ref, wv_ref, bv_ref, v_ref),
    ):
        out[...] = (dot_nn(source[...], weight[...]) + row_of(bias)).astype(bf16)


def project(pick, x, rel_table, weights, biases):
    width = x.shape[1]
    group = 2 * LANES
    whole = lambda value: pl.BlockSpec(value.shape, lambda n: (0, 0))
    col = lambda value: pl.BlockSpec((value.shape[0], group), lambda n: (0, n))
    outs = [x, x, x, rel_table, rel_table, pick]
    return pl.pallas_call(
        project_kernel,
        grid=(width // group,),
        in_specs=[whole(pick), whole(x), whole(rel_table)]
        + [col(value) for value in weights]
        + [pl.BlockSpec((group,), lambda n: (n,))] * 3,
        out_specs=[col(value) for value in outs]
        + [pl.BlockSpec((pick.shape[0], width), lambda n: (0, 0))],
        out_shape=[jax.ShapeDtypeStruct((value.shape[0], width), bf16) for value in outs + [pick]],
        compiler_params=PARAMS,
        cost_estimate=lasting(6.0),
        name="project",
    )(pick, x, rel_table, *weights, *biases)


def picked_kernel(
    pos_ref, rel_ref, qc_ref, k_ref, v_ref, pk_ref, pq_ref,
    x_ref, wo_ref, bo_ref, gain_ref, bias_ref,
    ctx_ref, prob_ref, key_ref, word_ref, wordc_ref, normed_ref, inv_ref, low_ref,
    packed, cpick, relc, keyc, attn, base,
):
    seq = k_ref.shape[0]
    picks = qc_ref.shape[0]
    chunks = seq // LANES

    @pl.when(pl.program_id(0) == 0)
    def _():
        row = lax.broadcasted_iota(jnp.int32, (seq, seq), 0)
        col = lax.broadcasted_iota(jnp.int32, (seq, seq), 1)
        side = pk_ref.shape[0] // 2
        step = jnp.sum(jnp.where(col == row - 1, rel_ref[...] - side, 0), axis=1, keepdims=True)
        steps = jnp.broadcast_to(step.astype(f32), (seq, LANES)).astype(bf16)
        word_ref[...] = dot_nn((col <= row).astype(f32).astype(bf16), steps).astype(jnp.int32)
        id_bases(rel_ref, base)
        for n in range(picks):
            place = jnp.maximum(pos_ref[n], 0)
            relc[n : n + 1, :] = rel_ref[pl.ds(place, 1), :]
            wordc_ref[n : n + 1, :] = word_ref[pl.ds(place, 1), :]

    zero = jnp.zeros((), bf16)
    table = both_alignments(pq_ref[...])
    keys = [dot_nt(jnp.where(head_lanes(a), k_ref[...], zero), table) for a in range(2)]
    unit = pack_heads(keys[0], keys[1], packed, longest(k_ref[...]) * longest(pq_ref[...]))
    for a in range(2):
        cpick[a] = dot_nt(jnp.where(head_lanes(a), qc_ref[...], zero), pk_ref[...])
    for g in range(chunks):
        for c in range(chunks):
            parts = []
            for start in range(g * LANES, (g + 1) * LANES, ROWS):
                parts.append(picked_words(packed, rel_ref, base, slice(start, start + ROWS), c))
            block = jnp.concatenate(parts, axis=0).T
            for a, value in enumerate(unpack_heads(block, unit)):
                key_ref[a, c * LANES : (c + 1) * LANES, g * LANES : (g + 1) * LANES] = value

    for n in range(picks):
        place = jnp.maximum(pos_ref[n], 0)
        for a in range(2):
            keyc[a, n : n + 1, :] = key_ref[a, pl.ds(place, 1), :]
    for a in range(2):
        mine = head_lanes(a)
        direct = dot_nt(jnp.where(mine, qc_ref[...], zero), k_ref[...])
        scores = []
        for c in range(chunks):
            ids = relc[:, c * LANES : (c + 1) * LANES]
            index = ids & (LANES - 1)
            value = jnp.take_along_axis(cpick[a, :, :LANES], index, axis=1)
            for n in range(1, pk_ref.shape[0] // LANES):
                other = cpick[a, :, n * LANES : (n + 1) * LANES]
                value = jnp.where(
                    ids >= n * LANES, jnp.take_along_axis(other, index, axis=1), value
                )
            cols = slice(c * LANES, (c + 1) * LANES)
            scores.append(direct[:, cols] + value + keyc[a, :, cols])
        weights = softmax_weights(scores)
        inverse = 1.0 / jnp.sum(sum(weights[1:], weights[0]), axis=1, keepdims=True)
        probs = jnp.concatenate([(weight * inverse).astype(bf16) for weight in weights], axis=1)
        prob_ref[a] = probs
        mixed = dot_nn(probs, v_ref[...]).astype(bf16)
        ctx_ref[...] = mixed if a == 0 else jnp.where(mine, mixed, ctx_ref[...])

    part = dot_nn(ctx_ref[...], wo_ref[...])

    @pl.when(pl.program_id(0) == 0)
    def _():
        attn[...] = x_ref[...].astype(f32) + row_of(bo_ref) + part

    @pl.when(pl.program_id(0) > 0)
    def _():
        attn[...] += part

    @pl.when(pl.program_id(0) == pl.num_programs(0) - 1)
    def _():
        normed, inv_std = norm_stats(attn[...])
        normed_ref[...] = normed
        inv_ref[...] = jnp.broadcast_to(inv_std, (picks, LANES))
        low_ref[...] = (normed * row_of(gain_ref) + row_of(bias_ref)).astype(bf16)


def attend_picked(
    positions, rel_ids, q_pick, k, v, pos_query, pos_key, x_pick, w_out, b_out, gain, bias
):
    seq, width = k.shape
    picks = q_pick.shape[0]
    table = pos_key.shape[0]
    pairs = width // LANES
    whole = lambda rows, cols: pl.BlockSpec((rows, cols), lambda h: (0, 0))
    line = pl.BlockSpec((width,), lambda h: (0,))
    col = lambda rows: pl.BlockSpec((rows, LANES), lambda h: (0, h))
    heads = lambda rows: pl.BlockSpec((2, rows, seq), lambda h: (h, 0, 0))
    return pl.pallas_call(
        picked_kernel,
        grid=(pairs,),
        in_specs=[
            pl.BlockSpec(memory_space=pltpu.SMEM), whole(seq, seq),
            col(picks), col(seq), col(seq), col(table), col(table),
            whole(picks, width), pl.BlockSpec((LANES, width), lambda h: (h, 0)), line, line, line,
        ],
        out_specs=[
            col(picks), heads(picks), heads(seq), whole(seq, LANES), whole(picks, LANES),
            whole(picks, width), whole(picks, LANES), whole(picks, width),
        ],
        out_shape=[
            jax.ShapeDtypeStruct((picks, width), bf16),
            jax.ShapeDtypeStruct((2 * pairs, picks, seq), bf16),
            jax.ShapeDtypeStruct((2 * pairs, seq, seq), f32),
            jax.ShapeDtypeStruct((seq, LANES), jnp.int32),
            jax.ShapeDtypeStruct((picks, LANES), jnp.int32),
            jax.ShapeDtypeStruct((picks, width), f32),
            jax.ShapeDtypeStruct((picks, LANES), f32),
            jax.ShapeDtypeStruct((picks, width), bf16),
        ],
        scratch_shapes=[
            pltpu.VMEM((seq, 2 * table), jnp.int32),
            pltpu.VMEM((2, picks, table), f32),
            pltpu.VMEM((picks, seq), jnp.int32),
            pltpu.VMEM((2, picks, seq), f32),
            pltpu.VMEM((picks, width), f32),
            pltpu.SMEM((seq // HALF * (seq // LANES),), jnp.int32),
        ],
        compiler_params=PARAMS,
        cost_estimate=lasting(5.0 * pairs),
        name="attend_picked",
    )(
        positions, rel_ids, q_pick, k, v, pos_key, pos_query, x_pick, w_out, b_out, gain, bias
    )


def full_kernel(rel_ref, q_ref, k_ref, v_ref, pk_ref, key_ref, ctx_ref, *scratch):
    seq = rel_ref.shape[0]
    chunks = seq // LANES
    base, scratch = scratch[-1], scratch[:-1]
    count = len(scratch) // 3

    @pl.when(pl.program_id(0) == 0)
    def _():
        id_bases(rel_ref, base)

    zero = jnp.zeros((), bf16)
    units = []
    for n in range(count):
        packed, direct, low = scratch[3 * n : 3 * n + 3]
        lanes = slice(n * LANES, (n + 1) * LANES)
        q, pos = q_ref[:, lanes], pk_ref[:, lanes]
        table = both_alignments(pos)
        far = []
        for a in range(2):
            q_a = jnp.where(head_lanes(a), q, zero)
            far.append(dot_nt(q_a, table))
            direct[a] = dot_nt(q_a, k_ref[:, lanes])
        units.append(pack_heads(far[0], far[1], packed, longest(q) * longest(pos)))
    for n in range(count):
        packed, direct, low = scratch[3 * n : 3 * n + 3]
        lanes = slice(n * LANES, (n + 1) * LANES)
        for start in range(0, seq, HALF):
            rows = slice(start, start + HALF)
            scores = [[], []]
            for c in range(chunks):
                cols = slice(c * LANES, (c + 1) * LANES)
                values = unpack_heads(picked_words(packed, rel_ref, base, rows, c), units[n])
                for a in range(2):
                    scores[a].append(
                        values[a] + direct[a, rows, cols] + key_ref[2 * n + a, rows, cols]
                    )
            for a in range(2):
                for c, weight in enumerate(softmax_weights(scores[a])):
                    low[a, rows, c * LANES : (c + 1) * LANES] = weight.astype(bf16)
        v = v_ref[:, lanes]
        mixed = [
            dot_nn(low[a], jnp.where(head_lanes(a), v, jnp.ones((), bf16))) for a in range(2)
        ]
        upper = head_lanes(0)
        totals = pltpu.roll(jnp.where(upper, mixed[1], mixed[0]), HEAD, 1)
        ctx_ref[:, lanes] = (jnp.where(upper, mixed[0], mixed[1]) * (1.0 / totals)).astype(bf16)


def attend_full(rel_ids, q, k, v, pos_key, key_scores, first, pairs):
    seq = k.shape[0]
    table = pos_key.shape[0]
    per = AT_ONCE
    wide = per * LANES
    col = lambda rows: pl.BlockSpec((rows, wide), lambda h: (0, h + first // per))
    return pl.pallas_call(
        full_kernel,
        grid=(pairs // per,),
        in_specs=[
            pl.BlockSpec((seq, seq), lambda h: (0, 0)),
            col(seq), col(seq), col(seq), col(table),
            pl.BlockSpec((2 * per, seq, seq), lambda h: (h + first // per, 0, 0)),
        ],
        out_specs=pl.BlockSpec((seq, wide), lambda h: (0, h)),
        out_shape=jax.ShapeDtypeStruct((seq, pairs * LANES), bf16),
        scratch_shapes=[
            pltpu.VMEM((seq, 2 * table), jnp.int32),
            pltpu.VMEM((2, seq, seq), f32),
            pltpu.VMEM((2, seq, seq), bf16),
        ]
        * per
        + [pltpu.SMEM((seq // HALF * (seq // LANES),), jnp.int32)],
        compiler_params=PARAMS,
        cost_estimate=lasting(4.2 * pairs),
        name="attend_full",
    )(rel_ids, q, k, v, pos_key, key_scores)


def back_kernel(
    row_ref, word_ref, wordc_ref, qc_ref, k_ref, v_ref, prob_ref, pk_ref, pq_ref,
    dz2_ref, mine_ref, got_ref, normed_ref, inv_ref, gain_ref, wo_ref, early_ref,
    dq_ref, dk_ref, dv_ref, dpos_ref, dz1_ref, dattn_ref, sum_ref,
    side, sidec, moved, movedc, expand, shrink, base,
):
    seq = k_ref.shape[0]
    picks = qc_ref.shape[0]
    table = pk_ref.shape[0]
    chunks = seq // LANES

    @pl.when(pl.program_id(0) == 0)
    def _():
        words = word_ref[...]
        for c in range(chunks):
            side[:, c * LANES : (c + 1) * LANES] = member_chunk(words, c, seq - 1)
            sidec[:, c * LANES : (c + 1) * LANES] = member_chunk(wordc_ref[...], c, seq - 1)
        group_bases(words, base)
        moved[...] = jnp.zeros_like(moved)
        edge = expand.shape[1]
        for n, start in ((0, 0), (1, 2 * seq - edge)):
            ids = row_ref[start : start + edge, :] - n * (table - LANES)
            chosen = (ids == lane_iota(edge)).astype(f32).astype(bf16)
            expand[n] = chosen
            shrink[n] = chosen.T
        dh1 = dz2_ref[...] + mine_ref[...].astype(f32) + got_ref[...].astype(f32)
        dz1, g_gain, g_bias = norm_backward(dh1, normed_ref[...], inv_ref[:, :1], row_of(gain_ref))
        dz1_ref[...] = dz1
        dattn = dz1.astype(bf16)
        dattn_ref[...] = dattn
        sum_ref[...] = jnp.concatenate(
            [col_sum(dattn.astype(f32)), g_gain, g_bias, early_ref[:5]], axis=0
        )

    lane = lane_iota()
    scale = 1.0 / math.sqrt(3.0 * HEAD)
    zero = jnp.zeros((), bf16)
    heads = range(2)
    upper = head_lanes(0)
    join = lambda pair: jnp.where(upper, pair[0], pair[1])
    side[:, seq:] = k_ref[...]
    sidec[:, seq:] = qc_ref[...]
    dctx = dot_nt(dattn_ref[...], wo_ref[...]).astype(bf16)
    dprobs = [dot_nt(jnp.where(head_lanes(a), dctx, zero), v_ref[...]) for a in heads]

    def widened(ref):
        ends = [
            dot_nn(expand[n], ref[at : at + LANES, :]).astype(bf16)
            for n, at in ((0, 0), (1, table - LANES))
        ]
        return jnp.concatenate([ends[0], ref[LANES : table - LANES, :], ends[1]], axis=0)

    far_key, far_query = widened(pk_ref), widened(pq_ref)
    gs = []
    for a in heads:
        probs = prob_ref[a].astype(f32)
        prod = probs * dprobs[a]
        gs.append(((prod - probs * jnp.sum(prod, axis=1, keepdims=True)) * scale).astype(bf16))
    outs = [dot_tn(gs[a], sidec[...]) for a in heads]
    outcs = [dot_nn(gs[a], side[...]) for a in heads]
    dv_ref[...] = join([dot_tn(prob_ref[a], dctx) for a in heads]).astype(bf16)
    place = lane - 1 - wordc_ref[...]
    index = place & (LANES - 1)
    blank = jnp.zeros((picks, LANES), f32)
    for a in heads:
        turned = [
            jnp.take_along_axis(outcs[a][:, c * LANES : (c + 1) * LANES], index, axis=1)
            for c in range(chunks)
        ]
        for c in range(2 * chunks):
            value = turned[c] if c < chunks else blank
            for n in range(1, chunks + 1):
                other = turned[c - n] if 0 <= c - n < chunks else blank
                value = jnp.where(place < -LANES * (n - 1), other, value)
            movedc[a, :, c * LANES : (c + 1) * LANES] = value.astype(bf16)
    unshift_in_order(outs, word_ref, base, moved)
    dq = [outcs[a][:, seq:] + dot_nn(movedc[a], far_key) for a in heads]
    dq_ref[...] = join(dq).astype(bf16)
    dk = [outs[a][:, seq:] + dot_nn(moved[a, :, : 2 * seq], far_query) for a in heads]
    dk_ref[...] = join(dk).astype(bf16)
    far = [
        join([dot_tn(movedc[a], qc_ref[...]) for a in heads]),
        join([dot_tn(moved[a, :, : 2 * seq], k_ref[...]) for a in heads]),
    ]
    edge = expand.shape[1]
    for n, value in enumerate(far):
        value = value.astype(bf16)
        dpos_ref[n, :LANES, :] = dot_nn(shrink[0], value[:edge]).astype(bf16)
        dpos_ref[n, LANES : table - LANES, :] = value[edge : 2 * seq - edge]
        dpos_ref[n, table - LANES :, :] = dot_nn(shrink[1], value[2 * seq - edge :]).astype(bf16)


def attend_back(
    table_of, words, words_pick, q_pick, k, v, probs, pos_query, pos_key,
    dz2, mine, got, normed, inv_std, gain, w_out, early,
):
    seq, width = k.shape
    picks = q_pick.shape[0]
    table = pos_key.shape[0]
    pairs = width // LANES
    edge = seq - table // 4
    whole = lambda value: pl.BlockSpec(value.shape, lambda h: (0,) * value.ndim)
    col = lambda rows: pl.BlockSpec((rows, LANES), lambda h: (0, h))
    shape = lambda rows: jax.ShapeDtypeStruct((rows, width), bf16)
    return pl.pallas_call(
        back_kernel,
        grid=(pairs,),
        in_specs=[
            whole(table_of), whole(words), whole(words_pick),
            col(picks), col(seq), col(seq),
            pl.BlockSpec((2, picks, seq), lambda h: (h, 0, 0)),
            col(table), col(table),
            whole(dz2), whole(mine), whole(got), whole(normed), whole(inv_std), whole(gain),
            pl.BlockSpec((LANES, width), lambda h: (h, 0)), whole(early),
        ],
        out_specs=[
            col(picks), col(seq), col(seq),
            pl.BlockSpec((2, table, LANES), lambda h: (0, 0, h)),
            whole(dz2), whole(dz2), whole(early),
        ],
        out_shape=[
            shape(picks), shape(seq), shape(seq),
            jax.ShapeDtypeStruct((2, table, width), bf16),
            jax.ShapeDtypeStruct((picks, width), f32),
            shape(picks),
            jax.ShapeDtypeStruct(early.shape, f32),
        ],
        scratch_shapes=[
            pltpu.VMEM((seq, seq + LANES), bf16),
            pltpu.VMEM((picks, seq + LANES), bf16),
            pltpu.VMEM((2, seq, 2 * seq + 2 * LANES), bf16),
            pltpu.VMEM((2, picks, 2 * seq), bf16),
            pltpu.VMEM((2, edge, LANES), bf16),
            pltpu.VMEM((2, LANES, edge), bf16),
            pltpu.SMEM((seq // LANES,), jnp.int32),
        ],
        compiler_params=PARAMS,
        cost_estimate=lasting(4.0 * pairs),
        name="attend_back",
    )(
        table_of, words, words_pick, q_pick, k, v, probs, pos_key, pos_query,
        dz2, mine, got, normed, inv_std, gain, w_out, early,
    )


def turn_kernel(
    n_all, me_ref, order_ref, x_ref, xpick_ref, cpick_ref, rel_ref, x_out, xpick_out, cpick_out, rel_out
):
    picked = order_rows(order_ref, me_ref, x_ref.shape[1], n_all)
    for ref, out in ((x_ref, x_out), (xpick_ref, xpick_out), (cpick_ref, cpick_out), (rel_ref, rel_out)):
        out[...] = dot_nt(picked, ref[...]).astype(bf16)


def block_rows(ref, me_ref):
    return me_ref[0] ^ jnp.where(me_ref[1] == 0, ref[:, 0:1], ref[:, 1:2])


def order_rows(ref, me_ref, length, n_all):
    source = block_rows(ref, me_ref) * (length // n_all) + ref[:, 2:3]
    spot = lax.broadcasted_iota(jnp.int32, (ref.shape[0], length), 1)
    return (spot == source).astype(f32).astype(bf16)


def turn_blocks(n_all, me, order, x, x_pick, ctx_pick, rel_table):
    width = x.shape[1]
    group = 2 * LANES
    whole = lambda value: pl.BlockSpec(value.shape, lambda n: (0, 0))
    row = lambda count: pl.BlockSpec((group, count), lambda n: (n, 0))
    given = [x, x_pick, ctx_pick, rel_table]
    return pl.pallas_call(
        functools.partial(turn_kernel, n_all),
        grid=(width // group,),
        in_specs=[pl.BlockSpec(memory_space=pltpu.SMEM), row(LANES)]
        + [whole(value) for value in given],
        out_specs=[row(value.shape[0]) for value in given],
        out_shape=[jax.ShapeDtypeStruct(value.shape[::-1], bf16) for value in given],
        compiler_params=PARAMS,
        cost_estimate=lasting(5.2),
        name="turn_blocks",
    )(me, order, *given)


def norm_picked_kernel(
    normed_ref, gain1_ref, bias1_ref, mine_ref, got_ref, bdown_ref, gain2_ref, grad_ref, pick_ref,
    dz2_ref, low_ref, sum_ref,
):
    h1 = normed_ref[...] * row_of(gain1_ref) + row_of(bias1_ref)
    branch = mine_ref[...].astype(f32) + got_ref[...].astype(f32) + row_of(bdown_ref)
    normed, inv_std = norm_stats(h1 + branch)
    used = jnp.sum(pick_ref[...].astype(f32), axis=1, keepdims=True)
    cot = jnp.where(used > 0.0, grad_ref[...].astype(f32), 0.0)
    dz2, g_gain, g_bias = norm_backward(cot, normed, inv_std, row_of(gain2_ref))
    dz2_ref[...] = dz2
    low = dz2.astype(bf16)
    low_ref[...] = low
    sum_ref[...] = jnp.concatenate(
        [col_sum(low.astype(f32)), g_gain, g_bias, jnp.zeros((5, h1.shape[1]), f32)], axis=0
    )


def norm_picked(normed, gain1, bias1, mine, got, b_down, gain2, grads, pick):
    picks, width = normed.shape
    return pl.pallas_call(
        norm_picked_kernel,
        out_shape=[
            jax.ShapeDtypeStruct((picks, width), f32),
            jax.ShapeDtypeStruct((picks, width), bf16),
            jax.ShapeDtypeStruct((8, width), f32),
        ],
        compiler_params=PARAMS,
        cost_estimate=lasting(2.4),
        name="norm_picked",
    )(normed, gain1, bias1, mine, got, b_down, gain2, grads, pick)


def ffn_full_kernel(
    x_ref, ctx_ref, ctx2_ref, wo_ref, bo_ref, gain1_ref, bias1_ref, bdown_ref, gain2_ref, bias2_ref,
    bin_ref, bin2_ref, bin3_ref, win_ref, down_ref, win2_ref, down2_ref, win3_ref, down3_ref,
    out_ref, h1, low, total, win_here, down_here, win_sem, down_sem,
):
    rows, width = x_ref.shape
    tile = win_here.shape[2]
    parts = [(win_ref, down_ref, bin_ref, n * tile) for n in range(win_ref.shape[1] // tile)]
    parts += [(win2_ref, down2_ref, bin2_ref, 0), (win3_ref, down3_ref, bin3_ref, 0)]

    def copies(n):
        w_ref, d_ref, _, at = parts[n]
        return (
            pltpu.make_async_copy(w_ref.at[:, at : at + tile], win_here.at[n], win_sem.at[n]),
            pltpu.make_async_copy(d_ref.at[at : at + tile, :], down_here.at[n], down_sem.at[n]),
        )

    for n in range(len(parts)):
        for copy in copies(n):
            copy.start()
    attn = dot_nn(ctx_ref[...], wo_ref[: ctx_ref.shape[1]]) + dot_nn(
        ctx2_ref[...], wo_ref[ctx_ref.shape[1] :]
    )
    normed, _ = norm_stats(x_ref[...].astype(f32) + (attn + row_of(bo_ref)))
    value = normed * row_of(gain1_ref) + row_of(bias1_ref)
    h1[...] = value
    low[...] = value.astype(bf16)
    step = rows // 2
    for n in range(len(parts)):
        for copy in copies(n):
            copy.wait()
        bias = parts[n][2][:, parts[n][3] : parts[n][3] + tile]
        for at in range(0, rows, step):
            pre = dot_nn(low[at : at + step], win_here[n]) + bias
            part = dot_nn((pre * normal_cdf(pre)).astype(bf16), down_here[n])
            total[at : at + step] = part if n == 0 else total[at : at + step] + part
    normed, _ = norm_stats(h1[...] + (total[...] + row_of(bdown_ref)))
    out_ref[...] = (normed * row_of(gain2_ref) + row_of(bias2_ref)).astype(bf16)


def ffn_full(x, ctx, w_out, b_out, gain1, bias1, shards, b_down, gain2, bias2):
    rows, width = x.shape
    tile = shards[1][0].shape[1]
    count = shards[0][0].shape[1] // tile + 2
    held = [x, ctx[0], ctx[1], w_out, b_out, gain1, bias1, b_down, gain2, bias2]
    held += [shard[2] for shard in shards]
    moved = [value for shard in shards for value in shard[:2]]
    return pl.pallas_call(
        ffn_full_kernel,
        in_specs=[pl.BlockSpec(memory_space=pltpu.VMEM)] * len(held)
        + [pl.BlockSpec(memory_space=pl.ANY)] * len(moved),
        out_specs=pl.BlockSpec(memory_space=pltpu.VMEM),
        out_shape=jax.ShapeDtypeStruct((rows, width), bf16),
        scratch_shapes=[
            pltpu.VMEM((rows, width), f32), pltpu.VMEM((rows, width), bf16), pltpu.VMEM((rows, width), f32),
            pltpu.VMEM((count, width, tile), bf16), pltpu.VMEM((count, tile, width), bf16),
            pltpu.SemaphoreType.DMA((count,)), pltpu.SemaphoreType.DMA((count,)),
        ],
        compiler_params=PARAMS,
        cost_estimate=lasting(10.9),
        name="ffn_full",
    )(*held, *moved)


def token_grads_kernel(pick_ref, dz1_ref, dq_ref, dk_ref, dv_ref, wq_ref, wk_ref, wv_ref, out_ref):
    sparse = dz1_ref[...] + dot_nt(dq_ref[...], wq_ref[...])
    upper = sparse.astype(bf16)
    lower = (sparse - upper.astype(f32)).astype(bf16)
    out_ref[...] = (
        dot_nt(dk_ref[...], wk_ref[...])
        + dot_nt(dv_ref[...], wv_ref[...])
        + dot_tn(pick_ref[...], upper)
        + dot_tn(pick_ref[...], lower)
    )


def token_grads(pick, dz1, dq, dk, dv, w_query, w_key, w_value):
    seq, width = dk.shape
    group = 2 * LANES
    whole = lambda value: pl.BlockSpec(value.shape, lambda n: (0, 0))
    col = lambda rows: pl.BlockSpec((rows, group), lambda n: (0, n))
    row = pl.BlockSpec((group, width), lambda n: (n, 0))
    return pl.pallas_call(
        token_grads_kernel,
        grid=(width // group,),
        in_specs=[whole(pick), col(dz1.shape[0]), whole(dq), whole(dk), whole(dv), row, row, row],
        out_specs=col(seq),
        out_shape=jax.ShapeDtypeStruct((seq, width), f32),
        compiler_params=PARAMS,
        cost_estimate=lasting(5.9),
        name="token_grads",
    )(pick, dz1, dq, dk, dv, w_query, w_key, w_value)


def grads_kernel(
    n_all, n_ffn, unit, me_ref, order_ref, relorder_ref, taker_ref,
    x_ref, rel_ref, xpick_ref, cpick_ref, dpos_ref,
    dq_ref, dk_ref, dv_ref, dattn_ref, dposk_ref, dposq_ref, wq_ref, wk_ref,
    early_ref, bin_ref, bin2_ref, kept_ref, sent_ref, dpos,
):
    width = x_ref.shape[0]
    group = 2 * LANES

    def put(at, value):
        value = value.astype(bf16)
        for n in range(value.shape[0] // group):
            kept_ref[at + n] = value[n * group : n * group + LANES]
            sent_ref[at + n] = value[n * group + LANES : (n + 1) * group]

    @pl.when(pl.program_id(0) == 0)
    def _():
        rows = order_rows(relorder_ref, me_ref, dpos_ref.shape[1], n_all)
        for n in range(2):
            dpos[n] = dot_nn(rows, dpos_ref[n]).astype(bf16)

    count = width // group
    put(0, dot_nn(xpick_ref[...], dq_ref[...]) + dot_nn(rel_ref[...], dposq_ref[0]))
    put(count, dot_nn(x_ref[...], dk_ref[...]) + dot_nn(rel_ref[...], dposk_ref[0]))
    put(2 * count, dot_nn(x_ref[...], dv_ref[...]))
    put(3 * count, dot_nn(cpick_ref[...], dattn_ref[...]))
    put(4 * count, dot_nt(dpos[0], wk_ref[...]) + dot_nt(dpos[1], wq_ref[...]))

    total = lambda value: col_sum(value.astype(f32))
    values = jnp.concatenate(
        [
            total(dq_ref[...]) + total(dposq_ref[0]),
            total(dk_ref[...]) + total(dposk_ref[0]),
            total(dv_ref[...]),
            early_ref[:6],
            bin_ref[:1],
            bin2_ref[:1],
            jnp.zeros((5, group), f32),
        ],
        axis=0,
    )
    block = block_rows(order_ref[:group, :], me_ref)
    ours = (block % n_ffn) == (me_ref[0] % n_ffn)
    tok_place = jnp.where(ours, block // n_ffn, -1)
    first = 4 * count + dpos.shape[1] // group
    row = lax.broadcasted_iota(jnp.int32, (group, 1), 0) % unit
    for n in range(16 // unit):
        rows = slice(n * unit, (n + 1) * unit)
        spread = lambda value: jnp.concatenate([value[rows]] * (group // unit), axis=0)
        taker = jnp.where(row + n * unit < VECTORS, block, tok_place)
        put(first + n, jnp.where(spread(taker_ref[...]) == taker, spread(values), 0.0))


def weight_grads(
    n_all, n_ffn, unit, me, order, rel_order, takers, x, rel, x_pick, c_pick, dpos, dq, dk, dv, dattn,
    w_query, w_key, early, bins,
):
    width, seq = x.shape
    group = 2 * LANES
    planes = 4 * (width // group) + dpos.shape[1] // group + 16 // unit
    whole = lambda value: pl.BlockSpec(value.shape, lambda n: (0,) * value.ndim)
    col = lambda value: pl.BlockSpec((value.shape[0], group), lambda n: (0, n))
    row = lambda value: pl.BlockSpec((group, value.shape[1]), lambda n: (n, 0))
    plane = lambda t: pl.BlockSpec((1, dpos.shape[1], group), lambda n: (t, 0, n))
    block = pl.BlockSpec((planes, LANES, group), lambda n: (0, 0, n))
    return pl.pallas_call(
        functools.partial(grads_kernel, n_all, n_ffn, unit),
        grid=(width // group,),
        in_specs=[
            pl.BlockSpec(memory_space=pltpu.SMEM), whole(order), whole(rel_order), col(takers),
            whole(x), whole(rel), whole(x_pick), whole(c_pick), whole(dpos),
            col(dq), col(dk), col(dv), col(dattn), plane(0), plane(1), row(w_query), row(w_key),
            col(early), col(bins), pl.BlockSpec((8, group), lambda n: (0, n + width // group)),
        ],
        out_specs=[block] * 2,
        out_shape=[jax.ShapeDtypeStruct((planes, LANES, width), bf16)] * 2,
        scratch_shapes=[pltpu.VMEM(dpos.shape, bf16)],
        compiler_params=PARAMS,
        cost_estimate=lasting(11.7),
        name="weight_grads",
    )(
        me, order, rel_order, takers, x, rel, x_pick, c_pick, dpos, dq, dk, dv, dattn, dpos, dpos,
        w_query, w_key, early, bins, bins,
    )


def swap(values, axis, bit):
    size = lax.axis_size(axis)
    return lax.ppermute(values, axis, [(n, n ^ bit) for n in range(size)])


def after(values, *others):
    return lax.optimization_barrier((values, others))[0]


class Halving:
    def __init__(self, axes, core, near, size):
        rest = [1 << n for n in range(size.bit_length() - 1) if (1 << n) != core]
        near = [bit for bit in near if bit in rest]
        rest = [bit for bit in rest if bit not in near]
        turned = near[-1:] + near[:-1]
        self.axes, self.core, self.size = axes, core, size
        self.orders = [[core] + near + rest, [core] + turned + rest]
        self.steps = len(self.orders[0])
        self.me = lax.axis_index(axes)
        self.upper = (self.me // core) % 2

    def core_of(self, place):
        return (place // self.core) % 2

    def send(self, values, step):
        pairs = [(n, n ^ self.orders[self.core_of(n)][step]) for n in range(self.size)]
        return lax.ppermute(values, self.axes, pairs)

    def relative(self, upper):
        masks = []
        for place in range(self.size):
            bits = [(place >> (self.steps - 1 - step)) & 1 for step in range(self.steps)]
            order = self.orders[upper ^ bits[0]]
            mask = 0
            for step, bit in enumerate(bits):
                mask ^= bit * order[step]
            masks.append(mask)
        return np.array(masks, np.int32)

    def order(self, length, unit):
        spots = np.arange(length)
        group = self.size * unit
        place = spots % group // unit
        rows = [self.relative(upper)[place] for upper in range(2)]
        rows.append(spots // group * unit + spots % unit)
        return np.stack(rows).astype(np.int32)

    def matrix(self, length, unit):
        first, second, inner = self.order(length, unit)
        source = (self.me ^ jnp.where(self.upper == 0, first, second)) * (length // self.size) + inner
        spot = lax.broadcasted_iota(jnp.int32, (length, length), 0)
        return (spot == source[None, :]).astype(bf16)


def local(
    tokens, rel_ids, mask_pos, grad_vals, w_query, w_key, w_value, w_out, b_query, b_key,
    b_value, b_out, rel_table, ln1_gain, ln1_bias, w_in, b_in, w_down, b_down, ln2_gain, ln2_bias,
):
    assert rel_ids.shape[0] == 1
    seq, width = tokens.shape
    table_rows = rel_table.shape[0]
    hidden_cols = w_in.shape[1]
    pairs = width // LANES
    n_tok = lax.axis_size("tok")
    n_ffn = lax.axis_size("ffn")
    n_all = n_tok * n_ffn
    low = lambda value: value.astype(bf16)
    wide = lambda value: value.astype(f32)
    rel_ids, positions, grad_vals = rel_ids[0], mask_pos[0], grad_vals[0]

    over_all = Halving(("tok", "ffn"), n_ffn, [2 * n_ffn, 1, 4 * n_ffn], n_all)
    own, own_rel = width // n_all, table_rows // n_all
    unit = math.gcd(own, own_rel)
    group = n_all * unit
    over_tok = Halving("tok", 1, [2, 4], n_tok)
    pad = lambda value, count: np.pad(value, ((0, count - value.shape[0]), (0, 0)))
    order = jnp.asarray(pad(over_all.order(width, unit), LANES).T)
    rel_order = jnp.asarray(pad(over_all.order(table_rows, unit), LANES).T)
    spots = np.arange(width)
    takers = [spots // own] * VECTORS
    takers += [(spots + n * width) // (hidden_cols // n_tok) for n in range(hidden_cols // width)]
    takers = np.stack(takers).astype(np.int32)
    takers = jnp.asarray(np.pad(takers, ((0, 16 - takers.shape[0]), (0, 0)), constant_values=-2))
    me = jnp.stack([over_all.me, over_all.upper])
    table_of = jnp.asarray(np.repeat(distance_rows(seq, table_rows)[:, None], LANES, 1))

    core = lax.axis_index("tok") % 2
    half_cols = hidden_cols // 2
    bias_row = b_in.reshape(1, hidden_cols)
    in_half = lax.dynamic_slice_in_dim(w_in, core * half_cols, half_cols, 1)
    down_half = lax.dynamic_slice_in_dim(w_down, core * half_cols, half_cols, 0)

    pick = low(positions[:, None] == lax.broadcasted_iota(jnp.int32, (positions.shape[0], seq), 1))
    q, k, v, pos_query, pos_key, q_pick, x_pick = project(
        pick, tokens, rel_table, (w_query, w_key, w_value), (b_query, b_key, b_value)
    )
    ctx_pick, probs, key_scores, words, words_pick, normed1, inv1, h1_mine = attend_picked(
        positions, rel_ids, q_pick, k, v, pos_query, pos_key, x_pick, w_out, b_out, ln1_gain, ln1_bias
    )

    h1_theirs = swap(h1_mine, "ffn", 1)
    bias_theirs = swap(bias_row, "ffn", 1)
    x_turned, x_pick_turned, c_pick_turned, rel_turned = turn_blocks(
        n_all, me, order, tokens, x_pick, ctx_pick, rel_table
    )
    h1_both = jnp.concatenate([h1_mine, after(h1_theirs, x_turned)], axis=0)
    count = h1_mine.shape[0]
    pre = dot_nn(h1_both, w_in) + b_in
    cdf = normal_cdf(pre)
    hidden = low(pre * cdf)
    slope = cdf + pre * (jnp.exp(-0.5 * pre * pre) * (1.0 / math.sqrt(2.0 * math.pi)))
    part = low(dot_nn(hidden, w_down))
    got = swap(part[count:], "ffn", 1)
    tok_order = over_tok.matrix(width, width // n_tok)
    h1_left = low(dot_nn(h1_both, lax.optimization_barrier(tok_order)))
    in_half = after(in_half, part)
    got = after(got, h1_left, in_half)
    dz2, dffn, early = norm_picked(
        normed1, ln1_gain, ln1_bias, part[:count], got, b_down, ln2_gain, grad_vals, pick
    )
    down_half = after(down_half, dffn)
    dffn_both = jnp.concatenate([dffn, after(swap(dffn, "ffn", 1), down_half)], axis=0)
    dpre = low(dot_nt(dffn_both, w_down) * slope)
    dpart = low(dot_nt(dpre, w_in))
    dgot = swap(dpart[count:], "ffn", 1)

    def halves(values, axis):
        size = values.shape[axis] // 2
        cut = lambda at: lax.slice_in_dim(values, at, at + size, axis=axis)
        return cut(0), cut(size)

    add = lambda one, other: low(wide(one) + wide(other))

    def next_halves(kept, got, axis):
        return [add(one, other) for one, other in zip(halves(kept, axis), halves(got, axis))]

    dpre_later = after(dpre, dpart)
    dffn_left = low(dot_nn(after(dffn_both, dpart), tok_order))
    gb_in = dot_nn(jnp.ones((8, 2 * count), bf16), dpre_later)
    lefts, rights = (h1_left, dffn_left), (dpre_later, hidden)
    middle, quarter = width // 2, width // 4
    ffn_sent = [low(dot_tn(one[:, middle:], other)) for one, other in zip(lefts, rights)]
    dgot, ffn_sent = lax.optimization_barrier((dgot, ffn_sent))
    ffn_got = [over_tok.send(value, 0) for value in ffn_sent]
    far_in = swap(after(in_half, dgot, ffn_sent), "ffn", 1)

    def ffn_piece(at):
        return [
            low(dot_tn(one[:, at : at + quarter], other) + wide(value[at : at + quarter]))
            for one, other, value in zip(lefts, rights, ffn_got)
        ]

    ffn_sent = ffn_piece(quarter)
    ffn_kept = ffn_piece(0)
    ffn_got = [over_tok.send(value, 1) for value in ffn_sent]

    def ffn_next(step, kept, got):
        if step < over_tok.steps:
            pieces = [next_halves(one, other, 0) for one, other in zip(kept, got)]
            return [piece[0] for piece in pieces], [over_tok.send(piece[1], step) for piece in pieces]
        return [add(one, other) for one, other in zip(kept, got)], None

    dq, dk, dv, dpos, dz1, dattn, early = attend_back(
        table_of, words, words_pick, q_pick, k, v, probs, pos_query, pos_key,
        dz2, dpart[:count], after(dgot, in_half, ffn_sent, ffn_kept), normed1, inv1, ln1_gain, w_out, early,
    )
    far_in, ffn_got = after((far_in, ffn_got), dk)
    ffn_kept, ffn_got = ffn_next(2, ffn_kept, ffn_got)
    near_in = swap(far_in, "tok", 1)
    far_down = swap(after(down_half, far_in), "ffn", 1)
    all_kept, all_sent = weight_grads(
        n_all, n_ffn, unit, me, order, rel_order, takers,
        x_turned, rel_turned, x_pick_turned, c_pick_turned, dpos, dq, after(dk, far_in, ffn_kept), dv,
        dattn, w_query, w_key, early, gb_in,
    )
    all_got = over_all.send(all_sent, 0)
    dk_later, dq_later = after((dk, dq), all_sent)
    grad_tokens = token_grads(pick, dz1, dq_later, dk_later, dv, w_query, w_key, w_value)
    all_kept, all_sent = next_halves(all_kept, after(all_got, grad_tokens), 1)
    ffn_step = 3
    ffn_got = after(ffn_got, grad_tokens)

    def attend(first, count, q):
        return attend_full(rel_ids, q, k, v, pos_key, key_scores, first, count)

    ctx = []
    cuts = [(0, FIRST_PAIRS), (FIRST_PAIRS, pairs - FIRST_PAIRS)]
    for step in range(1, over_all.steps):
        all_got = over_all.send(all_sent, step)
        if step <= 2:
            ctx.append(attend(*cuts[step - 1], after(q, all_sent)))
            all_got = after(all_got, ctx[-1])
            if step == 1:
                far_down = after(far_down, ctx[-1])
                near_down = swap(far_down, "tok", 1)
                all_got = after(all_got, far_down)
        elif step == 4:
            biases = [
                lax.dynamic_slice_in_dim(bias_theirs, at * half_cols, half_cols, 1)
                for at in (core, 1 - core)
            ]
            shards = [
                (w_in, w_down, bias_row), (far_in, far_down, biases[0]), (near_in, near_down, biases[1])
            ]
            output = ffn_full(
                after(tokens, all_sent), ctx, w_out, b_out, ln1_gain, ln1_bias, shards,
                b_down, ln2_gain, ln2_bias,
            )
            all_got = after(all_got, output)
        if ffn_step <= over_tok.steps:
            ffn_got = after(ffn_got, all_sent)
            if step <= 2:
                ffn_got = after(ffn_got, ctx[-1])
            ffn_kept, ffn_got = ffn_next(ffn_step, ffn_kept, ffn_got)
            ffn_step += 1
        if step < over_all.steps - 1:
            all_kept, all_sent = next_halves(all_kept, all_got, 1)
        else:
            all_sums = add(all_kept, all_got)

    planes = 4 * (width // group) + table_rows // group
    vectors = wide(all_sums[planes:].reshape(16, width))
    all_sums = all_sums[:planes].reshape(planes * unit, width)
    s_w = [wide(all_sums[n * own : (n + 1) * own]) for n in range(4)]
    s_rel = wide(all_sums[4 * own :])
    s_vec = lax.dynamic_slice_in_dim(vectors[:VECTORS], over_all.me * own, own, 1)
    part = hidden_cols // n_tok
    bins = vectors[VECTORS : VECTORS + hidden_cols // width].reshape(1, hidden_cols)
    s_bin = lax.dynamic_slice_in_dim(bins, lax.axis_index("tok") * part, part, 1)
    return (
        output,
        grad_tokens,
        s_w[0],
        s_w[1],
        s_w[2],
        s_w[3],
        s_vec[0],
        s_vec[1],
        s_vec[2],
        s_vec[3],
        s_rel,
        s_vec[4],
        s_vec[5],
        wide(ffn_kept[0]),
        s_bin,
        jnp.transpose(wide(ffn_kept[1])),
        s_vec[6],
        s_vec[7],
        s_vec[8],
    )


def solution(mesh):
    every = ("tok", "ffn")
    placed = (
        P(every, None), P(every, None, None), P(every, None), P(every, None, None),
        P(), P(), P(), P(), P(), P(), P(), P(), P(), P(), P(),
        P(None, "ffn"), P("ffn"), P("ffn", None), P(), P(), P(),
    )
    given = (
        P(every, None), P(every, None),
        P(every, None), P(every, None), P(every, None), P(every, None),
        P(every), P(every), P(every), P(every),
        P(every, None), P(every), P(every),
        P("tok", "ffn"), P("ffn", "tok"), P("ffn", "tok"),
        P(every), P(every), P(every),
    )
    return jax.shard_map(local, mesh=mesh, in_specs=placed, out_specs=given, check_vma=False)
```

```python
import functools
import math

import numpy as np

import jax
import jax.numpy as jnp
from jax import lax
from jax.experimental import pallas as pl
from jax.experimental.pallas import tpu as pltpu
from jax.sharding import PartitionSpec as P

HEAD = 64
LANES = 128
HALF = 64
ROWS = 32
AT_ONCE = 2
PICKED_AT_ONCE = 2
FIRST_PAIRS = 4
VECTORS = 9
norm_eps = 1e-07
bf16 = jnp.bfloat16
f32 = jnp.float32
PARAMS = pltpu.CompilerParams(vmem_limit_bytes=60 * 2**20)


def lasting(micros):
    return pl.CostEstimate(
        flops=int(micros * 1.1e9), bytes_accessed=int(micros * 3.4e6), transcendentals=0
    )


def dot_nn(first_op, second_op):
    return lax.dot_general(
        first_op, second_op, (((1,), (0,)), ((), ())), preferred_element_type=f32
    )


def dot_nt(first_op, second_op):
    return lax.dot_general(
        first_op, second_op, (((1,), (1,)), ((), ())), preferred_element_type=f32
    )


def dot_tn(first_op, second_op):
    return lax.dot_general(
        first_op, second_op, (((0,), (0,)), ((), ())), preferred_element_type=f32
    )


def distance_rows(seq_len, table_rows):
    side = table_rows // 2
    middle = side // 2
    rows = []
    for m in range(2 * seq_len):
        offset = max(m - seq_len, 1 - seq_len)
        size = abs(offset)
        if size > middle:
            ratio = math.log(size / middle) / math.log((2 * side - 1) / middle)
            size = int(math.ceil(ratio * (middle - 1))) + middle
        rows.append(side + (size if offset > 0 else -size))
    return np.array(rows, dtype=np.int32)


def lane_iota(rows=1):
    return lax.broadcasted_iota(jnp.int32, (rows, LANES), 1)


def member_chunk(words, c, last):
    return (last - words == lane_iota(words.shape[0]) + c * LANES).astype(f32).astype(bf16)


def id_bases(rel_ref, base):
    seq = rel_ref.shape[0]
    chunks = seq // LANES
    last = chunks * 2 - 2
    for g in range(seq // HALF):
        for c in range(chunks):
            block = rel_ref[g * HALF : (g + 1) * HALF, c * LANES : (c + 1) * LANES]
            base[g * chunks + c] = jnp.minimum(jnp.min(block) // HALF, last)


def both_alignments(table):
    return jnp.concatenate([table, table[HALF:], table[:HALF]], axis=0)


def longest(rows):
    wide = rows.astype(f32)
    return jnp.sqrt(jnp.max(jnp.sum(wide * wide, axis=1, keepdims=True), axis=0, keepdims=True))


def pack_heads(first, second, dest, top):
    top = jnp.maximum(top, 1e-30)
    scale = 32000.0 / top
    upper = (first * scale).astype(jnp.int32)
    lower = (second * scale).astype(jnp.int32)
    dest[...] = upper * 65536 + lower
    return top * (1.0 / 32000.0)


def unpack_heads(words, step):
    lower = lax.shift_right_arithmetic(lax.shift_left(words, 16), 16)
    return words.astype(f32) * (step * (1.0 / 65536.0)), lower.astype(f32) * step


def picked_words(source, rel_ref, base, rows, c):
    chunks = rel_ref.shape[1] // LANES
    first = base[(rows.start // HALF) * chunks + c]
    place = rel_ref[rows, c * LANES : (c + 1) * LANES] - first * HALF
    index = place & (LANES - 1)
    at = pl.multiple_of((first % 2) * (chunks * LANES) + (first // 2) * LANES, LANES)
    near = jnp.take_along_axis(source[rows, pl.ds(at, LANES)], index, axis=1)
    at = pl.multiple_of(at + LANES, LANES)
    far = jnp.take_along_axis(source[rows, pl.ds(at, LANES)], index, axis=1)
    return jnp.where(place < LANES, near, far)


def unshift_in_order(sources, words_ref, base, dest):
    seq = words_ref.shape[0]
    chunks = seq // LANES
    lane = lane_iota()
    zero = jnp.zeros((ROWS, LANES), f32)
    for g in range(chunks):
        first = base[g]
        for sub in range(LANES // ROWS):
            start = g * LANES + sub * ROWS
            rows = slice(start, start + ROWS)
            place = lane - 1 - words_ref[rows, :] + first * LANES
            index = place & (LANES - 1)
            near = place >= 0
            mid = place >= -LANES
            for a, source in enumerate(sources):
                turned = [
                    jnp.take_along_axis(
                        source[rows, c * LANES : (c + 1) * LANES], index, axis=1
                    )
                    for c in range(chunks)
                ]
                turned = [zero, zero] + turned + [zero, zero]
                for c in range(chunks + 2):
                    value = jnp.where(near, turned[c + 2], jnp.where(mid, turned[c + 1], turned[c]))
                    at = pl.multiple_of((first + c) * LANES, LANES)
                    dest[a, rows, pl.ds(at, LANES)] = value.astype(bf16)


def group_bases(words, base):
    seq = words.shape[0]
    for g in range(seq // LANES):
        base[g] = (jnp.min(words[g * LANES : (g + 1) * LANES]) + 1) // LANES


def softmax_weights(scores):
    factor = math.log2(math.e) / math.sqrt(3.0 * HEAD)
    top = jnp.max(functools.reduce(jnp.maximum, scores), axis=1, keepdims=True)
    return [jnp.exp2((score - top) * factor) for score in scores]


def head_lanes(a):
    return (lane_iota() < HEAD) if a == 0 else (lane_iota() >= HEAD)


def row_of(ref):
    return ref[...].reshape(1, ref.shape[0])


def norm_stats(values):
    centered = values - jnp.mean(values, axis=1, keepdims=True)
    inv_std = lax.rsqrt(jnp.mean(centered * centered, axis=1, keepdims=True) + norm_eps)
    return centered * inv_std, inv_std


def norm_backward(upstream, normed, inv_std, norm_gain):
    scaled = upstream * norm_gain
    adjusted = (
        scaled
        - jnp.mean(scaled, axis=1, keepdims=True)
        - normed * jnp.mean(scaled * normed, axis=1, keepdims=True)
    )
    return inv_std * adjusted, col_sum(upstream * normed), col_sum(upstream)


def col_sum(values):
    return jnp.sum(values, axis=0, keepdims=True)


def normal_cdf(pre_act):
    return 0.5 * (1.0 + lax.erf(pre_act * (1.0 / math.sqrt(2.0))))


def project_kernel(
    pick_ref, x_ref, rel_ref, wq_ref, wk_ref, wv_ref, bq_ref, bk_ref, bv_ref,
    q_ref, k_ref, v_ref, pq_ref, pk_ref, qpick_ref, xpick_ref,
):
    @pl.when(pl.program_id(0) == 0)
    def _():
        xpick_ref[...] = dot_nn(pick_ref[...], x_ref[...]).astype(bf16)

    for source, weight, bias, out in (
        (xpick_ref, wq_ref, bq_ref, qpick_ref),
        (x_ref, wk_ref, bk_ref, k_ref),
        (rel_ref, wk_ref, bk_ref, pk_ref),
        (rel_ref, wq_ref, bq_ref, pq_ref),
        (x_ref, wq_ref, bq_ref, q_ref),
        (x_ref, wv_ref, bv_ref, v_ref),
    ):
        out[...] = (dot_nn(source[...], weight[...]) + row_of(bias)).astype(bf16)


def project(pick, x, rel_table, weights, biases):
    width = x.shape[1]
    group = 2 * LANES
    whole = lambda value: pl.BlockSpec(value.shape, lambda n: (0, 0))
    col = lambda value: pl.BlockSpec((value.shape[0], group), lambda n: (0, n))
    outs = [x, x, x, rel_table, rel_table, pick]
    return pl.pallas_call(
        project_kernel,
        grid=(width // group,),
        in_specs=[whole(pick), whole(x), whole(rel_table)]
        + [col(value) for value in weights]
        + [pl.BlockSpec((group,), lambda n: (n,))] * 3,
        out_specs=[col(value) for value in outs]
        + [pl.BlockSpec((pick.shape[0], width), lambda n: (0, 0))],
        out_shape=[jax.ShapeDtypeStruct((value.shape[0], width), bf16) for value in outs + [pick]],
        compiler_params=PARAMS,
        cost_estimate=lasting(6.0),
        name="project",
    )(pick, x, rel_table, *weights, *biases)


def picked_kernel(
    pos_ref, rel_ref, qc_ref, k_ref, v_ref, pk_ref, pq_ref,
    x_ref, wo_ref, bo_ref, gain_ref, bias_ref,
    ctx_ref, prob_ref, key_ref, word_ref, wordc_ref, normed_ref, inv_ref, low_ref,
    packed, cpick, direct, relc, keyc, attn, base,
):
    seq = k_ref.shape[0]
    picks = qc_ref.shape[0]
    chunks = seq // LANES
    units, far_units = [], []

    @pl.when(pl.program_id(0) == 0)
    def _():
        row = lax.broadcasted_iota(jnp.int32, (seq, seq), 0)
        col = lax.broadcasted_iota(jnp.int32, (seq, seq), 1)
        side = pk_ref.shape[0] // 2
        step = jnp.sum(jnp.where(col == row - 1, rel_ref[...] - side, 0), axis=1, keepdims=True)
        steps = jnp.broadcast_to(step.astype(f32), (seq, LANES)).astype(bf16)
        word_ref[...] = dot_nn((col <= row).astype(f32).astype(bf16), steps).astype(jnp.int32)
        id_bases(rel_ref, base)
        for n in range(picks):
            place = jnp.maximum(pos_ref[n], 0)
            relc[n : n + 1, :] = rel_ref[pl.ds(place, 1), :]
            wordc_ref[n : n + 1, :] = word_ref[pl.ds(place, 1), :]

    zero = jnp.zeros((), bf16)
    upper = head_lanes(0)
    for m in range(PICKED_AT_ONCE):
        lanes = slice(m * LANES, (m + 1) * LANES)
        k_pair, q_pair, pq = k_ref[:, lanes], qc_ref[:, lanes], pq_ref[:, lanes]
        table = both_alignments(pq)
        keys = [dot_nt(jnp.where(head_lanes(a), k_pair, zero), table) for a in range(2)]
        unit = pack_heads(keys[0], keys[1], packed.at[m], longest(k_pair) * longest(pq))
        units.append(unit)
        pk = pk_ref[:, lanes]
        far = []
        for a in range(2):
            q_a = jnp.where(head_lanes(a), q_pair, zero)
            far.append(dot_nt(q_a, pk))
            direct[2 * m + a] = dot_nt(q_a, k_pair)
        far_units.append(pack_heads(far[0], far[1], cpick.at[m], longest(q_pair) * longest(pk)))
    for m in range(PICKED_AT_ONCE):
        lanes = slice(m * LANES, (m + 1) * LANES)
        for g in range(chunks):
            for c in range(chunks):
                parts = []
                for start in range(g * LANES, (g + 1) * LANES, ROWS):
                    parts.append(
                        picked_words(packed.at[m], rel_ref, base, slice(start, start + ROWS), c)
                    )
                block = jnp.concatenate(parts, axis=0).T
                for a, value in enumerate(unpack_heads(block, units[m])):
                    key_ref[2 * m + a, c * LANES : (c + 1) * LANES, g * LANES : (g + 1) * LANES] = value
        for n in range(picks):
            place = jnp.maximum(pos_ref[n], 0)
            for a in range(2 * m, 2 * m + 2):
                keyc[a, n : n + 1, :] = key_ref[a, pl.ds(place, 1), :]
        scores = [[], []]
        for c in range(chunks):
            ids = relc[:, c * LANES : (c + 1) * LANES]
            index = ids & (LANES - 1)
            value = jnp.take_along_axis(cpick[m, :, :LANES], index, axis=1)
            for n in range(1, pk_ref.shape[0] // LANES):
                other = cpick[m, :, n * LANES : (n + 1) * LANES]
                value = jnp.where(
                    ids >= n * LANES, jnp.take_along_axis(other, index, axis=1), value
                )
            cols = slice(c * LANES, (c + 1) * LANES)
            for a, far in enumerate(unpack_heads(value, far_units[m])):
                scores[a].append(direct[2 * m + a, :, cols] + far + keyc[2 * m + a, :, cols])
        mixed = []
        for a in range(2 * m, 2 * m + 2):
            weights = softmax_weights(scores[a % 2])
            inverse = 1.0 / jnp.sum(sum(weights[1:], weights[0]), axis=1, keepdims=True)
            probs = jnp.concatenate([(weight * inverse).astype(bf16) for weight in weights], axis=1)
            prob_ref[a] = probs
            mixed.append(dot_nn(probs, v_ref[:, lanes]).astype(bf16))
        ctx_ref[:, lanes] = jnp.where(upper, mixed[0], mixed[1])

    part = dot_nn(ctx_ref[...], wo_ref[...])

    @pl.when(pl.program_id(0) == 0)
    def _():
        attn[...] = x_ref[...].astype(f32) + row_of(bo_ref) + part

    @pl.when(pl.program_id(0) > 0)
    def _():
        attn[...] += part

    @pl.when(pl.program_id(0) == pl.num_programs(0) - 1)
    def _():
        normed, inv_std = norm_stats(attn[...])
        normed_ref[...] = normed
        inv_ref[...] = jnp.broadcast_to(inv_std, (picks, LANES))
        low_ref[...] = (normed * row_of(gain_ref) + row_of(bias_ref)).astype(bf16)


def attend_picked(
    positions, rel_ids, q_pick, k, v, pos_query, pos_key, x_pick, w_out, b_out, gain, bias
):
    seq, width = k.shape
    picks = q_pick.shape[0]
    table = pos_key.shape[0]
    pairs = width // LANES
    whole = lambda rows, cols: pl.BlockSpec((rows, cols), lambda h: (0, 0))
    line = pl.BlockSpec((width,), lambda h: (0,))
    per = PICKED_AT_ONCE
    wide = per * LANES
    col = lambda rows: pl.BlockSpec((rows, wide), lambda h: (0, h))
    heads = lambda rows: pl.BlockSpec((2 * per, rows, seq), lambda h: (h, 0, 0))
    return pl.pallas_call(
        picked_kernel,
        grid=(pairs // per,),
        in_specs=[
            pl.BlockSpec(memory_space=pltpu.SMEM), whole(seq, seq),
            col(picks), col(seq), col(seq), col(table), col(table),
            whole(picks, width), pl.BlockSpec((wide, width), lambda h: (h, 0)), line, line, line,
        ],
        out_specs=[
            col(picks), heads(picks), heads(seq), whole(seq, LANES), whole(picks, LANES),
            whole(picks, width), whole(picks, LANES), whole(picks, width),
        ],
        out_shape=[
            jax.ShapeDtypeStruct((picks, width), bf16),
            jax.ShapeDtypeStruct((2 * pairs, picks, seq), bf16),
            jax.ShapeDtypeStruct((2 * pairs, seq, seq), f32),
            jax.ShapeDtypeStruct((seq, LANES), jnp.int32),
            jax.ShapeDtypeStruct((picks, LANES), jnp.int32),
            jax.ShapeDtypeStruct((picks, width), f32),
            jax.ShapeDtypeStruct((picks, LANES), f32),
            jax.ShapeDtypeStruct((picks, width), bf16),
        ],
        scratch_shapes=[
            pltpu.VMEM((per, seq, 2 * table), jnp.int32),
            pltpu.VMEM((per, picks, table), jnp.int32),
            pltpu.VMEM((2 * per, picks, seq), f32),
            pltpu.VMEM((picks, seq), jnp.int32),
            pltpu.VMEM((2 * per, picks, seq), f32),
            pltpu.VMEM((picks, width), f32),
            pltpu.SMEM((seq // HALF * (seq // LANES),), jnp.int32),
        ],
        compiler_params=PARAMS,
        cost_estimate=lasting(5.0 * pairs),
        name="attend_picked",
    )(
        positions, rel_ids, q_pick, k, v, pos_key, pos_query, x_pick, w_out, b_out, gain, bias
    )


def full_kernel(rel_ref, q_ref, k_ref, v_ref, pk_ref, key_ref, ctx_ref, *scratch):
    seq = rel_ref.shape[0]
    chunks = seq // LANES
    base, scratch = scratch[-1], scratch[:-1]
    count = len(scratch) // 3

    @pl.when(pl.program_id(0) == 0)
    def _():
        id_bases(rel_ref, base)

    zero = jnp.zeros((), bf16)
    units = []
    for n in range(count):
        packed, direct, low = scratch[3 * n : 3 * n + 3]
        lanes = slice(n * LANES, (n + 1) * LANES)
        q, pos = q_ref[:, lanes], pk_ref[:, lanes]
        table = both_alignments(pos)
        far = []
        for a in range(2):
            q_a = jnp.where(head_lanes(a), q, zero)
            far.append(dot_nt(q_a, table))
            direct[a] = dot_nt(q_a, k_ref[:, lanes])
        units.append(pack_heads(far[0], far[1], packed, longest(q) * longest(pos)))
    for n in range(count):
        packed, direct, low = scratch[3 * n : 3 * n + 3]
        lanes = slice(n * LANES, (n + 1) * LANES)
        for start in range(0, seq, HALF):
            rows = slice(start, start + HALF)
            scores = [[], []]
            for c in range(chunks):
                cols = slice(c * LANES, (c + 1) * LANES)
                values = unpack_heads(picked_words(packed, rel_ref, base, rows, c), units[n])
                for a in range(2):
                    scores[a].append(
                        values[a] + direct[a, rows, cols] + key_ref[2 * n + a, rows, cols]
                    )
            for a in range(2):
                for c, weight in enumerate(softmax_weights(scores[a])):
                    low[a, rows, c * LANES : (c + 1) * LANES] = weight.astype(bf16)
        v = v_ref[:, lanes]
        mixed = [
            dot_nn(low[a], jnp.where(head_lanes(a), v, jnp.ones((), bf16))) for a in range(2)
        ]
        upper = head_lanes(0)
        totals = pltpu.roll(jnp.where(upper, mixed[1], mixed[0]), HEAD, 1)
        ctx_ref[:, lanes] = (jnp.where(upper, mixed[0], mixed[1]) * (1.0 / totals)).astype(bf16)


def attend_full(rel_ids, q, k, v, pos_key, key_scores, first, pairs):
    seq = k.shape[0]
    table = pos_key.shape[0]
    per = AT_ONCE
    wide = per * LANES
    col = lambda rows: pl.BlockSpec((rows, wide), lambda h: (0, h + first // per))
    return pl.pallas_call(
        full_kernel,
        grid=(pairs // per,),
        in_specs=[
            pl.BlockSpec((seq, seq), lambda h: (0, 0)),
            col(seq), col(seq), col(seq), col(table),
            pl.BlockSpec((2 * per, seq, seq), lambda h: (h + first // per, 0, 0)),
        ],
        out_specs=pl.BlockSpec((seq, wide), lambda h: (0, h)),
        out_shape=jax.ShapeDtypeStruct((seq, pairs * LANES), bf16),
        scratch_shapes=[
            pltpu.VMEM((seq, 2 * table), jnp.int32),
            pltpu.VMEM((2, seq, seq), f32),
            pltpu.VMEM((2, seq, seq), bf16),
        ]
        * per
        + [pltpu.SMEM((seq // HALF * (seq // LANES),), jnp.int32)],
        compiler_params=PARAMS,
        cost_estimate=lasting(4.2 * pairs),
        name="attend_full",
    )(rel_ids, q, k, v, pos_key, key_scores)


def back_kernel(
    row_ref, word_ref, wordc_ref, qc_ref, k_ref, v_ref, prob_ref, pk_ref, pq_ref,
    dz2_ref, mine_ref, got_ref, normed_ref, inv_ref, gain_ref, wo_ref, early_ref,
    dq_ref, dk_ref, dv_ref, dpos_ref, dz1_ref, dattn_ref, sum_ref,
    side, sidec, moved, movedc, expand, shrink, base,
):
    seq = k_ref.shape[0]
    picks = qc_ref.shape[0]
    table = pk_ref.shape[0]
    chunks = seq // LANES

    @pl.when(pl.program_id(0) == 0)
    def _():
        words = word_ref[...]
        for c in range(chunks):
            side[:, c * LANES : (c + 1) * LANES] = member_chunk(words, c, seq - 1)
            sidec[:, c * LANES : (c + 1) * LANES] = member_chunk(wordc_ref[...], c, seq - 1)
        group_bases(words, base)
        moved[...] = jnp.zeros_like(moved)
        edge = expand.shape[1]
        for n, start in ((0, 0), (1, 2 * seq - edge)):
            ids = row_ref[start : start + edge, :] - n * (table - LANES)
            chosen = (ids == lane_iota(edge)).astype(f32).astype(bf16)
            expand[n] = chosen
            shrink[n] = chosen.T
        dh1 = dz2_ref[...] + mine_ref[...].astype(f32) + got_ref[...].astype(f32)
        dz1, g_gain, g_bias = norm_backward(dh1, normed_ref[...], inv_ref[:, :1], row_of(gain_ref))
        dz1_ref[...] = dz1
        dattn = dz1.astype(bf16)
        dattn_ref[...] = dattn
        sum_ref[...] = jnp.concatenate(
            [col_sum(dattn.astype(f32)), g_gain, g_bias, early_ref[:5]], axis=0
        )

    lane = lane_iota()
    scale = 1.0 / math.sqrt(3.0 * HEAD)
    zero = jnp.zeros((), bf16)
    heads = range(2)
    upper = head_lanes(0)
    join = lambda pair: jnp.where(upper, pair[0], pair[1])
    side[:, seq:] = k_ref[...]
    sidec[:, seq:] = qc_ref[...]
    dctx = dot_nt(dattn_ref[...], wo_ref[...]).astype(bf16)
    dprobs = [dot_nt(jnp.where(head_lanes(a), dctx, zero), v_ref[...]) for a in heads]

    def widened(ref):
        ends = [
            dot_nn(expand[n], ref[at : at + LANES, :]).astype(bf16)
            for n, at in ((0, 0), (1, table - LANES))
        ]
        return jnp.concatenate([ends[0], ref[LANES : table - LANES, :], ends[1]], axis=0)

    far_key, far_query = widened(pk_ref), widened(pq_ref)
    gs = []
    for a in heads:
        probs = prob_ref[a].astype(f32)
        prod = probs * dprobs[a]
        gs.append(((prod - probs * jnp.sum(prod, axis=1, keepdims=True)) * scale).astype(bf16))
    outs = [dot_tn(gs[a], sidec[...]) for a in heads]
    outcs = [dot_nn(gs[a], side[...]) for a in heads]
    dv_ref[...] = join([dot_tn(prob_ref[a], dctx) for a in heads]).astype(bf16)
    place = lane - 1 - wordc_ref[...]
    index = place & (LANES - 1)
    blank = jnp.zeros((picks, LANES), f32)
    for a in heads:
        turned = [
            jnp.take_along_axis(outcs[a][:, c * LANES : (c + 1) * LANES], index, axis=1)
            for c in range(chunks)
        ]
        for c in range(2 * chunks):
            value = turned[c] if c < chunks else blank
            for n in range(1, chunks + 1):
                other = turned[c - n] if 0 <= c - n < chunks else blank
                value = jnp.where(place < -LANES * (n - 1), other, value)
            movedc[a, :, c * LANES : (c + 1) * LANES] = value.astype(bf16)
    unshift_in_order(outs, word_ref, base, moved)
    dq = [outcs[a][:, seq:] + dot_nn(movedc[a], far_key) for a in heads]
    dq_ref[...] = join(dq).astype(bf16)
    dk = [outs[a][:, seq:] + dot_nn(moved[a, :, : 2 * seq], far_query) for a in heads]
    dk_ref[...] = join(dk).astype(bf16)
    far = [
        join([dot_tn(movedc[a], qc_ref[...]) for a in heads]),
        join([dot_tn(moved[a, :, : 2 * seq], k_ref[...]) for a in heads]),
    ]
    edge = expand.shape[1]
    for n, value in enumerate(far):
        value = value.astype(bf16)
        dpos_ref[n, :LANES, :] = dot_nn(shrink[0], value[:edge]).astype(bf16)
        dpos_ref[n, LANES : table - LANES, :] = value[edge : 2 * seq - edge]
        dpos_ref[n, table - LANES :, :] = dot_nn(shrink[1], value[2 * seq - edge :]).astype(bf16)


def attend_back(
    table_of, words, words_pick, q_pick, k, v, probs, pos_query, pos_key,
    dz2, mine, got, normed, inv_std, gain, w_out, early,
):
    seq, width = k.shape
    picks = q_pick.shape[0]
    table = pos_key.shape[0]
    pairs = width // LANES
    edge = seq - table // 4
    whole = lambda value: pl.BlockSpec(value.shape, lambda h: (0,) * value.ndim)
    col = lambda rows: pl.BlockSpec((rows, LANES), lambda h: (0, h))
    shape = lambda rows: jax.ShapeDtypeStruct((rows, width), bf16)
    return pl.pallas_call(
        back_kernel,
        grid=(pairs,),
        in_specs=[
            whole(table_of), whole(words), whole(words_pick),
            col(picks), col(seq), col(seq),
            pl.BlockSpec((2, picks, seq), lambda h: (h, 0, 0)),
            col(table), col(table),
            whole(dz2), whole(mine), whole(got), whole(normed), whole(inv_std), whole(gain),
            pl.BlockSpec((LANES, width), lambda h: (h, 0)), whole(early),
        ],
        out_specs=[
            col(picks), col(seq), col(seq),
            pl.BlockSpec((2, table, LANES), lambda h: (0, 0, h)),
            whole(dz2), whole(dz2), whole(early),
        ],
        out_shape=[
            shape(picks), shape(seq), shape(seq),
            jax.ShapeDtypeStruct((2, table, width), bf16),
            jax.ShapeDtypeStruct((picks, width), f32),
            shape(picks),
            jax.ShapeDtypeStruct(early.shape, f32),
        ],
        scratch_shapes=[
            pltpu.VMEM((seq, seq + LANES), bf16),
            pltpu.VMEM((picks, seq + LANES), bf16),
            pltpu.VMEM((2, seq, 2 * seq + 2 * LANES), bf16),
            pltpu.VMEM((2, picks, 2 * seq), bf16),
            pltpu.VMEM((2, edge, LANES), bf16),
            pltpu.VMEM((2, LANES, edge), bf16),
            pltpu.SMEM((seq // LANES,), jnp.int32),
        ],
        compiler_params=PARAMS,
        cost_estimate=lasting(4.0 * pairs),
        name="attend_back",
    )(
        table_of, words, words_pick, q_pick, k, v, probs, pos_key, pos_query,
        dz2, mine, got, normed, inv_std, gain, w_out, early,
    )


def turn_kernel(
    n_all, me_ref, order_ref, x_ref, xpick_ref, cpick_ref, rel_ref, x_out, xpick_out, cpick_out, rel_out
):
    picked = order_rows(order_ref, me_ref, x_ref.shape[1], n_all)
    for ref, out in ((x_ref, x_out), (xpick_ref, xpick_out), (cpick_ref, cpick_out), (rel_ref, rel_out)):
        out[...] = dot_nt(picked, ref[...]).astype(bf16)


def block_rows(ref, me_ref):
    return me_ref[0] ^ jnp.where(me_ref[1] == 0, ref[:, 0:1], ref[:, 1:2])


def order_rows(ref, me_ref, length, n_all):
    source = block_rows(ref, me_ref) * (length // n_all) + ref[:, 2:3]
    spot = lax.broadcasted_iota(jnp.int32, (ref.shape[0], length), 1)
    return (spot == source).astype(f32).astype(bf16)


def turn_blocks(n_all, me, order, x, x_pick, ctx_pick, rel_table):
    width = x.shape[1]
    group = 2 * LANES
    whole = lambda value: pl.BlockSpec(value.shape, lambda n: (0, 0))
    row = lambda count: pl.BlockSpec((group, count), lambda n: (n, 0))
    given = [x, x_pick, ctx_pick, rel_table]
    return pl.pallas_call(
        functools.partial(turn_kernel, n_all),
        grid=(width // group,),
        in_specs=[pl.BlockSpec(memory_space=pltpu.SMEM), row(LANES)]
        + [whole(value) for value in given],
        out_specs=[row(value.shape[0]) for value in given],
        out_shape=[jax.ShapeDtypeStruct(value.shape[::-1], bf16) for value in given],
        compiler_params=PARAMS,
        cost_estimate=lasting(5.2),
        name="turn_blocks",
    )(me, order, *given)


def norm_picked_kernel(
    normed_ref, gain1_ref, bias1_ref, mine_ref, got_ref, bdown_ref, gain2_ref, grad_ref, pick_ref,
    dz2_ref, low_ref, sum_ref,
):
    h1 = normed_ref[...] * row_of(gain1_ref) + row_of(bias1_ref)
    branch = mine_ref[...].astype(f32) + got_ref[...].astype(f32) + row_of(bdown_ref)
    normed, inv_std = norm_stats(h1 + branch)
    used = jnp.sum(pick_ref[...].astype(f32), axis=1, keepdims=True)
    cot = jnp.where(used > 0.0, grad_ref[...].astype(f32), 0.0)
    dz2, g_gain, g_bias = norm_backward(cot, normed, inv_std, row_of(gain2_ref))
    dz2_ref[...] = dz2
    low = dz2.astype(bf16)
    low_ref[...] = low
    sum_ref[...] = jnp.concatenate(
        [col_sum(low.astype(f32)), g_gain, g_bias, jnp.zeros((5, h1.shape[1]), f32)], axis=0
    )


def norm_picked(normed, gain1, bias1, mine, got, b_down, gain2, grads, pick):
    picks, width = normed.shape
    return pl.pallas_call(
        norm_picked_kernel,
        out_shape=[
            jax.ShapeDtypeStruct((picks, width), f32),
            jax.ShapeDtypeStruct((picks, width), bf16),
            jax.ShapeDtypeStruct((8, width), f32),
        ],
        compiler_params=PARAMS,
        cost_estimate=lasting(2.4),
        name="norm_picked",
    )(normed, gain1, bias1, mine, got, b_down, gain2, grads, pick)


def ffn_full_kernel(
    x_ref, ctx_ref, ctx2_ref, wo_ref, bo_ref, gain1_ref, bias1_ref, bdown_ref, gain2_ref, bias2_ref,
    bin_ref, bin2_ref, bin3_ref, win_ref, down_ref, win2_ref, down2_ref, win3_ref, down3_ref,
    out_ref, h1, low, total, win_here, down_here, win_sem, down_sem,
):
    rows, width = x_ref.shape
    tile = win_here.shape[2]
    parts = [(win_ref, down_ref, bin_ref, n * tile) for n in range(win_ref.shape[1] // tile)]
    parts += [(win2_ref, down2_ref, bin2_ref, 0), (win3_ref, down3_ref, bin3_ref, 0)]

    def copies(n):
        w_ref, d_ref, _, at = parts[n]
        return (
            pltpu.make_async_copy(w_ref.at[:, at : at + tile], win_here.at[n], win_sem.at[n]),
            pltpu.make_async_copy(d_ref.at[at : at + tile, :], down_here.at[n], down_sem.at[n]),
        )

    for n in range(len(parts)):
        for copy in copies(n):
            copy.start()
    attn = dot_nn(ctx_ref[...], wo_ref[: ctx_ref.shape[1]]) + dot_nn(
        ctx2_ref[...], wo_ref[ctx_ref.shape[1] :]
    )
    normed, _ = norm_stats(x_ref[...].astype(f32) + (attn + row_of(bo_ref)))
    value = normed * row_of(gain1_ref) + row_of(bias1_ref)
    h1[...] = value
    low[...] = value.astype(bf16)
    step = rows // 2
    for n in range(len(parts)):
        for copy in copies(n):
            copy.wait()
        bias = parts[n][2][:, parts[n][3] : parts[n][3] + tile]
        for at in range(0, rows, step):
            pre = dot_nn(low[at : at + step], win_here[n]) + bias
            part = dot_nn((pre * normal_cdf(pre)).astype(bf16), down_here[n])
            total[at : at + step] = part if n == 0 else total[at : at + step] + part
    normed, _ = norm_stats(h1[...] + (total[...] + row_of(bdown_ref)))
    out_ref[...] = (normed * row_of(gain2_ref) + row_of(bias2_ref)).astype(bf16)


def ffn_full(x, ctx, w_out, b_out, gain1, bias1, shards, b_down, gain2, bias2):
    rows, width = x.shape
    tile = shards[1][0].shape[1]
    count = shards[0][0].shape[1] // tile + 2
    held = [x, ctx[0], ctx[1], w_out, b_out, gain1, bias1, b_down, gain2, bias2]
    held += [shard[2] for shard in shards]
    moved = [value for shard in shards for value in shard[:2]]
    return pl.pallas_call(
        ffn_full_kernel,
        in_specs=[pl.BlockSpec(memory_space=pltpu.VMEM)] * len(held)
        + [pl.BlockSpec(memory_space=pl.ANY)] * len(moved),
        out_specs=pl.BlockSpec(memory_space=pltpu.VMEM),
        out_shape=jax.ShapeDtypeStruct((rows, width), bf16),
        scratch_shapes=[
            pltpu.VMEM((rows, width), f32), pltpu.VMEM((rows, width), bf16), pltpu.VMEM((rows, width), f32),
            pltpu.VMEM((count, width, tile), bf16), pltpu.VMEM((count, tile, width), bf16),
            pltpu.SemaphoreType.DMA((count,)), pltpu.SemaphoreType.DMA((count,)),
        ],
        compiler_params=PARAMS,
        cost_estimate=lasting(10.9),
        name="ffn_full",
    )(*held, *moved)


def token_grads_kernel(pick_ref, dz1_ref, dq_ref, dk_ref, dv_ref, wq_ref, wk_ref, wv_ref, out_ref):
    sparse = dz1_ref[...] + dot_nt(dq_ref[...], wq_ref[...])
    upper = sparse.astype(bf16)
    lower = (sparse - upper.astype(f32)).astype(bf16)
    out_ref[...] = (
        dot_nt(dk_ref[...], wk_ref[...])
        + dot_nt(dv_ref[...], wv_ref[...])
        + dot_tn(pick_ref[...], upper)
        + dot_tn(pick_ref[...], lower)
    )


def token_grads(pick, dz1, dq, dk, dv, w_query, w_key, w_value):
    seq, width = dk.shape
    group = 2 * LANES
    whole = lambda value: pl.BlockSpec(value.shape, lambda n: (0, 0))
    col = lambda rows: pl.BlockSpec((rows, group), lambda n: (0, n))
    row = pl.BlockSpec((group, width), lambda n: (n, 0))
    return pl.pallas_call(
        token_grads_kernel,
        grid=(width // group,),
        in_specs=[whole(pick), col(dz1.shape[0]), whole(dq), whole(dk), whole(dv), row, row, row],
        out_specs=col(seq),
        out_shape=jax.ShapeDtypeStruct((seq, width), f32),
        compiler_params=PARAMS,
        cost_estimate=lasting(5.9),
        name="token_grads",
    )(pick, dz1, dq, dk, dv, w_query, w_key, w_value)


def grads_kernel(
    n_all, n_ffn, unit, me_ref, order_ref, relorder_ref, taker_ref,
    x_ref, rel_ref, xpick_ref, cpick_ref, dpos_ref, dq_ref, dk_ref, dv_ref, dattn_ref,
    early_ref, bin_ref, wq_ref, wk_ref, kept_ref, sent_ref, weights, sems,
):
    width = dk_ref.shape[1]
    table = dpos_ref.shape[1]
    group = 2 * LANES
    step = pl.program_id(0)
    copies = [
        pltpu.make_async_copy(ref, weights.at[n], sems.at[n])
        for n, ref in enumerate((wk_ref, wq_ref))
    ]

    def put(at, value):
        value = value.astype(bf16)
        kept_ref[at] = value[:LANES]
        sent_ref[at] = value[LANES:]

    @pl.when(step == 0)
    def _():
        for copy in copies:
            copy.start()

    @pl.when(step < width // group)
    def _():
        put(0, dot_nn(xpick_ref[...], dq_ref[...]) + dot_nn(rel_ref[...], dpos_ref[1]))
        put(1, dot_nn(x_ref[...], dk_ref[...]) + dot_nn(rel_ref[...], dpos_ref[0]))
        put(2, dot_nn(x_ref[...], dv_ref[...]))
        put(3, dot_nn(cpick_ref[...], dattn_ref[...]))

    @pl.when(step == width // group)
    def _():
        for copy in copies:
            copy.wait()
        rows = order_rows(relorder_ref, me_ref, table, n_all)
        far = [dot_nn(rows, dpos_ref[n]).astype(bf16) for n in range(2)]
        value = dot_nt(far[0], weights[0]) + dot_nt(far[1], weights[1])
        for n in range(table // group):
            put(n, value[n * group : (n + 1) * group])

        total = lambda value: col_sum(value.astype(f32))
        bins = [bin_ref[:1, at : at + width] for at in range(0, bin_ref.shape[1], width)]
        values = [
            total(dq_ref[...]) + total(dpos_ref[1]),
            total(dk_ref[...]) + total(dpos_ref[0]),
            total(dv_ref[...]),
            early_ref[:6],
        ]
        values += bins + [jnp.zeros((16 - VECTORS - len(bins), width), f32)]
        values = jnp.concatenate(values, axis=0)
        block = block_rows(order_ref[:group, :], me_ref)
        ours = (block % n_ffn) == (me_ref[0] % n_ffn)
        tok_place = jnp.where(ours, block // n_ffn, -1)
        row = lax.broadcasted_iota(jnp.int32, (group, 1), 0) % unit
        for n in range(16 // unit):
            rows = slice(n * unit, (n + 1) * unit)
            spread = lambda value: jnp.concatenate([value[rows]] * (group // unit), axis=0)
            taker = jnp.where(row + n * unit < VECTORS, block, tok_place)
            put(table // group + n, jnp.where(spread(taker_ref[...]) == taker, spread(values), 0.0))


def weight_grads(
    n_all, n_ffn, unit, me, order, rel_order, takers, x, rel, x_pick, c_pick, dpos, dq, dk, dv, dattn,
    w_query, w_key, early, bins,
):
    seq, width = dk.shape
    group = 2 * LANES
    steps = width // group
    each = max(4, dpos.shape[1] // group + 16 // unit)
    whole = lambda value: pl.BlockSpec(value.shape, lambda n: (0,) * value.ndim)
    row = lambda value: pl.BlockSpec((group, value.shape[1]), lambda n: (jnp.minimum(n, steps - 1), 0))
    block = pl.BlockSpec((each, LANES, width), lambda n: (n, 0, 0))
    return pl.pallas_call(
        functools.partial(grads_kernel, n_all, n_ffn, unit),
        grid=(steps + 1,),
        in_specs=[pl.BlockSpec(memory_space=pltpu.SMEM)]
        + [whole(value) for value in (order, rel_order, takers)]
        + [row(value) for value in (x, rel, x_pick, c_pick)]
        + [whole(value) for value in (dpos, dq, dk, dv, dattn, early, bins)]
        + [pl.BlockSpec(memory_space=pl.ANY)] * 2,
        out_specs=[block] * 2,
        out_shape=[jax.ShapeDtypeStruct((each * (steps + 1), LANES, width), bf16)] * 2,
        scratch_shapes=[
            pltpu.VMEM((2,) + w_query.shape, bf16), pltpu.SemaphoreType.DMA((2,)),
        ],
        compiler_params=PARAMS,
        cost_estimate=lasting(7.0),
        name="weight_grads",
    )(
        me, order, rel_order, takers, x, rel, x_pick, c_pick, dpos, dq, dk, dv, dattn, early, bins,
        w_query, w_key,
    )


def swap(values, axis, bit):
    size = lax.axis_size(axis)
    return lax.ppermute(values, axis, [(n, n ^ bit) for n in range(size)])


def after(values, *others):
    return lax.optimization_barrier((values, others))[0]


class Halving:
    def __init__(self, axes, core, near, size):
        rest = [1 << n for n in range(size.bit_length() - 1) if (1 << n) != core]
        near = [bit for bit in near if bit in rest]
        rest = [bit for bit in rest if bit not in near]
        turned = near[-1:] + near[:-1]
        self.axes, self.core, self.size = axes, core, size
        self.orders = [[core] + near + rest, [core] + turned + rest]
        self.steps = len(self.orders[0])
        self.me = lax.axis_index(axes)
        self.upper = (self.me // core) % 2

    def core_of(self, place):
        return (place // self.core) % 2

    def send(self, values, step):
        pairs = [(n, n ^ self.orders[self.core_of(n)][step]) for n in range(self.size)]
        return lax.ppermute(values, self.axes, pairs)

    def relative(self, upper):
        masks = []
        for place in range(self.size):
            bits = [(place >> (self.steps - 1 - step)) & 1 for step in range(self.steps)]
            order = self.orders[upper ^ bits[0]]
            mask = 0
            for step, bit in enumerate(bits):
                mask ^= bit * order[step]
            masks.append(mask)
        return np.array(masks, np.int32)

    def order(self, length, unit):
        spots = np.arange(length)
        group = self.size * unit
        place = spots % group // unit
        rows = [self.relative(upper)[place] for upper in range(2)]
        rows.append(spots // group * unit + spots % unit)
        return np.stack(rows).astype(np.int32)

    def matrix(self, length, unit):
        first, second, inner = self.order(length, unit)
        source = (self.me ^ jnp.where(self.upper == 0, first, second)) * (length // self.size) + inner
        spot = lax.broadcasted_iota(jnp.int32, (length, length), 0)
        return (spot == source[None, :]).astype(bf16)


def local(
    tokens, rel_ids, mask_pos, grad_vals, w_query, w_key, w_value, w_out, b_query, b_key,
    b_value, b_out, rel_table, ln1_gain, ln1_bias, w_in, b_in, w_down, b_down, ln2_gain, ln2_bias,
):
    assert rel_ids.shape[0] == 1
    seq, width = tokens.shape
    table_rows = rel_table.shape[0]
    hidden_cols = w_in.shape[1]
    pairs = width // LANES
    n_tok = lax.axis_size("tok")
    n_ffn = lax.axis_size("ffn")
    n_all = n_tok * n_ffn
    low = lambda value: value.astype(bf16)
    wide = lambda value: value.astype(f32)
    rel_ids, positions, grad_vals = rel_ids[0], mask_pos[0], grad_vals[0]

    over_all = Halving(("tok", "ffn"), n_ffn, [2 * n_ffn, 1, 4 * n_ffn], n_all)
    own, own_rel = width // n_all, table_rows // n_all
    unit = math.gcd(own, own_rel)
    group = n_all * unit
    over_tok = Halving("tok", 1, [2, 4], n_tok)
    pad = lambda value, count: np.pad(value, ((0, count - value.shape[0]), (0, 0)))
    order = jnp.asarray(pad(over_all.order(width, unit), LANES).T)
    rel_order = jnp.asarray(pad(over_all.order(table_rows, unit), LANES).T)
    spots = np.arange(width)
    takers = [spots // own] * VECTORS
    takers += [(spots + n * width) // (hidden_cols // n_tok) for n in range(hidden_cols // width)]
    takers = np.stack(takers).astype(np.int32)
    takers = jnp.asarray(np.pad(takers, ((0, 16 - takers.shape[0]), (0, 0)), constant_values=-2))
    me = jnp.stack([over_all.me, over_all.upper])
    table_of = jnp.asarray(np.repeat(distance_rows(seq, table_rows)[:, None], LANES, 1))

    core = lax.axis_index("tok") % 2
    half_cols = hidden_cols // 2
    bias_row = b_in.reshape(1, hidden_cols)
    in_half = lax.dynamic_slice_in_dim(w_in, core * half_cols, half_cols, 1)
    down_half = lax.dynamic_slice_in_dim(w_down, core * half_cols, half_cols, 0)

    pick = low(positions[:, None] == lax.broadcasted_iota(jnp.int32, (positions.shape[0], seq), 1))
    q, k, v, pos_query, pos_key, q_pick, x_pick = project(
        pick, tokens, rel_table, (w_query, w_key, w_value), (b_query, b_key, b_value)
    )
    ctx_pick, probs, key_scores, words, words_pick, normed1, inv1, h1_mine = attend_picked(
        positions, rel_ids, q_pick, k, v, pos_query, pos_key, x_pick, w_out, b_out, ln1_gain, ln1_bias
    )

    h1_theirs = swap(h1_mine, "ffn", 1)
    bias_theirs = swap(bias_row, "ffn", 1)
    x_turned, x_pick_turned, c_pick_turned, rel_turned = turn_blocks(
        n_all, me, order, tokens, x_pick, ctx_pick, rel_table
    )
    h1_both = jnp.concatenate([h1_mine, after(h1_theirs, x_turned, bias_theirs)], axis=0)
    count = h1_mine.shape[0]
    pre = dot_nn(h1_both, w_in) + b_in
    cdf = normal_cdf(pre)
    hidden = low(pre * cdf)
    slope = cdf + pre * (jnp.exp(-0.5 * pre * pre) * (1.0 / math.sqrt(2.0 * math.pi)))
    part = low(dot_nn(hidden, w_down))
    got = swap(part[count:], "ffn", 1)
    tok_order = over_tok.matrix(width, width // n_tok)
    h1_left = low(dot_nn(h1_both, lax.optimization_barrier(tok_order)))
    in_half = after(in_half, part)
    got = after(got, h1_left, in_half)
    dz2, dffn, early = norm_picked(
        normed1, ln1_gain, ln1_bias, part[:count], got, b_down, ln2_gain, grad_vals, pick
    )
    down_half = after(down_half, dffn)
    dffn_both = jnp.concatenate([dffn, after(swap(dffn, "ffn", 1), down_half)], axis=0)
    dpre = low(dot_nt(dffn_both, w_down) * slope)
    dpart = low(dot_nt(dpre, w_in))
    dgot = swap(dpart[count:], "ffn", 1)

    def halves(values, axis):
        size = values.shape[axis] // 2
        cut = lambda at: lax.slice_in_dim(values, at, at + size, axis=axis)
        return cut(0), cut(size)

    add = lambda one, other: low(wide(one) + wide(other))

    def next_halves(kept, got, axis):
        return [add(one, other) for one, other in zip(halves(kept, axis), halves(got, axis))]

    dpre_later = after(dpre, dpart)
    dffn_left = low(dot_nn(after(dffn_both, dpart), tok_order))
    gb_in = dot_nn(jnp.ones((8, 2 * count), bf16), dpre_later)
    lefts, rights = (h1_left, dffn_left), (dpre_later, hidden)
    middle, quarter = width // 2, width // 4
    ffn_sent = [low(dot_tn(one[:, middle:], other)) for one, other in zip(lefts, rights)]
    dgot, ffn_sent = lax.optimization_barrier((dgot, ffn_sent))
    ffn_got = [over_tok.send(value, 0) for value in ffn_sent]
    far_in = swap(after(in_half, dgot, ffn_sent), "ffn", 1)

    def ffn_piece(at):
        return [
            low(dot_tn(one[:, at : at + quarter], other) + wide(value[at : at + quarter]))
            for one, other, value in zip(lefts, rights, ffn_got)
        ]

    ffn_sent = ffn_piece(quarter)
    ffn_kept = ffn_piece(0)
    ffn_got = [over_tok.send(value, 1) for value in ffn_sent]

    def ffn_next(step, kept, got):
        if step < over_tok.steps:
            pieces = [next_halves(one, other, 0) for one, other in zip(kept, got)]
            return [piece[0] for piece in pieces], [over_tok.send(piece[1], step) for piece in pieces]
        return [add(one, other) for one, other in zip(kept, got)], None

    dq, dk, dv, dpos, dz1, dattn, early = attend_back(
        table_of, words, words_pick, q_pick, k, v, probs, pos_query, pos_key,
        dz2, dpart[:count], after(dgot, in_half, ffn_sent, ffn_kept), normed1, inv1, ln1_gain, w_out, early,
    )
    far_in, ffn_got = after((far_in, ffn_got), dk)
    ffn_kept, ffn_got = ffn_next(2, ffn_kept, ffn_got)
    near_in = swap(far_in, "tok", 1)
    far_down = swap(after(down_half, far_in), "ffn", 1)
    all_kept, all_sent = weight_grads(
        n_all, n_ffn, unit, me, order, rel_order, takers,
        x_turned, rel_turned, x_pick_turned, c_pick_turned, dpos, dq, after(dk, far_in, ffn_kept), dv,
        dattn, w_query, w_key, early, gb_in,
    )
    all_got = over_all.send(all_sent, 0)
    dk_later, dq_later = after((dk, dq), all_sent)
    grad_tokens = token_grads(pick, dz1, dq_later, dk_later, dv, w_query, w_key, w_value)
    all_kept, all_sent = next_halves(all_kept, after(all_got, grad_tokens), 1)
    ffn_step = 3
    ffn_got = after(ffn_got, grad_tokens)

    def attend(first, count, q):
        return attend_full(rel_ids, q, k, v, pos_key, key_scores, first, count)

    ctx = []
    cuts = [(0, FIRST_PAIRS), (FIRST_PAIRS, pairs - FIRST_PAIRS)]
    for step in range(1, over_all.steps):
        all_got = over_all.send(all_sent, step)
        if step <= 2:
            ctx.append(attend(*cuts[step - 1], after(q, all_sent)))
            all_got = after(all_got, ctx[-1])
            if step == 1:
                far_down = after(far_down, ctx[-1])
                near_down = swap(far_down, "tok", 1)
                all_got = after(all_got, far_down)
        elif step == 4:
            biases = [
                lax.dynamic_slice_in_dim(bias_theirs, at * half_cols, half_cols, 1)
                for at in (core, 1 - core)
            ]
            shards = [
                (w_in, w_down, bias_row), (far_in, far_down, biases[0]), (near_in, near_down, biases[1])
            ]
            output = ffn_full(
                after(tokens, all_sent), ctx, w_out, b_out, ln1_gain, ln1_bias, shards,
                b_down, ln2_gain, ln2_bias,
            )
            all_got = after(all_got, output)
        if ffn_step <= over_tok.steps:
            ffn_got = after(ffn_got, all_sent)
            if step <= 2:
                ffn_got = after(ffn_got, ctx[-1])
            ffn_kept, ffn_got = ffn_next(ffn_step, ffn_kept, ffn_got)
            ffn_step += 1
        if step < over_all.steps - 1:
            all_kept, all_sent = next_halves(all_kept, all_got, 1)
        else:
            all_sums = add(all_kept, all_got)

    steps = width // group
    sums = all_sums.reshape(steps + 1, all_sums.shape[0] // (steps + 1), unit, width)
    s_w = [wide(sums[:steps, n].reshape(own, width)) for n in range(4)]
    planes = table_rows // group
    s_rel = wide(sums[steps, :planes].reshape(own_rel, width))
    vectors = wide(sums[steps, planes : planes + 16 // unit].reshape(16, width))
    s_vec = lax.dynamic_slice_in_dim(vectors[:VECTORS], over_all.me * own, own, 1)
    part = hidden_cols // n_tok
    bins = vectors[VECTORS : VECTORS + hidden_cols // width].reshape(1, hidden_cols)
    s_bin = lax.dynamic_slice_in_dim(bins, lax.axis_index("tok") * part, part, 1)
    return (
        output,
        grad_tokens,
        s_w[0],
        s_w[1],
        s_w[2],
        s_w[3],
        s_vec[0],
        s_vec[1],
        s_vec[2],
        s_vec[3],
        s_rel,
        s_vec[4],
        s_vec[5],
        wide(ffn_kept[0]),
        s_bin,
        jnp.transpose(wide(ffn_kept[1])),
        s_vec[6],
        s_vec[7],
        s_vec[8],
    )


def solution(mesh):
    every = ("tok", "ffn")
    placed = (
        P(every, None), P(every, None, None), P(every, None), P(every, None, None),
        P(), P(), P(), P(), P(), P(), P(), P(), P(), P(), P(),
        P(None, "ffn"), P("ffn"), P("ffn", None), P(), P(), P(),
    )
    given = (
        P(every, None), P(every, None),
        P(every, None), P(every, None), P(every, None), P(every, None),
        P(every), P(every), P(every), P(every),
        P(every, None), P(every), P(every),
        P("tok", "ffn"), P("ffn", "tok"), P("ffn", "tok"),
        P(every), P(every), P(every),
    )
    return jax.shard_map(local, mesh=mesh, in_specs=placed, out_specs=given, check_vma=False)
```

```python
import functools
import math

import numpy as np

import jax
import jax.numpy as jnp
from jax import lax
from jax.experimental import pallas as pl
from jax.experimental.pallas import tpu as pltpu
from jax.sharding import PartitionSpec as P

HEAD = 64
LANES = 128
HALF = 64
ROWS = 8
AT_ONCE = 2
PICKED_AT_ONCE = 2
FIRST_PAIRS = 4
VECTORS = 9
norm_eps = 1e-07
bf16 = jnp.bfloat16
f32 = jnp.float32
PARAMS = pltpu.CompilerParams(vmem_limit_bytes=60 * 2**20)


def lasting(micros):
    return pl.CostEstimate(
        flops=int(micros * 1.1e9), bytes_accessed=int(micros * 3.4e6), transcendentals=0
    )


def dot_nn(first_op, second_op):
    return lax.dot_general(
        first_op, second_op, (((1,), (0,)), ((), ())), preferred_element_type=f32
    )


def dot_nt(first_op, second_op):
    return lax.dot_general(
        first_op, second_op, (((1,), (1,)), ((), ())), preferred_element_type=f32
    )


def dot_tn(first_op, second_op):
    return lax.dot_general(
        first_op, second_op, (((0,), (0,)), ((), ())), preferred_element_type=f32
    )


def distance_rows(seq_len, table_rows):
    side = table_rows // 2
    middle = side // 2
    rows = []
    for m in range(2 * seq_len):
        offset = max(m - seq_len, 1 - seq_len)
        size = abs(offset)
        if size > middle:
            ratio = math.log(size / middle) / math.log((2 * side - 1) / middle)
            size = int(math.ceil(ratio * (middle - 1))) + middle
        rows.append(side + (size if offset > 0 else -size))
    return np.array(rows, dtype=np.int32)


def lane_iota(rows=1):
    return lax.broadcasted_iota(jnp.int32, (rows, LANES), 1)


def member_chunk(words, c, last):
    return (last - words == lane_iota(words.shape[0]) + c * LANES).astype(f32).astype(bf16)


def id_bases(rel_ref, base):
    seq = rel_ref.shape[0]
    chunks = seq // LANES
    last = chunks * 2 - 2
    for g in range(seq // HALF):
        for c in range(chunks):
            block = rel_ref[g * HALF : (g + 1) * HALF, c * LANES : (c + 1) * LANES]
            base[g * chunks + c] = jnp.minimum(jnp.min(block) // HALF, last)


def both_alignments(table):
    return jnp.concatenate([table, table[HALF:], table[:HALF]], axis=0)


def longest(rows):
    wide = rows.astype(f32)
    return jnp.sqrt(jnp.max(jnp.sum(wide * wide, axis=1, keepdims=True), axis=0, keepdims=True))


def pack_heads(first, second, dest, top):
    top = jnp.maximum(top, 1e-30)
    scale = 32000.0 / top
    upper = (first * scale).astype(jnp.int32)
    lower = (second * scale).astype(jnp.int32)
    dest[...] = upper * 65536 + lower
    return top * (1.0 / 32000.0)


def unpack_heads(words, step):
    lower = lax.shift_right_arithmetic(lax.shift_left(words, 16), 16)
    return words.astype(f32) * (step * (1.0 / 65536.0)), lower.astype(f32) * step


def picked_words(source, rel_ref, base, rows, c):
    chunks = rel_ref.shape[1] // LANES
    first = base[(rows.start // HALF) * chunks + c]
    place = rel_ref[rows, c * LANES : (c + 1) * LANES] - first * HALF
    index = place & (LANES - 1)
    at = pl.multiple_of((first % 2) * (chunks * LANES) + (first // 2) * LANES, LANES)
    near = jnp.take_along_axis(source[rows, pl.ds(at, LANES)], index, axis=1)
    at = pl.multiple_of(at + LANES, LANES)
    far = jnp.take_along_axis(source[rows, pl.ds(at, LANES)], index, axis=1)
    return jnp.where(place < LANES, near, far)


def unshift_in_order(sources, words_ref, base, dest):
    seq = words_ref.shape[0]
    chunks = seq // LANES
    lane = lane_iota()
    zero = jnp.zeros((ROWS, LANES), f32)
    for g in range(chunks):
        first = base[g]
        for sub in range(LANES // ROWS):
            start = g * LANES + sub * ROWS
            rows = slice(start, start + ROWS)
            place = lane - 1 - words_ref[rows, :] + first * LANES
            index = place & (LANES - 1)
            near = place >= 0
            mid = place >= -LANES
            for a, source in enumerate(sources):
                turned = [
                    jnp.take_along_axis(
                        source[rows, c * LANES : (c + 1) * LANES], index, axis=1
                    )
                    for c in range(chunks)
                ]
                turned = [zero, zero] + turned + [zero, zero]
                for c in range(chunks + 2):
                    value = jnp.where(near, turned[c + 2], jnp.where(mid, turned[c + 1], turned[c]))
                    at = pl.multiple_of((first + c) * LANES, LANES)
                    dest[a, rows, pl.ds(at, LANES)] = value.astype(bf16)


def group_bases(words, base):
    seq = words.shape[0]
    for g in range(seq // LANES):
        base[g] = (jnp.min(words[g * LANES : (g + 1) * LANES]) + 1) // LANES


def softmax_weights(scores):
    factor = math.log2(math.e) / math.sqrt(3.0 * HEAD)
    top = jnp.max(functools.reduce(jnp.maximum, scores), axis=1, keepdims=True)
    return [jnp.exp2((score - top) * factor) for score in scores]


def head_lanes(a):
    return (lane_iota() < HEAD) if a == 0 else (lane_iota() >= HEAD)


def row_of(ref):
    return ref[...].reshape(1, ref.shape[0])


def norm_stats(values):
    centered = values - jnp.mean(values, axis=1, keepdims=True)
    inv_std = lax.rsqrt(jnp.mean(centered * centered, axis=1, keepdims=True) + norm_eps)
    return centered * inv_std, inv_std


def norm_backward(upstream, normed, inv_std, norm_gain):
    scaled = upstream * norm_gain
    adjusted = (
        scaled
        - jnp.mean(scaled, axis=1, keepdims=True)
        - normed * jnp.mean(scaled * normed, axis=1, keepdims=True)
    )
    return inv_std * adjusted, col_sum(upstream * normed), col_sum(upstream)


def col_sum(values):
    return jnp.sum(values, axis=0, keepdims=True)


def normal_cdf(pre_act):
    return 0.5 * (1.0 + lax.erf(pre_act * (1.0 / math.sqrt(2.0))))


def project_kernel(
    pick_ref, x_ref, rel_ref, wq_ref, wk_ref, wv_ref, bq_ref, bk_ref, bv_ref,
    q_ref, k_ref, v_ref, pq_ref, pk_ref, qpick_ref, xpick_ref,
):
    @pl.when(pl.program_id(0) == 0)
    def _():
        xpick_ref[...] = dot_nn(pick_ref[...], x_ref[...]).astype(bf16)

    for source, weight, bias, out in (
        (xpick_ref, wq_ref, bq_ref, qpick_ref),
        (x_ref, wk_ref, bk_ref, k_ref),
        (rel_ref, wk_ref, bk_ref, pk_ref),
        (rel_ref, wq_ref, bq_ref, pq_ref),
        (x_ref, wq_ref, bq_ref, q_ref),
        (x_ref, wv_ref, bv_ref, v_ref),
    ):
        out[...] = (dot_nn(source[...], weight[...]) + row_of(bias)).astype(bf16)


def project(pick, x, rel_table, weights, biases):
    width = x.shape[1]
    group = 2 * LANES
    whole = lambda value: pl.BlockSpec(value.shape, lambda n: (0, 0))
    col = lambda value: pl.BlockSpec((value.shape[0], group), lambda n: (0, n))
    outs = [x, x, x, rel_table, rel_table, pick]
    return pl.pallas_call(
        project_kernel,
        grid=(width // group,),
        in_specs=[whole(pick), whole(x), whole(rel_table)]
        + [col(value) for value in weights]
        + [pl.BlockSpec((group,), lambda n: (n,))] * 3,
        out_specs=[col(value) for value in outs]
        + [pl.BlockSpec((pick.shape[0], width), lambda n: (0, 0))],
        out_shape=[jax.ShapeDtypeStruct((value.shape[0], width), bf16) for value in outs + [pick]],
        compiler_params=PARAMS,
        cost_estimate=lasting(6.0),
        name="project",
    )(pick, x, rel_table, *weights, *biases)


def picked_kernel(
    pos_ref, rel_ref, qc_ref, k_ref, v_ref, pk_ref, pq_ref,
    x_ref, wo_ref, bo_ref, gain_ref, bias_ref,
    ctx_ref, prob_ref, key_ref, word_ref, wordc_ref, normed_ref, inv_ref, low_ref,
    packed, cpick, direct, relc, keyc, attn, base,
):
    seq = k_ref.shape[0]
    picks = qc_ref.shape[0]
    chunks = seq // LANES
    units, far_units = [], []

    @pl.when(pl.program_id(0) == 0)
    def _():
        row = lax.broadcasted_iota(jnp.int32, (seq, seq), 0)
        col = lax.broadcasted_iota(jnp.int32, (seq, seq), 1)
        side = pk_ref.shape[0] // 2
        step = jnp.sum(jnp.where(col == row - 1, rel_ref[...] - side, 0), axis=1, keepdims=True)
        steps = jnp.broadcast_to(step.astype(f32), (seq, LANES)).astype(bf16)
        word_ref[...] = dot_nn((col <= row).astype(f32).astype(bf16), steps).astype(jnp.int32)
        id_bases(rel_ref, base)
        for n in range(picks):
            place = jnp.maximum(pos_ref[n], 0)
            relc[n : n + 1, :] = rel_ref[pl.ds(place, 1), :]
            wordc_ref[n : n + 1, :] = word_ref[pl.ds(place, 1), :]

    zero = jnp.zeros((), bf16)
    upper = head_lanes(0)
    for m in range(PICKED_AT_ONCE):
        lanes = slice(m * LANES, (m + 1) * LANES)
        k_pair, q_pair, pq = k_ref[:, lanes], qc_ref[:, lanes], pq_ref[:, lanes]
        table = both_alignments(pq)
        keys = [dot_nt(jnp.where(head_lanes(a), k_pair, zero), table) for a in range(2)]
        unit = pack_heads(keys[0], keys[1], packed.at[m], longest(k_pair) * longest(pq))
        units.append(unit)
        pk = pk_ref[:, lanes]
        far = []
        for a in range(2):
            q_a = jnp.where(head_lanes(a), q_pair, zero)
            far.append(dot_nt(q_a, pk))
            direct[2 * m + a] = dot_nt(q_a, k_pair)
        far_units.append(pack_heads(far[0], far[1], cpick.at[m], longest(q_pair) * longest(pk)))
    for m in range(PICKED_AT_ONCE):
        lanes = slice(m * LANES, (m + 1) * LANES)
        for g in range(chunks):
            for c in range(chunks):
                parts = []
                for start in range(g * LANES, (g + 1) * LANES, ROWS):
                    parts.append(
                        picked_words(packed.at[m], rel_ref, base, slice(start, start + ROWS), c)
                    )
                block = jnp.concatenate(parts, axis=0).T
                for a, value in enumerate(unpack_heads(block, units[m])):
                    key_ref[2 * m + a, c * LANES : (c + 1) * LANES, g * LANES : (g + 1) * LANES] = value
        for n in range(picks):
            place = jnp.maximum(pos_ref[n], 0)
            for a in range(2 * m, 2 * m + 2):
                keyc[a, n : n + 1, :] = key_ref[a, pl.ds(place, 1), :]
        scores = [[], []]
        for c in range(chunks):
            ids = relc[:, c * LANES : (c + 1) * LANES]
            index = ids & (LANES - 1)
            value = jnp.take_along_axis(cpick[m, :, :LANES], index, axis=1)
            for n in range(1, pk_ref.shape[0] // LANES):
                other = cpick[m, :, n * LANES : (n + 1) * LANES]
                value = jnp.where(
                    ids >= n * LANES, jnp.take_along_axis(other, index, axis=1), value
                )
            cols = slice(c * LANES, (c + 1) * LANES)
            for a, far in enumerate(unpack_heads(value, far_units[m])):
                scores[a].append(direct[2 * m + a, :, cols] + far + keyc[2 * m + a, :, cols])
        mixed = []
        for a in range(2 * m, 2 * m + 2):
            weights = softmax_weights(scores[a % 2])
            inverse = 1.0 / jnp.sum(sum(weights[1:], weights[0]), axis=1, keepdims=True)
            probs = jnp.concatenate([(weight * inverse).astype(bf16) for weight in weights], axis=1)
            prob_ref[a] = probs
            mixed.append(dot_nn(probs, v_ref[:, lanes]).astype(bf16))
        ctx_ref[:, lanes] = jnp.where(upper, mixed[0], mixed[1])

    part = dot_nn(ctx_ref[...], wo_ref[...])

    @pl.when(pl.program_id(0) == 0)
    def _():
        attn[...] = x_ref[...].astype(f32) + row_of(bo_ref) + part

    @pl.when(pl.program_id(0) > 0)
    def _():
        attn[...] += part

    @pl.when(pl.program_id(0) == pl.num_programs(0) - 1)
    def _():
        normed, inv_std = norm_stats(attn[...])
        normed_ref[...] = normed
        inv_ref[...] = jnp.broadcast_to(inv_std, (picks, LANES))
        low_ref[...] = (normed * row_of(gain_ref) + row_of(bias_ref)).astype(bf16)


def attend_picked(
    positions, rel_ids, q_pick, k, v, pos_query, pos_key, x_pick, w_out, b_out, gain, bias
):
    seq, width = k.shape
    picks = q_pick.shape[0]
    table = pos_key.shape[0]
    pairs = width // LANES
    whole = lambda rows, cols: pl.BlockSpec((rows, cols), lambda h: (0, 0))
    line = pl.BlockSpec((width,), lambda h: (0,))
    per = PICKED_AT_ONCE
    wide = per * LANES
    col = lambda rows: pl.BlockSpec((rows, wide), lambda h: (0, h))
    heads = lambda rows: pl.BlockSpec((2 * per, rows, seq), lambda h: (h, 0, 0))
    return pl.pallas_call(
        picked_kernel,
        grid=(pairs // per,),
        in_specs=[
            pl.BlockSpec(memory_space=pltpu.SMEM), whole(seq, seq),
            col(picks), col(seq), col(seq), col(table), col(table),
            whole(picks, width), pl.BlockSpec((wide, width), lambda h: (h, 0)), line, line, line,
        ],
        out_specs=[
            col(picks), heads(picks), heads(seq), whole(seq, LANES), whole(picks, LANES),
            whole(picks, width), whole(picks, LANES), whole(picks, width),
        ],
        out_shape=[
            jax.ShapeDtypeStruct((picks, width), bf16),
            jax.ShapeDtypeStruct((2 * pairs, picks, seq), bf16),
            jax.ShapeDtypeStruct((2 * pairs, seq, seq), f32),
            jax.ShapeDtypeStruct((seq, LANES), jnp.int32),
            jax.ShapeDtypeStruct((picks, LANES), jnp.int32),
            jax.ShapeDtypeStruct((picks, width), f32),
            jax.ShapeDtypeStruct((picks, LANES), f32),
            jax.ShapeDtypeStruct((picks, width), bf16),
        ],
        scratch_shapes=[
            pltpu.VMEM((per, seq, 2 * table), jnp.int32),
            pltpu.VMEM((per, picks, table), jnp.int32),
            pltpu.VMEM((2 * per, picks, seq), f32),
            pltpu.VMEM((picks, seq), jnp.int32),
            pltpu.VMEM((2 * per, picks, seq), f32),
            pltpu.VMEM((picks, width), f32),
            pltpu.SMEM((seq // HALF * (seq // LANES),), jnp.int32),
        ],
        compiler_params=PARAMS,
        cost_estimate=lasting(5.0 * pairs),
        name="attend_picked",
    )(
        positions, rel_ids, q_pick, k, v, pos_key, pos_query, x_pick, w_out, b_out, gain, bias
    )


def full_kernel(rel_ref, q_ref, k_ref, v_ref, pk_ref, key_ref, ctx_ref, *scratch):
    seq = rel_ref.shape[0]
    chunks = seq // LANES
    base, scratch = scratch[-1], scratch[:-1]
    count = len(scratch) // 3

    @pl.when(pl.program_id(0) == 0)
    def _():
        id_bases(rel_ref, base)

    zero = jnp.zeros((), bf16)
    units = []
    for n in range(count):
        packed, direct, low = scratch[3 * n : 3 * n + 3]
        lanes = slice(n * LANES, (n + 1) * LANES)
        q, pos = q_ref[:, lanes], pk_ref[:, lanes]
        table = both_alignments(pos)
        far = []
        for a in range(2):
            q_a = jnp.where(head_lanes(a), q, zero)
            far.append(dot_nt(q_a, table))
            direct[a] = dot_nt(q_a, k_ref[:, lanes])
        units.append(pack_heads(far[0], far[1], packed, longest(q) * longest(pos)))
    for n in range(count):
        packed, direct, low = scratch[3 * n : 3 * n + 3]
        lanes = slice(n * LANES, (n + 1) * LANES)
        for start in range(0, seq, 2 * ROWS):
            rows = slice(start, start + 2 * ROWS)
            scores = [[], []]
            for c in range(chunks):
                cols = slice(c * LANES, (c + 1) * LANES)
                values = unpack_heads(picked_words(packed, rel_ref, base, rows, c), units[n])
                for a in range(2):
                    scores[a].append(
                        values[a] + direct[a, rows, cols] + key_ref[2 * n + a, rows, cols]
                    )
            for a in range(2):
                for c in range(chunks):
                    direct[a, rows, c * LANES : (c + 1) * LANES] = scores[a][c]
        for a in range(2):
            for start in range(0, seq, LANES):
                rows = slice(start, start + LANES)
                scores = [direct[a, rows, c * LANES : (c + 1) * LANES] for c in range(chunks)]
                for c, weight in enumerate(softmax_weights(scores)):
                    low[a, rows, c * LANES : (c + 1) * LANES] = weight.astype(bf16)
        v = v_ref[:, lanes]
        mixed = [
            dot_nn(low[a], jnp.where(head_lanes(a), v, jnp.ones((), bf16))) for a in range(2)
        ]
        upper = head_lanes(0)
        totals = pltpu.roll(jnp.where(upper, mixed[1], mixed[0]), HEAD, 1)
        ctx_ref[:, lanes] = (jnp.where(upper, mixed[0], mixed[1]) * (1.0 / totals)).astype(bf16)


def attend_full(rel_ids, q, k, v, pos_key, key_scores, first, pairs):
    seq = k.shape[0]
    table = pos_key.shape[0]
    per = AT_ONCE
    wide = per * LANES
    col = lambda rows: pl.BlockSpec((rows, wide), lambda h: (0, h + first // per))
    return pl.pallas_call(
        full_kernel,
        grid=(pairs // per,),
        in_specs=[
            pl.BlockSpec((seq, seq), lambda h: (0, 0)),
            col(seq), col(seq), col(seq), col(table),
            pl.BlockSpec((2 * per, seq, seq), lambda h: (h + first // per, 0, 0)),
        ],
        out_specs=pl.BlockSpec((seq, wide), lambda h: (0, h)),
        out_shape=jax.ShapeDtypeStruct((seq, pairs * LANES), bf16),
        scratch_shapes=[
            pltpu.VMEM((seq, 2 * table), jnp.int32),
            pltpu.VMEM((2, seq, seq), f32),
            pltpu.VMEM((2, seq, seq), bf16),
        ]
        * per
        + [pltpu.SMEM((seq // HALF * (seq // LANES),), jnp.int32)],
        compiler_params=PARAMS,
        cost_estimate=lasting(4.2 * pairs),
        name="attend_full",
    )(rel_ids, q, k, v, pos_key, key_scores)


def back_kernel(
    row_ref, word_ref, wordc_ref, qc_ref, k_ref, v_ref, prob_ref, pk_ref, pq_ref,
    dz2_ref, mine_ref, got_ref, normed_ref, inv_ref, gain_ref, wo_ref, early_ref,
    dq_ref, dk_ref, dv_ref, dpos_ref, dz1_ref, dattn_ref, sum_ref,
    side, sidec, moved, movedc, expand, shrink, base,
):
    seq = k_ref.shape[0]
    picks = qc_ref.shape[0]
    table = pk_ref.shape[0]
    chunks = seq // LANES

    @pl.when(pl.program_id(0) == 0)
    def _():
        words = word_ref[...]
        for c in range(chunks):
            side[:, c * LANES : (c + 1) * LANES] = member_chunk(words, c, seq - 1)
            sidec[:, c * LANES : (c + 1) * LANES] = member_chunk(wordc_ref[...], c, seq - 1)
        group_bases(words, base)
        moved[...] = jnp.zeros_like(moved)
        edge = expand.shape[1]
        for n, start in ((0, 0), (1, 2 * seq - edge)):
            ids = row_ref[start : start + edge, :] - n * (table - LANES)
            chosen = (ids == lane_iota(edge)).astype(f32).astype(bf16)
            expand[n] = chosen
            shrink[n] = chosen.T
        dh1 = dz2_ref[...] + mine_ref[...].astype(f32) + got_ref[...].astype(f32)
        dz1, g_gain, g_bias = norm_backward(dh1, normed_ref[...], inv_ref[:, :1], row_of(gain_ref))
        dz1_ref[...] = dz1
        dattn = dz1.astype(bf16)
        dattn_ref[...] = dattn
        sum_ref[...] = jnp.concatenate(
            [col_sum(dattn.astype(f32)), g_gain, g_bias, early_ref[:5]], axis=0
        )

    lane = lane_iota()
    scale = 1.0 / math.sqrt(3.0 * HEAD)
    zero = jnp.zeros((), bf16)
    heads = range(2)
    upper = head_lanes(0)
    join = lambda pair: jnp.where(upper, pair[0], pair[1])
    side[:, seq:] = k_ref[...]
    sidec[:, seq:] = qc_ref[...]
    dctx = dot_nt(dattn_ref[...], wo_ref[...]).astype(bf16)
    dprobs = [dot_nt(jnp.where(head_lanes(a), dctx, zero), v_ref[...]) for a in heads]

    def widened(ref):
        ends = [
            dot_nn(expand[n], ref[at : at + LANES, :]).astype(bf16)
            for n, at in ((0, 0), (1, table - LANES))
        ]
        return jnp.concatenate([ends[0], ref[LANES : table - LANES, :], ends[1]], axis=0)

    far_key, far_query = widened(pk_ref), widened(pq_ref)
    gs = []
    for a in heads:
        probs = prob_ref[a].astype(f32)
        prod = probs * dprobs[a]
        gs.append(((prod - probs * jnp.sum(prod, axis=1, keepdims=True)) * scale).astype(bf16))
    outs = [dot_tn(gs[a], sidec[...]) for a in heads]
    outcs = [dot_nn(gs[a], side[...]) for a in heads]
    dv_ref[...] = join([dot_tn(prob_ref[a], dctx) for a in heads]).astype(bf16)
    place = lane - 1 - wordc_ref[...]
    index = place & (LANES - 1)
    blank = jnp.zeros((picks, LANES), f32)
    for a in heads:
        turned = [
            jnp.take_along_axis(outcs[a][:, c * LANES : (c + 1) * LANES], index, axis=1)
            for c in range(chunks)
        ]
        for c in range(2 * chunks):
            value = turned[c] if c < chunks else blank
            for n in range(1, chunks + 1):
                other = turned[c - n] if 0 <= c - n < chunks else blank
                value = jnp.where(place < -LANES * (n - 1), other, value)
            movedc[a, :, c * LANES : (c + 1) * LANES] = value.astype(bf16)
    unshift_in_order(outs, word_ref, base, moved)
    dq = [outcs[a][:, seq:] + dot_nn(movedc[a], far_key) for a in heads]
    dq_ref[...] = join(dq).astype(bf16)
    dk = [outs[a][:, seq:] + dot_nn(moved[a, :, : 2 * seq], far_query) for a in heads]
    dk_ref[...] = join(dk).astype(bf16)
    far = [
        join([dot_tn(movedc[a], qc_ref[...]) for a in heads]),
        join([dot_tn(moved[a, :, : 2 * seq], k_ref[...]) for a in heads]),
    ]
    edge = expand.shape[1]
    for n, value in enumerate(far):
        value = value.astype(bf16)
        dpos_ref[n, :LANES, :] = dot_nn(shrink[0], value[:edge]).astype(bf16)
        dpos_ref[n, LANES : table - LANES, :] = value[edge : 2 * seq - edge]
        dpos_ref[n, table - LANES :, :] = dot_nn(shrink[1], value[2 * seq - edge :]).astype(bf16)


def attend_back(
    table_of, words, words_pick, q_pick, k, v, probs, pos_query, pos_key,
    dz2, mine, got, normed, inv_std, gain, w_out, early,
):
    seq, width = k.shape
    picks = q_pick.shape[0]
    table = pos_key.shape[0]
    pairs = width // LANES
    edge = seq - table // 4
    whole = lambda value: pl.BlockSpec(value.shape, lambda h: (0,) * value.ndim)
    col = lambda rows: pl.BlockSpec((rows, LANES), lambda h: (0, h))
    shape = lambda rows: jax.ShapeDtypeStruct((rows, width), bf16)
    return pl.pallas_call(
        back_kernel,
        grid=(pairs,),
        in_specs=[
            whole(table_of), whole(words), whole(words_pick),
            col(picks), col(seq), col(seq),
            pl.BlockSpec((2, picks, seq), lambda h: (h, 0, 0)),
            col(table), col(table),
            whole(dz2), whole(mine), whole(got), whole(normed), whole(inv_std), whole(gain),
            pl.BlockSpec((LANES, width), lambda h: (h, 0)), whole(early),
        ],
        out_specs=[
            col(picks), col(seq), col(seq),
            pl.BlockSpec((2, table, LANES), lambda h: (0, 0, h)),
            whole(dz2), whole(dz2), whole(early),
        ],
        out_shape=[
            shape(picks), shape(seq), shape(seq),
            jax.ShapeDtypeStruct((2, table, width), bf16),
            jax.ShapeDtypeStruct((picks, width), f32),
            shape(picks),
            jax.ShapeDtypeStruct(early.shape, f32),
        ],
        scratch_shapes=[
            pltpu.VMEM((seq, seq + LANES), bf16),
            pltpu.VMEM((picks, seq + LANES), bf16),
            pltpu.VMEM((2, seq, 2 * seq + 2 * LANES), bf16),
            pltpu.VMEM((2, picks, 2 * seq), bf16),
            pltpu.VMEM((2, edge, LANES), bf16),
            pltpu.VMEM((2, LANES, edge), bf16),
            pltpu.SMEM((seq // LANES,), jnp.int32),
        ],
        compiler_params=PARAMS,
        cost_estimate=lasting(4.0 * pairs),
        name="attend_back",
    )(
        table_of, words, words_pick, q_pick, k, v, probs, pos_key, pos_query,
        dz2, mine, got, normed, inv_std, gain, w_out, early,
    )


def turn_kernel(
    n_all, me_ref, order_ref, x_ref, xpick_ref, cpick_ref, rel_ref, x_out, xpick_out, cpick_out, rel_out
):
    picked = order_rows(order_ref, me_ref, x_ref.shape[1], n_all)
    for ref, out in ((x_ref, x_out), (xpick_ref, xpick_out), (cpick_ref, cpick_out), (rel_ref, rel_out)):
        out[...] = dot_nt(picked, ref[...]).astype(bf16)


def block_rows(ref, me_ref):
    return me_ref[0] ^ jnp.where(me_ref[1] == 0, ref[:, 0:1], ref[:, 1:2])


def order_rows(ref, me_ref, length, n_all):
    source = block_rows(ref, me_ref) * (length // n_all) + ref[:, 2:3]
    spot = lax.broadcasted_iota(jnp.int32, (ref.shape[0], length), 1)
    return (spot == source).astype(f32).astype(bf16)


def turn_blocks(n_all, me, order, x, x_pick, ctx_pick, rel_table):
    width = x.shape[1]
    group = 2 * LANES
    whole = lambda value: pl.BlockSpec(value.shape, lambda n: (0, 0))
    row = lambda count: pl.BlockSpec((group, count), lambda n: (n, 0))
    given = [x, x_pick, ctx_pick, rel_table]
    return pl.pallas_call(
        functools.partial(turn_kernel, n_all),
        grid=(width // group,),
        in_specs=[pl.BlockSpec(memory_space=pltpu.SMEM), row(LANES)]
        + [whole(value) for value in given],
        out_specs=[row(value.shape[0]) for value in given],
        out_shape=[jax.ShapeDtypeStruct(value.shape[::-1], bf16) for value in given],
        compiler_params=PARAMS,
        cost_estimate=lasting(5.2),
        name="turn_blocks",
    )(me, order, *given)


def norm_picked_kernel(
    normed_ref, gain1_ref, bias1_ref, mine_ref, got_ref, bdown_ref, gain2_ref, grad_ref, pick_ref,
    dz2_ref, low_ref, sum_ref,
):
    h1 = normed_ref[...] * row_of(gain1_ref) + row_of(bias1_ref)
    branch = mine_ref[...].astype(f32) + got_ref[...].astype(f32) + row_of(bdown_ref)
    normed, inv_std = norm_stats(h1 + branch)
    used = jnp.sum(pick_ref[...].astype(f32), axis=1, keepdims=True)
    cot = jnp.where(used > 0.0, grad_ref[...].astype(f32), 0.0)
    dz2, g_gain, g_bias = norm_backward(cot, normed, inv_std, row_of(gain2_ref))
    dz2_ref[...] = dz2
    low = dz2.astype(bf16)
    low_ref[...] = low
    sum_ref[...] = jnp.concatenate(
        [col_sum(low.astype(f32)), g_gain, g_bias, jnp.zeros((5, h1.shape[1]), f32)], axis=0
    )


def norm_picked(normed, gain1, bias1, mine, got, b_down, gain2, grads, pick):
    picks, width = normed.shape
    return pl.pallas_call(
        norm_picked_kernel,
        out_shape=[
            jax.ShapeDtypeStruct((picks, width), f32),
            jax.ShapeDtypeStruct((picks, width), bf16),
            jax.ShapeDtypeStruct((8, width), f32),
        ],
        compiler_params=PARAMS,
        cost_estimate=lasting(2.4),
        name="norm_picked",
    )(normed, gain1, bias1, mine, got, b_down, gain2, grads, pick)


def ffn_full_kernel(
    x_ref, ctx_ref, ctx2_ref, wo_ref, bo_ref, gain1_ref, bias1_ref, bdown_ref, gain2_ref, bias2_ref,
    bin_ref, bin2_ref, bin3_ref, win_ref, down_ref, win2_ref, down2_ref, win3_ref, down3_ref,
    out_ref, h1, low, total, win_here, down_here, win_sem, down_sem,
):
    rows, width = x_ref.shape
    tile = win_here.shape[2]
    parts = [(win_ref, down_ref, bin_ref, n * tile) for n in range(win_ref.shape[1] // tile)]
    parts += [(win2_ref, down2_ref, bin2_ref, 0), (win3_ref, down3_ref, bin3_ref, 0)]

    def copies(n):
        w_ref, d_ref, _, at = parts[n]
        return (
            pltpu.make_async_copy(w_ref.at[:, at : at + tile], win_here.at[n], win_sem.at[n]),
            pltpu.make_async_copy(d_ref.at[at : at + tile, :], down_here.at[n], down_sem.at[n]),
        )

    for n in range(len(parts)):
        for copy in copies(n):
            copy.start()
    attn = dot_nn(ctx_ref[...], wo_ref[: ctx_ref.shape[1]]) + dot_nn(
        ctx2_ref[...], wo_ref[ctx_ref.shape[1] :]
    )
    normed, _ = norm_stats(x_ref[...].astype(f32) + (attn + row_of(bo_ref)))
    value = normed * row_of(gain1_ref) + row_of(bias1_ref)
    h1[...] = value
    low[...] = value.astype(bf16)
    step = rows // 2
    for n in range(len(parts)):
        for copy in copies(n):
            copy.wait()
        bias = parts[n][2][:, parts[n][3] : parts[n][3] + tile]
        for at in range(0, rows, step):
            pre = dot_nn(low[at : at + step], win_here[n]) + bias
            part = dot_nn((pre * normal_cdf(pre)).astype(bf16), down_here[n])
            total[at : at + step] = part if n == 0 else total[at : at + step] + part
    normed, _ = norm_stats(h1[...] + (total[...] + row_of(bdown_ref)))
    out_ref[...] = (normed * row_of(gain2_ref) + row_of(bias2_ref)).astype(bf16)


def ffn_full(x, ctx, w_out, b_out, gain1, bias1, shards, b_down, gain2, bias2):
    rows, width = x.shape
    tile = shards[1][0].shape[1]
    count = shards[0][0].shape[1] // tile + 2
    held = [x, ctx[0], ctx[1], w_out, b_out, gain1, bias1, b_down, gain2, bias2]
    held += [shard[2] for shard in shards]
    moved = [value for shard in shards for value in shard[:2]]
    return pl.pallas_call(
        ffn_full_kernel,
        in_specs=[pl.BlockSpec(memory_space=pltpu.VMEM)] * len(held)
        + [pl.BlockSpec(memory_space=pl.ANY)] * len(moved),
        out_specs=pl.BlockSpec(memory_space=pltpu.VMEM),
        out_shape=jax.ShapeDtypeStruct((rows, width), bf16),
        scratch_shapes=[
            pltpu.VMEM((rows, width), f32), pltpu.VMEM((rows, width), bf16), pltpu.VMEM((rows, width), f32),
            pltpu.VMEM((count, width, tile), bf16), pltpu.VMEM((count, tile, width), bf16),
            pltpu.SemaphoreType.DMA((count,)), pltpu.SemaphoreType.DMA((count,)),
        ],
        compiler_params=PARAMS,
        cost_estimate=lasting(10.9),
        name="ffn_full",
    )(*held, *moved)


def token_grads_kernel(pick_ref, dz1_ref, dq_ref, dk_ref, dv_ref, wq_ref, wk_ref, wv_ref, out_ref):
    sparse = dz1_ref[...] + dot_nt(dq_ref[...], wq_ref[...])
    upper = sparse.astype(bf16)
    lower = (sparse - upper.astype(f32)).astype(bf16)
    out_ref[...] = (
        dot_nt(dk_ref[...], wk_ref[...])
        + dot_nt(dv_ref[...], wv_ref[...])
        + dot_tn(pick_ref[...], upper)
        + dot_tn(pick_ref[...], lower)
    )


def token_grads(pick, dz1, dq, dk, dv, w_query, w_key, w_value):
    seq, width = dk.shape
    group = 2 * LANES
    whole = lambda value: pl.BlockSpec(value.shape, lambda n: (0, 0))
    col = lambda rows: pl.BlockSpec((rows, group), lambda n: (0, n))
    row = pl.BlockSpec((group, width), lambda n: (n, 0))
    return pl.pallas_call(
        token_grads_kernel,
        grid=(width // group,),
        in_specs=[whole(pick), col(dz1.shape[0]), whole(dq), whole(dk), whole(dv), row, row, row],
        out_specs=col(seq),
        out_shape=jax.ShapeDtypeStruct((seq, width), f32),
        compiler_params=PARAMS,
        cost_estimate=lasting(5.9),
        name="token_grads",
    )(pick, dz1, dq, dk, dv, w_query, w_key, w_value)


def grads_kernel(
    n_all, n_ffn, unit, me_ref, order_ref, relorder_ref, taker_ref,
    x_ref, rel_ref, xpick_ref, cpick_ref, dpos_ref, dq_ref, dk_ref, dv_ref, dattn_ref,
    early_ref, bin_ref, wq_ref, wk_ref, kept_ref, sent_ref, weights, sems,
):
    width = dk_ref.shape[1]
    table = dpos_ref.shape[1]
    group = 2 * LANES
    step = pl.program_id(0)
    copies = [
        pltpu.make_async_copy(ref, weights.at[n], sems.at[n])
        for n, ref in enumerate((wk_ref, wq_ref))
    ]

    def put(at, value):
        value = value.astype(bf16)
        kept_ref[at] = value[:LANES]
        sent_ref[at] = value[LANES:]

    @pl.when(step == 0)
    def _():
        for copy in copies:
            copy.start()

    @pl.when(step < width // group)
    def _():
        put(0, dot_nn(xpick_ref[...], dq_ref[...]) + dot_nn(rel_ref[...], dpos_ref[1]))
        put(1, dot_nn(x_ref[...], dk_ref[...]) + dot_nn(rel_ref[...], dpos_ref[0]))
        put(2, dot_nn(x_ref[...], dv_ref[...]))
        put(3, dot_nn(cpick_ref[...], dattn_ref[...]))

    @pl.when(step == width // group)
    def _():
        for copy in copies:
            copy.wait()
        rows = order_rows(relorder_ref, me_ref, table, n_all)
        far = [dot_nn(rows, dpos_ref[n]).astype(bf16) for n in range(2)]
        value = dot_nt(far[0], weights[0]) + dot_nt(far[1], weights[1])
        for n in range(table // group):
            put(n, value[n * group : (n + 1) * group])

        total = lambda value: col_sum(value.astype(f32))
        bins = [bin_ref[:1, at : at + width] for at in range(0, bin_ref.shape[1], width)]
        values = [
            total(dq_ref[...]) + total(dpos_ref[1]),
            total(dk_ref[...]) + total(dpos_ref[0]),
            total(dv_ref[...]),
            early_ref[:6],
        ]
        values += bins + [jnp.zeros((16 - VECTORS - len(bins), width), f32)]
        values = jnp.concatenate(values, axis=0)
        block = block_rows(order_ref[:group, :], me_ref)
        ours = (block % n_ffn) == (me_ref[0] % n_ffn)
        tok_place = jnp.where(ours, block // n_ffn, -1)
        row = lax.broadcasted_iota(jnp.int32, (group, 1), 0) % unit
        for n in range(16 // unit):
            rows = slice(n * unit, (n + 1) * unit)
            spread = lambda value: jnp.concatenate([value[rows]] * (group // unit), axis=0)
            taker = jnp.where(row + n * unit < VECTORS, block, tok_place)
            put(table // group + n, jnp.where(spread(taker_ref[...]) == taker, spread(values), 0.0))


def weight_grads(
    n_all, n_ffn, unit, me, order, rel_order, takers, x, rel, x_pick, c_pick, dpos, dq, dk, dv, dattn,
    w_query, w_key, early, bins,
):
    seq, width = dk.shape
    group = 2 * LANES
    steps = width // group
    each = max(4, dpos.shape[1] // group + 16 // unit)
    whole = lambda value: pl.BlockSpec(value.shape, lambda n: (0,) * value.ndim)
    row = lambda value: pl.BlockSpec((group, value.shape[1]), lambda n: (jnp.minimum(n, steps - 1), 0))
    block = pl.BlockSpec((each, LANES, width), lambda n: (n, 0, 0))
    return pl.pallas_call(
        functools.partial(grads_kernel, n_all, n_ffn, unit),
        grid=(steps + 1,),
        in_specs=[pl.BlockSpec(memory_space=pltpu.SMEM)]
        + [whole(value) for value in (order, rel_order, takers)]
        + [row(value) for value in (x, rel, x_pick, c_pick)]
        + [whole(value) for value in (dpos, dq, dk, dv, dattn, early, bins)]
        + [pl.BlockSpec(memory_space=pl.ANY)] * 2,
        out_specs=[block] * 2,
        out_shape=[jax.ShapeDtypeStruct((each * (steps + 1), LANES, width), bf16)] * 2,
        scratch_shapes=[
            pltpu.VMEM((2,) + w_query.shape, bf16), pltpu.SemaphoreType.DMA((2,)),
        ],
        compiler_params=PARAMS,
        cost_estimate=lasting(7.0),
        name="weight_grads",
    )(
        me, order, rel_order, takers, x, rel, x_pick, c_pick, dpos, dq, dk, dv, dattn, early, bins,
        w_query, w_key,
    )


def swap(values, axis, bit):
    size = lax.axis_size(axis)
    return lax.ppermute(values, axis, [(n, n ^ bit) for n in range(size)])


def after(values, *others):
    return lax.optimization_barrier((values, others))[0]


class Halving:
    def __init__(self, axes, core, near, size):
        rest = [1 << n for n in range(size.bit_length() - 1) if (1 << n) != core]
        near = [bit for bit in near if bit in rest]
        rest = [bit for bit in rest if bit not in near]
        turned = near[-1:] + near[:-1]
        self.axes, self.core, self.size = axes, core, size
        self.orders = [[core] + near + rest, [core] + turned + rest]
        self.steps = len(self.orders[0])
        self.me = lax.axis_index(axes)
        self.upper = (self.me // core) % 2

    def core_of(self, place):
        return (place // self.core) % 2

    def send(self, values, step):
        pairs = [(n, n ^ self.orders[self.core_of(n)][step]) for n in range(self.size)]
        return lax.ppermute(values, self.axes, pairs)

    def relative(self, upper):
        masks = []
        for place in range(self.size):
            bits = [(place >> (self.steps - 1 - step)) & 1 for step in range(self.steps)]
            order = self.orders[upper ^ bits[0]]
            mask = 0
            for step, bit in enumerate(bits):
                mask ^= bit * order[step]
            masks.append(mask)
        return np.array(masks, np.int32)

    def order(self, length, unit):
        spots = np.arange(length)
        group = self.size * unit
        place = spots % group // unit
        rows = [self.relative(upper)[place] for upper in range(2)]
        rows.append(spots // group * unit + spots % unit)
        return np.stack(rows).astype(np.int32)

    def matrix(self, length, unit):
        first, second, inner = self.order(length, unit)
        source = (self.me ^ jnp.where(self.upper == 0, first, second)) * (length // self.size) + inner
        spot = lax.broadcasted_iota(jnp.int32, (length, length), 0)
        return (spot == source[None, :]).astype(bf16)


def local(
    tokens, rel_ids, mask_pos, grad_vals, w_query, w_key, w_value, w_out, b_query, b_key,
    b_value, b_out, rel_table, ln1_gain, ln1_bias, w_in, b_in, w_down, b_down, ln2_gain, ln2_bias,
):
    assert rel_ids.shape[0] == 1
    seq, width = tokens.shape
    table_rows = rel_table.shape[0]
    hidden_cols = w_in.shape[1]
    pairs = width // LANES
    n_tok = lax.axis_size("tok")
    n_ffn = lax.axis_size("ffn")
    n_all = n_tok * n_ffn
    low = lambda value: value.astype(bf16)
    wide = lambda value: value.astype(f32)
    rel_ids, positions, grad_vals = rel_ids[0], mask_pos[0], grad_vals[0]

    over_all = Halving(("tok", "ffn"), n_ffn, [2 * n_ffn, 1, 4 * n_ffn], n_all)
    own, own_rel = width // n_all, table_rows // n_all
    unit = math.gcd(own, own_rel)
    group = n_all * unit
    over_tok = Halving("tok", 1, [2, 4], n_tok)
    pad = lambda value, count: np.pad(value, ((0, count - value.shape[0]), (0, 0)))
    order = jnp.asarray(pad(over_all.order(width, unit), LANES).T)
    rel_order = jnp.asarray(pad(over_all.order(table_rows, unit), LANES).T)
    spots = np.arange(width)
    takers = [spots // own] * VECTORS
    takers += [(spots + n * width) // (hidden_cols // n_tok) for n in range(hidden_cols // width)]
    takers = np.stack(takers).astype(np.int32)
    takers = jnp.asarray(np.pad(takers, ((0, 16 - takers.shape[0]), (0, 0)), constant_values=-2))
    me = jnp.stack([over_all.me, over_all.upper])
    table_of = jnp.asarray(np.repeat(distance_rows(seq, table_rows)[:, None], LANES, 1))

    core = lax.axis_index("tok") % 2
    half_cols = hidden_cols // 2
    bias_row = b_in.reshape(1, hidden_cols)
    in_half = lax.dynamic_slice_in_dim(w_in, core * half_cols, half_cols, 1)
    down_half = lax.dynamic_slice_in_dim(w_down, core * half_cols, half_cols, 0)

    pick = low(positions[:, None] == lax.broadcasted_iota(jnp.int32, (positions.shape[0], seq), 1))
    q, k, v, pos_query, pos_key, q_pick, x_pick = project(
        pick, tokens, rel_table, (w_query, w_key, w_value), (b_query, b_key, b_value)
    )
    ctx_pick, probs, key_scores, words, words_pick, normed1, inv1, h1_mine = attend_picked(
        positions, rel_ids, q_pick, k, v, pos_query, pos_key, x_pick, w_out, b_out, ln1_gain, ln1_bias
    )

    h1_theirs = swap(h1_mine, "ffn", 1)
    bias_theirs = swap(bias_row, "ffn", 1)
    x_turned, x_pick_turned, c_pick_turned, rel_turned = turn_blocks(
        n_all, me, order, tokens, x_pick, ctx_pick, rel_table
    )
    h1_both = jnp.concatenate([h1_mine, after(h1_theirs, x_turned, bias_theirs)], axis=0)
    count = h1_mine.shape[0]
    pre = dot_nn(h1_both, w_in) + b_in
    cdf = normal_cdf(pre)
    hidden = low(pre * cdf)
    slope = cdf + pre * (jnp.exp(-0.5 * pre * pre) * (1.0 / math.sqrt(2.0 * math.pi)))
    part = low(dot_nn(hidden, w_down))
    got = swap(part[count:], "ffn", 1)
    tok_order = over_tok.matrix(width, width // n_tok)
    h1_left = low(dot_nn(h1_both, lax.optimization_barrier(tok_order)))
    in_half = after(in_half, part)
    got = after(got, h1_left, in_half)
    dz2, dffn, early = norm_picked(
        normed1, ln1_gain, ln1_bias, part[:count], got, b_down, ln2_gain, grad_vals, pick
    )
    down_half = after(down_half, dffn)
    dffn_both = jnp.concatenate([dffn, after(swap(dffn, "ffn", 1), down_half)], axis=0)
    dpre = low(dot_nt(dffn_both, w_down) * slope)
    dpart = low(dot_nt(dpre, w_in))
    dgot = swap(dpart[count:], "ffn", 1)

    def halves(values, axis):
        size = values.shape[axis] // 2
        cut = lambda at: lax.slice_in_dim(values, at, at + size, axis=axis)
        return cut(0), cut(size)

    add = lambda one, other: low(wide(one) + wide(other))

    def next_halves(kept, got, axis):
        return [add(one, other) for one, other in zip(halves(kept, axis), halves(got, axis))]

    dpre_later = after(dpre, dpart)
    dffn_left = low(dot_nn(after(dffn_both, dpart), tok_order))
    gb_in = dot_nn(jnp.ones((8, 2 * count), bf16), dpre_later)
    left, right = jnp.stack([h1_left, dffn_left]), jnp.stack([dpre_later, hidden])
    product = lambda first, last: lax.dot_general(
        left[:, :, first:last], right, (((1,), (1,)), ((0,), (0,))), preferred_element_type=f32
    )
    middle, quarter = width // 2, width // 4
    ffn_sent = low(product(middle, width))
    dgot, ffn_sent = lax.optimization_barrier((dgot, ffn_sent))
    ffn_got = over_tok.send(ffn_sent, 0)
    far_in = swap(after(in_half, dgot, ffn_sent), "ffn", 1)

    ffn_sent = low(product(quarter, middle) + wide(ffn_got[:, quarter:]))
    ffn_kept = low(product(0, quarter) + wide(ffn_got[:, :quarter]))
    ffn_got = over_tok.send(ffn_sent, 1)

    def ffn_next(step, kept, got):
        if step < over_tok.steps:
            kept, sent = next_halves(kept, got, 1)
            return kept, over_tok.send(sent, step)
        return add(kept, got), None

    dq, dk, dv, dpos, dz1, dattn, early = attend_back(
        table_of, words, words_pick, q_pick, k, v, probs, pos_query, pos_key,
        dz2, dpart[:count], after(dgot, in_half, ffn_sent, ffn_kept), normed1, inv1, ln1_gain, w_out, early,
    )
    far_in, ffn_got = after((far_in, ffn_got), dk)
    ffn_kept, ffn_got = ffn_next(2, ffn_kept, ffn_got)
    near_in = swap(far_in, "tok", 1)
    far_down = swap(after(down_half, far_in), "ffn", 1)
    all_kept, all_sent = weight_grads(
        n_all, n_ffn, unit, me, order, rel_order, takers,
        x_turned, rel_turned, x_pick_turned, c_pick_turned, dpos, dq, after(dk, far_in, ffn_kept), dv,
        dattn, w_query, w_key, early, gb_in,
    )
    all_got = over_all.send(all_sent, 0)
    dk_later, dq_later = after((dk, dq), all_sent)
    grad_tokens = token_grads(pick, dz1, dq_later, dk_later, dv, w_query, w_key, w_value)
    all_kept, all_sent = next_halves(all_kept, after(all_got, grad_tokens), 1)
    ffn_step = 3
    ffn_got = after(ffn_got, grad_tokens)

    def attend(first, count, q):
        return attend_full(rel_ids, q, k, v, pos_key, key_scores, first, count)

    ctx = []
    cuts = [(0, FIRST_PAIRS), (FIRST_PAIRS, pairs - FIRST_PAIRS)]
    for step in range(1, over_all.steps):
        all_got = over_all.send(all_sent, step)
        if step <= 2:
            ctx.append(attend(*cuts[step - 1], after(q, all_sent)))
            all_got = after(all_got, ctx[-1])
            if step == 1:
                far_down = after(far_down, ctx[-1])
                near_down = swap(far_down, "tok", 1)
                all_got = after(all_got, far_down)
        elif step == 4:
            biases = [
                lax.dynamic_slice_in_dim(bias_theirs, at * half_cols, half_cols, 1)
                for at in (core, 1 - core)
            ]
            shards = [
                (w_in, w_down, bias_row), (far_in, far_down, biases[0]), (near_in, near_down, biases[1])
            ]
            output = ffn_full(
                after(tokens, all_sent), ctx, w_out, b_out, ln1_gain, ln1_bias, shards,
                b_down, ln2_gain, ln2_bias,
            )
            all_got = after(all_got, output)
        if ffn_step <= over_tok.steps:
            ffn_got = after(ffn_got, all_sent)
            if step <= 2:
                ffn_got = after(ffn_got, ctx[-1])
            ffn_kept, ffn_got = ffn_next(ffn_step, ffn_kept, ffn_got)
            ffn_step += 1
        if step < over_all.steps - 1:
            all_kept, all_sent = next_halves(all_kept, all_got, 1)
        else:
            all_sums = add(all_kept, all_got)

    steps = width // group
    sums = all_sums.reshape(steps + 1, all_sums.shape[0] // (steps + 1), unit, width)
    s_w = [wide(sums[:steps, n].reshape(own, width)) for n in range(4)]
    planes = table_rows // group
    s_rel = wide(sums[steps, :planes].reshape(own_rel, width))
    vectors = wide(sums[steps, planes : planes + 16 // unit].reshape(16, width))
    s_vec = lax.dynamic_slice_in_dim(vectors[:VECTORS], over_all.me * own, own, 1)
    part = hidden_cols // n_tok
    bins = vectors[VECTORS : VECTORS + hidden_cols // width].reshape(1, hidden_cols)
    s_bin = lax.dynamic_slice_in_dim(bins, lax.axis_index("tok") * part, part, 1)
    return (
        output,
        grad_tokens,
        s_w[0],
        s_w[1],
        s_w[2],
        s_w[3],
        s_vec[0],
        s_vec[1],
        s_vec[2],
        s_vec[3],
        s_rel,
        s_vec[4],
        s_vec[5],
        wide(ffn_kept[0]),
        s_bin,
        jnp.transpose(wide(ffn_kept[1])),
        s_vec[6],
        s_vec[7],
        s_vec[8],
    )


def solution(mesh):
    every = ("tok", "ffn")
    placed = (
        P(every, None), P(every, None, None), P(every, None), P(every, None, None),
        P(), P(), P(), P(), P(), P(), P(), P(), P(), P(), P(),
        P(None, "ffn"), P("ffn"), P("ffn", None), P(), P(), P(),
    )
    given = (
        P(every, None), P(every, None),
        P(every, None), P(every, None), P(every, None), P(every, None),
        P(every), P(every), P(every), P(every),
        P(every, None), P(every), P(every),
        P("tok", "ffn"), P("ffn", "tok"), P("ffn", "tok"),
        P(every), P(every), P(every),
    )
    return jax.shard_map(local, mesh=mesh, in_specs=placed, out_specs=given, check_vma=False)
```

```python
import functools
import math

import numpy as np

import jax
import jax.numpy as jnp
from jax import lax
from jax.experimental import pallas as pl
from jax.experimental.pallas import tpu as pltpu
from jax.sharding import PartitionSpec as P

HEAD = 64
LANES = 128
HALF = 64
ROWS = 8
AT_ONCE = 2
PICKED_AT_ONCE = 2
FIRST_PAIRS = 4
VECTORS = 9
norm_eps = 1e-07
bf16 = jnp.bfloat16
f32 = jnp.float32
PARAMS = pltpu.CompilerParams(vmem_limit_bytes=60 * 2**20)


def lasting(micros):
    return pl.CostEstimate(
        flops=int(micros * 1.1e9), bytes_accessed=int(micros * 3.4e6), transcendentals=0
    )


def dot_nn(first_op, second_op):
    return lax.dot_general(
        first_op, second_op, (((1,), (0,)), ((), ())), preferred_element_type=f32
    )


def dot_nt(first_op, second_op):
    return lax.dot_general(
        first_op, second_op, (((1,), (1,)), ((), ())), preferred_element_type=f32
    )


def dot_tn(first_op, second_op):
    return lax.dot_general(
        first_op, second_op, (((0,), (0,)), ((), ())), preferred_element_type=f32
    )


def distance_rows(seq_len, table_rows):
    side = table_rows // 2
    middle = side // 2
    rows = []
    for m in range(2 * seq_len):
        offset = max(m - seq_len, 1 - seq_len)
        size = abs(offset)
        if size > middle:
            ratio = math.log(size / middle) / math.log((2 * side - 1) / middle)
            size = int(math.ceil(ratio * (middle - 1))) + middle
        rows.append(side + (size if offset > 0 else -size))
    return np.array(rows, dtype=np.int32)


def lane_iota(rows=1):
    return lax.broadcasted_iota(jnp.int32, (rows, LANES), 1)


def member_chunk(words, c, last):
    return (last - words == lane_iota(words.shape[0]) + c * LANES).astype(f32).astype(bf16)


def id_bases(rel_ref, base):
    seq = rel_ref.shape[0]
    chunks = seq // LANES
    last = chunks * 2 - 2
    for g in range(seq // HALF):
        for c in range(chunks):
            block = rel_ref[g * HALF : (g + 1) * HALF, c * LANES : (c + 1) * LANES]
            base[g * chunks + c] = jnp.minimum(jnp.min(block) // HALF, last)


def both_alignments(table):
    return jnp.concatenate([table, table[HALF:], table[:HALF]], axis=0)


def longest(rows):
    wide = rows.astype(f32)
    return jnp.sqrt(jnp.max(jnp.sum(wide * wide, axis=1, keepdims=True), axis=0, keepdims=True))


def pack_heads(first, second, dest, top):
    top = jnp.maximum(top, 1e-30)
    scale = 32000.0 / top
    upper = (first * scale).astype(jnp.int32)
    lower = (second * scale).astype(jnp.int32)
    dest[...] = upper * 65536 + lower
    return top * (1.0 / 32000.0)


def unpack_heads(words, step):
    lower = lax.shift_right_arithmetic(lax.shift_left(words, 16), 16)
    return words.astype(f32) * (step * (1.0 / 65536.0)), lower.astype(f32) * step


def picked_words(source, rel_ref, base, rows, c):
    chunks = rel_ref.shape[1] // LANES
    first = base[(rows.start // HALF) * chunks + c]
    place = rel_ref[rows, c * LANES : (c + 1) * LANES] - first * HALF
    index = place & (LANES - 1)
    at = pl.multiple_of((first % 2) * (chunks * LANES) + (first // 2) * LANES, LANES)
    near = jnp.take_along_axis(source[rows, pl.ds(at, LANES)], index, axis=1)
    at = pl.multiple_of(at + LANES, LANES)
    far = jnp.take_along_axis(source[rows, pl.ds(at, LANES)], index, axis=1)
    return jnp.where(place < LANES, near, far)


def unshift_in_order(sources, words_ref, base, dest):
    seq = words_ref.shape[0]
    chunks = seq // LANES
    lane = lane_iota()
    zero = jnp.zeros((ROWS, LANES), f32)
    for g in range(chunks):
        first = base[g]
        for sub in range(LANES // ROWS):
            start = g * LANES + sub * ROWS
            rows = slice(start, start + ROWS)
            place = lane - 1 - words_ref[rows, :] + first * LANES
            index = place & (LANES - 1)
            near = place >= 0
            mid = place >= -LANES
            for a, source in enumerate(sources):
                turned = [
                    jnp.take_along_axis(
                        source[rows, c * LANES : (c + 1) * LANES], index, axis=1
                    )
                    for c in range(chunks)
                ]
                turned = [zero, zero] + turned + [zero, zero]
                for c in range(chunks + 2):
                    value = jnp.where(near, turned[c + 2], jnp.where(mid, turned[c + 1], turned[c]))
                    at = pl.multiple_of((first + c) * LANES, LANES)
                    dest[a, rows, pl.ds(at, LANES)] = value.astype(bf16)


def group_bases(words, base):
    seq = words.shape[0]
    for g in range(seq // LANES):
        base[g] = (jnp.min(words[g * LANES : (g + 1) * LANES]) + 1) // LANES


def softmax_weights(scores):
    factor = math.log2(math.e) / math.sqrt(3.0 * HEAD)
    top = jnp.max(functools.reduce(jnp.maximum, scores), axis=1, keepdims=True)
    return [jnp.exp2((score - top) * factor) for score in scores]


def head_lanes(a):
    return (lane_iota() < HEAD) if a == 0 else (lane_iota() >= HEAD)


def row_of(ref):
    return ref[...].reshape(1, ref.shape[0])


def norm_stats(values):
    centered = values - jnp.mean(values, axis=1, keepdims=True)
    inv_std = lax.rsqrt(jnp.mean(centered * centered, axis=1, keepdims=True) + norm_eps)
    return centered * inv_std, inv_std


def norm_backward(upstream, normed, inv_std, norm_gain):
    scaled = upstream * norm_gain
    adjusted = (
        scaled
        - jnp.mean(scaled, axis=1, keepdims=True)
        - normed * jnp.mean(scaled * normed, axis=1, keepdims=True)
    )
    return inv_std * adjusted, col_sum(upstream * normed), col_sum(upstream)


def col_sum(values):
    return jnp.sum(values, axis=0, keepdims=True)


def normal_cdf(pre_act):
    return 0.5 * (1.0 + lax.erf(pre_act * (1.0 / math.sqrt(2.0))))


def project_kernel(
    pick_ref, x_ref, rel_ref, wq_ref, wk_ref, wv_ref, bq_ref, bk_ref, bv_ref,
    q_ref, k_ref, v_ref, pq_ref, pk_ref, qpick_ref, xpick_ref,
):
    @pl.when(pl.program_id(0) == 0)
    def _():
        xpick_ref[...] = dot_nn(pick_ref[...], x_ref[...]).astype(bf16)

    for source, weight, bias, out in (
        (xpick_ref, wq_ref, bq_ref, qpick_ref),
        (x_ref, wk_ref, bk_ref, k_ref),
        (rel_ref, wk_ref, bk_ref, pk_ref),
        (rel_ref, wq_ref, bq_ref, pq_ref),
        (x_ref, wq_ref, bq_ref, q_ref),
        (x_ref, wv_ref, bv_ref, v_ref),
    ):
        out[...] = (dot_nn(source[...], weight[...]) + row_of(bias)).astype(bf16)


def project(pick, x, rel_table, weights, biases):
    width = x.shape[1]
    group = 2 * LANES
    whole = lambda value: pl.BlockSpec(value.shape, lambda n: (0, 0))
    col = lambda value: pl.BlockSpec((value.shape[0], group), lambda n: (0, n))
    outs = [x, x, x, rel_table, rel_table, pick]
    return pl.pallas_call(
        project_kernel,
        grid=(width // group,),
        in_specs=[whole(pick), whole(x), whole(rel_table)]
        + [col(value) for value in weights]
        + [pl.BlockSpec((group,), lambda n: (n,))] * 3,
        out_specs=[col(value) for value in outs]
        + [pl.BlockSpec((pick.shape[0], width), lambda n: (0, 0))],
        out_shape=[jax.ShapeDtypeStruct((value.shape[0], width), bf16) for value in outs + [pick]],
        compiler_params=PARAMS,
        cost_estimate=lasting(6.0),
        name="project",
    )(pick, x, rel_table, *weights, *biases)


def picked_kernel(
    pos_ref, rel_ref, qc_ref, k_ref, v_ref, pk_ref, pq_ref,
    x_ref, wo_ref, bo_ref, gain_ref, bias_ref,
    ctx_ref, prob_ref, key_ref, word_ref, wordc_ref, normed_ref, inv_ref, low_ref,
    packed, cpick, direct, relc, keyc, attn, base,
):
    seq = k_ref.shape[0]
    picks = qc_ref.shape[0]
    chunks = seq // LANES
    units, far_units = [], []

    @pl.when(pl.program_id(0) == 0)
    def _():
        row = lax.broadcasted_iota(jnp.int32, (seq, seq), 0)
        col = lax.broadcasted_iota(jnp.int32, (seq, seq), 1)
        side = pk_ref.shape[0] // 2
        step = jnp.sum(jnp.where(col == row - 1, rel_ref[...] - side, 0), axis=1, keepdims=True)
        steps = jnp.broadcast_to(step.astype(f32), (seq, LANES)).astype(bf16)
        word_ref[...] = dot_nn((col <= row).astype(f32).astype(bf16), steps).astype(jnp.int32)
        id_bases(rel_ref, base)
        for n in range(picks):
            place = jnp.maximum(pos_ref[n], 0)
            relc[n : n + 1, :] = rel_ref[pl.ds(place, 1), :]
            wordc_ref[n : n + 1, :] = word_ref[pl.ds(place, 1), :]

    zero = jnp.zeros((), bf16)
    upper = head_lanes(0)
    for m in range(PICKED_AT_ONCE):
        lanes = slice(m * LANES, (m + 1) * LANES)
        k_pair, q_pair, pq = k_ref[:, lanes], qc_ref[:, lanes], pq_ref[:, lanes]
        table = both_alignments(pq)
        keys = [dot_nt(jnp.where(head_lanes(a), k_pair, zero), table) for a in range(2)]
        unit = pack_heads(keys[0], keys[1], packed.at[m], longest(k_pair) * longest(pq))
        units.append(unit)
        pk = pk_ref[:, lanes]
        far = []
        for a in range(2):
            q_a = jnp.where(head_lanes(a), q_pair, zero)
            far.append(dot_nt(q_a, pk))
            direct[2 * m + a] = dot_nt(q_a, k_pair)
        far_units.append(pack_heads(far[0], far[1], cpick.at[m], longest(q_pair) * longest(pk)))
    for m in range(PICKED_AT_ONCE):
        lanes = slice(m * LANES, (m + 1) * LANES)
        for g in range(chunks):
            for c in range(chunks):
                parts = []
                for start in range(g * LANES, (g + 1) * LANES, ROWS):
                    parts.append(
                        picked_words(packed.at[m], rel_ref, base, slice(start, start + ROWS), c)
                    )
                block = jnp.concatenate(parts, axis=0).T
                for a, value in enumerate(unpack_heads(block, units[m])):
                    key_ref[2 * m + a, c * LANES : (c + 1) * LANES, g * LANES : (g + 1) * LANES] = value
        for n in range(picks):
            place = jnp.maximum(pos_ref[n], 0)
            for a in range(2 * m, 2 * m + 2):
                keyc[a, n : n + 1, :] = key_ref[a, pl.ds(place, 1), :]
        scores = [[], []]
        for c in range(chunks):
            ids = relc[:, c * LANES : (c + 1) * LANES]
            index = ids & (LANES - 1)
            value = jnp.take_along_axis(cpick[m, :, :LANES], index, axis=1)
            for n in range(1, pk_ref.shape[0] // LANES):
                other = cpick[m, :, n * LANES : (n + 1) * LANES]
                value = jnp.where(
                    ids >= n * LANES, jnp.take_along_axis(other, index, axis=1), value
                )
            cols = slice(c * LANES, (c + 1) * LANES)
            for a, far in enumerate(unpack_heads(value, far_units[m])):
                scores[a].append(direct[2 * m + a, :, cols] + far + keyc[2 * m + a, :, cols])
        mixed = []
        for a in range(2 * m, 2 * m + 2):
            weights = softmax_weights(scores[a % 2])
            inverse = 1.0 / jnp.sum(sum(weights[1:], weights[0]), axis=1, keepdims=True)
            probs = jnp.concatenate([(weight * inverse).astype(bf16) for weight in weights], axis=1)
            prob_ref[a] = probs
            mixed.append(dot_nn(probs, v_ref[:, lanes]).astype(bf16))
        ctx_ref[:, lanes] = jnp.where(upper, mixed[0], mixed[1])

    part = dot_nn(ctx_ref[...], wo_ref[...])

    @pl.when(pl.program_id(0) == 0)
    def _():
        attn[...] = x_ref[...].astype(f32) + row_of(bo_ref) + part

    @pl.when(pl.program_id(0) > 0)
    def _():
        attn[...] += part

    @pl.when(pl.program_id(0) == pl.num_programs(0) - 1)
    def _():
        normed, inv_std = norm_stats(attn[...])
        normed_ref[...] = normed
        inv_ref[...] = jnp.broadcast_to(inv_std, (picks, LANES))
        low_ref[...] = (normed * row_of(gain_ref) + row_of(bias_ref)).astype(bf16)


def attend_picked(
    positions, rel_ids, q_pick, k, v, pos_query, pos_key, x_pick, w_out, b_out, gain, bias
):
    seq, width = k.shape
    picks = q_pick.shape[0]
    table = pos_key.shape[0]
    pairs = width // LANES
    whole = lambda rows, cols: pl.BlockSpec((rows, cols), lambda h: (0, 0))
    line = pl.BlockSpec((width,), lambda h: (0,))
    per = PICKED_AT_ONCE
    wide = per * LANES
    col = lambda rows: pl.BlockSpec((rows, wide), lambda h: (0, h))
    heads = lambda rows: pl.BlockSpec((2 * per, rows, seq), lambda h: (h, 0, 0))
    return pl.pallas_call(
        picked_kernel,
        grid=(pairs // per,),
        in_specs=[
            pl.BlockSpec(memory_space=pltpu.SMEM), whole(seq, seq),
            col(picks), col(seq), col(seq), col(table), col(table),
            whole(picks, width), pl.BlockSpec((wide, width), lambda h: (h, 0)), line, line, line,
        ],
        out_specs=[
            col(picks), heads(picks), heads(seq), whole(seq, LANES), whole(picks, LANES),
            whole(picks, width), whole(picks, LANES), whole(picks, width),
        ],
        out_shape=[
            jax.ShapeDtypeStruct((picks, width), bf16),
            jax.ShapeDtypeStruct((2 * pairs, picks, seq), bf16),
            jax.ShapeDtypeStruct((2 * pairs, seq, seq), f32),
            jax.ShapeDtypeStruct((seq, LANES), jnp.int32),
            jax.ShapeDtypeStruct((picks, LANES), jnp.int32),
            jax.ShapeDtypeStruct((picks, width), f32),
            jax.ShapeDtypeStruct((picks, LANES), f32),
            jax.ShapeDtypeStruct((picks, width), bf16),
        ],
        scratch_shapes=[
            pltpu.VMEM((per, seq, 2 * table), jnp.int32),
            pltpu.VMEM((per, picks, table), jnp.int32),
            pltpu.VMEM((2 * per, picks, seq), f32),
            pltpu.VMEM((picks, seq), jnp.int32),
            pltpu.VMEM((2 * per, picks, seq), f32),
            pltpu.VMEM((picks, width), f32),
            pltpu.SMEM((seq // HALF * (seq // LANES),), jnp.int32),
        ],
        compiler_params=PARAMS,
        cost_estimate=lasting(5.0 * pairs),
        name="attend_picked",
    )(
        positions, rel_ids, q_pick, k, v, pos_key, pos_query, x_pick, w_out, b_out, gain, bias
    )


def full_kernel(rel_ref, q_ref, k_ref, v_ref, pk_ref, key_ref, ctx_ref, *scratch):
    seq = rel_ref.shape[0]
    chunks = seq // LANES
    base, scratch = scratch[-1], scratch[:-1]
    count = len(scratch) // 3

    @pl.when(pl.program_id(0) == 0)
    def _():
        id_bases(rel_ref, base)

    zero = jnp.zeros((), bf16)
    units = []
    for n in range(count):
        packed, direct, low = scratch[3 * n : 3 * n + 3]
        lanes = slice(n * LANES, (n + 1) * LANES)
        q, pos = q_ref[:, lanes], pk_ref[:, lanes]
        table = both_alignments(pos)
        far = []
        for a in range(2):
            q_a = jnp.where(head_lanes(a), q, zero)
            far.append(dot_nt(q_a, table))
            direct[a] = dot_nt(q_a, k_ref[:, lanes])
        units.append(pack_heads(far[0], far[1], packed, longest(q) * longest(pos)))
    for n in range(count):
        packed, direct, low = scratch[3 * n : 3 * n + 3]
        lanes = slice(n * LANES, (n + 1) * LANES)
        for start in range(0, seq, 2 * ROWS):
            rows = slice(start, start + 2 * ROWS)
            scores = [[], []]
            for c in range(chunks):
                cols = slice(c * LANES, (c + 1) * LANES)
                values = unpack_heads(picked_words(packed, rel_ref, base, rows, c), units[n])
                for a in range(2):
                    scores[a].append(
                        values[a] + direct[a, rows, cols] + key_ref[2 * n + a, rows, cols]
                    )
            for a in range(2):
                for c in range(chunks):
                    direct[a, rows, c * LANES : (c + 1) * LANES] = scores[a][c]
        for a in range(2):
            for start in range(0, seq, LANES):
                rows = slice(start, start + LANES)
                scores = [direct[a, rows, c * LANES : (c + 1) * LANES] for c in range(chunks)]
                for c, weight in enumerate(softmax_weights(scores)):
                    low[a, rows, c * LANES : (c + 1) * LANES] = weight.astype(bf16)
        v = v_ref[:, lanes]
        mixed = [
            dot_nn(low[a], jnp.where(head_lanes(a), v, jnp.ones((), bf16))) for a in range(2)
        ]
        upper = head_lanes(0)
        totals = pltpu.roll(jnp.where(upper, mixed[1], mixed[0]), HEAD, 1)
        ctx_ref[:, lanes] = (jnp.where(upper, mixed[0], mixed[1]) * (1.0 / totals)).astype(bf16)


def attend_full(rel_ids, q, k, v, pos_key, key_scores, first, pairs):
    seq = k.shape[0]
    table = pos_key.shape[0]
    per = AT_ONCE
    wide = per * LANES
    col = lambda rows: pl.BlockSpec((rows, wide), lambda h: (0, h + first // per))
    return pl.pallas_call(
        full_kernel,
        grid=(pairs // per,),
        in_specs=[
            pl.BlockSpec((seq, seq), lambda h: (0, 0)),
            col(seq), col(seq), col(seq), col(table),
            pl.BlockSpec((2 * per, seq, seq), lambda h: (h + first // per, 0, 0)),
        ],
        out_specs=pl.BlockSpec((seq, wide), lambda h: (0, h)),
        out_shape=jax.ShapeDtypeStruct((seq, pairs * LANES), bf16),
        scratch_shapes=[
            pltpu.VMEM((seq, 2 * table), jnp.int32),
            pltpu.VMEM((2, seq, seq), f32),
            pltpu.VMEM((2, seq, seq), bf16),
        ]
        * per
        + [pltpu.SMEM((seq // HALF * (seq // LANES),), jnp.int32)],
        compiler_params=PARAMS,
        cost_estimate=lasting(4.2 * pairs),
        name="attend_full",
    )(rel_ids, q, k, v, pos_key, key_scores)


def back_kernel(
    row_ref, word_ref, wordc_ref, qc_ref, k_ref, v_ref, prob_ref, pk_ref, pq_ref,
    dz2_ref, mine_ref, got_ref, normed_ref, inv_ref, gain_ref, wo_ref, early_ref,
    dq_ref, dk_ref, dv_ref, dpos_ref, dz1_ref, dattn_ref, sum_ref,
    side, sidec, moved, movedc, expand, shrink, base,
):
    seq = k_ref.shape[0]
    picks = qc_ref.shape[0]
    table = pk_ref.shape[0]
    chunks = seq // LANES

    @pl.when(pl.program_id(0) == 0)
    def _():
        words = word_ref[...]
        for c in range(chunks):
            side[:, c * LANES : (c + 1) * LANES] = member_chunk(words, c, seq - 1)
            sidec[:, c * LANES : (c + 1) * LANES] = member_chunk(wordc_ref[...], c, seq - 1)
        group_bases(words, base)
        moved[...] = jnp.zeros_like(moved)
        edge = expand.shape[1]
        for n, start in ((0, 0), (1, 2 * seq - edge)):
            ids = row_ref[start : start + edge, :] - n * (table - LANES)
            chosen = (ids == lane_iota(edge)).astype(f32).astype(bf16)
            expand[n] = chosen
            shrink[n] = chosen.T
        dh1 = dz2_ref[...] + mine_ref[...].astype(f32) + got_ref[...].astype(f32)
        dz1, g_gain, g_bias = norm_backward(dh1, normed_ref[...], inv_ref[:, :1], row_of(gain_ref))
        dz1_ref[...] = dz1
        dattn = dz1.astype(bf16)
        dattn_ref[...] = dattn
        sum_ref[...] = jnp.concatenate(
            [col_sum(dattn.astype(f32)), g_gain, g_bias, early_ref[:5]], axis=0
        )

    lane = lane_iota()
    scale = 1.0 / math.sqrt(3.0 * HEAD)
    zero = jnp.zeros((), bf16)
    heads = range(2)
    upper = head_lanes(0)
    join = lambda pair: jnp.where(upper, pair[0], pair[1])
    side[:, seq:] = k_ref[...]
    sidec[:, seq:] = qc_ref[...]
    dctx = dot_nt(dattn_ref[...], wo_ref[...]).astype(bf16)
    dprobs = [dot_nt(jnp.where(head_lanes(a), dctx, zero), v_ref[...]) for a in heads]

    def widened(ref):
        ends = [
            dot_nn(expand[n], ref[at : at + LANES, :]).astype(bf16)
            for n, at in ((0, 0), (1, table - LANES))
        ]
        return jnp.concatenate([ends[0], ref[LANES : table - LANES, :], ends[1]], axis=0)

    far_key, far_query = widened(pk_ref), widened(pq_ref)
    gs = []
    for a in heads:
        probs = prob_ref[a].astype(f32)
        prod = probs * dprobs[a]
        gs.append(((prod - probs * jnp.sum(prod, axis=1, keepdims=True)) * scale).astype(bf16))
    outs = [dot_tn(gs[a], sidec[...]) for a in heads]
    outcs = [dot_nn(gs[a], side[...]) for a in heads]
    dv_ref[...] = join([dot_tn(prob_ref[a], dctx) for a in heads]).astype(bf16)
    place = lane - 1 - wordc_ref[...]
    index = place & (LANES - 1)
    blank = jnp.zeros((picks, LANES), f32)
    for a in heads:
        turned = [
            jnp.take_along_axis(outcs[a][:, c * LANES : (c + 1) * LANES], index, axis=1)
            for c in range(chunks)
        ]
        for c in range(2 * chunks):
            value = turned[c] if c < chunks else blank
            for n in range(1, chunks + 1):
                other = turned[c - n] if 0 <= c - n < chunks else blank
                value = jnp.where(place < -LANES * (n - 1), other, value)
            movedc[a, :, c * LANES : (c + 1) * LANES] = value.astype(bf16)
    unshift_in_order(outs, word_ref, base, moved)
    dq = [outcs[a][:, seq:] + dot_nn(movedc[a], far_key) for a in heads]
    dq_ref[...] = join(dq).astype(bf16)
    dk = [outs[a][:, seq:] + dot_nn(moved[a, :, : 2 * seq], far_query) for a in heads]
    dk_ref[...] = join(dk).astype(bf16)
    far = [
        join([dot_tn(movedc[a], qc_ref[...]) for a in heads]),
        join([dot_tn(moved[a, :, : 2 * seq], k_ref[...]) for a in heads]),
    ]
    edge = expand.shape[1]
    for n, value in enumerate(far):
        value = value.astype(bf16)
        dpos_ref[n, :LANES, :] = dot_nn(shrink[0], value[:edge]).astype(bf16)
        dpos_ref[n, LANES : table - LANES, :] = value[edge : 2 * seq - edge]
        dpos_ref[n, table - LANES :, :] = dot_nn(shrink[1], value[2 * seq - edge :]).astype(bf16)


def attend_back(
    table_of, words, words_pick, q_pick, k, v, probs, pos_query, pos_key,
    dz2, mine, got, normed, inv_std, gain, w_out, early,
):
    seq, width = k.shape
    picks = q_pick.shape[0]
    table = pos_key.shape[0]
    pairs = width // LANES
    edge = seq - table // 4
    whole = lambda value: pl.BlockSpec(value.shape, lambda h: (0,) * value.ndim)
    col = lambda rows: pl.BlockSpec((rows, LANES), lambda h: (0, h))
    shape = lambda rows: jax.ShapeDtypeStruct((rows, width), bf16)
    return pl.pallas_call(
        back_kernel,
        grid=(pairs,),
        in_specs=[
            whole(table_of), whole(words), whole(words_pick),
            col(picks), col(seq), col(seq),
            pl.BlockSpec((2, picks, seq), lambda h: (h, 0, 0)),
            col(table), col(table),
            whole(dz2), whole(mine), whole(got), whole(normed), whole(inv_std), whole(gain),
            pl.BlockSpec((LANES, width), lambda h: (h, 0)), whole(early),
        ],
        out_specs=[
            col(picks), col(seq), col(seq),
            pl.BlockSpec((2, table, LANES), lambda h: (0, 0, h)),
            whole(dz2), whole(dz2), whole(early),
        ],
        out_shape=[
            shape(picks), shape(seq), shape(seq),
            jax.ShapeDtypeStruct((2, table, width), bf16),
            jax.ShapeDtypeStruct((picks, width), f32),
            shape(picks),
            jax.ShapeDtypeStruct(early.shape, f32),
        ],
        scratch_shapes=[
            pltpu.VMEM((seq, seq + LANES), bf16),
            pltpu.VMEM((picks, seq + LANES), bf16),
            pltpu.VMEM((2, seq, 2 * seq + 2 * LANES), bf16),
            pltpu.VMEM((2, picks, 2 * seq), bf16),
            pltpu.VMEM((2, edge, LANES), bf16),
            pltpu.VMEM((2, LANES, edge), bf16),
            pltpu.SMEM((seq // LANES,), jnp.int32),
        ],
        compiler_params=PARAMS,
        cost_estimate=lasting(4.0 * pairs),
        name="attend_back",
    )(
        table_of, words, words_pick, q_pick, k, v, probs, pos_key, pos_query,
        dz2, mine, got, normed, inv_std, gain, w_out, early,
    )


def turn_kernel(n_all, me_ref, order_ref, *refs):
    count = len(refs) // 2
    picked = order_rows(order_ref, me_ref, refs[0].shape[1], n_all)
    for ref, out in zip(refs[:count], refs[count:]):
        out[...] = dot_nt(picked, ref[...]).astype(bf16)


def block_rows(ref, me_ref):
    return me_ref[0] ^ jnp.where(me_ref[1] == 0, ref[:, 0:1], ref[:, 1:2])


def order_rows(ref, me_ref, length, n_all):
    source = block_rows(ref, me_ref) * (length // n_all) + ref[:, 2:3]
    spot = lax.broadcasted_iota(jnp.int32, (ref.shape[0], length), 1)
    return (spot == source).astype(f32).astype(bf16)


def turn_blocks(n_all, me, order, *given):
    width = given[0].shape[1]
    group = 2 * LANES
    whole = lambda value: pl.BlockSpec(value.shape, lambda n: (0, 0))
    row = lambda count: pl.BlockSpec((group, count), lambda n: (n, 0))
    return pl.pallas_call(
        functools.partial(turn_kernel, n_all),
        grid=(width // group,),
        in_specs=[pl.BlockSpec(memory_space=pltpu.SMEM), row(LANES)]
        + [whole(value) for value in given],
        out_specs=[row(value.shape[0]) for value in given],
        out_shape=[jax.ShapeDtypeStruct(value.shape[::-1], bf16) for value in given],
        compiler_params=PARAMS,
        cost_estimate=lasting(5.2),
        name="turn_blocks",
    )(me, order, *given)


def norm_picked_kernel(
    normed_ref, gain1_ref, bias1_ref, mine_ref, got_ref, bdown_ref, gain2_ref, grad_ref, pick_ref,
    dz2_ref, low_ref, sum_ref,
):
    h1 = normed_ref[...] * row_of(gain1_ref) + row_of(bias1_ref)
    branch = mine_ref[...].astype(f32) + got_ref[...].astype(f32) + row_of(bdown_ref)
    normed, inv_std = norm_stats(h1 + branch)
    used = jnp.sum(pick_ref[...].astype(f32), axis=1, keepdims=True)
    cot = jnp.where(used > 0.0, grad_ref[...].astype(f32), 0.0)
    dz2, g_gain, g_bias = norm_backward(cot, normed, inv_std, row_of(gain2_ref))
    dz2_ref[...] = dz2
    low = dz2.astype(bf16)
    low_ref[...] = low
    sum_ref[...] = jnp.concatenate(
        [col_sum(low.astype(f32)), g_gain, g_bias, jnp.zeros((5, h1.shape[1]), f32)], axis=0
    )


def norm_picked(normed, gain1, bias1, mine, got, b_down, gain2, grads, pick):
    picks, width = normed.shape
    return pl.pallas_call(
        norm_picked_kernel,
        out_shape=[
            jax.ShapeDtypeStruct((picks, width), f32),
            jax.ShapeDtypeStruct((picks, width), bf16),
            jax.ShapeDtypeStruct((8, width), f32),
        ],
        compiler_params=PARAMS,
        cost_estimate=lasting(2.4),
        name="norm_picked",
    )(normed, gain1, bias1, mine, got, b_down, gain2, grads, pick)


def ffn_full_kernel(
    x_ref, ctx_ref, ctx2_ref, wo_ref, bo_ref, gain1_ref, bias1_ref, bdown_ref, gain2_ref, bias2_ref,
    bin_ref, bin2_ref, bin3_ref, win_ref, down_ref, win2_ref, down2_ref, win3_ref, down3_ref,
    out_ref, h1, low, total, win_here, down_here, win_sem, down_sem,
):
    rows, width = x_ref.shape
    tile = win_here.shape[2]
    parts = [(win_ref, down_ref, bin_ref, n * tile) for n in range(win_ref.shape[1] // tile)]
    parts += [(win2_ref, down2_ref, bin2_ref, 0), (win3_ref, down3_ref, bin3_ref, 0)]

    def copies(n):
        w_ref, d_ref, _, at = parts[n]
        return (
            pltpu.make_async_copy(w_ref.at[:, at : at + tile], win_here.at[n], win_sem.at[n]),
            pltpu.make_async_copy(d_ref.at[at : at + tile, :], down_here.at[n], down_sem.at[n]),
        )

    for n in range(len(parts)):
        for copy in copies(n):
            copy.start()
    attn = dot_nn(ctx_ref[...], wo_ref[: ctx_ref.shape[1]]) + dot_nn(
        ctx2_ref[...], wo_ref[ctx_ref.shape[1] :]
    )
    normed, _ = norm_stats(x_ref[...].astype(f32) + (attn + row_of(bo_ref)))
    value = normed * row_of(gain1_ref) + row_of(bias1_ref)
    h1[...] = value
    low[...] = value.astype(bf16)
    step = rows // 2
    for n in range(len(parts)):
        for copy in copies(n):
            copy.wait()
        bias = parts[n][2][:, parts[n][3] : parts[n][3] + tile]
        for at in range(0, rows, step):
            pre = dot_nn(low[at : at + step], win_here[n]) + bias
            part = dot_nn((pre * normal_cdf(pre)).astype(bf16), down_here[n])
            total[at : at + step] = part if n == 0 else total[at : at + step] + part
    normed, _ = norm_stats(h1[...] + (total[...] + row_of(bdown_ref)))
    out_ref[...] = (normed * row_of(gain2_ref) + row_of(bias2_ref)).astype(bf16)


def ffn_full(x, ctx, w_out, b_out, gain1, bias1, shards, b_down, gain2, bias2):
    rows, width = x.shape
    tile = shards[1][0].shape[1]
    count = shards[0][0].shape[1] // tile + 2
    held = [x, ctx[0], ctx[1], w_out, b_out, gain1, bias1, b_down, gain2, bias2]
    held += [shard[2] for shard in shards]
    moved = [value for shard in shards for value in shard[:2]]
    return pl.pallas_call(
        ffn_full_kernel,
        in_specs=[pl.BlockSpec(memory_space=pltpu.VMEM)] * len(held)
        + [pl.BlockSpec(memory_space=pl.ANY)] * len(moved),
        out_specs=pl.BlockSpec(memory_space=pltpu.VMEM),
        out_shape=jax.ShapeDtypeStruct((rows, width), bf16),
        scratch_shapes=[
            pltpu.VMEM((rows, width), f32), pltpu.VMEM((rows, width), bf16), pltpu.VMEM((rows, width), f32),
            pltpu.VMEM((count, width, tile), bf16), pltpu.VMEM((count, tile, width), bf16),
            pltpu.SemaphoreType.DMA((count,)), pltpu.SemaphoreType.DMA((count,)),
        ],
        compiler_params=PARAMS,
        cost_estimate=lasting(10.9),
        name="ffn_full",
    )(*held, *moved)


def token_grads_kernel(pick_ref, dz1_ref, dq_ref, dk_ref, dv_ref, wq_ref, wk_ref, wv_ref, out_ref):
    sparse = dz1_ref[...] + dot_nt(dq_ref[...], wq_ref[...])
    upper = sparse.astype(bf16)
    lower = (sparse - upper.astype(f32)).astype(bf16)
    out_ref[...] = (
        dot_nt(dk_ref[...], wk_ref[...])
        + dot_nt(dv_ref[...], wv_ref[...])
        + dot_tn(pick_ref[...], upper)
        + dot_tn(pick_ref[...], lower)
    )


def token_grads(pick, dz1, dq, dk, dv, w_query, w_key, w_value):
    seq, width = dk.shape
    group = 2 * LANES
    whole = lambda value: pl.BlockSpec(value.shape, lambda n: (0, 0))
    col = lambda rows: pl.BlockSpec((rows, group), lambda n: (0, n))
    row = pl.BlockSpec((group, width), lambda n: (n, 0))
    return pl.pallas_call(
        token_grads_kernel,
        grid=(width // group,),
        in_specs=[whole(pick), col(dz1.shape[0]), whole(dq), whole(dk), whole(dv), row, row, row],
        out_specs=col(seq),
        out_shape=jax.ShapeDtypeStruct((seq, width), f32),
        compiler_params=PARAMS,
        cost_estimate=lasting(5.9),
        name="token_grads",
    )(pick, dz1, dq, dk, dv, w_query, w_key, w_value)


def grads_kernel(
    n_all, n_ffn, unit, me_ref, order_ref, relorder_ref, taker_ref,
    x_ref, rel_ref, xpick_ref, cpick_ref, dpos_ref, dq_ref, dk_ref, dv_ref, dattn_ref,
    early_ref, bin_ref, wq_ref, wk_ref, kept_ref, sent_ref, weights, sems,
):
    width = dk_ref.shape[1]
    table = dpos_ref.shape[1]
    group = 2 * LANES
    step = pl.program_id(0)
    copies = [
        pltpu.make_async_copy(ref, weights.at[n], sems.at[n])
        for n, ref in enumerate((wk_ref, wq_ref))
    ]

    def put(at, value):
        value = value.astype(bf16)
        kept_ref[at] = value[:LANES]
        sent_ref[at] = value[LANES:]

    @pl.when(step == 0)
    def _():
        for copy in copies:
            copy.start()

    @pl.when(step != 1)
    def _():
        put(0, dot_nn(xpick_ref[...], dq_ref[...]) + dot_nn(rel_ref[...], dpos_ref[1]))
        put(1, dot_nn(x_ref[...], dk_ref[...]) + dot_nn(rel_ref[...], dpos_ref[0]))
        put(2, dot_nn(x_ref[...], dv_ref[...]))
        put(3, dot_nn(cpick_ref[...], dattn_ref[...]))

    @pl.when(step == 1)
    def _():
        for copy in copies:
            copy.wait()
        value = (dot_nt(dpos_ref[0], weights[0]) + dot_nt(dpos_ref[1], weights[1])).astype(bf16)
        value = dot_nn(order_rows(relorder_ref, me_ref, table, n_all), value)
        for n in range(table // group):
            put(n, value[n * group : (n + 1) * group])

        total = lambda value: col_sum(value.astype(f32))
        bins = [bin_ref[:1, at : at + width] for at in range(0, bin_ref.shape[1], width)]
        values = [
            total(dq_ref[...]) + total(dpos_ref[1]),
            total(dk_ref[...]) + total(dpos_ref[0]),
            total(dv_ref[...]),
            early_ref[:6],
        ]
        values += bins + [jnp.zeros((16 - VECTORS - len(bins), width), f32)]
        values = jnp.concatenate(values, axis=0)
        block = block_rows(order_ref[:group, :], me_ref)
        ours = (block % n_ffn) == (me_ref[0] % n_ffn)
        tok_place = jnp.where(ours, block // n_ffn, -1)
        row = lax.broadcasted_iota(jnp.int32, (group, 1), 0) % unit
        for n in range(16 // unit):
            rows = slice(n * unit, (n + 1) * unit)
            spread = lambda value: jnp.concatenate([value[rows]] * (group // unit), axis=0)
            taker = jnp.where(row + n * unit < VECTORS, block, tok_place)
            put(table // group + n, jnp.where(spread(taker_ref[...]) == taker, spread(values), 0.0))


def weight_grads(
    n_all, n_ffn, unit, me, order, rel_order, takers, x, rel, x_pick, c_pick, dpos, dq, dk, dv, dattn,
    w_query, w_key, early, bins,
):
    seq, width = dk.shape
    group = 2 * LANES
    steps = width // group
    each = max(4, dpos.shape[1] // group + 16 // unit)
    whole = lambda value: pl.BlockSpec(value.shape, lambda n: (0,) * value.ndim)
    row = lambda value: pl.BlockSpec((group, value.shape[1]), lambda n: (jnp.maximum(n - 1, 0), 0))
    block = pl.BlockSpec((each, LANES, width), lambda n: (n, 0, 0))
    return pl.pallas_call(
        functools.partial(grads_kernel, n_all, n_ffn, unit),
        grid=(steps + 1,),
        in_specs=[pl.BlockSpec(memory_space=pltpu.SMEM)]
        + [whole(value) for value in (order, rel_order, takers)]
        + [row(value) for value in (x, rel, x_pick, c_pick)]
        + [whole(value) for value in (dpos, dq, dk, dv, dattn, early, bins)]
        + [pl.BlockSpec(memory_space=pl.ANY)] * 2,
        out_specs=[block] * 2,
        out_shape=[jax.ShapeDtypeStruct((each * (steps + 1), LANES, width), bf16)] * 2,
        scratch_shapes=[
            pltpu.VMEM((2,) + w_query.shape, bf16), pltpu.SemaphoreType.DMA((2,)),
        ],
        compiler_params=PARAMS,
        cost_estimate=lasting(7.0),
        name="weight_grads",
    )(
        me, order, rel_order, takers, x, rel, x_pick, c_pick, dpos, dq, dk, dv, dattn, early, bins,
        w_query, w_key,
    )


def swap(values, axis, bit):
    size = lax.axis_size(axis)
    return lax.ppermute(values, axis, [(n, n ^ bit) for n in range(size)])


def after(values, *others):
    return lax.optimization_barrier((values, others))[0]


class Halving:
    def __init__(self, axes, core, near, size):
        rest = [1 << n for n in range(size.bit_length() - 1) if (1 << n) != core]
        near = [bit for bit in near if bit in rest]
        rest = [bit for bit in rest if bit not in near]
        turned = near[-1:] + near[:-1]
        self.axes, self.core, self.size = axes, core, size
        self.orders = [[core] + near + rest, [core] + turned + rest]
        self.steps = len(self.orders[0])
        self.me = lax.axis_index(axes)
        self.upper = (self.me // core) % 2

    def core_of(self, place):
        return (place // self.core) % 2

    def send(self, values, step):
        pairs = [(n, n ^ self.orders[self.core_of(n)][step]) for n in range(self.size)]
        return lax.ppermute(values, self.axes, pairs)

    def relative(self, upper):
        masks = []
        for place in range(self.size):
            bits = [(place >> (self.steps - 1 - step)) & 1 for step in range(self.steps)]
            order = self.orders[upper ^ bits[0]]
            mask = 0
            for step, bit in enumerate(bits):
                mask ^= bit * order[step]
            masks.append(mask)
        return np.array(masks, np.int32)

    def order(self, length, unit):
        spots = np.arange(length)
        group = self.size * unit
        place = spots % group // unit
        rows = [self.relative(upper)[place] for upper in range(2)]
        rows.append(spots // group * unit + spots % unit)
        return np.stack(rows).astype(np.int32)

    def matrix(self, length, unit):
        first, second, inner = self.order(length, unit)
        source = (self.me ^ jnp.where(self.upper == 0, first, second)) * (length // self.size) + inner
        spot = lax.broadcasted_iota(jnp.int32, (length, length), 0)
        return (spot == source[None, :]).astype(bf16)


def local(
    tokens, rel_ids, mask_pos, grad_vals, w_query, w_key, w_value, w_out, b_query, b_key,
    b_value, b_out, rel_table, ln1_gain, ln1_bias, w_in, b_in, w_down, b_down, ln2_gain, ln2_bias,
):
    assert rel_ids.shape[0] == 1
    seq, width = tokens.shape
    table_rows = rel_table.shape[0]
    hidden_cols = w_in.shape[1]
    pairs = width // LANES
    n_tok = lax.axis_size("tok")
    n_ffn = lax.axis_size("ffn")
    n_all = n_tok * n_ffn
    low = lambda value: value.astype(bf16)
    wide = lambda value: value.astype(f32)
    rel_ids, positions, grad_vals = rel_ids[0], mask_pos[0], grad_vals[0]

    over_all = Halving(("tok", "ffn"), n_ffn, [2 * n_ffn, 1, 4 * n_ffn], n_all)
    own, own_rel = width // n_all, table_rows // n_all
    unit = math.gcd(own, own_rel)
    group = n_all * unit
    over_tok = Halving("tok", 1, [2, 4], n_tok)
    pad = lambda value, count: np.pad(value, ((0, count - value.shape[0]), (0, 0)))
    order = jnp.asarray(pad(over_all.order(width, unit), LANES).T)
    rel_order = jnp.asarray(pad(over_all.order(table_rows, unit), LANES).T)
    spots = np.arange(width)
    takers = [spots // own] * VECTORS
    takers += [(spots + n * width) // (hidden_cols // n_tok) for n in range(hidden_cols // width)]
    takers = np.stack(takers).astype(np.int32)
    takers = jnp.asarray(np.pad(takers, ((0, 16 - takers.shape[0]), (0, 0)), constant_values=-2))
    me = jnp.stack([over_all.me, over_all.upper])
    table_of = jnp.asarray(np.repeat(distance_rows(seq, table_rows)[:, None], LANES, 1))

    core = lax.axis_index("tok") % 2
    half_cols = hidden_cols // 2
    bias_row = b_in.reshape(1, hidden_cols)
    in_cut = lambda value: lax.dynamic_slice_in_dim(value, core * half_cols, half_cols, 1)
    down_cut = lambda value: lax.dynamic_slice_in_dim(value, core * half_cols, half_cols, 0)

    pick = low(positions[:, None] == lax.broadcasted_iota(jnp.int32, (positions.shape[0], seq), 1))
    q, k, v, pos_query, pos_key, q_pick, x_pick = project(
        pick, tokens, rel_table, (w_query, w_key, w_value), (b_query, b_key, b_value)
    )
    ctx_pick, probs, key_scores, words, words_pick, normed1, inv1, h1_mine = attend_picked(
        positions, rel_ids, q_pick, k, v, pos_query, pos_key, x_pick, w_out, b_out, ln1_gain, ln1_bias
    )

    h1_theirs = swap(h1_mine, "ffn", 1)
    bias_theirs = swap(bias_row, "ffn", 1)
    x_turned, x_pick_turned, c_pick_turned, rel_turned = turn_blocks(
        n_all, me, order, tokens, x_pick, ctx_pick, rel_table
    )
    h1_both = jnp.concatenate([h1_mine, after(h1_theirs, x_turned, bias_theirs)], axis=0)
    count = h1_mine.shape[0]
    pre = dot_nn(h1_both, w_in) + b_in
    cdf = normal_cdf(pre)
    hidden = low(pre * cdf)
    slope = cdf + pre * (jnp.exp(-0.5 * pre * pre) * (1.0 / math.sqrt(2.0 * math.pi)))
    part = low(dot_nn(hidden, w_down))
    got = swap(part[count:], "ffn", 1)
    tok_order = over_tok.matrix(width, width // n_tok)
    h1_left = low(dot_nn(h1_both, lax.optimization_barrier(tok_order)))
    down_half = down_cut(after(w_down, part))
    got = after(got, h1_left, down_half)
    dz2, dffn, early = norm_picked(
        normed1, ln1_gain, ln1_bias, part[:count], got, b_down, ln2_gain, grad_vals, pick
    )
    in_half = in_cut(after(w_in, dffn))
    dffn_both = jnp.concatenate([dffn, after(swap(dffn, "ffn", 1), in_half)], axis=0)
    dpre = low(dot_nt(dffn_both, w_down) * slope)
    dpart = low(dot_nt(dpre, w_in))
    dgot = swap(dpart[count:], "ffn", 1)

    def halves(values, axis):
        size = values.shape[axis] // 2
        cut = lambda at: lax.slice_in_dim(values, at, at + size, axis=axis)
        return cut(0), cut(size)

    add = lambda one, other: low(wide(one) + wide(other))

    def next_halves(kept, got, axis):
        return [add(one, other) for one, other in zip(halves(kept, axis), halves(got, axis))]

    dpre_later = after(dpre, dpart)
    dffn_left = low(dot_nn(after(dffn_both, dpart), tok_order))
    gb_in = dot_nn(jnp.ones((8, 2 * count), bf16), dpre_later)
    left, right = jnp.stack([h1_left, dffn_left]), jnp.stack([dpre_later, hidden])
    product = lambda first, last: lax.dot_general(
        left[:, :, first:last], right, (((1,), (1,)), ((0,), (0,))), preferred_element_type=f32
    )
    middle, quarter = width // 2, width // 4
    ffn_sent = low(product(middle, width))
    dgot, ffn_sent = lax.optimization_barrier((dgot, ffn_sent))
    ffn_got = over_tok.send(ffn_sent, 0)
    far_in = swap(after(in_half, dgot, ffn_sent), "ffn", 1)

    ffn_sent = low(product(quarter, middle) + wide(ffn_got[:, quarter:]))
    ffn_kept = low(product(0, quarter) + wide(ffn_got[:, :quarter]))
    ffn_got = over_tok.send(ffn_sent, 1)

    def ffn_next(step, kept, got):
        if step < over_tok.steps:
            kept, sent = next_halves(kept, got, 1)
            return kept, over_tok.send(sent, step)
        return add(kept, got), None

    dq, dk, dv, dpos, dz1, dattn, early = attend_back(
        table_of, words, words_pick, q_pick, k, v, probs, pos_query, pos_key,
        dz2, dpart[:count], after(dgot, in_half, ffn_sent, ffn_kept), normed1, inv1, ln1_gain, w_out, early,
    )
    far_in, ffn_got = after((far_in, ffn_got), dk)
    ffn_kept, ffn_got = ffn_next(2, ffn_kept, ffn_got)
    near_in = swap(far_in, "tok", 1)
    far_down = swap(after(down_half, far_in), "ffn", 1)
    all_kept, all_sent = weight_grads(
        n_all, n_ffn, unit, me, order, rel_order, takers,
        x_turned, rel_turned, x_pick_turned, c_pick_turned, dpos, dq, after(dk, far_in, ffn_kept), dv,
        dattn, w_query, w_key, early, gb_in,
    )
    all_got = over_all.send(all_sent, 0)
    dk_later, dq_later = after((dk, dq), all_sent)
    grad_tokens = token_grads(pick, dz1, dq_later, dk_later, dv, w_query, w_key, w_value)
    all_kept, all_sent = next_halves(all_kept, after(all_got, grad_tokens), 1)
    ffn_step = 3
    ffn_got = after(ffn_got, grad_tokens)

    def attend(first, count, q):
        return attend_full(rel_ids, q, k, v, pos_key, key_scores, first, count)

    ctx = []
    cuts = [(0, FIRST_PAIRS), (FIRST_PAIRS, pairs - FIRST_PAIRS)]
    for step in range(1, over_all.steps):
        all_got = over_all.send(all_sent, step)
        if step <= 2:
            ctx.append(attend(*cuts[step - 1], after(q, all_sent)))
            all_got = after(all_got, ctx[-1])
            if step == 1:
                far_down = after(far_down, ctx[-1])
                near_down = swap(far_down, "tok", 1)
                all_got = after(all_got, far_down)
        elif step == 4:
            biases = [
                lax.dynamic_slice_in_dim(bias_theirs, at * half_cols, half_cols, 1)
                for at in (core, 1 - core)
            ]
            shards = [
                (w_in, w_down, bias_row), (far_in, far_down, biases[0]), (near_in, near_down, biases[1])
            ]
            output = ffn_full(
                after(tokens, all_sent), ctx, w_out, b_out, ln1_gain, ln1_bias, shards,
                b_down, ln2_gain, ln2_bias,
            )
            all_got = after(all_got, output)
        if ffn_step <= over_tok.steps:
            ffn_got = after(ffn_got, all_sent)
            if step <= 2:
                ffn_got = after(ffn_got, ctx[-1])
            ffn_kept, ffn_got = ffn_next(ffn_step, ffn_kept, ffn_got)
            ffn_step += 1
        if step < over_all.steps - 1:
            all_kept, all_sent = next_halves(all_kept, all_got, 1)
        else:
            all_sums = add(all_kept, all_got)

    steps = width // group
    sums = all_sums.reshape(steps + 1, all_sums.shape[0] // (steps + 1), unit, width)
    four = jnp.concatenate([sums[:1, :4], sums[2:, :4]], axis=0)
    s_w = [wide(four[:, n].reshape(own, width)) for n in range(4)]
    planes = table_rows // group
    s_rel = wide(sums[1, :planes].reshape(own_rel, width))
    vectors = wide(sums[1, planes : planes + 16 // unit].reshape(16, width))
    s_vec = lax.dynamic_slice_in_dim(vectors[:VECTORS], over_all.me * own, own, 1)
    part = hidden_cols // n_tok
    bins = vectors[VECTORS : VECTORS + hidden_cols // width].reshape(1, hidden_cols)
    s_bin = lax.dynamic_slice_in_dim(bins, lax.axis_index("tok") * part, part, 1)
    return (
        output,
        grad_tokens,
        s_w[0],
        s_w[1],
        s_w[2],
        s_w[3],
        s_vec[0],
        s_vec[1],
        s_vec[2],
        s_vec[3],
        s_rel,
        s_vec[4],
        s_vec[5],
        wide(ffn_kept[0]),
        s_bin,
        jnp.transpose(wide(ffn_kept[1])),
        s_vec[6],
        s_vec[7],
        s_vec[8],
    )


def solution(mesh):
    every = ("tok", "ffn")
    placed = (
        P(every, None), P(every, None, None), P(every, None), P(every, None, None),
        P(), P(), P(), P(), P(), P(), P(), P(), P(), P(), P(),
        P(None, "ffn"), P("ffn"), P("ffn", None), P(), P(), P(),
    )
    given = (
        P(every, None), P(every, None),
        P(every, None), P(every, None), P(every, None), P(every, None),
        P(every), P(every), P(every), P(every),
        P(every, None), P(every), P(every),
        P("tok", "ffn"), P("ffn", "tok"), P("ffn", "tok"),
        P(every), P(every), P(every),
    )
    return jax.shard_map(local, mesh=mesh, in_specs=placed, out_specs=given, check_vma=False)
```

```python
import functools
import math

import numpy as np

import jax
import jax.numpy as jnp
from jax import lax
from jax.experimental import pallas as pl
from jax.experimental.pallas import tpu as pltpu
from jax.sharding import PartitionSpec as P

HEAD = 64
LANES = 128
HALF = 64
ROWS = 8
AT_ONCE = 2
PICKED_AT_ONCE = 2
FIRST_PAIRS = 4
VECTORS = 9
norm_eps = 1e-07
bf16 = jnp.bfloat16
f32 = jnp.float32
PARAMS = pltpu.CompilerParams(vmem_limit_bytes=60 * 2**20)
SMALL = pltpu.CompilerParams(vmem_limit_bytes=24 * 2**20)


def lasting(micros):
    return pl.CostEstimate(
        flops=int(micros * 1.1e9), bytes_accessed=int(micros * 3.4e6), transcendentals=0
    )


def dot_nn(first_op, second_op):
    return lax.dot_general(
        first_op, second_op, (((1,), (0,)), ((), ())), preferred_element_type=f32
    )


def dot_nt(first_op, second_op):
    return lax.dot_general(
        first_op, second_op, (((1,), (1,)), ((), ())), preferred_element_type=f32
    )


def dot_tn(first_op, second_op):
    return lax.dot_general(
        first_op, second_op, (((0,), (0,)), ((), ())), preferred_element_type=f32
    )


def distance_rows(seq_len, table_rows):
    side = table_rows // 2
    middle = side // 2
    rows = []
    for m in range(2 * seq_len):
        offset = max(m - seq_len, 1 - seq_len)
        size = abs(offset)
        if size > middle:
            ratio = math.log(size / middle) / math.log((2 * side - 1) / middle)
            size = int(math.ceil(ratio * (middle - 1))) + middle
        rows.append(side + (size if offset > 0 else -size))
    return np.array(rows, dtype=np.int32)


def lane_iota(rows=1):
    return lax.broadcasted_iota(jnp.int32, (rows, LANES), 1)


def member_chunk(words, c, last):
    return (last - words == lane_iota(words.shape[0]) + c * LANES).astype(f32).astype(bf16)


def id_bases(rel_ref, base):
    seq = rel_ref.shape[0]
    chunks = seq // LANES
    last = chunks * 2 - 2
    for g in range(seq // HALF):
        for c in range(chunks):
            block = rel_ref[g * HALF : (g + 1) * HALF, c * LANES : (c + 1) * LANES]
            base[g * chunks + c] = jnp.minimum(jnp.min(block) // HALF, last)


def both_alignments(table):
    return jnp.concatenate([table, table[HALF:], table[:HALF]], axis=0)


def longest(rows):
    wide = rows.astype(f32)
    return jnp.sqrt(jnp.max(jnp.sum(wide * wide, axis=1, keepdims=True), axis=0, keepdims=True))


def pack_heads(first, second, dest, top):
    top = jnp.maximum(top, 1e-30)
    scale = 32000.0 / top
    upper = (first * scale).astype(jnp.int32)
    lower = (second * scale).astype(jnp.int32)
    dest[...] = upper * 65536 + lower
    return top * (1.0 / 32000.0)


def unpack_heads(words, step):
    lower = lax.shift_right_arithmetic(lax.shift_left(words, 16), 16)
    return words.astype(f32) * (step * (1.0 / 65536.0)), lower.astype(f32) * step


def picked_words(source, rel_ref, base, rows, c):
    chunks = rel_ref.shape[1] // LANES
    first = base[(rows.start // HALF) * chunks + c]
    place = rel_ref[rows, c * LANES : (c + 1) * LANES] - first * HALF
    index = place & (LANES - 1)
    at = pl.multiple_of((first % 2) * (chunks * LANES) + (first // 2) * LANES, LANES)
    near = jnp.take_along_axis(source[rows, pl.ds(at, LANES)], index, axis=1)
    at = pl.multiple_of(at + LANES, LANES)
    far = jnp.take_along_axis(source[rows, pl.ds(at, LANES)], index, axis=1)
    return jnp.where(place < LANES, near, far)


def unshift_in_order(sources, words_ref, base, dest):
    seq = words_ref.shape[0]
    chunks = seq // LANES
    lane = lane_iota()
    zero = jnp.zeros((ROWS, LANES), f32)
    for g in range(chunks):
        first = base[g]
        for sub in range(LANES // ROWS):
            start = g * LANES + sub * ROWS
            rows = slice(start, start + ROWS)
            place = lane - 1 - words_ref[rows, :] + first * LANES
            index = place & (LANES - 1)
            near = place >= 0
            mid = place >= -LANES
            for a, source in enumerate(sources):
                turned = [
                    jnp.take_along_axis(
                        source[rows, c * LANES : (c + 1) * LANES], index, axis=1
                    )
                    for c in range(chunks)
                ]
                turned = [zero, zero] + turned + [zero, zero]
                for c in range(chunks + 2):
                    value = jnp.where(near, turned[c + 2], jnp.where(mid, turned[c + 1], turned[c]))
                    at = pl.multiple_of((first + c) * LANES, LANES)
                    dest[a, rows, pl.ds(at, LANES)] = value.astype(bf16)


def group_bases(words, base):
    seq = words.shape[0]
    for g in range(seq // LANES):
        base[g] = (jnp.min(words[g * LANES : (g + 1) * LANES]) + 1) // LANES


def softmax_weights(scores):
    factor = math.log2(math.e) / math.sqrt(3.0 * HEAD)
    top = jnp.max(functools.reduce(jnp.maximum, scores), axis=1, keepdims=True)
    return [jnp.exp2((score - top) * factor) for score in scores]


def head_lanes(a):
    return (lane_iota() < HEAD) if a == 0 else (lane_iota() >= HEAD)


def row_of(ref):
    return ref[...].reshape(1, ref.shape[0])


def norm_stats(values):
    centered = values - jnp.mean(values, axis=1, keepdims=True)
    inv_std = lax.rsqrt(jnp.mean(centered * centered, axis=1, keepdims=True) + norm_eps)
    return centered * inv_std, inv_std


def norm_backward(upstream, normed, inv_std, norm_gain):
    scaled = upstream * norm_gain
    adjusted = (
        scaled
        - jnp.mean(scaled, axis=1, keepdims=True)
        - normed * jnp.mean(scaled * normed, axis=1, keepdims=True)
    )
    return inv_std * adjusted, col_sum(upstream * normed), col_sum(upstream)


def col_sum(values):
    return jnp.sum(values, axis=0, keepdims=True)


def normal_cdf(pre_act):
    return 0.5 * (1.0 + lax.erf(pre_act * (1.0 / math.sqrt(2.0))))


def project_kernel(
    pick_ref, x_ref, rel_ref, wq_ref, wk_ref, wv_ref, bq_ref, bk_ref, bv_ref,
    q_ref, k_ref, v_ref, pq_ref, pk_ref, qpick_ref, xpick_ref,
):
    @pl.when(pl.program_id(0) == 0)
    def _():
        xpick_ref[...] = dot_nn(pick_ref[...], x_ref[...]).astype(bf16)

    for source, weight, bias, out in (
        (xpick_ref, wq_ref, bq_ref, qpick_ref),
        (x_ref, wk_ref, bk_ref, k_ref),
        (rel_ref, wk_ref, bk_ref, pk_ref),
        (rel_ref, wq_ref, bq_ref, pq_ref),
        (x_ref, wq_ref, bq_ref, q_ref),
        (x_ref, wv_ref, bv_ref, v_ref),
    ):
        out[...] = (dot_nn(source[...], weight[...]) + row_of(bias)).astype(bf16)


def project(pick, x, rel_table, weights, biases):
    width = x.shape[1]
    group = 2 * LANES
    whole = lambda value: pl.BlockSpec(value.shape, lambda n: (0, 0))
    col = lambda value: pl.BlockSpec((value.shape[0], group), lambda n: (0, n))
    outs = [x, x, x, rel_table, rel_table, pick]
    return pl.pallas_call(
        project_kernel,
        grid=(width // group,),
        in_specs=[whole(pick), whole(x), whole(rel_table)]
        + [col(value) for value in weights]
        + [pl.BlockSpec((group,), lambda n: (n,))] * 3,
        out_specs=[col(value) for value in outs]
        + [pl.BlockSpec((pick.shape[0], width), lambda n: (0, 0))],
        out_shape=[jax.ShapeDtypeStruct((value.shape[0], width), bf16) for value in outs + [pick]],
        compiler_params=PARAMS,
        cost_estimate=lasting(6.0),
        name="project",
    )(pick, x, rel_table, *weights, *biases)


def picked_kernel(
    pos_ref, rel_ref, qc_ref, k_ref, v_ref, pk_ref, pq_ref,
    x_ref, wo_ref, bo_ref, gain_ref, bias_ref,
    ctx_ref, prob_ref, key_ref, word_ref, wordc_ref, normed_ref, inv_ref, low_ref,
    packed, cpick, direct, relc, keyc, attn, base,
):
    seq = k_ref.shape[0]
    picks = qc_ref.shape[0]
    chunks = seq // LANES
    units, far_units = [], []

    @pl.when(pl.program_id(0) == 0)
    def _():
        row = lax.broadcasted_iota(jnp.int32, (seq, seq), 0)
        col = lax.broadcasted_iota(jnp.int32, (seq, seq), 1)
        side = pk_ref.shape[0] // 2
        step = jnp.sum(jnp.where(col == row - 1, rel_ref[...] - side, 0), axis=1, keepdims=True)
        steps = jnp.broadcast_to(step.astype(f32), (seq, LANES)).astype(bf16)
        word_ref[...] = dot_nn((col <= row).astype(f32).astype(bf16), steps).astype(jnp.int32)
        id_bases(rel_ref, base)
        for n in range(picks):
            place = jnp.maximum(pos_ref[n], 0)
            relc[n : n + 1, :] = rel_ref[pl.ds(place, 1), :]
            wordc_ref[n : n + 1, :] = word_ref[pl.ds(place, 1), :]

    zero = jnp.zeros((), bf16)
    upper = head_lanes(0)
    for m in range(PICKED_AT_ONCE):
        lanes = slice(m * LANES, (m + 1) * LANES)
        k_pair, q_pair, pq = k_ref[:, lanes], qc_ref[:, lanes], pq_ref[:, lanes]
        table = both_alignments(pq)
        keys = [dot_nt(jnp.where(head_lanes(a), k_pair, zero), table) for a in range(2)]
        unit = pack_heads(keys[0], keys[1], packed.at[m], longest(k_pair) * longest(pq))
        units.append(unit)
        pk = pk_ref[:, lanes]
        far = []
        for a in range(2):
            q_a = jnp.where(head_lanes(a), q_pair, zero)
            far.append(dot_nt(q_a, pk))
            direct[2 * m + a] = dot_nt(q_a, k_pair)
        far_units.append(pack_heads(far[0], far[1], cpick.at[m], longest(q_pair) * longest(pk)))
    for m in range(PICKED_AT_ONCE):
        lanes = slice(m * LANES, (m + 1) * LANES)
        for g in range(chunks):
            for c in range(chunks):
                parts = []
                for start in range(g * LANES, (g + 1) * LANES, ROWS):
                    parts.append(
                        picked_words(packed.at[m], rel_ref, base, slice(start, start + ROWS), c)
                    )
                block = jnp.concatenate(parts, axis=0).T
                for a, value in enumerate(unpack_heads(block, units[m])):
                    key_ref[2 * m + a, c * LANES : (c + 1) * LANES, g * LANES : (g + 1) * LANES] = value
        for n in range(picks):
            place = jnp.maximum(pos_ref[n], 0)
            for a in range(2 * m, 2 * m + 2):
                keyc[a, n : n + 1, :] = key_ref[a, pl.ds(place, 1), :]
        scores = [[], []]
        for c in range(chunks):
            ids = relc[:, c * LANES : (c + 1) * LANES]
            index = ids & (LANES - 1)
            value = jnp.take_along_axis(cpick[m, :, :LANES], index, axis=1)
            for n in range(1, pk_ref.shape[0] // LANES):
                other = cpick[m, :, n * LANES : (n + 1) * LANES]
                value = jnp.where(
                    ids >= n * LANES, jnp.take_along_axis(other, index, axis=1), value
                )
            cols = slice(c * LANES, (c + 1) * LANES)
            for a, far in enumerate(unpack_heads(value, far_units[m])):
                scores[a].append(direct[2 * m + a, :, cols] + far + keyc[2 * m + a, :, cols])
        mixed = []
        for a in range(2 * m, 2 * m + 2):
            weights = softmax_weights(scores[a % 2])
            inverse = 1.0 / jnp.sum(sum(weights[1:], weights[0]), axis=1, keepdims=True)
            probs = jnp.concatenate([(weight * inverse).astype(bf16) for weight in weights], axis=1)
            prob_ref[a] = probs
            mixed.append(dot_nn(probs, v_ref[:, lanes]).astype(bf16))
        ctx_ref[:, lanes] = jnp.where(upper, mixed[0], mixed[1])

    part = dot_nn(ctx_ref[...], wo_ref[...])

    @pl.when(pl.program_id(0) == 0)
    def _():
        attn[...] = x_ref[...].astype(f32) + row_of(bo_ref) + part

    @pl.when(pl.program_id(0) > 0)
    def _():
        attn[...] += part

    @pl.when(pl.program_id(0) == pl.num_programs(0) - 1)
    def _():
        normed, inv_std = norm_stats(attn[...])
        normed_ref[...] = normed
        inv_ref[...] = jnp.broadcast_to(inv_std, (picks, LANES))
        low_ref[...] = (normed * row_of(gain_ref) + row_of(bias_ref)).astype(bf16)


def attend_picked(
    positions, rel_ids, q_pick, k, v, pos_query, pos_key, x_pick, w_out, b_out, gain, bias
):
    seq, width = k.shape
    picks = q_pick.shape[0]
    table = pos_key.shape[0]
    pairs = width // LANES
    whole = lambda rows, cols: pl.BlockSpec((rows, cols), lambda h: (0, 0))
    line = pl.BlockSpec((width,), lambda h: (0,))
    per = PICKED_AT_ONCE
    wide = per * LANES
    col = lambda rows: pl.BlockSpec((rows, wide), lambda h: (0, h))
    heads = lambda rows: pl.BlockSpec((2 * per, rows, seq), lambda h: (h, 0, 0))
    return pl.pallas_call(
        picked_kernel,
        grid=(pairs // per,),
        in_specs=[
            pl.BlockSpec(memory_space=pltpu.SMEM), whole(seq, seq),
            col(picks), col(seq), col(seq), col(table), col(table),
            whole(picks, width), pl.BlockSpec((wide, width), lambda h: (h, 0)), line, line, line,
        ],
        out_specs=[
            col(picks), heads(picks), heads(seq), whole(seq, LANES), whole(picks, LANES),
            whole(picks, width), whole(picks, LANES), whole(picks, width),
        ],
        out_shape=[
            jax.ShapeDtypeStruct((picks, width), bf16),
            jax.ShapeDtypeStruct((2 * pairs, picks, seq), bf16),
            jax.ShapeDtypeStruct((2 * pairs, seq, seq), f32),
            jax.ShapeDtypeStruct((seq, LANES), jnp.int32),
            jax.ShapeDtypeStruct((picks, LANES), jnp.int32),
            jax.ShapeDtypeStruct((picks, width), f32),
            jax.ShapeDtypeStruct((picks, LANES), f32),
            jax.ShapeDtypeStruct((picks, width), bf16),
        ],
        scratch_shapes=[
            pltpu.VMEM((per, seq, 2 * table), jnp.int32),
            pltpu.VMEM((per, picks, table), jnp.int32),
            pltpu.VMEM((2 * per, picks, seq), f32),
            pltpu.VMEM((picks, seq), jnp.int32),
            pltpu.VMEM((2 * per, picks, seq), f32),
            pltpu.VMEM((picks, width), f32),
            pltpu.SMEM((seq // HALF * (seq // LANES),), jnp.int32),
        ],
        compiler_params=PARAMS,
        cost_estimate=lasting(5.0 * pairs),
        name="attend_picked",
    )(
        positions, rel_ids, q_pick, k, v, pos_key, pos_query, x_pick, w_out, b_out, gain, bias
    )


def full_kernel(rel_ref, q_ref, k_ref, v_ref, pk_ref, key_ref, ctx_ref, *scratch):
    seq = rel_ref.shape[0]
    chunks = seq // LANES
    base, scratch = scratch[-1], scratch[:-1]
    count = len(scratch) // 3

    @pl.when(pl.program_id(0) == 0)
    def _():
        id_bases(rel_ref, base)

    zero = jnp.zeros((), bf16)
    units = []
    for n in range(count):
        packed, direct, low = scratch[3 * n : 3 * n + 3]
        lanes = slice(n * LANES, (n + 1) * LANES)
        q, pos = q_ref[:, lanes], pk_ref[:, lanes]
        table = both_alignments(pos)
        far = []
        for a in range(2):
            q_a = jnp.where(head_lanes(a), q, zero)
            far.append(dot_nt(q_a, table))
            direct[a] = dot_nt(q_a, k_ref[:, lanes])
        units.append(pack_heads(far[0], far[1], packed, longest(q) * longest(pos)))
    for n in range(count):
        packed, direct, low = scratch[3 * n : 3 * n + 3]
        lanes = slice(n * LANES, (n + 1) * LANES)
        for start in range(0, seq, 2 * ROWS):
            rows = slice(start, start + 2 * ROWS)
            scores = [[], []]
            for c in range(chunks):
                cols = slice(c * LANES, (c + 1) * LANES)
                values = unpack_heads(picked_words(packed, rel_ref, base, rows, c), units[n])
                for a in range(2):
                    scores[a].append(
                        values[a] + direct[a, rows, cols] + key_ref[2 * n + a, rows, cols]
                    )
            for a in range(2):
                for c in range(chunks):
                    direct[a, rows, c * LANES : (c + 1) * LANES] = scores[a][c]
        for a in range(2):
            for start in range(0, seq, LANES):
                rows = slice(start, start + LANES)
                scores = [direct[a, rows, c * LANES : (c + 1) * LANES] for c in range(chunks)]
                for c, weight in enumerate(softmax_weights(scores)):
                    low[a, rows, c * LANES : (c + 1) * LANES] = weight.astype(bf16)
        v = v_ref[:, lanes]
        mixed = [
            dot_nn(low[a], jnp.where(head_lanes(a), v, jnp.ones((), bf16))) for a in range(2)
        ]
        upper = head_lanes(0)
        totals = pltpu.roll(jnp.where(upper, mixed[1], mixed[0]), HEAD, 1)
        ctx_ref[:, lanes] = (jnp.where(upper, mixed[0], mixed[1]) * (1.0 / totals)).astype(bf16)


def attend_full(rel_ids, q, k, v, pos_key, key_scores, first, pairs):
    seq = k.shape[0]
    table = pos_key.shape[0]
    per = AT_ONCE
    wide = per * LANES
    col = lambda rows: pl.BlockSpec((rows, wide), lambda h: (0, h + first // per))
    return pl.pallas_call(
        full_kernel,
        grid=(pairs // per,),
        in_specs=[
            pl.BlockSpec((seq, seq), lambda h: (0, 0)),
            col(seq), col(seq), col(seq), col(table),
            pl.BlockSpec((2 * per, seq, seq), lambda h: (h + first // per, 0, 0)),
        ],
        out_specs=pl.BlockSpec((seq, wide), lambda h: (0, h)),
        out_shape=jax.ShapeDtypeStruct((seq, pairs * LANES), bf16),
        scratch_shapes=[
            pltpu.VMEM((seq, 2 * table), jnp.int32),
            pltpu.VMEM((2, seq, seq), f32),
            pltpu.VMEM((2, seq, seq), bf16),
        ]
        * per
        + [pltpu.SMEM((seq // HALF * (seq // LANES),), jnp.int32)],
        compiler_params=PARAMS,
        cost_estimate=lasting(4.2 * pairs),
        name="attend_full",
    )(rel_ids, q, k, v, pos_key, key_scores)


def back_kernel(
    row_ref, word_ref, wordc_ref, qc_ref, k_ref, v_ref, prob_ref, pk_ref, pq_ref,
    dz2_ref, mine_ref, got_ref, normed_ref, inv_ref, gain_ref, wo_ref, early_ref,
    dq_ref, dk_ref, dv_ref, dpos_ref, dz1_ref, dattn_ref, sum_ref,
    side, sidec, moved, movedc, expand, shrink, base,
):
    seq = k_ref.shape[0]
    picks = qc_ref.shape[0]
    table = pk_ref.shape[0]
    chunks = seq // LANES

    @pl.when(pl.program_id(0) == 0)
    def _():
        words = word_ref[...]
        for c in range(chunks):
            side[:, c * LANES : (c + 1) * LANES] = member_chunk(words, c, seq - 1)
            sidec[:, c * LANES : (c + 1) * LANES] = member_chunk(wordc_ref[...], c, seq - 1)
        group_bases(words, base)
        moved[...] = jnp.zeros_like(moved)
        edge = expand.shape[1]
        for n, start in ((0, 0), (1, 2 * seq - edge)):
            ids = row_ref[start : start + edge, :] - n * (table - LANES)
            chosen = (ids == lane_iota(edge)).astype(f32).astype(bf16)
            expand[n] = chosen
            shrink[n] = chosen.T
        dh1 = dz2_ref[...] + mine_ref[...].astype(f32) + got_ref[...].astype(f32)
        dz1, g_gain, g_bias = norm_backward(dh1, normed_ref[...], inv_ref[:, :1], row_of(gain_ref))
        dz1_ref[...] = dz1
        dattn = dz1.astype(bf16)
        dattn_ref[...] = dattn
        sum_ref[...] = jnp.concatenate(
            [col_sum(dattn.astype(f32)), g_gain, g_bias, early_ref[:5]], axis=0
        )

    lane = lane_iota()
    scale = 1.0 / math.sqrt(3.0 * HEAD)
    zero = jnp.zeros((), bf16)
    heads = range(2)
    upper = head_lanes(0)
    join = lambda pair: jnp.where(upper, pair[0], pair[1])
    side[:, seq:] = k_ref[...]
    sidec[:, seq:] = qc_ref[...]
    dctx = dot_nt(dattn_ref[...], wo_ref[...]).astype(bf16)
    dprobs = [dot_nt(jnp.where(head_lanes(a), dctx, zero), v_ref[...]) for a in heads]

    def widened(ref):
        ends = [
            dot_nn(expand[n], ref[at : at + LANES, :]).astype(bf16)
            for n, at in ((0, 0), (1, table - LANES))
        ]
        return jnp.concatenate([ends[0], ref[LANES : table - LANES, :], ends[1]], axis=0)

    far_key, far_query = widened(pk_ref), widened(pq_ref)
    gs = []
    for a in heads:
        probs = prob_ref[a].astype(f32)
        prod = probs * dprobs[a]
        gs.append(((prod - probs * jnp.sum(prod, axis=1, keepdims=True)) * scale).astype(bf16))
    outs = [dot_tn(gs[a], sidec[...]) for a in heads]
    outcs = [dot_nn(gs[a], side[...]) for a in heads]
    dv_ref[...] = join([dot_tn(prob_ref[a], dctx) for a in heads]).astype(bf16)
    place = lane - 1 - wordc_ref[...]
    index = place & (LANES - 1)
    blank = jnp.zeros((picks, LANES), f32)
    for a in heads:
        turned = [
            jnp.take_along_axis(outcs[a][:, c * LANES : (c + 1) * LANES], index, axis=1)
            for c in range(chunks)
        ]
        for c in range(2 * chunks):
            value = turned[c] if c < chunks else blank
            for n in range(1, chunks + 1):
                other = turned[c - n] if 0 <= c - n < chunks else blank
                value = jnp.where(place < -LANES * (n - 1), other, value)
            movedc[a, :, c * LANES : (c + 1) * LANES] = value.astype(bf16)
    unshift_in_order(outs, word_ref, base, moved)
    dq = [outcs[a][:, seq:] + dot_nn(movedc[a], far_key) for a in heads]
    dq_ref[...] = join(dq).astype(bf16)
    dk = [outs[a][:, seq:] + dot_nn(moved[a, :, : 2 * seq], far_query) for a in heads]
    dk_ref[...] = join(dk).astype(bf16)
    far = [
        join([dot_tn(movedc[a], qc_ref[...]) for a in heads]),
        join([dot_tn(moved[a, :, : 2 * seq], k_ref[...]) for a in heads]),
    ]
    edge = expand.shape[1]
    for n, value in enumerate(far):
        value = value.astype(bf16)
        dpos_ref[n, :LANES, :] = dot_nn(shrink[0], value[:edge]).astype(bf16)
        dpos_ref[n, LANES : table - LANES, :] = value[edge : 2 * seq - edge]
        dpos_ref[n, table - LANES :, :] = dot_nn(shrink[1], value[2 * seq - edge :]).astype(bf16)


def attend_back(
    table_of, words, words_pick, q_pick, k, v, probs, pos_query, pos_key,
    dz2, mine, got, normed, inv_std, gain, w_out, early,
):
    seq, width = k.shape
    picks = q_pick.shape[0]
    table = pos_key.shape[0]
    pairs = width // LANES
    edge = seq - table // 4
    whole = lambda value: pl.BlockSpec(value.shape, lambda h: (0,) * value.ndim)
    col = lambda rows: pl.BlockSpec((rows, LANES), lambda h: (0, h))
    shape = lambda rows: jax.ShapeDtypeStruct((rows, width), bf16)
    return pl.pallas_call(
        back_kernel,
        grid=(pairs,),
        in_specs=[
            whole(table_of), whole(words), whole(words_pick),
            col(picks), col(seq), col(seq),
            pl.BlockSpec((2, picks, seq), lambda h: (h, 0, 0)),
            col(table), col(table),
            whole(dz2), whole(mine), whole(got), whole(normed), whole(inv_std), whole(gain),
            pl.BlockSpec((LANES, width), lambda h: (h, 0)), whole(early),
        ],
        out_specs=[
            col(picks), col(seq), col(seq),
            pl.BlockSpec((2, table, LANES), lambda h: (0, 0, h)),
            whole(dz2), whole(dz2), whole(early),
        ],
        out_shape=[
            shape(picks), shape(seq), shape(seq),
            jax.ShapeDtypeStruct((2, table, width), bf16),
            jax.ShapeDtypeStruct((picks, width), f32),
            shape(picks),
            jax.ShapeDtypeStruct(early.shape, f32),
        ],
        scratch_shapes=[
            pltpu.VMEM((seq, seq + LANES), bf16),
            pltpu.VMEM((picks, seq + LANES), bf16),
            pltpu.VMEM((2, seq, 2 * seq + 2 * LANES), bf16),
            pltpu.VMEM((2, picks, 2 * seq), bf16),
            pltpu.VMEM((2, edge, LANES), bf16),
            pltpu.VMEM((2, LANES, edge), bf16),
            pltpu.SMEM((seq // LANES,), jnp.int32),
        ],
        compiler_params=PARAMS,
        cost_estimate=lasting(4.0 * pairs),
        name="attend_back",
    )(
        table_of, words, words_pick, q_pick, k, v, probs, pos_key, pos_query,
        dz2, mine, got, normed, inv_std, gain, w_out, early,
    )


def turn_kernel(
    n_all, me_ref, order_ref, x_ref, xpick_ref, cpick_ref, rel_ref, x_out, xpick_out, cpick_out, rel_out
):
    picked = order_rows(order_ref, me_ref, x_ref.shape[1], n_all)
    for ref, out in ((x_ref, x_out), (xpick_ref, xpick_out), (cpick_ref, cpick_out), (rel_ref, rel_out)):
        out[...] = dot_nt(picked, ref[...]).astype(bf16)


def block_rows(ref, me_ref):
    return me_ref[0] ^ jnp.where(me_ref[1] == 0, ref[:, 0:1], ref[:, 1:2])


def order_rows(ref, me_ref, length, n_all):
    source = block_rows(ref, me_ref) * (length // n_all) + ref[:, 2:3]
    spot = lax.broadcasted_iota(jnp.int32, (ref.shape[0], length), 1)
    return (spot == source).astype(f32).astype(bf16)


def turn_blocks(n_all, me, order, x, x_pick, ctx_pick, rel_table):
    width = x.shape[1]
    group = 2 * LANES
    whole = lambda value: pl.BlockSpec(value.shape, lambda n: (0, 0))
    row = lambda count: pl.BlockSpec((group, count), lambda n: (n, 0))
    given = [x, x_pick, ctx_pick, rel_table]
    return pl.pallas_call(
        functools.partial(turn_kernel, n_all),
        grid=(width // group,),
        in_specs=[pl.BlockSpec(memory_space=pltpu.SMEM), row(LANES)]
        + [whole(value) for value in given],
        out_specs=[row(value.shape[0]) for value in given],
        out_shape=[jax.ShapeDtypeStruct(value.shape[::-1], bf16) for value in given],
        compiler_params=PARAMS,
        cost_estimate=lasting(5.2),
        name="turn_blocks",
    )(me, order, *given)


def norm_picked_kernel(
    normed_ref, gain1_ref, bias1_ref, mine_ref, got_ref, bdown_ref, gain2_ref, grad_ref, pick_ref,
    dz2_ref, low_ref, sum_ref,
):
    h1 = normed_ref[...] * row_of(gain1_ref) + row_of(bias1_ref)
    branch = mine_ref[...].astype(f32) + got_ref[...].astype(f32) + row_of(bdown_ref)
    normed, inv_std = norm_stats(h1 + branch)
    used = jnp.sum(pick_ref[...].astype(f32), axis=1, keepdims=True)
    cot = jnp.where(used > 0.0, grad_ref[...].astype(f32), 0.0)
    dz2, g_gain, g_bias = norm_backward(cot, normed, inv_std, row_of(gain2_ref))
    dz2_ref[...] = dz2
    low = dz2.astype(bf16)
    low_ref[...] = low
    sum_ref[...] = jnp.concatenate(
        [col_sum(low.astype(f32)), g_gain, g_bias, jnp.zeros((5, h1.shape[1]), f32)], axis=0
    )


def norm_picked(normed, gain1, bias1, mine, got, b_down, gain2, grads, pick):
    picks, width = normed.shape
    return pl.pallas_call(
        norm_picked_kernel,
        out_shape=[
            jax.ShapeDtypeStruct((picks, width), f32),
            jax.ShapeDtypeStruct((picks, width), bf16),
            jax.ShapeDtypeStruct((8, width), f32),
        ],
        compiler_params=SMALL,
        cost_estimate=lasting(2.4),
        name="norm_picked",
    )(normed, gain1, bias1, mine, got, b_down, gain2, grads, pick)


def ffn_full_kernel(
    x_ref, ctx_ref, ctx2_ref, wo_ref, bo_ref, gain1_ref, bias1_ref, bdown_ref, gain2_ref, bias2_ref,
    bin_ref, bin2_ref, bin3_ref, win_ref, down_ref, win2_ref, down2_ref, win3_ref, down3_ref,
    out_ref, h1, low, total, win_here, down_here, win_sem, down_sem,
):
    rows, width = x_ref.shape
    tile = win_here.shape[2]
    parts = [(win_ref, down_ref, bin_ref, n * tile) for n in range(win_ref.shape[1] // tile)]
    parts += [(win2_ref, down2_ref, bin2_ref, 0), (win3_ref, down3_ref, bin3_ref, 0)]

    def copies(n):
        w_ref, d_ref, _, at = parts[n]
        return (
            pltpu.make_async_copy(w_ref.at[:, at : at + tile], win_here.at[n], win_sem.at[n]),
            pltpu.make_async_copy(d_ref.at[at : at + tile, :], down_here.at[n], down_sem.at[n]),
        )

    for n in range(len(parts)):
        for copy in copies(n):
            copy.start()
    attn = dot_nn(ctx_ref[...], wo_ref[: ctx_ref.shape[1]]) + dot_nn(
        ctx2_ref[...], wo_ref[ctx_ref.shape[1] :]
    )
    normed, _ = norm_stats(x_ref[...].astype(f32) + (attn + row_of(bo_ref)))
    value = normed * row_of(gain1_ref) + row_of(bias1_ref)
    h1[...] = value
    low[...] = value.astype(bf16)
    step = rows // 2
    for n in range(len(parts)):
        for copy in copies(n):
            copy.wait()
        bias = parts[n][2][:, parts[n][3] : parts[n][3] + tile]
        for at in range(0, rows, step):
            pre = dot_nn(low[at : at + step], win_here[n]) + bias
            part = dot_nn((pre * normal_cdf(pre)).astype(bf16), down_here[n])
            total[at : at + step] = part if n == 0 else total[at : at + step] + part
    normed, _ = norm_stats(h1[...] + (total[...] + row_of(bdown_ref)))
    out_ref[...] = (normed * row_of(gain2_ref) + row_of(bias2_ref)).astype(bf16)


def ffn_full(x, ctx, w_out, b_out, gain1, bias1, shards, b_down, gain2, bias2):
    rows, width = x.shape
    tile = shards[1][0].shape[1]
    count = shards[0][0].shape[1] // tile + 2
    held = [x, ctx[0], ctx[1], w_out, b_out, gain1, bias1, b_down, gain2, bias2]
    held += [shard[2] for shard in shards]
    moved = [value for shard in shards for value in shard[:2]]
    return pl.pallas_call(
        ffn_full_kernel,
        in_specs=[pl.BlockSpec(memory_space=pltpu.VMEM)] * len(held)
        + [pl.BlockSpec(memory_space=pl.ANY)] * len(moved),
        out_specs=pl.BlockSpec(memory_space=pltpu.VMEM),
        out_shape=jax.ShapeDtypeStruct((rows, width), bf16),
        scratch_shapes=[
            pltpu.VMEM((rows, width), f32), pltpu.VMEM((rows, width), bf16), pltpu.VMEM((rows, width), f32),
            pltpu.VMEM((count, width, tile), bf16), pltpu.VMEM((count, tile, width), bf16),
            pltpu.SemaphoreType.DMA((count,)), pltpu.SemaphoreType.DMA((count,)),
        ],
        compiler_params=PARAMS,
        cost_estimate=lasting(10.9),
        name="ffn_full",
    )(*held, *moved)


def token_grads_kernel(pick_ref, dz1_ref, dq_ref, dk_ref, dv_ref, wq_ref, wk_ref, wv_ref, out_ref):
    sparse = dz1_ref[...] + dot_nt(dq_ref[...], wq_ref[...])
    upper = sparse.astype(bf16)
    lower = (sparse - upper.astype(f32)).astype(bf16)
    out_ref[...] = (
        dot_nt(dk_ref[...], wk_ref[...])
        + dot_nt(dv_ref[...], wv_ref[...])
        + dot_tn(pick_ref[...], upper)
        + dot_tn(pick_ref[...], lower)
    )


def token_grads(pick, dz1, dq, dk, dv, w_query, w_key, w_value):
    seq, width = dk.shape
    group = 2 * LANES
    whole = lambda value: pl.BlockSpec(value.shape, lambda n: (0, 0))
    col = lambda rows: pl.BlockSpec((rows, group), lambda n: (0, n))
    row = pl.BlockSpec((group, width), lambda n: (n, 0))
    return pl.pallas_call(
        token_grads_kernel,
        grid=(width // group,),
        in_specs=[whole(pick), col(dz1.shape[0]), whole(dq), whole(dk), whole(dv), row, row, row],
        out_specs=col(seq),
        out_shape=jax.ShapeDtypeStruct((seq, width), f32),
        compiler_params=PARAMS,
        cost_estimate=lasting(5.9),
        name="token_grads",
    )(pick, dz1, dq, dk, dv, w_query, w_key, w_value)


def grads_kernel(
    n_all, n_ffn, unit, me_ref, order_ref, relorder_ref, taker_ref,
    x_ref, rel_ref, xpick_ref, cpick_ref, dpos_ref, dq_ref, dk_ref, dv_ref, dattn_ref,
    early_ref, bin_ref, wq_ref, wk_ref, kept_ref, sent_ref, weights, sems,
):
    width = dk_ref.shape[1]
    table = dpos_ref.shape[1]
    group = 2 * LANES
    step = pl.program_id(0)
    copies = [
        pltpu.make_async_copy(ref, weights.at[n], sems.at[n])
        for n, ref in enumerate((wk_ref, wq_ref))
    ]

    def put(at, value):
        value = value.astype(bf16)
        kept_ref[at] = value[:LANES]
        sent_ref[at] = value[LANES:]

    @pl.when(step == 0)
    def _():
        for copy in copies:
            copy.start()

    @pl.when(step < width // group)
    def _():
        put(0, dot_nn(xpick_ref[...], dq_ref[...]) + dot_nn(rel_ref[...], dpos_ref[1]))
        put(1, dot_nn(x_ref[...], dk_ref[...]) + dot_nn(rel_ref[...], dpos_ref[0]))
        put(2, dot_nn(x_ref[...], dv_ref[...]))
        put(3, dot_nn(cpick_ref[...], dattn_ref[...]))

    @pl.when(step == width // group)
    def _():
        for copy in copies:
            copy.wait()
        rows = order_rows(relorder_ref, me_ref, table, n_all)
        far = [dot_nn(rows, dpos_ref[n]).astype(bf16) for n in range(2)]
        value = dot_nt(far[0], weights[0]) + dot_nt(far[1], weights[1])
        for n in range(table // group):
            put(n, value[n * group : (n + 1) * group])

        total = lambda value: col_sum(value.astype(f32))
        bins = [bin_ref[:1, at : at + width] for at in range(0, bin_ref.shape[1], width)]
        values = [
            total(dq_ref[...]) + total(dpos_ref[1]),
            total(dk_ref[...]) + total(dpos_ref[0]),
            total(dv_ref[...]),
            early_ref[:6],
        ]
        values += bins + [jnp.zeros((16 - VECTORS - len(bins), width), f32)]
        values = jnp.concatenate(values, axis=0)
        block = block_rows(order_ref[:group, :], me_ref)
        ours = (block % n_ffn) == (me_ref[0] % n_ffn)
        tok_place = jnp.where(ours, block // n_ffn, -1)
        row = lax.broadcasted_iota(jnp.int32, (group, 1), 0) % unit
        for n in range(16 // unit):
            rows = slice(n * unit, (n + 1) * unit)
            spread = lambda value: jnp.concatenate([value[rows]] * (group // unit), axis=0)
            taker = jnp.where(row + n * unit < VECTORS, block, tok_place)
            put(table // group + n, jnp.where(spread(taker_ref[...]) == taker, spread(values), 0.0))


def weight_grads(
    n_all, n_ffn, unit, me, order, rel_order, takers, x, rel, x_pick, c_pick, dpos, dq, dk, dv, dattn,
    w_query, w_key, early, bins,
):
    seq, width = dk.shape
    group = 2 * LANES
    steps = width // group
    each = max(4, dpos.shape[1] // group + 16 // unit)
    whole = lambda value: pl.BlockSpec(value.shape, lambda n: (0,) * value.ndim)
    row = lambda value: pl.BlockSpec((group, value.shape[1]), lambda n: (jnp.minimum(n, steps - 1), 0))
    block = pl.BlockSpec((each, LANES, width), lambda n: (n, 0, 0))
    return pl.pallas_call(
        functools.partial(grads_kernel, n_all, n_ffn, unit),
        grid=(steps + 1,),
        in_specs=[pl.BlockSpec(memory_space=pltpu.SMEM)]
        + [whole(value) for value in (order, rel_order, takers)]
        + [row(value) for value in (x, rel, x_pick, c_pick)]
        + [whole(value) for value in (dpos, dq, dk, dv, dattn, early, bins)]
        + [pl.BlockSpec(memory_space=pl.ANY)] * 2,
        out_specs=[block] * 2,
        out_shape=[jax.ShapeDtypeStruct((each * (steps + 1), LANES, width), bf16)] * 2,
        scratch_shapes=[
            pltpu.VMEM((2,) + w_query.shape, bf16), pltpu.SemaphoreType.DMA((2,)),
        ],
        compiler_params=PARAMS,
        cost_estimate=lasting(7.0),
        name="weight_grads",
    )(
        me, order, rel_order, takers, x, rel, x_pick, c_pick, dpos, dq, dk, dv, dattn, early, bins,
        w_query, w_key,
    )


def swap(values, axis, bit):
    size = lax.axis_size(axis)
    return lax.ppermute(values, axis, [(n, n ^ bit) for n in range(size)])


def after(values, *others):
    return lax.optimization_barrier((values, others))[0]


class Halving:
    def __init__(self, axes, core, near, size):
        rest = [1 << n for n in range(size.bit_length() - 1) if (1 << n) != core]
        near = [bit for bit in near if bit in rest]
        rest = [bit for bit in rest if bit not in near]
        turned = near[-1:] + near[:-1]
        self.axes, self.core, self.size = axes, core, size
        self.orders = [[core] + near + rest, [core] + turned + rest]
        self.steps = len(self.orders[0])
        self.me = lax.axis_index(axes)
        self.upper = (self.me // core) % 2

    def core_of(self, place):
        return (place // self.core) % 2

    def send(self, values, step):
        pairs = [(n, n ^ self.orders[self.core_of(n)][step]) for n in range(self.size)]
        return lax.ppermute(values, self.axes, pairs)

    def relative(self, upper):
        masks = []
        for place in range(self.size):
            bits = [(place >> (self.steps - 1 - step)) & 1 for step in range(self.steps)]
            order = self.orders[upper ^ bits[0]]
            mask = 0
            for step, bit in enumerate(bits):
                mask ^= bit * order[step]
            masks.append(mask)
        return np.array(masks, np.int32)

    def order(self, length, unit):
        spots = np.arange(length)
        group = self.size * unit
        place = spots % group // unit
        rows = [self.relative(upper)[place] for upper in range(2)]
        rows.append(spots // group * unit + spots % unit)
        return np.stack(rows).astype(np.int32)

    def matrix(self, length, unit):
        first, second, inner = self.order(length, unit)
        source = (self.me ^ jnp.where(self.upper == 0, first, second)) * (length // self.size) + inner
        spot = lax.broadcasted_iota(jnp.int32, (length, length), 0)
        return (spot == source[None, :]).astype(bf16)


def local(
    tokens, rel_ids, mask_pos, grad_vals, w_query, w_key, w_value, w_out, b_query, b_key,
    b_value, b_out, rel_table, ln1_gain, ln1_bias, w_in, b_in, w_down, b_down, ln2_gain, ln2_bias,
):
    assert rel_ids.shape[0] == 1
    seq, width = tokens.shape
    table_rows = rel_table.shape[0]
    hidden_cols = w_in.shape[1]
    pairs = width // LANES
    n_tok = lax.axis_size("tok")
    n_ffn = lax.axis_size("ffn")
    n_all = n_tok * n_ffn
    low = lambda value: value.astype(bf16)
    wide = lambda value: value.astype(f32)
    rel_ids, positions, grad_vals = rel_ids[0], mask_pos[0], grad_vals[0]

    over_all = Halving(("tok", "ffn"), n_ffn, [2 * n_ffn, 1, 4 * n_ffn], n_all)
    own, own_rel = width // n_all, table_rows // n_all
    unit = math.gcd(own, own_rel)
    group = n_all * unit
    over_tok = Halving("tok", 1, [2, 4], n_tok)
    pad = lambda value, count: np.pad(value, ((0, count - value.shape[0]), (0, 0)))
    order = jnp.asarray(pad(over_all.order(width, unit), LANES).T)
    rel_order = jnp.asarray(pad(over_all.order(table_rows, unit), LANES).T)
    spots = np.arange(width)
    takers = [spots // own] * VECTORS
    takers += [(spots + n * width) // (hidden_cols // n_tok) for n in range(hidden_cols // width)]
    takers = np.stack(takers).astype(np.int32)
    takers = jnp.asarray(np.pad(takers, ((0, 16 - takers.shape[0]), (0, 0)), constant_values=-2))
    me = jnp.stack([over_all.me, over_all.upper])
    table_of = jnp.asarray(np.repeat(distance_rows(seq, table_rows)[:, None], LANES, 1))

    core = lax.axis_index("tok") % 2
    half_cols = hidden_cols // 2
    bias_row = b_in.reshape(1, hidden_cols)
    in_half = lax.dynamic_slice_in_dim(w_in, core * half_cols, half_cols, 1)
    down_half = lax.dynamic_slice_in_dim(w_down, core * half_cols, half_cols, 0)

    pick = low(positions[:, None] == lax.broadcasted_iota(jnp.int32, (positions.shape[0], seq), 1))
    q, k, v, pos_query, pos_key, q_pick, x_pick = project(
        pick, tokens, rel_table, (w_query, w_key, w_value), (b_query, b_key, b_value)
    )
    ctx_pick, probs, key_scores, words, words_pick, normed1, inv1, h1_mine = attend_picked(
        positions, rel_ids, q_pick, k, v, pos_query, pos_key, x_pick, w_out, b_out, ln1_gain, ln1_bias
    )

    h1_theirs = swap(h1_mine, "ffn", 1)
    bias_theirs = swap(bias_row, "ffn", 1)
    x_turned, x_pick_turned, c_pick_turned, rel_turned = turn_blocks(
        n_all, me, order, tokens, x_pick, ctx_pick, rel_table
    )
    h1_both = jnp.concatenate([h1_mine, after(h1_theirs, x_turned, bias_theirs)], axis=0)
    count = h1_mine.shape[0]
    pre = dot_nn(h1_both, w_in) + b_in
    cdf = normal_cdf(pre)
    hidden = low(pre * cdf)
    slope = cdf + pre * (jnp.exp(-0.5 * pre * pre) * (1.0 / math.sqrt(2.0 * math.pi)))
    part = low(dot_nn(hidden, w_down))
    got = swap(part[count:], "ffn", 1)
    tok_order = over_tok.matrix(width, width // n_tok)
    h1_left = low(dot_nn(h1_both, lax.optimization_barrier(tok_order)))
    in_half = after(in_half, part)
    got = after(got, h1_left, in_half)
    dz2, dffn, early = norm_picked(
        normed1, ln1_gain, ln1_bias, part[:count], got, b_down, ln2_gain, grad_vals, pick
    )
    down_half = after(down_half, dffn)
    dffn_both = jnp.concatenate([dffn, after(swap(dffn, "ffn", 1), down_half)], axis=0)
    dpre = low(dot_nt(dffn_both, w_down) * slope)
    dpart = low(dot_nt(dpre, w_in))
    dgot = swap(dpart[count:], "ffn", 1)

    def halves(values, axis):
        size = values.shape[axis] // 2
        cut = lambda at: lax.slice_in_dim(values, at, at + size, axis=axis)
        return cut(0), cut(size)

    add = lambda one, other: low(wide(one) + wide(other))

    def next_halves(kept, got, axis):
        return [add(one, other) for one, other in zip(halves(kept, axis), halves(got, axis))]

    dpre_later = after(dpre, dpart)
    dffn_left = low(dot_nn(after(dffn_both, dpart), tok_order))
    gb_in = dot_nn(jnp.ones((8, 2 * count), bf16), dpre_later)
    left, right = jnp.stack([h1_left, dffn_left]), jnp.stack([dpre_later, hidden])
    product = lambda first, last: lax.dot_general(
        left[:, :, first:last], right, (((1,), (1,)), ((0,), (0,))), preferred_element_type=f32
    )
    middle, quarter = width // 2, width // 4
    ffn_sent = low(product(middle, width))
    dgot, ffn_sent = lax.optimization_barrier((dgot, ffn_sent))
    ffn_got = over_tok.send(ffn_sent, 0)
    far_in = swap(after(in_half, dgot, ffn_sent), "ffn", 1)

    ffn_sent = low(product(quarter, middle) + wide(ffn_got[:, quarter:]))
    ffn_kept = low(product(0, quarter) + wide(ffn_got[:, :quarter]))
    ffn_got = over_tok.send(ffn_sent, 1)

    def ffn_next(step, kept, got):
        if step < over_tok.steps:
            kept, sent = next_halves(kept, got, 1)
            return kept, over_tok.send(sent, step)
        return add(kept, got), None

    dq, dk, dv, dpos, dz1, dattn, early = attend_back(
        table_of, words, words_pick, q_pick, k, v, probs, pos_query, pos_key,
        dz2, dpart[:count], after(dgot, in_half, ffn_sent, ffn_kept), normed1, inv1, ln1_gain, w_out, early,
    )
    far_in, ffn_got = after((far_in, ffn_got), dk)
    ffn_kept, ffn_got = ffn_next(2, ffn_kept, ffn_got)
    near_in = swap(far_in, "tok", 1)
    far_down = swap(after(down_half, far_in), "ffn", 1)
    all_kept, all_sent = weight_grads(
        n_all, n_ffn, unit, me, order, rel_order, takers,
        x_turned, rel_turned, x_pick_turned, c_pick_turned, dpos, dq, after(dk, far_in, ffn_kept), dv,
        dattn, w_query, w_key, early, gb_in,
    )
    all_got = over_all.send(all_sent, 0)
    dk_later, dq_later = after((dk, dq), all_sent)
    grad_tokens = token_grads(pick, dz1, dq_later, dk_later, dv, w_query, w_key, w_value)
    all_kept, all_sent = next_halves(all_kept, after(all_got, grad_tokens), 1)
    ffn_step = 3
    ffn_got = after(ffn_got, grad_tokens)

    def attend(first, count, q):
        return attend_full(rel_ids, q, k, v, pos_key, key_scores, first, count)

    ctx = []
    cuts = [(0, FIRST_PAIRS), (FIRST_PAIRS, pairs - FIRST_PAIRS)]
    for step in range(1, over_all.steps):
        all_got = over_all.send(all_sent, step)
        if step <= 2:
            ctx.append(attend(*cuts[step - 1], after(q, all_sent)))
            all_got = after(all_got, ctx[-1])
            if step == 1:
                far_down = after(far_down, ctx[-1])
                near_down = swap(far_down, "tok", 1)
                all_got = after(all_got, far_down)
        elif step == 4:
            biases = [
                lax.dynamic_slice_in_dim(bias_theirs, at * half_cols, half_cols, 1)
                for at in (core, 1 - core)
            ]
            shards = [
                (w_in, w_down, bias_row), (far_in, far_down, biases[0]), (near_in, near_down, biases[1])
            ]
            output = ffn_full(
                after(tokens, all_sent), ctx, w_out, b_out, ln1_gain, ln1_bias, shards,
                b_down, ln2_gain, ln2_bias,
            )
            all_got = after(all_got, output)
        if ffn_step <= over_tok.steps:
            ffn_got = after(ffn_got, all_sent)
            if step <= 2:
                ffn_got = after(ffn_got, ctx[-1])
            ffn_kept, ffn_got = ffn_next(ffn_step, ffn_kept, ffn_got)
            ffn_step += 1
        if step < over_all.steps - 1:
            all_kept, all_sent = next_halves(all_kept, all_got, 1)
        else:
            all_sums = add(all_kept, all_got)

    steps = width // group
    sums = all_sums.reshape(steps + 1, all_sums.shape[0] // (steps + 1), unit, width)
    s_w = [wide(sums[:steps, n].reshape(own, width)) for n in range(4)]
    planes = table_rows // group
    s_rel = wide(sums[steps, :planes].reshape(own_rel, width))
    vectors = wide(sums[steps, planes : planes + 16 // unit].reshape(16, width))
    s_vec = lax.dynamic_slice_in_dim(vectors[:VECTORS], over_all.me * own, own, 1)
    part = hidden_cols // n_tok
    bins = vectors[VECTORS : VECTORS + hidden_cols // width].reshape(1, hidden_cols)
    s_bin = lax.dynamic_slice_in_dim(bins, lax.axis_index("tok") * part, part, 1)
    return (
        output,
        grad_tokens,
        s_w[0],
        s_w[1],
        s_w[2],
        s_w[3],
        s_vec[0],
        s_vec[1],
        s_vec[2],
        s_vec[3],
        s_rel,
        s_vec[4],
        s_vec[5],
        wide(ffn_kept[0]),
        s_bin,
        jnp.transpose(wide(ffn_kept[1])),
        s_vec[6],
        s_vec[7],
        s_vec[8],
    )


def solution(mesh):
    every = ("tok", "ffn")
    placed = (
        P(every, None), P(every, None, None), P(every, None), P(every, None, None),
        P(), P(), P(), P(), P(), P(), P(), P(), P(), P(), P(),
        P(None, "ffn"), P("ffn"), P("ffn", None), P(), P(), P(),
    )
    given = (
        P(every, None), P(every, None),
        P(every, None), P(every, None), P(every, None), P(every, None),
        P(every), P(every), P(every), P(every),
        P(every, None), P(every), P(every),
        P("tok", "ffn"), P("ffn", "tok"), P("ffn", "tok"),
        P(every), P(every), P(every),
    )
    return jax.shard_map(local, mesh=mesh, in_specs=placed, out_specs=given, check_vma=False)
```

```python
import functools
import math

import numpy as np

import jax
import jax.numpy as jnp
from jax import lax
from jax.experimental import pallas as pl
from jax.experimental.pallas import tpu as pltpu
from jax.sharding import PartitionSpec as P

HEAD = 64
LANES = 128
HALF = 64
ROWS = 8
AT_ONCE = 2
PICKED_AT_ONCE = 2
FIRST_PAIRS = 4
VECTORS = 9
norm_eps = 1e-07
bf16 = jnp.bfloat16
f32 = jnp.float32
PARAMS = pltpu.CompilerParams(vmem_limit_bytes=60 * 2**20)
SMALL = pltpu.CompilerParams(vmem_limit_bytes=24 * 2**20)


def lasting(micros):
    return pl.CostEstimate(
        flops=int(micros * 1.1e9), bytes_accessed=int(micros * 3.4e6), transcendentals=0
    )


def dot_nn(first_op, second_op):
    return lax.dot_general(
        first_op, second_op, (((1,), (0,)), ((), ())), preferred_element_type=f32
    )


def dot_nt(first_op, second_op):
    return lax.dot_general(
        first_op, second_op, (((1,), (1,)), ((), ())), preferred_element_type=f32
    )


def dot_tn(first_op, second_op):
    return lax.dot_general(
        first_op, second_op, (((0,), (0,)), ((), ())), preferred_element_type=f32
    )


def distance_rows(seq_len, table_rows):
    side = table_rows // 2
    middle = side // 2
    rows = []
    for m in range(2 * seq_len):
        offset = max(m - seq_len, 1 - seq_len)
        size = abs(offset)
        if size > middle:
            ratio = math.log(size / middle) / math.log((2 * side - 1) / middle)
            size = int(math.ceil(ratio * (middle - 1))) + middle
        rows.append(side + (size if offset > 0 else -size))
    return np.array(rows, dtype=np.int32)


def lane_iota(rows=1):
    return lax.broadcasted_iota(jnp.int32, (rows, LANES), 1)


def member_chunk(words, c, last):
    return (last - words == lane_iota(words.shape[0]) + c * LANES).astype(f32).astype(bf16)


def id_bases(rel_ref, base):
    seq = rel_ref.shape[0]
    chunks = seq // LANES
    last = chunks * 2 - 2
    for g in range(seq // HALF):
        for c in range(chunks):
            block = rel_ref[g * HALF : (g + 1) * HALF, c * LANES : (c + 1) * LANES]
            base[g * chunks + c] = jnp.minimum(jnp.min(block) // HALF, last)


def both_alignments(table):
    return jnp.concatenate([table, table[HALF:], table[:HALF]], axis=0)


def longest(rows):
    wide = rows.astype(f32)
    return jnp.sqrt(jnp.max(jnp.sum(wide * wide, axis=1, keepdims=True), axis=0, keepdims=True))


def pack_heads(first, second, dest, top):
    top = jnp.maximum(top, 1e-30)
    scale = 32000.0 / top
    upper = (first * scale).astype(jnp.int32)
    lower = (second * scale).astype(jnp.int32)
    dest[...] = upper * 65536 + lower
    return top * (1.0 / 32000.0)


def unpack_heads(words, step):
    lower = lax.shift_right_arithmetic(lax.shift_left(words, 16), 16)
    return words.astype(f32) * (step * (1.0 / 65536.0)), lower.astype(f32) * step


def picked_words(source, rel_ref, base, rows, c):
    chunks = rel_ref.shape[1] // LANES
    first = base[(rows.start // HALF) * chunks + c]
    place = rel_ref[rows, c * LANES : (c + 1) * LANES] - first * HALF
    index = place & (LANES - 1)
    at = pl.multiple_of((first % 2) * (chunks * LANES) + (first // 2) * LANES, LANES)
    near = jnp.take_along_axis(source[rows, pl.ds(at, LANES)], index, axis=1)
    at = pl.multiple_of(at + LANES, LANES)
    far = jnp.take_along_axis(source[rows, pl.ds(at, LANES)], index, axis=1)
    return jnp.where(place < LANES, near, far)


def unshift_in_order(sources, words_ref, base, dest):
    seq = words_ref.shape[0]
    chunks = seq // LANES
    lane = lane_iota()
    zero = jnp.zeros((ROWS, LANES), f32)
    for g in range(chunks):
        first = base[g]
        for sub in range(LANES // ROWS):
            start = g * LANES + sub * ROWS
            rows = slice(start, start + ROWS)
            place = lane - 1 - words_ref[rows, :] + first * LANES
            index = place & (LANES - 1)
            near = place >= 0
            mid = place >= -LANES
            for a, source in enumerate(sources):
                turned = [
                    jnp.take_along_axis(
                        source[rows, c * LANES : (c + 1) * LANES], index, axis=1
                    )
                    for c in range(chunks)
                ]
                turned = [zero, zero] + turned + [zero, zero]
                for c in range(chunks + 2):
                    value = jnp.where(near, turned[c + 2], jnp.where(mid, turned[c + 1], turned[c]))
                    at = pl.multiple_of((first + c) * LANES, LANES)
                    dest[a, rows, pl.ds(at, LANES)] = value.astype(bf16)


def group_bases(words, base):
    seq = words.shape[0]
    for g in range(seq // LANES):
        base[g] = (jnp.min(words[g * LANES : (g + 1) * LANES]) + 1) // LANES


def softmax_weights(scores):
    factor = math.log2(math.e) / math.sqrt(3.0 * HEAD)
    top = jnp.max(functools.reduce(jnp.maximum, scores), axis=1, keepdims=True)
    return [jnp.exp2((score - top) * factor) for score in scores]


def head_lanes(a):
    return (lane_iota() < HEAD) if a == 0 else (lane_iota() >= HEAD)


def row_of(ref):
    return ref[...].reshape(1, ref.shape[0])


def norm_stats(values):
    centered = values - jnp.mean(values, axis=1, keepdims=True)
    inv_std = lax.rsqrt(jnp.mean(centered * centered, axis=1, keepdims=True) + norm_eps)
    return centered * inv_std, inv_std


def norm_backward(upstream, normed, inv_std, norm_gain):
    scaled = upstream * norm_gain
    adjusted = (
        scaled
        - jnp.mean(scaled, axis=1, keepdims=True)
        - normed * jnp.mean(scaled * normed, axis=1, keepdims=True)
    )
    return inv_std * adjusted, col_sum(upstream * normed), col_sum(upstream)


def col_sum(values):
    return jnp.sum(values, axis=0, keepdims=True)


def normal_cdf(pre_act):
    return 0.5 * (1.0 + lax.erf(pre_act * (1.0 / math.sqrt(2.0))))


def project_kernel(
    pick_ref, x_ref, rel_ref, wq_ref, wk_ref, wv_ref, bq_ref, bk_ref, bv_ref,
    q_ref, k_ref, v_ref, pq_ref, pk_ref, qpick_ref, xpick_ref,
):
    @pl.when(pl.program_id(0) == 0)
    def _():
        xpick_ref[...] = dot_nn(pick_ref[...], x_ref[...]).astype(bf16)

    for source, weight, bias, out in (
        (xpick_ref, wq_ref, bq_ref, qpick_ref),
        (x_ref, wk_ref, bk_ref, k_ref),
        (rel_ref, wk_ref, bk_ref, pk_ref),
        (rel_ref, wq_ref, bq_ref, pq_ref),
        (x_ref, wq_ref, bq_ref, q_ref),
        (x_ref, wv_ref, bv_ref, v_ref),
    ):
        out[...] = (dot_nn(source[...], weight[...]) + row_of(bias)).astype(bf16)


def project(pick, x, rel_table, weights, biases):
    width = x.shape[1]
    group = 2 * LANES
    whole = lambda value: pl.BlockSpec(value.shape, lambda n: (0, 0))
    col = lambda value: pl.BlockSpec((value.shape[0], group), lambda n: (0, n))
    outs = [x, x, x, rel_table, rel_table, pick]
    return pl.pallas_call(
        project_kernel,
        grid=(width // group,),
        in_specs=[whole(pick), whole(x), whole(rel_table)]
        + [col(value) for value in weights]
        + [pl.BlockSpec((group,), lambda n: (n,))] * 3,
        out_specs=[col(value) for value in outs]
        + [pl.BlockSpec((pick.shape[0], width), lambda n: (0, 0))],
        out_shape=[jax.ShapeDtypeStruct((value.shape[0], width), bf16) for value in outs + [pick]],
        compiler_params=PARAMS,
        cost_estimate=lasting(6.0),
        name="project",
    )(pick, x, rel_table, *weights, *biases)


def picked_kernel(
    pos_ref, rel_ref, qc_ref, k_ref, v_ref, pk_ref, pq_ref,
    x_ref, wo_ref, bo_ref, gain_ref, bias_ref,
    ctx_ref, prob_ref, key_ref, word_ref, wordc_ref, normed_ref, inv_ref, low_ref,
    packed, cpick, direct, relc, keyc, attn, base,
):
    seq = k_ref.shape[0]
    picks = qc_ref.shape[0]
    chunks = seq // LANES
    units, far_units = [], []

    @pl.when(pl.program_id(0) == 0)
    def _():
        row = lax.broadcasted_iota(jnp.int32, (seq, seq), 0)
        col = lax.broadcasted_iota(jnp.int32, (seq, seq), 1)
        side = pk_ref.shape[0] // 2
        step = jnp.sum(jnp.where(col == row - 1, rel_ref[...] - side, 0), axis=1, keepdims=True)
        steps = jnp.broadcast_to(step.astype(f32), (seq, LANES)).astype(bf16)
        word_ref[...] = dot_nn((col <= row).astype(f32).astype(bf16), steps).astype(jnp.int32)
        id_bases(rel_ref, base)
        for n in range(picks):
            place = jnp.maximum(pos_ref[n], 0)
            relc[n : n + 1, :] = rel_ref[pl.ds(place, 1), :]
            wordc_ref[n : n + 1, :] = word_ref[pl.ds(place, 1), :]

    zero = jnp.zeros((), bf16)
    upper = head_lanes(0)
    for m in range(PICKED_AT_ONCE):
        lanes = slice(m * LANES, (m + 1) * LANES)
        k_pair, q_pair, pq = k_ref[:, lanes], qc_ref[:, lanes], pq_ref[:, lanes]
        table = both_alignments(pq)
        keys = [dot_nt(jnp.where(head_lanes(a), k_pair, zero), table) for a in range(2)]
        unit = pack_heads(keys[0], keys[1], packed.at[m], longest(k_pair) * longest(pq))
        units.append(unit)
        pk = pk_ref[:, lanes]
        far = []
        for a in range(2):
            q_a = jnp.where(head_lanes(a), q_pair, zero)
            far.append(dot_nt(q_a, pk))
            direct[2 * m + a] = dot_nt(q_a, k_pair)
        far_units.append(pack_heads(far[0], far[1], cpick.at[m], longest(q_pair) * longest(pk)))
    for m in range(PICKED_AT_ONCE):
        lanes = slice(m * LANES, (m + 1) * LANES)
        for g in range(chunks):
            for c in range(chunks):
                parts = []
                for start in range(g * LANES, (g + 1) * LANES, ROWS):
                    parts.append(
                        picked_words(packed.at[m], rel_ref, base, slice(start, start + ROWS), c)
                    )
                block = jnp.concatenate(parts, axis=0).T
                for a, value in enumerate(unpack_heads(block, units[m])):
                    key_ref[2 * m + a, c * LANES : (c + 1) * LANES, g * LANES : (g + 1) * LANES] = value
        for n in range(picks):
            place = jnp.maximum(pos_ref[n], 0)
            for a in range(2 * m, 2 * m + 2):
                keyc[a, n : n + 1, :] = key_ref[a, pl.ds(place, 1), :]
        scores = [[], []]
        for c in range(chunks):
            ids = relc[:, c * LANES : (c + 1) * LANES]
            index = ids & (LANES - 1)
            value = jnp.take_along_axis(cpick[m, :, :LANES], index, axis=1)
            for n in range(1, pk_ref.shape[0] // LANES):
                other = cpick[m, :, n * LANES : (n + 1) * LANES]
                value = jnp.where(
                    ids >= n * LANES, jnp.take_along_axis(other, index, axis=1), value
                )
            cols = slice(c * LANES, (c + 1) * LANES)
            for a, far in enumerate(unpack_heads(value, far_units[m])):
                scores[a].append(direct[2 * m + a, :, cols] + far + keyc[2 * m + a, :, cols])
        mixed = []
        for a in range(2 * m, 2 * m + 2):
            weights = softmax_weights(scores[a % 2])
            inverse = 1.0 / jnp.sum(sum(weights[1:], weights[0]), axis=1, keepdims=True)
            probs = jnp.concatenate([(weight * inverse).astype(bf16) for weight in weights], axis=1)
            prob_ref[a] = probs
            mixed.append(dot_nn(probs, v_ref[:, lanes]).astype(bf16))
        ctx_ref[:, lanes] = jnp.where(upper, mixed[0], mixed[1])

    part = dot_nn(ctx_ref[...], wo_ref[...])

    @pl.when(pl.program_id(0) == 0)
    def _():
        attn[...] = x_ref[...].astype(f32) + row_of(bo_ref) + part

    @pl.when(pl.program_id(0) > 0)
    def _():
        attn[...] += part

    @pl.when(pl.program_id(0) == pl.num_programs(0) - 1)
    def _():
        normed, inv_std = norm_stats(attn[...])
        normed_ref[...] = normed
        inv_ref[...] = jnp.broadcast_to(inv_std, (picks, LANES))
        low_ref[...] = (normed * row_of(gain_ref) + row_of(bias_ref)).astype(bf16)


def attend_picked(
    positions, rel_ids, q_pick, k, v, pos_query, pos_key, x_pick, w_out, b_out, gain, bias
):
    seq, width = k.shape
    picks = q_pick.shape[0]
    table = pos_key.shape[0]
    pairs = width // LANES
    whole = lambda rows, cols: pl.BlockSpec((rows, cols), lambda h: (0, 0))
    line = pl.BlockSpec((width,), lambda h: (0,))
    per = PICKED_AT_ONCE
    wide = per * LANES
    col = lambda rows: pl.BlockSpec((rows, wide), lambda h: (0, h))
    heads = lambda rows: pl.BlockSpec((2 * per, rows, seq), lambda h: (h, 0, 0))
    return pl.pallas_call(
        picked_kernel,
        grid=(pairs // per,),
        in_specs=[
            pl.BlockSpec(memory_space=pltpu.SMEM), whole(seq, seq),
            col(picks), col(seq), col(seq), col(table), col(table),
            whole(picks, width), pl.BlockSpec((wide, width), lambda h: (h, 0)), line, line, line,
        ],
        out_specs=[
            col(picks), heads(picks), heads(seq), whole(seq, LANES), whole(picks, LANES),
            whole(picks, width), whole(picks, LANES), whole(picks, width),
        ],
        out_shape=[
            jax.ShapeDtypeStruct((picks, width), bf16),
            jax.ShapeDtypeStruct((2 * pairs, picks, seq), bf16),
            jax.ShapeDtypeStruct((2 * pairs, seq, seq), f32),
            jax.ShapeDtypeStruct((seq, LANES), jnp.int32),
            jax.ShapeDtypeStruct((picks, LANES), jnp.int32),
            jax.ShapeDtypeStruct((picks, width), f32),
            jax.ShapeDtypeStruct((picks, LANES), f32),
            jax.ShapeDtypeStruct((picks, width), bf16),
        ],
        scratch_shapes=[
            pltpu.VMEM((per, seq, 2 * table), jnp.int32),
            pltpu.VMEM((per, picks, table), jnp.int32),
            pltpu.VMEM((2 * per, picks, seq), f32),
            pltpu.VMEM((picks, seq), jnp.int32),
            pltpu.VMEM((2 * per, picks, seq), f32),
            pltpu.VMEM((picks, width), f32),
            pltpu.SMEM((seq // HALF * (seq // LANES),), jnp.int32),
        ],
        compiler_params=PARAMS,
        cost_estimate=lasting(5.0 * pairs),
        name="attend_picked",
    )(
        positions, rel_ids, q_pick, k, v, pos_key, pos_query, x_pick, w_out, b_out, gain, bias
    )


def full_kernel(rel_ref, q_ref, k_ref, v_ref, pk_ref, key_ref, ctx_ref, *scratch):
    seq = rel_ref.shape[0]
    chunks = seq // LANES
    base, scratch = scratch[-1], scratch[:-1]
    count = len(scratch) // 3

    @pl.when(pl.program_id(0) == 0)
    def _():
        id_bases(rel_ref, base)

    zero = jnp.zeros((), bf16)
    units = []
    for n in range(count):
        packed, direct, low = scratch[3 * n : 3 * n + 3]
        lanes = slice(n * LANES, (n + 1) * LANES)
        q, pos = q_ref[:, lanes], pk_ref[:, lanes]
        table = both_alignments(pos)
        far = []
        for a in range(2):
            q_a = jnp.where(head_lanes(a), q, zero)
            far.append(dot_nt(q_a, table))
            direct[a] = dot_nt(q_a, k_ref[:, lanes])
        units.append(pack_heads(far[0], far[1], packed, longest(q) * longest(pos)))
    for n in range(count):
        packed, direct, low = scratch[3 * n : 3 * n + 3]
        lanes = slice(n * LANES, (n + 1) * LANES)
        for start in range(0, seq, 2 * ROWS):
            rows = slice(start, start + 2 * ROWS)
            scores = [[], []]
            for c in range(chunks):
                cols = slice(c * LANES, (c + 1) * LANES)
                values = unpack_heads(picked_words(packed, rel_ref, base, rows, c), units[n])
                for a in range(2):
                    scores[a].append(
                        values[a] + direct[a, rows, cols] + key_ref[2 * n + a, rows, cols]
                    )
            for a in range(2):
                for c in range(chunks):
                    direct[a, rows, c * LANES : (c + 1) * LANES] = scores[a][c]
        for a in range(2):
            for start in range(0, seq, LANES):
                rows = slice(start, start + LANES)
                scores = [direct[a, rows, c * LANES : (c + 1) * LANES] for c in range(chunks)]
                for c, weight in enumerate(softmax_weights(scores)):
                    low[a, rows, c * LANES : (c + 1) * LANES] = weight.astype(bf16)
        v = v_ref[:, lanes]
        mixed = [
            dot_nn(low[a], jnp.where(head_lanes(a), v, jnp.ones((), bf16))) for a in range(2)
        ]
        upper = head_lanes(0)
        totals = pltpu.roll(jnp.where(upper, mixed[1], mixed[0]), HEAD, 1)
        ctx_ref[:, lanes] = (jnp.where(upper, mixed[0], mixed[1]) * (1.0 / totals)).astype(bf16)


def attend_full(rel_ids, q, k, v, pos_key, key_scores, first, pairs):
    seq = k.shape[0]
    table = pos_key.shape[0]
    per = AT_ONCE
    wide = per * LANES
    col = lambda rows: pl.BlockSpec((rows, wide), lambda h: (0, h + first // per))
    return pl.pallas_call(
        full_kernel,
        grid=(pairs // per,),
        in_specs=[
            pl.BlockSpec((seq, seq), lambda h: (0, 0)),
            col(seq), col(seq), col(seq), col(table),
            pl.BlockSpec((2 * per, seq, seq), lambda h: (h + first // per, 0, 0)),
        ],
        out_specs=pl.BlockSpec((seq, wide), lambda h: (0, h)),
        out_shape=jax.ShapeDtypeStruct((seq, pairs * LANES), bf16),
        scratch_shapes=[
            pltpu.VMEM((seq, 2 * table), jnp.int32),
            pltpu.VMEM((2, seq, seq), f32),
            pltpu.VMEM((2, seq, seq), bf16),
        ]
        * per
        + [pltpu.SMEM((seq // HALF * (seq // LANES),), jnp.int32)],
        compiler_params=PARAMS,
        cost_estimate=lasting(4.2 * pairs),
        name="attend_full",
    )(rel_ids, q, k, v, pos_key, key_scores)


def back_kernel(
    row_ref, word_ref, wordc_ref, qc_ref, k_ref, v_ref, prob_ref, pk_ref, pq_ref,
    dz2_ref, mine_ref, got_ref, normed_ref, inv_ref, gain_ref, wo_ref, early_ref,
    dq_ref, dk_ref, dv_ref, dpos_ref, dz1_ref, dattn_ref, sum_ref,
    side, sidec, moved, movedc, expand, shrink, base,
):
    seq = k_ref.shape[0]
    picks = qc_ref.shape[0]
    table = pk_ref.shape[0]
    chunks = seq // LANES

    @pl.when(pl.program_id(0) == 0)
    def _():
        words = word_ref[...]
        for c in range(chunks):
            side[:, c * LANES : (c + 1) * LANES] = member_chunk(words, c, seq - 1)
            sidec[:, c * LANES : (c + 1) * LANES] = member_chunk(wordc_ref[...], c, seq - 1)
        group_bases(words, base)
        moved[...] = jnp.zeros_like(moved)
        edge = expand.shape[1]
        for n, start in ((0, 0), (1, 2 * seq - edge)):
            ids = row_ref[start : start + edge, :] - n * (table - LANES)
            chosen = (ids == lane_iota(edge)).astype(f32).astype(bf16)
            expand[n] = chosen
            shrink[n] = chosen.T
        dh1 = dz2_ref[...] + mine_ref[...].astype(f32) + got_ref[...].astype(f32)
        dz1, g_gain, g_bias = norm_backward(dh1, normed_ref[...], inv_ref[:, :1], row_of(gain_ref))
        dz1_ref[...] = dz1
        dattn = dz1.astype(bf16)
        dattn_ref[...] = dattn
        sum_ref[...] = jnp.concatenate(
            [col_sum(dattn.astype(f32)), g_gain, g_bias, early_ref[:5]], axis=0
        )

    lane = lane_iota()
    scale = 1.0 / math.sqrt(3.0 * HEAD)
    zero = jnp.zeros((), bf16)
    heads = range(2)
    upper = head_lanes(0)
    join = lambda pair: jnp.where(upper, pair[0], pair[1])
    side[:, seq:] = k_ref[...]
    sidec[:, seq:] = qc_ref[...]
    dctx = dot_nt(dattn_ref[...], wo_ref[...]).astype(bf16)
    dprobs = [dot_nt(jnp.where(head_lanes(a), dctx, zero), v_ref[...]) for a in heads]

    def widened(ref):
        ends = [
            dot_nn(expand[n], ref[at : at + LANES, :]).astype(bf16)
            for n, at in ((0, 0), (1, table - LANES))
        ]
        return jnp.concatenate([ends[0], ref[LANES : table - LANES, :], ends[1]], axis=0)

    far_key, far_query = widened(pk_ref), widened(pq_ref)
    gs = []
    for a in heads:
        probs = prob_ref[a].astype(f32)
        prod = probs * dprobs[a]
        gs.append(((prod - probs * jnp.sum(prod, axis=1, keepdims=True)) * scale).astype(bf16))
    outs = [dot_tn(gs[a], sidec[...]) for a in heads]
    outcs = [dot_nn(gs[a], side[...]) for a in heads]
    dv_ref[...] = join([dot_tn(prob_ref[a], dctx) for a in heads]).astype(bf16)
    place = lane - 1 - wordc_ref[...]
    index = place & (LANES - 1)
    blank = jnp.zeros((picks, LANES), f32)
    for a in heads:
        turned = [
            jnp.take_along_axis(outcs[a][:, c * LANES : (c + 1) * LANES], index, axis=1)
            for c in range(chunks)
        ]
        for c in range(2 * chunks):
            value = turned[c] if c < chunks else blank
            for n in range(1, chunks + 1):
                other = turned[c - n] if 0 <= c - n < chunks else blank
                value = jnp.where(place < -LANES * (n - 1), other, value)
            movedc[a, :, c * LANES : (c + 1) * LANES] = value.astype(bf16)
    unshift_in_order(outs, word_ref, base, moved)
    dq = [outcs[a][:, seq:] + dot_nn(movedc[a], far_key) for a in heads]
    dq_ref[...] = join(dq).astype(bf16)
    dk = [outs[a][:, seq:] + dot_nn(moved[a, :, : 2 * seq], far_query) for a in heads]
    dk_ref[...] = join(dk).astype(bf16)
    far = [
        join([dot_tn(movedc[a], qc_ref[...]) for a in heads]),
        join([dot_tn(moved[a, :, : 2 * seq], k_ref[...]) for a in heads]),
    ]
    edge = expand.shape[1]
    for n, value in enumerate(far):
        value = value.astype(bf16)
        dpos_ref[n, :LANES, :] = dot_nn(shrink[0], value[:edge]).astype(bf16)
        dpos_ref[n, LANES : table - LANES, :] = value[edge : 2 * seq - edge]
        dpos_ref[n, table - LANES :, :] = dot_nn(shrink[1], value[2 * seq - edge :]).astype(bf16)


def attend_back(
    table_of, words, words_pick, q_pick, k, v, probs, pos_query, pos_key,
    dz2, mine, got, normed, inv_std, gain, w_out, early,
):
    seq, width = k.shape
    picks = q_pick.shape[0]
    table = pos_key.shape[0]
    pairs = width // LANES
    edge = seq - table // 4
    whole = lambda value: pl.BlockSpec(value.shape, lambda h: (0,) * value.ndim)
    col = lambda rows: pl.BlockSpec((rows, LANES), lambda h: (0, h))
    shape = lambda rows: jax.ShapeDtypeStruct((rows, width), bf16)
    return pl.pallas_call(
        back_kernel,
        grid=(pairs,),
        in_specs=[
            whole(table_of), whole(words), whole(words_pick),
            col(picks), col(seq), col(seq),
            pl.BlockSpec((2, picks, seq), lambda h: (h, 0, 0)),
            col(table), col(table),
            whole(dz2), whole(mine), whole(got), whole(normed), whole(inv_std), whole(gain),
            pl.BlockSpec((LANES, width), lambda h: (h, 0)), whole(early),
        ],
        out_specs=[
            col(picks), col(seq), col(seq),
            pl.BlockSpec((2, table, LANES), lambda h: (0, 0, h)),
            whole(dz2), whole(dz2), whole(early),
        ],
        out_shape=[
            shape(picks), shape(seq), shape(seq),
            jax.ShapeDtypeStruct((2, table, width), bf16),
            jax.ShapeDtypeStruct((picks, width), f32),
            shape(picks),
            jax.ShapeDtypeStruct(early.shape, f32),
        ],
        scratch_shapes=[
            pltpu.VMEM((seq, seq + LANES), bf16),
            pltpu.VMEM((picks, seq + LANES), bf16),
            pltpu.VMEM((2, seq, 2 * seq + 2 * LANES), bf16),
            pltpu.VMEM((2, picks, 2 * seq), bf16),
            pltpu.VMEM((2, edge, LANES), bf16),
            pltpu.VMEM((2, LANES, edge), bf16),
            pltpu.SMEM((seq // LANES,), jnp.int32),
        ],
        compiler_params=PARAMS,
        cost_estimate=lasting(4.0 * pairs),
        name="attend_back",
    )(
        table_of, words, words_pick, q_pick, k, v, probs, pos_key, pos_query,
        dz2, mine, got, normed, inv_std, gain, w_out, early,
    )


def turn_kernel(
    n_all, me_ref, order_ref, x_ref, xpick_ref, cpick_ref, rel_ref, x_out, xpick_out, cpick_out, rel_out
):
    picked = order_rows(order_ref, me_ref, x_ref.shape[1], n_all)
    for ref, out in ((x_ref, x_out), (xpick_ref, xpick_out), (cpick_ref, cpick_out), (rel_ref, rel_out)):
        out[...] = dot_nt(picked, ref[...]).astype(bf16)


def block_rows(ref, me_ref):
    return me_ref[0] ^ jnp.where(me_ref[1] == 0, ref[:, 0:1], ref[:, 1:2])


def order_rows(ref, me_ref, length, n_all):
    source = block_rows(ref, me_ref) * (length // n_all) + ref[:, 2:3]
    spot = lax.broadcasted_iota(jnp.int32, (ref.shape[0], length), 1)
    return (spot == source).astype(f32).astype(bf16)


def turn_blocks(n_all, me, order, x, x_pick, ctx_pick, rel_table):
    width = x.shape[1]
    group = 2 * LANES
    whole = lambda value: pl.BlockSpec(value.shape, lambda n: (0, 0))
    row = lambda count: pl.BlockSpec((group, count), lambda n: (n, 0))
    given = [x, x_pick, ctx_pick, rel_table]
    return pl.pallas_call(
        functools.partial(turn_kernel, n_all),
        grid=(width // group,),
        in_specs=[pl.BlockSpec(memory_space=pltpu.SMEM), row(LANES)]
        + [whole(value) for value in given],
        out_specs=[row(value.shape[0]) for value in given],
        out_shape=[jax.ShapeDtypeStruct(value.shape[::-1], bf16) for value in given],
        compiler_params=PARAMS,
        cost_estimate=lasting(5.2),
        name="turn_blocks",
    )(me, order, *given)


def norm_picked_kernel(
    normed_ref, gain1_ref, bias1_ref, mine_ref, got_ref, bdown_ref, gain2_ref, grad_ref, pick_ref,
    dz2_ref, low_ref, sum_ref,
):
    h1 = normed_ref[...] * row_of(gain1_ref) + row_of(bias1_ref)
    branch = mine_ref[...].astype(f32) + got_ref[...].astype(f32) + row_of(bdown_ref)
    normed, inv_std = norm_stats(h1 + branch)
    used = jnp.sum(pick_ref[...].astype(f32), axis=1, keepdims=True)
    cot = jnp.where(used > 0.0, grad_ref[...].astype(f32), 0.0)
    dz2, g_gain, g_bias = norm_backward(cot, normed, inv_std, row_of(gain2_ref))
    dz2_ref[...] = dz2
    low = dz2.astype(bf16)
    low_ref[...] = low
    sum_ref[...] = jnp.concatenate(
        [col_sum(low.astype(f32)), g_gain, g_bias, jnp.zeros((5, h1.shape[1]), f32)], axis=0
    )


def norm_picked(normed, gain1, bias1, mine, got, b_down, gain2, grads, pick):
    picks, width = normed.shape
    return pl.pallas_call(
        norm_picked_kernel,
        out_shape=[
            jax.ShapeDtypeStruct((picks, width), f32),
            jax.ShapeDtypeStruct((picks, width), bf16),
            jax.ShapeDtypeStruct((8, width), f32),
        ],
        compiler_params=SMALL,
        cost_estimate=lasting(2.4),
        name="norm_picked",
    )(normed, gain1, bias1, mine, got, b_down, gain2, grads, pick)


def ffn_full_kernel(
    x_ref, ctx_ref, ctx2_ref, wo_ref, bo_ref, gain1_ref, bias1_ref, bdown_ref, gain2_ref, bias2_ref,
    bin_ref, bin2_ref, bin3_ref, win_ref, down_ref, win2_ref, down2_ref, win3_ref, down3_ref,
    out_ref, h1, low, total, win_here, down_here, win_sem, down_sem,
):
    rows, width = x_ref.shape
    tile = win_here.shape[2]
    parts = [(win_ref, down_ref, bin_ref, n * tile) for n in range(win_ref.shape[1] // tile)]
    parts += [(win2_ref, down2_ref, bin2_ref, 0), (win3_ref, down3_ref, bin3_ref, 0)]

    def copies(n):
        w_ref, d_ref, _, at = parts[n]
        return (
            pltpu.make_async_copy(w_ref.at[:, at : at + tile], win_here.at[n], win_sem.at[n]),
            pltpu.make_async_copy(d_ref.at[at : at + tile, :], down_here.at[n], down_sem.at[n]),
        )

    for n in range(len(parts)):
        for copy in copies(n):
            copy.start()
    attn = dot_nn(ctx_ref[...], wo_ref[: ctx_ref.shape[1]]) + dot_nn(
        ctx2_ref[...], wo_ref[ctx_ref.shape[1] :]
    )
    normed, _ = norm_stats(x_ref[...].astype(f32) + (attn + row_of(bo_ref)))
    value = normed * row_of(gain1_ref) + row_of(bias1_ref)
    h1[...] = value
    low[...] = value.astype(bf16)
    step = rows // 2
    for n in range(len(parts)):
        for copy in copies(n):
            copy.wait()
        bias = parts[n][2][:, parts[n][3] : parts[n][3] + tile]
        for at in range(0, rows, step):
            pre = dot_nn(low[at : at + step], win_here[n]) + bias
            part = dot_nn((pre * normal_cdf(pre)).astype(bf16), down_here[n])
            total[at : at + step] = part if n == 0 else total[at : at + step] + part
    normed, _ = norm_stats(h1[...] + (total[...] + row_of(bdown_ref)))
    out_ref[...] = (normed * row_of(gain2_ref) + row_of(bias2_ref)).astype(bf16)


def ffn_full(x, ctx, w_out, b_out, gain1, bias1, shards, b_down, gain2, bias2):
    rows, width = x.shape
    tile = shards[1][0].shape[1]
    count = shards[0][0].shape[1] // tile + 2
    held = [x, ctx[0], ctx[1], w_out, b_out, gain1, bias1, b_down, gain2, bias2]
    held += [shard[2] for shard in shards]
    moved = [value for shard in shards for value in shard[:2]]
    return pl.pallas_call(
        ffn_full_kernel,
        in_specs=[pl.BlockSpec(memory_space=pltpu.VMEM)] * len(held)
        + [pl.BlockSpec(memory_space=pl.ANY)] * len(moved),
        out_specs=pl.BlockSpec(memory_space=pltpu.VMEM),
        out_shape=jax.ShapeDtypeStruct((rows, width), bf16),
        scratch_shapes=[
            pltpu.VMEM((rows, width), f32), pltpu.VMEM((rows, width), bf16), pltpu.VMEM((rows, width), f32),
            pltpu.VMEM((count, width, tile), bf16), pltpu.VMEM((count, tile, width), bf16),
            pltpu.SemaphoreType.DMA((count,)), pltpu.SemaphoreType.DMA((count,)),
        ],
        compiler_params=PARAMS,
        cost_estimate=lasting(10.9),
        name="ffn_full",
    )(*held, *moved)


def token_grads_kernel(pick_ref, dz1_ref, dq_ref, dk_ref, dv_ref, wq_ref, wk_ref, wv_ref, out_ref):
    sparse = dz1_ref[...] + dot_nt(dq_ref[...], wq_ref[...])
    upper = sparse.astype(bf16)
    lower = (sparse - upper.astype(f32)).astype(bf16)
    out_ref[...] = (
        dot_nt(dk_ref[...], wk_ref[...])
        + dot_nt(dv_ref[...], wv_ref[...])
        + dot_tn(pick_ref[...], upper)
        + dot_tn(pick_ref[...], lower)
    )


def token_grads(pick, dz1, dq, dk, dv, w_query, w_key, w_value):
    seq, width = dk.shape
    group = 2 * LANES
    whole = lambda value: pl.BlockSpec(value.shape, lambda n: (0, 0))
    col = lambda rows: pl.BlockSpec((rows, group), lambda n: (0, n))
    row = pl.BlockSpec((group, width), lambda n: (n, 0))
    return pl.pallas_call(
        token_grads_kernel,
        grid=(width // group,),
        in_specs=[whole(pick), col(dz1.shape[0]), whole(dq), whole(dk), whole(dv), row, row, row],
        out_specs=col(seq),
        out_shape=jax.ShapeDtypeStruct((seq, width), f32),
        compiler_params=PARAMS,
        cost_estimate=lasting(5.9),
        name="token_grads",
    )(pick, dz1, dq, dk, dv, w_query, w_key, w_value)


def grads_kernel(
    n_all, n_ffn, unit, me_ref, order_ref, relorder_ref, taker_ref,
    x_ref, rel_ref, xpick_ref, cpick_ref, dpos_ref, dq_ref, dk_ref, dv_ref, dattn_ref,
    early_ref, bin_ref, wq_ref, wk_ref, kept_ref, sent_ref, weights, sems,
):
    width = dk_ref.shape[1]
    table = dpos_ref.shape[1]
    group = 2 * LANES
    step = pl.program_id(0)
    copies = [
        pltpu.make_async_copy(ref, weights.at[n], sems.at[n])
        for n, ref in enumerate((wk_ref, wq_ref))
    ]

    def put(at, value):
        value = value.astype(bf16)
        kept_ref[at] = value[:LANES]
        sent_ref[at] = value[LANES:]

    @pl.when(step == 0)
    def _():
        for copy in copies:
            copy.start()

    @pl.when(step != 1)
    def _():
        put(0, dot_nn(xpick_ref[...], dq_ref[...]) + dot_nn(rel_ref[...], dpos_ref[1]))
        put(1, dot_nn(x_ref[...], dk_ref[...]) + dot_nn(rel_ref[...], dpos_ref[0]))
        put(2, dot_nn(x_ref[...], dv_ref[...]))
        put(3, dot_nn(cpick_ref[...], dattn_ref[...]))

    @pl.when(step == 1)
    def _():
        for copy in copies:
            copy.wait()
        value = (dot_nt(dpos_ref[0], weights[0]) + dot_nt(dpos_ref[1], weights[1])).astype(bf16)
        value = dot_nn(order_rows(relorder_ref, me_ref, table, n_all), value)
        for n in range(table // group):
            put(n, value[n * group : (n + 1) * group])

        total = lambda value: col_sum(value.astype(f32))
        bins = [bin_ref[:1, at : at + width] for at in range(0, bin_ref.shape[1], width)]
        values = [
            total(dq_ref[...]) + total(dpos_ref[1]),
            total(dk_ref[...]) + total(dpos_ref[0]),
            total(dv_ref[...]),
            early_ref[:6],
        ]
        values += bins + [jnp.zeros((16 - VECTORS - len(bins), width), f32)]
        values = jnp.concatenate(values, axis=0)
        block = block_rows(order_ref[:group, :], me_ref)
        ours = (block % n_ffn) == (me_ref[0] % n_ffn)
        tok_place = jnp.where(ours, block // n_ffn, -1)
        row = lax.broadcasted_iota(jnp.int32, (group, 1), 0) % unit
        for n in range(16 // unit):
            rows = slice(n * unit, (n + 1) * unit)
            spread = lambda value: jnp.concatenate([value[rows]] * (group // unit), axis=0)
            taker = jnp.where(row + n * unit < VECTORS, block, tok_place)
            put(table // group + n, jnp.where(spread(taker_ref[...]) == taker, spread(values), 0.0))


def weight_grads(
    n_all, n_ffn, unit, me, order, rel_order, takers, x, rel, x_pick, c_pick, dpos, dq, dk, dv, dattn,
    w_query, w_key, early, bins,
):
    seq, width = dk.shape
    group = 2 * LANES
    steps = width // group
    each = max(4, dpos.shape[1] // group + 16 // unit)
    whole = lambda value: pl.BlockSpec(value.shape, lambda n: (0,) * value.ndim)
    row = lambda value: pl.BlockSpec((group, value.shape[1]), lambda n: (jnp.maximum(n - 1, 0), 0))
    block = pl.BlockSpec((each, LANES, width), lambda n: (n, 0, 0))
    return pl.pallas_call(
        functools.partial(grads_kernel, n_all, n_ffn, unit),
        grid=(steps + 1,),
        in_specs=[pl.BlockSpec(memory_space=pltpu.SMEM)]
        + [whole(value) for value in (order, rel_order, takers)]
        + [row(value) for value in (x, rel, x_pick, c_pick)]
        + [whole(value) for value in (dpos, dq, dk, dv, dattn, early, bins)]
        + [pl.BlockSpec(memory_space=pl.ANY)] * 2,
        out_specs=[block] * 2,
        out_shape=[jax.ShapeDtypeStruct((each * (steps + 1), LANES, width), bf16)] * 2,
        scratch_shapes=[
            pltpu.VMEM((2,) + w_query.shape, bf16), pltpu.SemaphoreType.DMA((2,)),
        ],
        compiler_params=PARAMS,
        cost_estimate=lasting(7.0),
        name="weight_grads",
    )(
        me, order, rel_order, takers, x, rel, x_pick, c_pick, dpos, dq, dk, dv, dattn, early, bins,
        w_query, w_key,
    )


def swap(values, axis, bit):
    size = lax.axis_size(axis)
    return lax.ppermute(values, axis, [(n, n ^ bit) for n in range(size)])


def after(values, *others):
    return lax.optimization_barrier((values, others))[0]


class Halving:
    def __init__(self, axes, core, near, size):
        rest = [1 << n for n in range(size.bit_length() - 1) if (1 << n) != core]
        near = [bit for bit in near if bit in rest]
        rest = [bit for bit in rest if bit not in near]
        turned = near[-1:] + near[:-1]
        self.axes, self.core, self.size = axes, core, size
        self.orders = [[core] + near + rest, [core] + turned + rest]
        self.steps = len(self.orders[0])
        self.me = lax.axis_index(axes)
        self.upper = (self.me // core) % 2

    def core_of(self, place):
        return (place // self.core) % 2

    def send(self, values, step):
        pairs = [(n, n ^ self.orders[self.core_of(n)][step]) for n in range(self.size)]
        return lax.ppermute(values, self.axes, pairs)

    def relative(self, upper):
        masks = []
        for place in range(self.size):
            bits = [(place >> (self.steps - 1 - step)) & 1 for step in range(self.steps)]
            order = self.orders[upper ^ bits[0]]
            mask = 0
            for step, bit in enumerate(bits):
                mask ^= bit * order[step]
            masks.append(mask)
        return np.array(masks, np.int32)

    def order(self, length, unit):
        spots = np.arange(length)
        group = self.size * unit
        place = spots % group // unit
        rows = [self.relative(upper)[place] for upper in range(2)]
        rows.append(spots // group * unit + spots % unit)
        return np.stack(rows).astype(np.int32)

    def matrix(self, length, unit):
        first, second, inner = self.order(length, unit)
        source = (self.me ^ jnp.where(self.upper == 0, first, second)) * (length // self.size) + inner
        spot = lax.broadcasted_iota(jnp.int32, (length, length), 0)
        return (spot == source[None, :]).astype(bf16)


def local(
    tokens, rel_ids, mask_pos, grad_vals, w_query, w_key, w_value, w_out, b_query, b_key,
    b_value, b_out, rel_table, ln1_gain, ln1_bias, w_in, b_in, w_down, b_down, ln2_gain, ln2_bias,
):
    assert rel_ids.shape[0] == 1
    seq, width = tokens.shape
    table_rows = rel_table.shape[0]
    hidden_cols = w_in.shape[1]
    pairs = width // LANES
    n_tok = lax.axis_size("tok")
    n_ffn = lax.axis_size("ffn")
    n_all = n_tok * n_ffn
    low = lambda value: value.astype(bf16)
    wide = lambda value: value.astype(f32)
    rel_ids, positions, grad_vals = rel_ids[0], mask_pos[0], grad_vals[0]

    over_all = Halving(("tok", "ffn"), n_ffn, [2 * n_ffn, 1, 4 * n_ffn], n_all)
    own, own_rel = width // n_all, table_rows // n_all
    unit = math.gcd(own, own_rel)
    group = n_all * unit
    over_tok = Halving("tok", 1, [2, 4], n_tok)
    pad = lambda value, count: np.pad(value, ((0, count - value.shape[0]), (0, 0)))
    order = jnp.asarray(pad(over_all.order(width, unit), LANES).T)
    rel_order = jnp.asarray(pad(over_all.order(table_rows, unit), LANES).T)
    spots = np.arange(width)
    takers = [spots // own] * VECTORS
    takers += [(spots + n * width) // (hidden_cols // n_tok) for n in range(hidden_cols // width)]
    takers = np.stack(takers).astype(np.int32)
    takers = jnp.asarray(np.pad(takers, ((0, 16 - takers.shape[0]), (0, 0)), constant_values=-2))
    me = jnp.stack([over_all.me, over_all.upper])
    table_of = jnp.asarray(np.repeat(distance_rows(seq, table_rows)[:, None], LANES, 1))

    core = lax.axis_index("tok") % 2
    half_cols = hidden_cols // 2
    bias_row = b_in.reshape(1, hidden_cols)
    in_half = lax.dynamic_slice_in_dim(w_in, core * half_cols, half_cols, 1)
    down_half = lax.dynamic_slice_in_dim(w_down, core * half_cols, half_cols, 0)

    pick = low(positions[:, None] == lax.broadcasted_iota(jnp.int32, (positions.shape[0], seq), 1))
    q, k, v, pos_query, pos_key, q_pick, x_pick = project(
        pick, tokens, rel_table, (w_query, w_key, w_value), (b_query, b_key, b_value)
    )
    ctx_pick, probs, key_scores, words, words_pick, normed1, inv1, h1_mine = attend_picked(
        positions, rel_ids, q_pick, k, v, pos_query, pos_key, x_pick, w_out, b_out, ln1_gain, ln1_bias
    )

    h1_theirs = swap(h1_mine, "ffn", 1)
    bias_theirs = swap(bias_row, "ffn", 1)
    x_turned, x_pick_turned, c_pick_turned, rel_turned = turn_blocks(
        n_all, me, order, tokens, x_pick, ctx_pick, rel_table
    )
    h1_both = jnp.concatenate([h1_mine, after(h1_theirs, x_turned, bias_theirs)], axis=0)
    count = h1_mine.shape[0]
    pre = dot_nn(h1_both, w_in) + b_in
    cdf = normal_cdf(pre)
    hidden = low(pre * cdf)
    slope = cdf + pre * (jnp.exp(-0.5 * pre * pre) * (1.0 / math.sqrt(2.0 * math.pi)))
    part = low(dot_nn(hidden, w_down))
    got = swap(part[count:], "ffn", 1)
    tok_order = over_tok.matrix(width, width // n_tok)
    h1_left = low(dot_nn(h1_both, lax.optimization_barrier(tok_order)))
    in_half = after(in_half, part)
    got = after(got, h1_left, in_half)
    dz2, dffn, early = norm_picked(
        normed1, ln1_gain, ln1_bias, part[:count], got, b_down, ln2_gain, grad_vals, pick
    )
    down_half = after(down_half, dffn)
    dffn_both = jnp.concatenate([dffn, after(swap(dffn, "ffn", 1), down_half)], axis=0)
    dpre = low(dot_nt(dffn_both, w_down) * slope)
    dpart = low(dot_nt(dpre, w_in))
    dgot = swap(dpart[count:], "ffn", 1)

    def halves(values, axis):
        size = values.shape[axis] // 2
        cut = lambda at: lax.slice_in_dim(values, at, at + size, axis=axis)
        return cut(0), cut(size)

    add = lambda one, other: low(wide(one) + wide(other))

    def next_halves(kept, got, axis):
        return [add(one, other) for one, other in zip(halves(kept, axis), halves(got, axis))]

    dpre_later = after(dpre, dpart)
    dffn_left = low(dot_nn(after(dffn_both, dpart), tok_order))
    gb_in = dot_nn(jnp.ones((8, 2 * count), bf16), dpre_later)
    left, right = jnp.stack([h1_left, dffn_left]), jnp.stack([dpre_later, hidden])
    product = lambda first, last: lax.dot_general(
        left[:, :, first:last], right, (((1,), (1,)), ((0,), (0,))), preferred_element_type=f32
    )
    middle, quarter = width // 2, width // 4
    ffn_sent = low(product(middle, width))
    dgot, ffn_sent = lax.optimization_barrier((dgot, ffn_sent))
    ffn_got = over_tok.send(ffn_sent, 0)
    far_in = swap(after(in_half, dgot, ffn_sent), "ffn", 1)

    ffn_sent = low(product(quarter, middle) + wide(ffn_got[:, quarter:]))
    ffn_kept = low(product(0, quarter) + wide(ffn_got[:, :quarter]))
    ffn_got = over_tok.send(ffn_sent, 1)

    def ffn_next(step, kept, got):
        if step < over_tok.steps:
            kept, sent = next_halves(kept, got, 1)
            return kept, over_tok.send(sent, step)
        return add(kept, got), None

    dq, dk, dv, dpos, dz1, dattn, early = attend_back(
        table_of, words, words_pick, q_pick, k, v, probs, pos_query, pos_key,
        dz2, dpart[:count], after(dgot, in_half, ffn_sent, ffn_kept), normed1, inv1, ln1_gain, w_out, early,
    )
    far_in, ffn_got = after((far_in, ffn_got), dk)
    ffn_kept, ffn_got = ffn_next(2, ffn_kept, ffn_got)
    near_in = swap(far_in, "tok", 1)
    far_down = swap(after(down_half, far_in), "ffn", 1)
    all_kept, all_sent = weight_grads(
        n_all, n_ffn, unit, me, order, rel_order, takers,
        x_turned, rel_turned, x_pick_turned, c_pick_turned, dpos, dq, after(dk, far_in, ffn_kept), dv,
        dattn, w_query, w_key, early, gb_in,
    )
    all_got = over_all.send(all_sent, 0)
    dk_later, dq_later = after((dk, dq), all_sent)
    grad_tokens = token_grads(pick, dz1, dq_later, dk_later, dv, w_query, w_key, w_value)
    all_kept, all_sent = next_halves(all_kept, after(all_got, grad_tokens), 1)
    ffn_step = 3
    ffn_got = after(ffn_got, grad_tokens)

    def attend(first, count, q):
        return attend_full(rel_ids, q, k, v, pos_key, key_scores, first, count)

    ctx = []
    cuts = [(0, FIRST_PAIRS), (FIRST_PAIRS, pairs - FIRST_PAIRS)]
    for step in range(1, over_all.steps):
        all_got = over_all.send(all_sent, step)
        if step <= 2:
            ctx.append(attend(*cuts[step - 1], after(q, all_sent)))
            all_got = after(all_got, ctx[-1])
            if step == 1:
                far_down = after(far_down, ctx[-1])
                near_down = swap(far_down, "tok", 1)
                all_got = after(all_got, far_down)
        elif step == 4:
            biases = [
                lax.dynamic_slice_in_dim(bias_theirs, at * half_cols, half_cols, 1)
                for at in (core, 1 - core)
            ]
            shards = [
                (w_in, w_down, bias_row), (far_in, far_down, biases[0]), (near_in, near_down, biases[1])
            ]
            output = ffn_full(
                after(tokens, all_sent), ctx, w_out, b_out, ln1_gain, ln1_bias, shards,
                b_down, ln2_gain, ln2_bias,
            )
            all_got = after(all_got, output)
        if ffn_step <= over_tok.steps:
            ffn_got = after(ffn_got, all_sent)
            if step <= 2:
                ffn_got = after(ffn_got, ctx[-1])
            ffn_kept, ffn_got = ffn_next(ffn_step, ffn_kept, ffn_got)
            ffn_step += 1
        if step < over_all.steps - 1:
            all_kept, all_sent = next_halves(all_kept, all_got, 1)
        else:
            all_sums = add(all_kept, all_got)

    steps = width // group
    sums = all_sums.reshape(steps + 1, all_sums.shape[0] // (steps + 1), unit, width)
    four = jnp.concatenate([sums[:1, :4], sums[2:, :4]], axis=0)
    s_w = [wide(four[:, n].reshape(own, width)) for n in range(4)]
    planes = table_rows // group
    s_rel = wide(sums[1, :planes].reshape(own_rel, width))
    vectors = wide(sums[1, planes : planes + 16 // unit].reshape(16, width))
    s_vec = lax.dynamic_slice_in_dim(vectors[:VECTORS], over_all.me * own, own, 1)
    part = hidden_cols // n_tok
    bins = vectors[VECTORS : VECTORS + hidden_cols // width].reshape(1, hidden_cols)
    s_bin = lax.dynamic_slice_in_dim(bins, lax.axis_index("tok") * part, part, 1)
    return (
        output,
        grad_tokens,
        s_w[0],
        s_w[1],
        s_w[2],
        s_w[3],
        s_vec[0],
        s_vec[1],
        s_vec[2],
        s_vec[3],
        s_rel,
        s_vec[4],
        s_vec[5],
        wide(ffn_kept[0]),
        s_bin,
        jnp.transpose(wide(ffn_kept[1])),
        s_vec[6],
        s_vec[7],
        s_vec[8],
    )


def solution(mesh):
    every = ("tok", "ffn")
    placed = (
        P(every, None), P(every, None, None), P(every, None), P(every, None, None),
        P(), P(), P(), P(), P(), P(), P(), P(), P(), P(), P(),
        P(None, "ffn"), P("ffn"), P("ffn", None), P(), P(), P(),
    )
    given = (
        P(every, None), P(every, None),
        P(every, None), P(every, None), P(every, None), P(every, None),
        P(every), P(every), P(every), P(every),
        P(every, None), P(every), P(every),
        P("tok", "ffn"), P("ffn", "tok"), P("ffn", "tok"),
        P(every), P(every), P(every),
    )
    return jax.shard_map(local, mesh=mesh, in_specs=placed, out_specs=given, check_vma=False)
```
